32 devices in a mesh: rep: 4 (over x, core), shard: 8 (over z, y).
Axes of the slice: x: 2, y: 2, z: 4, core: 2. Of those that a mesh axis runs over, the one named last changes fastest.
Arguments:
- tokens: bfloat16 [32768, 768], P(('rep', 'shard')), may hold values from -6 to 6
- segment_ids: int32 [32, 1024], P(('rep', 'shard')), may hold values from 0 to 3, never falling along the last dimension, each value on 1 to 768 neighbouring positions
- norm1_gain: bfloat16 [768], P('shard'), may hold values from 0.5 to 1.5
- norm1_shift: bfloat16 [768], P('shard'), may hold values from -1.75 to 1.75
- w_qkv: bfloat16 [768, 2304], P('shard'), may hold values from -0.21875 to 0.21875
- q_bias: bfloat16 [768], P('shard'), may hold values from -3 to 3
- v_bias: bfloat16 [768], P('shard'), may hold values from -3 to 3
- w_out: bfloat16 [768, 768], P('shard'), may hold values from -0.875 to 0.875
- out_bias: bfloat16 [768], P('shard'), may hold values from -3 to 3
- norm2_gain: bfloat16 [768], P('shard'), may hold values from 0.5 to 1.5
- norm2_shift: bfloat16 [768], P('shard'), may hold values from -1.75 to 1.75
- w_fc: bfloat16 [768, 3072], P('shard'), may hold values from -0.21875 to 0.21875
- fc_bias: bfloat16 [3072], P('shard'), may hold values from -3 to 3
- w_proj: bfloat16 [3072, 768], P('shard'), may hold values from -0.109375 to 0.109375
- proj_bias: bfloat16 [768], P('shard'), may hold values from -3 to 3
- cotangent: bfloat16 [32768, 768], P(('rep', 'shard')), may hold values from -6 to 6
Outputs:
- layer_out: bfloat16 [32768, 768], P(('rep', 'shard'))
- grad_tokens: bfloat16 [32768, 768], P(('rep', 'shard'))
- grad_norm1_gain: float32 [768], P('shard')
- grad_norm1_shift: float32 [768], P('shard')
- grad_w_qkv: float32 [768, 2304], P('shard')
- grad_q_bias: float32 [768], P('shard')
- grad_v_bias: float32 [768], P('shard')
- grad_w_out: float32 [768, 768], P('shard')
- grad_out_bias: float32 [768], P('shard')
- grad_norm2_gain: float32 [768], P('shard')
- grad_norm2_shift: float32 [768], P('shard')
- grad_w_fc: float32 [768, 3072], P('shard')
- grad_fc_bias: float32 [3072], P('shard')
- grad_w_proj: float32 [3072, 768], P('shard')
- grad_proj_bias: float32 [768], P('shard')
The draws below stay inside these ranges and needn't reach their ends.
All inputs are finite; a program needn't handle non-finite values.
Results may differ from the reference program's by a relative error of at most 0.014.
Values may be sent and summed in bfloat16 or wider, within the bound.
A program may use at most 320 MiB of HBM per device.

```python
import math
import jax
import jax.numpy as jnp
import numpy as np
from jax import lax

D = 768
H = 12
HEAD = 64
FF = 3072
LEN = 1024
SEQS = 32
TOKENS = 32768


def shard_levels(key, extent, cuts, smallest, largest):
    def one(axis_at, shards_of):
        draws = jax.random.uniform(jax.random.fold_in(jax.random.fold_in(key, 6), axis_at), (shards_of,), jnp.float32, smallest / len(cuts), largest / len(cuts))
        return jnp.repeat(jnp.exp(draws), extent[axis_at] // shards_of).reshape((-1,) + (1,) * (len(extent) - axis_at - 1))

    gain = one(*cuts[0])
    for cut in cuts[1:]:
        gain = gain * one(*cut)
    return gain


def profile(amount, total, bound, skew):
    loads = [(1 << 20) // math.isqrt(standing ** skew) + 1 for standing in range(2, amount + 1)]
    rest, holding = total - bound - (amount - 1), [1] * (amount - 1)
    while rest > 0:
        candidates = [i for i in range(amount - 1) if holding[i] < bound]
        whole, budget = sum([loads[i] for i in candidates]), rest
        for i in candidates:
            extra = min(bound - holding[i], max(1, budget * loads[i] // whole), rest)
            holding[i] = holding[i] + extra
            rest = rest - extra
    return np.array([bound] + holding)


def ragged_sizes(stream_key, count, total, reach, slope):
    if count == 2:
        one = jax.random.randint(stream_key, (), max(1, total - reach), min(reach, total - 1) + 1)
        return jnp.stack([one, total - one])
    lengths = jnp.asarray(profile(count, total, reach, slope), jnp.int32)
    couples = (count - 1) // 2
    donor, taker = lengths[1:1 + 2 * couples:2], lengths[2:2 + 2 * couples:2]
    room = jnp.minimum(donor - 1, reach - taker)
    passed = jax.random.randint(jax.random.fold_in(stream_key, 1), (couples,), 0, 1 << 20) % (room + 1)
    lengths = lengths.at[1:1 + 2 * couples:2].set(donor - passed).at[2:2 + 2 * couples:2].set(taker + passed)
    return lengths[jax.random.permutation(jax.random.fold_in(stream_key, 2), count)]


def scatter_about(key, shape, width, limit, cuts=(), dtype=jnp.bfloat16):
    level = shard_levels(key, shape, cuts, -0.22, 0.18) if cuts else 1.0
    array = jax.random.normal(key, shape, jnp.float32) * width * level
    return jnp.minimum(jnp.maximum(array, -limit), limit).astype(dtype)


def setup_inputs(seed: int = 0) -> dict:
    seeds = jax.random.split(jax.random.key(seed), 17)
    return {
        "tokens": scatter_about(seeds[0], (TOKENS, D), 1.0, 6.0, ((0, 32),)),
        "segment_ids": jax.vmap(lambda own: jnp.searchsorted(jnp.cumsum(ragged_sizes(own, 4, LEN, LEN * 3 // 4, 0)), jnp.arange(LEN), side="right"))(jax.random.split(seeds[1], SEQS)).reshape((SEQS, LEN)).astype(jnp.int32),
        "norm1_gain": jnp.clip(1.0 + 0.1 * jax.random.normal(seeds[2], (D,), jnp.float32), 0.5, 1.5).astype(jnp.bfloat16),
        "norm1_shift": scatter_about(seeds[3], (D,), 0.3, 1.75, ((0, 8),)),
        "w_qkv": scatter_about(seeds[4], (D, 3 * D), D ** -0.5, 0.21875, ((0, 8),)),
        "q_bias": scatter_about(seeds[5], (D,), 0.5, 3.0, ((0, 8),)),
        "v_bias": scatter_about(seeds[6], (D,), 0.5, 3.0, ((0, 8),)),
        "w_out": scatter_about(seeds[7], (D, D), (D // 16) ** -0.5, 0.875, ((0, 8),)),
        "out_bias": scatter_about(seeds[8], (D,), 0.5, 3.0, ((0, 8),)),
        "norm2_gain": jnp.clip(1.0 + 0.1 * jax.random.normal(seeds[9], (D,), jnp.float32), 0.5, 1.5).astype(jnp.bfloat16),
        "norm2_shift": scatter_about(seeds[10], (D,), 0.3, 1.75, ((0, 8),)),
        "w_fc": scatter_about(seeds[11], (D, FF), D ** -0.5, 0.21875, ((0, 8),)),
        "fc_bias": scatter_about(seeds[12], (FF,), 0.5, 3.0, ((0, 8),)),
        "w_proj": scatter_about(seeds[13], (FF, D), FF ** -0.5, 0.109375, ((0, 8),)),
        "proj_bias": scatter_about(seeds[14], (D,), 0.5, 3.0, ((0, 8),)),
        "cotangent": scatter_about(seeds[15], (TOKENS, D), 1.0, 6.0, ((0, 32),)),
    }


@jax.custom_vjp
def low(v):
    return lax.optimization_barrier(v.astype(jnp.bfloat16)).astype(jnp.float32)

@jax.custom_vjp
def low_back(v):
    return v

def low_keep(v):
    return (low(v), None)

def low_pass(kept, grad):
    return (grad,)

def back_keep(v):
    return (v, None)

def back_low(kept, grad):
    return (low(grad),)
low.defvjp(low_keep, low_pass)
low_back.defvjp(back_keep, back_low)
EPSILON = 1e-05
HIGH = lax.Precision.HIGHEST

def layer_norm(values, norm_gain, norm_shift):
    row_mean = lax.optimization_barrier(jnp.mean(values, axis=-1, keepdims=True))
    centred = values - row_mean
    row_var = lax.optimization_barrier(jnp.mean(centred * centred, axis=-1, keepdims=True))
    return centred * lax.rsqrt(row_var + EPSILON) * norm_gain + norm_shift

def attend_one(pieces):
    queries, key_rows, value_rows, segment = pieces
    length = queries.shape[0]
    scores = jnp.einsum('qhd,khd->hqk', queries, key_rows, precision=HIGH) * HEAD ** (-0.5)
    scores = low_back(scores)
    position = jnp.arange(length)
    allowed = (segment[:, None] == segment[None, :]) & (position[None, :] <= position[:, None])
    scores = jnp.where(allowed[None], scores, -1e+30)
    row_max = lax.optimization_barrier(jnp.max(scores, axis=-1, keepdims=True))
    exp_terms = jnp.exp(scores - row_max)
    probs = low(exp_terms / lax.optimization_barrier(jnp.sum(exp_terms, axis=-1, keepdims=True)))
    return jnp.einsum('hqk,khd->qhd', probs, value_rows, precision=HIGH)

def forward_group(tok_rows, seg_rows, params):
    norm1_gain, norm1_shift, w_qkv, q_bias, v_bias, w_out, out_bias, norm2_gain, norm2_shift, w_fc, fc_bias, w_proj, proj_bias = params
    row_count = tok_rows.shape[0]
    normed1 = low(layer_norm(tok_rows, norm1_gain, norm1_shift))
    qkv_bias = jnp.concatenate([q_bias, jnp.zeros_like(q_bias), v_bias])
    projected = low(low_back(jnp.dot(normed1, w_qkv, precision=HIGH) + qkv_bias))
    projected = projected.reshape(-1, LEN, 3, H, HEAD)
    mixed = lax.map(jax.checkpoint(attend_one), (projected[:, :, 0], projected[:, :, 1], projected[:, :, 2], seg_rows))
    attended = low(low_back(mixed.reshape(row_count, D)))
    middle = tok_rows + low_back(jnp.dot(attended, w_out, precision=HIGH)) + out_bias
    normed2 = low(layer_norm(middle, norm2_gain, norm2_shift))
    preact = low_back(jnp.dot(normed2, w_fc, precision=HIGH) + fc_bias)
    activated = low(jax.nn.gelu(preact, approximate=True))
    return middle + jnp.dot(activated, w_proj, precision=HIGH) + proj_bias

def reference(tokens, segment_ids, norm1_gain, norm1_shift, w_qkv, q_bias, v_bias, w_out, out_bias, norm2_gain, norm2_shift, w_fc, fc_bias, w_proj, proj_bias, cotangent):
    params = (norm1_gain.astype(jnp.float32), norm1_shift.astype(jnp.float32), w_qkv.astype(jnp.float32), q_bias.astype(jnp.float32), v_bias.astype(jnp.float32), w_out.astype(jnp.float32), out_bias.astype(jnp.float32), norm2_gain.astype(jnp.float32), norm2_shift.astype(jnp.float32), w_fc.astype(jnp.float32), fc_bias.astype(jnp.float32), w_proj.astype(jnp.float32), proj_bias.astype(jnp.float32))
    group_size = 4
    token_groups = tokens.astype(jnp.float32).reshape(-1, group_size * LEN, D)
    segment_groups = segment_ids.reshape(-1, group_size, LEN)
    cot_groups = cotangent.astype(jnp.float32).reshape(-1, group_size * LEN, D)

    def one_group(sums, pieces):
        tok_rows, seg_rows, cot_rows = pieces
        out_rows, pull_back = jax.vjp(lambda rows, weights: forward_group(rows, seg_rows, weights), tok_rows, params)
        grad_rows, grad_weights = pull_back(cot_rows)
        sums = jax.tree.map(lambda a, b: a + b, sums, grad_weights)
        return (sums, (out_rows.astype(jnp.bfloat16), grad_rows.astype(jnp.bfloat16)))
    zero_sums = jax.tree.map(jnp.zeros_like, params)
    sums, (layer_out, grad_tokens) = lax.scan(one_group, zero_sums, (token_groups, segment_groups, cot_groups))
    return (layer_out.reshape(-1, D), grad_tokens.reshape(-1, D), sums[0], sums[1], sums[2], sums[3], sums[4], sums[5], sums[6], sums[7], sums[8], sums[9], sums[10], sums[11], sums[12])
```

```python
from functools import partial

import jax
import jax.numpy as jnp
from jax import lax
from jax.experimental import pallas as pl
from jax.experimental.pallas import tpu as pltpu
from jax.sharding import PartitionSpec as P

HEAD = 64
EPSILON = 1e-05
QUERY_BLOCK = 256
ROW_CHUNK = 256
MASKED = -1e30
GELU_SCALE = 0.7978845608028654
GELU_CUBE = 0.044715
VMEM_LIMIT = 62 << 20
NN = (((1,), (0,)), ((), ()))
NT = (((1,), (1,)), ((), ()))
f32 = jnp.float32
bf16 = jnp.bfloat16
WHOLE = pl.BlockSpec(memory_space=pltpu.VMEM)

GAIN1, SHIFT1, BIAS_Q, BIAS_V, BIAS_OUT, GAIN2, SHIFT2, BIAS_PROJ, BIAS_FC = range(9)


def matmul(left, right, dims):
    return lax.dot_general(left, right, dims, preferred_element_type=f32)


def normalized(values):
    centred = values - jnp.mean(values, axis=-1, keepdims=True)
    inverse = lax.rsqrt(jnp.mean(centred * centred, axis=-1, keepdims=True) + EPSILON)
    return centred * inverse, inverse


def norm_pull(grad_normed, gain_row, norm, inverse):
    scaled = grad_normed * gain_row
    return inverse * (
        scaled
        - jnp.mean(scaled, axis=-1, keepdims=True)
        - norm * jnp.mean(scaled * norm, axis=-1, keepdims=True)
    )


def total(values):
    return jnp.sum(values, axis=0, keepdims=True)


def block(index, size):
    return pl.ds(pl.multiple_of(index * size, size), size)


def build_mask(segment_ref, mask_ref):
    length = segment_ref.shape[1]
    query_seg = segment_ref[...].astype(f32)
    key_seg = jnp.transpose(jnp.broadcast_to(query_seg, (8, length)))[:, 0:1]
    for start in range(0, length, QUERY_BLOCK):
        stop = start + QUERY_BLOCK
        key_at = lax.broadcasted_iota(jnp.int32, (stop, QUERY_BLOCK), 0)
        query_at = lax.broadcasted_iota(jnp.int32, (stop, QUERY_BLOCK), 1) + start
        allowed = (key_seg[0:stop] == query_seg[:, start:stop]) & (key_at <= query_at)
        mask_ref[0:stop, start:stop] = jnp.where(allowed, 0.0, MASKED)


def half_lanes(which):
    lane = lax.broadcasted_iota(jnp.int32, (1, 2 * HEAD), 1)
    return (lane < HEAD) if which == 0 else (lane >= HEAD)


def keep_half(values, which):
    return jnp.where(half_lanes(which), values, jnp.zeros_like(values))


def attend_forward(pair, projected_ref, values_t_ref, mask_ref, attended_t_ref, lse_ref):
    length, width = projected_ref.shape[0], projected_ref.shape[1] // 3
    pairs = width // (2 * HEAD)
    queries = projected_ref[:, block(pair, 2 * HEAD)] * bf16(HEAD**-0.5)
    keys = projected_ref[:, block(pairs + pair, 2 * HEAD)]
    for which in range(2):
        head_queries = keep_half(queries, which)
        rows = block(2 * pair + which, HEAD)
        values_t = values_t_ref[rows, :]
        for start in range(0, length, QUERY_BLOCK):
            stop = start + QUERY_BLOCK
            scores = matmul(keys[0:stop], head_queries[start:stop], NT)
            scores = scores + mask_ref[0:stop, start:stop]
            top = jnp.max(scores, axis=0, keepdims=True)
            terms = jnp.exp(scores - top)
            sums = jnp.sum(terms, axis=0, keepdims=True)
            mixed = matmul(values_t[:, 0:stop], terms.astype(bf16), NN)
            attended_t_ref[rows, start:stop] = (mixed * (1.0 / sums)).astype(bf16)
            lse_ref[pl.ds(2 * pair + which, 1), start:stop] = top + jnp.log(sums)


def attend_backward(
    pair,
    projected_ref,
    keys_t_ref,
    grad_attended_ref,
    mask_ref,
    lse_ref,
    dots_ref,
    grad_queries_t_ref,
    grad_projected_ref,
    grad_keys_ref,
    grad_values_ref,
):
    length, width = projected_ref.shape[0], projected_ref.shape[1] // 3
    pairs = width // (2 * HEAD)
    scale_by = HEAD**-0.5
    queries = projected_ref[:, block(pair, 2 * HEAD)] * bf16(scale_by)
    keys = projected_ref[:, block(pairs + pair, 2 * HEAD)]
    values = projected_ref[:, block(2 * pairs + pair, 2 * HEAD)]
    grads = grad_attended_ref[:, block(pair, 2 * HEAD)]
    for start in reversed(range(0, length, QUERY_BLOCK)):
        stop = start + QUERY_BLOCK
        grad_keys = grad_values = 0.0
        for which in range(2):
            head = pl.ds(2 * pair + which, 1)
            rows = block(2 * pair + which, HEAD)
            query_rows = keep_half(queries[start:stop], which)
            grad_rows = keep_half(grads[start:stop], which)
            scores = matmul(keys[0:stop], query_rows, NT)
            probs = jnp.exp(scores + mask_ref[0:stop, start:stop] - lse_ref[head, start:stop])
            grad_probs = matmul(values[0:stop], grad_rows, NT)
            grad_scores = (probs * (grad_probs - dots_ref[head, start:stop])).astype(bf16)
            grad_values = grad_values + matmul(probs.astype(bf16), grad_rows, NN)
            grad_keys = grad_keys + matmul(grad_scores, query_rows, NN)
            grad_queries_t_ref[rows, start:stop] = (
                matmul(keys_t_ref[rows, 0:stop], grad_scores, NN) * scale_by
            )
        if stop == length:
            grad_keys_ref[...] = grad_keys
            grad_values_ref[...] = grad_values
        else:
            grad_keys_ref[0:stop] += grad_keys
            grad_values_ref[0:stop] += grad_values
    grad_projected_ref[:, block(pairs + pair, 2 * HEAD)] = grad_keys_ref[...].astype(bf16)
    grad_projected_ref[:, block(2 * pairs + pair, 2 * HEAD)] = grad_values_ref[...].astype(bf16)


def forward_kernel(
    tokens_ref,
    segment_ref,
    params_ref,
    w_qkv_ref,
    projected_ref,
    attended_t_ref,
    lse_ref,
    mask_ref,
    normed_ref,
    values_t_ref,
):
    length, width = tokens_ref.shape
    row = lambda at: params_ref[at : at + 1, :]
    for at in range(0, length, ROW_CHUNK):
        norm, _ = normalized(tokens_ref[at : at + ROW_CHUNK].astype(f32))
        normed_ref[at : at + ROW_CHUNK] = (norm * row(GAIN1) + row(SHIFT1)).astype(bf16)
    for part, bias in enumerate((row(BIAS_Q), 0.0, row(BIAS_V))):
        columns = slice(part * width, (part + 1) * width)
        projected_ref[:, columns] = (
            matmul(normed_ref[...], w_qkv_ref[:, columns], NN) + bias
        ).astype(bf16)
    build_mask(segment_ref, mask_ref)
    values_t_ref[...] = jnp.transpose(projected_ref[:, 2 * width :])

    @pl.loop(0, width // (2 * HEAD))
    def _(pair):
        attend_forward(pair, projected_ref, values_t_ref, mask_ref, attended_t_ref, lse_ref)


def hidden_kernel(
    attended_t_ref,
    tokens_ref,
    cotangent_ref,
    params_ref,
    w_out_ref,
    w_fc_ref,
    w_proj_ref,
    layer_out_ref,
    grad_middle_ref,
    grad_attended_ref,
    grad_w_out_ref,
    grad_w_fc_ref,
    grad_w_proj_t_ref,
    small_ref,
    middle_ref,
    normed_ref,
    normed_t_ref,
    cotangent_t_ref,
    mixed_ref,
    grad_normed_ref,
    activated_ref,
    grad_preact_ref,
):
    step, steps = pl.program_id(0), pl.num_programs(0)
    length, width = tokens_ref.shape
    row = lambda at: params_ref[at : at + 1, :]
    chunks = [slice(at, at + ROW_CHUNK) for at in range(0, length, ROW_CHUNK)]

    @pl.when(step == 0)
    def _():
        attended = jnp.transpose(attended_t_ref[...])
        middle_ref[...] = (
            tokens_ref[...].astype(f32) + matmul(attended, w_out_ref[...], NN) + row(BIAS_OUT)
        )
        for rows in chunks:
            norm, _ = normalized(middle_ref[rows])
            normed_ref[rows] = (norm * row(GAIN2) + row(SHIFT2)).astype(bf16)
        normed_t_ref[...] = jnp.transpose(normed_ref[...])
        cotangent_t_ref[...] = jnp.transpose(cotangent_ref[...])
        mixed_ref[...] = jnp.zeros_like(mixed_ref)
        grad_normed_ref[...] = jnp.zeros_like(grad_normed_ref)
        small_ref[...] = jnp.zeros_like(small_ref)

    bias_sum = 0.0
    bias_row = params_ref[pl.ds(BIAS_FC + step, 1), :]
    for rows in chunks:
        preact = matmul(normed_ref[rows], w_fc_ref[...], NN) + bias_row
        grad_act = matmul(cotangent_ref[rows], w_proj_ref[...], NT)
        square = preact * preact
        bend = jnp.tanh(GELU_SCALE * preact * (1.0 + GELU_CUBE * square))
        gate = 0.5 + 0.5 * bend
        activated_ref[rows] = (preact * gate).astype(bf16)
        slope = gate + (0.5 * GELU_SCALE) * preact * (1.0 - bend * bend) * (
            1.0 + (3 * GELU_CUBE) * square
        )
        grad_preact = (slope * grad_act).astype(bf16)
        grad_preact_ref[rows] = grad_preact
        bias_sum = bias_sum + total(grad_preact.astype(f32))
    small_ref[pl.ds(BIAS_FC + step, 1), :] = bias_sum
    mixed_ref[...] += matmul(activated_ref[...], w_proj_ref[...], NN)
    grad_w_proj_t_ref[...] = matmul(cotangent_t_ref[...], activated_ref[...], NN).astype(bf16)
    grad_w_fc_ref[...] = matmul(normed_t_ref[...], grad_preact_ref[...], NN).astype(bf16)
    grad_normed_ref[...] += matmul(grad_preact_ref[...], w_fc_ref[...], NT)

    @pl.when(step == steps - 1)
    def _():
        sums = [0.0] * 4
        for rows in chunks:
            middle = middle_ref[rows]
            layer_out_ref[rows] = (middle + mixed_ref[rows] + row(BIAS_PROJ)).astype(bf16)
            norm, inverse = normalized(middle)
            grad_normed = grad_normed_ref[rows]
            cotangent = cotangent_ref[rows].astype(f32)
            grad_middle = cotangent + norm_pull(grad_normed, row(GAIN2), norm, inverse)
            grad_middle_ref[rows] = grad_middle
            normed_ref[rows] = grad_middle.astype(bf16)
            terms = (grad_middle, grad_normed * norm, grad_normed, cotangent)
            sums = [a + total(b) for a, b in zip(sums, terms)]
        for at, value in zip((BIAS_OUT, GAIN2, SHIFT2, BIAS_PROJ), sums):
            small_ref[at : at + 1, :] = value
        grad_branch = normed_ref[...]
        grad_w_out_ref[...] = matmul(attended_t_ref[...], grad_branch, NN).astype(bf16)
        grad_attended_ref[...] = matmul(grad_branch, w_out_ref[...], NT).astype(bf16)


def backward_kernel(
    tokens_ref,
    segment_ref,
    params_ref,
    w_qkv_ref,
    projected_ref,
    attended_t_ref,
    lse_ref,
    grad_attended_ref,
    grad_middle_ref,
    small_in_ref,
    grad_tokens_ref,
    grad_w_qkv_ref,
    small_ref,
    mask_ref,
    wide_t_ref,
    grad_queries_t_ref,
    dots_ref,
    grad_projected_ref,
    grad_keys_ref,
    grad_values_ref,
):
    length, width = tokens_ref.shape
    row = lambda at: params_ref[at : at + 1, :]
    build_mask(segment_ref, mask_ref)
    wide_t_ref[...] = jnp.transpose(grad_attended_ref[...])
    for head in range(width // HEAD):
        rows = slice(head * HEAD, (head + 1) * HEAD)
        dots_ref[head : head + 1, :] = total(
            wide_t_ref[rows].astype(f32) * attended_t_ref[rows].astype(f32)
        )
    wide_t_ref[...] = jnp.transpose(projected_ref[:, width : 2 * width])

    @pl.loop(0, width // (2 * HEAD))
    def _(pair):
        attend_backward(
            pair,
            projected_ref,
            wide_t_ref,
            grad_attended_ref,
            mask_ref,
            lse_ref,
            dots_ref,
            grad_queries_t_ref,
            grad_projected_ref,
            grad_keys_ref,
            grad_values_ref,
        )

    grad_projected_ref[:, 0:width] = jnp.transpose(grad_queries_t_ref[...].astype(bf16))
    for at in range(0, length, ROW_CHUNK):
        norm, _ = normalized(tokens_ref[at : at + ROW_CHUNK].astype(f32))
        normed = (norm * row(GAIN1) + row(SHIFT1)).astype(bf16)
        wide_t_ref[:, at : at + ROW_CHUNK] = jnp.transpose(normed)
    small_ref[...] = small_in_ref[...]
    for part in range(3):
        columns = slice(part * width, (part + 1) * width)
        grad_part = grad_projected_ref[:, columns]
        grad_w_qkv_ref[:, columns] = matmul(wide_t_ref[...], grad_part, NN).astype(bf16)
        if part != 1:
            at = BIAS_Q if part == 0 else BIAS_V
            small_ref[at : at + 1, :] = total(grad_part.astype(f32))
    gain_sum = shift_sum = 0.0
    for at in range(0, length, ROW_CHUNK):
        rows = slice(at, at + ROW_CHUNK)
        grad_normed = matmul(grad_projected_ref[rows], w_qkv_ref[...], NT)
        norm, inverse = normalized(tokens_ref[rows].astype(f32))
        grad_rows = norm_pull(grad_normed, row(GAIN1), norm, inverse)
        grad_tokens_ref[rows] = (grad_middle_ref[rows] + grad_rows).astype(bf16)
        gain_sum = gain_sum + total(grad_normed * norm)
        shift_sum = shift_sum + total(grad_normed)
    small_ref[GAIN1 : GAIN1 + 1, :] = gain_sum
    small_ref[SHIFT1 : SHIFT1 + 1, :] = shift_sum


def kernel_params():
    return pltpu.CompilerParams(vmem_limit_bytes=VMEM_LIMIT)


def run_forward(tokens, segment, params, w_qkv):
    length, width = tokens.shape
    return pl.pallas_call(
        forward_kernel,
        in_specs=[WHOLE] * 4,
        out_specs=(WHOLE,) * 3,
        out_shape=(
            jax.ShapeDtypeStruct((length, 3 * width), bf16),
            jax.ShapeDtypeStruct((width, length), bf16),
            jax.ShapeDtypeStruct((16, length), f32),
        ),
        scratch_shapes=[
            pltpu.VMEM((length, length), f32),
            pltpu.VMEM((length, width), bf16),
            pltpu.VMEM((width, length), bf16),
        ],
        compiler_params=kernel_params(),
        name="forward",
    )(tokens, segment, params, w_qkv)


def run_hidden(attended_t, tokens, cotangent, params, w_out, w_fc, w_proj):
    length, width = tokens.shape
    hidden = w_fc.shape[1]
    shape = jax.ShapeDtypeStruct
    columns = pl.BlockSpec((width, width), lambda step: (0, step))
    return pl.pallas_call(
        hidden_kernel,
        grid=(hidden // width,),
        in_specs=[WHOLE] * 5 + [columns, pl.BlockSpec((width, width), lambda step: (step, 0))],
        out_specs=(WHOLE, WHOLE, WHOLE, WHOLE, columns, columns, WHOLE),
        out_shape=(
            shape((length, width), bf16),
            shape((length, width), f32),
            shape((length, width), bf16),
            shape((width, width), bf16),
            shape((width, hidden), bf16),
            shape((width, hidden), bf16),
            shape((16, width), f32),
        ),
        scratch_shapes=[
            pltpu.VMEM((length, width), f32),
            pltpu.VMEM((length, width), bf16),
            pltpu.VMEM((width, length), bf16),
            pltpu.VMEM((width, length), bf16),
            pltpu.VMEM((length, width), f32),
            pltpu.VMEM((length, width), f32),
            pltpu.VMEM((length, width), bf16),
            pltpu.VMEM((length, width), bf16),
        ],
        compiler_params=kernel_params(),
        name="hidden",
    )(attended_t, tokens, cotangent, params, w_out, w_fc, w_proj)


def run_backward(
    tokens, segment, params, w_qkv, projected, attended_t, lse, grad_attended, grad_middle, small
):
    length, width = tokens.shape
    shape = jax.ShapeDtypeStruct
    return pl.pallas_call(
        backward_kernel,
        in_specs=[WHOLE] * 10,
        out_specs=(WHOLE,) * 3,
        out_shape=(
            shape((length, width), bf16),
            shape((width, 3 * width), bf16),
            shape((16, width), f32),
        ),
        scratch_shapes=[
            pltpu.VMEM((length, length), f32),
            pltpu.VMEM((width, length), bf16),
            pltpu.VMEM((width, length), f32),
            pltpu.VMEM((16, length), f32),
            pltpu.VMEM((length, 3 * width), bf16),
            pltpu.VMEM((length, 2 * HEAD), f32),
            pltpu.VMEM((length, 2 * HEAD), f32),
        ],
        compiler_params=kernel_params(),
        name="backward",
    )(
        tokens,
        segment,
        params,
        w_qkv,
        projected,
        attended_t,
        lse,
        grad_attended,
        grad_middle,
        small,
    )


def on_device(
    tokens,
    segment_ids,
    norm1_gain,
    norm1_shift,
    w_qkv,
    q_bias,
    v_bias,
    w_out,
    out_bias,
    norm2_gain,
    norm2_shift,
    w_fc,
    fc_bias,
    w_proj,
    proj_bias,
    cotangent,
):
    width = tokens.shape[1]
    gather = partial(lax.all_gather, axis_name="shard", axis=0, tiled=True)
    vectors = (
        norm1_gain,
        norm1_shift,
        q_bias,
        v_bias,
        out_bias,
        norm2_gain,
        norm2_shift,
        proj_bias,
    )
    own = norm1_gain.shape[0]
    packed = jnp.concatenate(vectors + (fc_bias,))
    packed = lax.all_gather(packed, "shard", axis=0)
    rows = packed[:, : 8 * own].reshape(-1, 8, own).transpose(1, 0, 2).reshape(8, width)
    params = jnp.concatenate([rows, packed[:, 8 * own :].reshape(-1, width)]).astype(f32)
    params = jnp.pad(params, ((0, 16 - params.shape[0]), (0, 0)))
    full_qkv, full_out, full_fc, full_proj = (gather(w) for w in (w_qkv, w_out, w_fc, w_proj))
    projected, attended_t, lse = run_forward(tokens, segment_ids, params, full_qkv)
    (
        layer_out,
        grad_middle,
        grad_attended,
        grad_w_out,
        grad_w_fc,
        grad_w_proj_t,
        small,
    ) = run_hidden(attended_t, tokens, cotangent, params, full_out, full_fc, full_proj)
    grad_tokens, grad_w_qkv, small = run_backward(
        tokens,
        segment_ids,
        params,
        full_qkv,
        projected,
        attended_t,
        lse,
        grad_attended,
        grad_middle,
        small,
    )

    def reduced(grad, dim):
        mine = lax.psum_scatter(grad.astype(f32), "shard", scatter_dimension=dim, tiled=True)
        return lax.psum(mine.astype(bf16), "rep").astype(f32)

    sum_proj = reduced(grad_w_proj_t, 1).T
    sum_fc = reduced(grad_w_fc, 0)
    sum_out = reduced(grad_w_out, 0)
    sum_qkv = reduced(grad_w_qkv, 0)
    small = lax.psum(small, ("rep", "shard"))
    me = lax.axis_index("shard")
    mine = lax.dynamic_slice_in_dim(small[:8], me * own, own, 1)
    hidden_rows = small[BIAS_FC : BIAS_FC + w_fc.shape[1] // width].reshape(-1)
    mine_fc = lax.dynamic_slice_in_dim(hidden_rows, me * fc_bias.shape[0], fc_bias.shape[0], 0)
    return (
        layer_out,
        grad_tokens,
        mine[GAIN1],
        mine[SHIFT1],
        sum_qkv,
        mine[BIAS_Q],
        mine[BIAS_V],
        sum_out,
        mine[BIAS_OUT],
        mine[GAIN2],
        mine[SHIFT2],
        sum_fc,
        mine_fc,
        sum_proj,
        mine[BIAS_PROJ],
    )


def solution(mesh):
    rows, own, own_rows = P(("rep", "shard"), None), P("shard"), P("shard", None)
    in_specs = (
        rows,
        rows,
        own,
        own,
        own_rows,
        own,
        own,
        own_rows,
        own,
        own,
        own,
        own_rows,
        own,
        own_rows,
        own,
        rows,
    )
    out_specs = (
        rows,
        rows,
        own,
        own,
        own_rows,
        own,
        own,
        own_rows,
        own,
        own,
        own,
        own_rows,
        own,
        own_rows,
        own,
    )
    return jax.shard_map(
        on_device, mesh=mesh, in_specs=in_specs, out_specs=out_specs, check_vma=False
    )
```

```python
from functools import partial

import jax
import jax.numpy as jnp
from jax import lax
from jax.experimental import pallas as pl
from jax.experimental.pallas import tpu as pltpu
from jax.sharding import PartitionSpec as P

HEAD = 64
EPSILON = 1e-05
QUERY_BLOCK = 256
ROW_CHUNK = 256
MASKED = -1e30
GELU_SCALE = 0.7978845608028654
GELU_CUBE = 0.044715
VMEM_LIMIT = 62 << 20
NN = (((1,), (0,)), ((), ()))
NT = (((1,), (1,)), ((), ()))
f32 = jnp.float32
bf16 = jnp.bfloat16
WHOLE = pl.BlockSpec(memory_space=pltpu.VMEM)

GAIN1, SHIFT1, BIAS_Q, BIAS_V, BIAS_OUT, GAIN2, SHIFT2, BIAS_PROJ, BIAS_FC = range(9)


def matmul(left, right, dims):
    return lax.dot_general(left, right, dims, preferred_element_type=f32)


def normalized(values):
    centred = values - jnp.mean(values, axis=-1, keepdims=True)
    inverse = lax.rsqrt(jnp.mean(centred * centred, axis=-1, keepdims=True) + EPSILON)
    return centred * inverse, inverse


def norm_pull(grad_normed, gain_row, norm, inverse):
    scaled = grad_normed * gain_row
    return inverse * (
        scaled
        - jnp.mean(scaled, axis=-1, keepdims=True)
        - norm * jnp.mean(scaled * norm, axis=-1, keepdims=True)
    )


def total(values):
    return jnp.sum(values, axis=0, keepdims=True)


def block(index, size):
    return pl.ds(pl.multiple_of(index * size, size), size)


def build_mask(segment_ref, mask_ref):
    length = segment_ref.shape[1]
    query_seg = segment_ref[...].astype(f32)
    key_seg = jnp.transpose(jnp.broadcast_to(query_seg, (8, length)))[:, 0:1]
    for start in range(0, length, QUERY_BLOCK):
        stop = start + QUERY_BLOCK
        key_at = lax.broadcasted_iota(jnp.int32, (stop, QUERY_BLOCK), 0)
        query_at = lax.broadcasted_iota(jnp.int32, (stop, QUERY_BLOCK), 1) + start
        allowed = (key_seg[0:stop] == query_seg[:, start:stop]) & (key_at <= query_at)
        mask_ref[0:stop, start:stop] = jnp.where(allowed, 0.0, MASKED)


def half_lanes(which):
    lane = lax.broadcasted_iota(jnp.int32, (1, 2 * HEAD), 1)
    return (lane < HEAD) if which == 0 else (lane >= HEAD)


def keep_half(values, which):
    return jnp.where(half_lanes(which), values, jnp.zeros_like(values))


def attend_forward(pair, projected_ref, values_t_ref, mask_ref, attended_t_ref, lse_ref):
    length, width = projected_ref.shape[0], projected_ref.shape[1] // 3
    pairs = width // (2 * HEAD)
    queries = projected_ref[:, block(pair, 2 * HEAD)] * bf16(HEAD**-0.5)
    keys = projected_ref[:, block(pairs + pair, 2 * HEAD)]
    for which in range(2):
        head_queries = keep_half(queries, which)
        rows = block(2 * pair + which, HEAD)
        values_t = values_t_ref[rows, :]
        for start in range(0, length, QUERY_BLOCK):
            stop = start + QUERY_BLOCK
            scores = matmul(keys[0:stop], head_queries[start:stop], NT)
            scores = scores + mask_ref[0:stop, start:stop]
            top = jnp.max(scores, axis=0, keepdims=True)
            terms = jnp.exp(scores - top)
            sums = jnp.sum(terms, axis=0, keepdims=True)
            mixed = matmul(values_t[:, 0:stop], terms.astype(bf16), NN)
            attended_t_ref[rows, start:stop] = (mixed * (1.0 / sums)).astype(bf16)
            lse_ref[pl.ds(2 * pair + which, 1), start:stop] = top + jnp.log(sums)


def attend_backward(
    pair,
    projected_ref,
    keys_t_ref,
    grad_attended_ref,
    mask_ref,
    lse_ref,
    dots_ref,
    grad_queries_t_ref,
    grad_projected_ref,
    grad_keys_ref,
    grad_values_ref,
):
    length, width = projected_ref.shape[0], projected_ref.shape[1] // 3
    pairs = width // (2 * HEAD)
    scale_by = HEAD**-0.5
    queries = projected_ref[:, block(pair, 2 * HEAD)] * bf16(scale_by)
    keys = projected_ref[:, block(pairs + pair, 2 * HEAD)]
    values = projected_ref[:, block(2 * pairs + pair, 2 * HEAD)]
    grads = grad_attended_ref[:, block(pair, 2 * HEAD)]
    for start in reversed(range(0, length, QUERY_BLOCK)):
        stop = start + QUERY_BLOCK
        grad_keys = grad_values = 0.0
        for which in range(2):
            head = pl.ds(2 * pair + which, 1)
            rows = block(2 * pair + which, HEAD)
            query_rows = keep_half(queries[start:stop], which)
            grad_rows = keep_half(grads[start:stop], which)
            scores = matmul(keys[0:stop], query_rows, NT)
            probs = jnp.exp(scores + mask_ref[0:stop, start:stop] - lse_ref[head, start:stop])
            grad_probs = matmul(values[0:stop], grad_rows, NT)
            grad_scores = (probs * (grad_probs - dots_ref[head, start:stop])).astype(bf16)
            grad_values = grad_values + matmul(probs.astype(bf16), grad_rows, NN)
            grad_keys = grad_keys + matmul(grad_scores, query_rows, NN)
            grad_queries_t_ref[rows, start:stop] = (
                matmul(keys_t_ref[rows, 0:stop], grad_scores, NN) * scale_by
            ).astype(bf16)
        if stop == length:
            grad_keys_ref[...] = grad_keys
            grad_values_ref[...] = grad_values
        else:
            grad_keys_ref[0:stop] += grad_keys
            grad_values_ref[0:stop] += grad_values
    grad_projected_ref[:, block(pairs + pair, 2 * HEAD)] = grad_keys_ref[...].astype(bf16)
    grad_projected_ref[:, block(2 * pairs + pair, 2 * HEAD)] = grad_values_ref[...].astype(bf16)


MESH = pl.DeviceIdType.MESH
HBM = pl.BlockSpec(memory_space=pl.ANY)


def flip(value, bits):
    bit = 1
    while bit <= bits:
        if bits & bit:
            value = value + bit - 2 * bit * ((value // bit) % 2)
        bit *= 2
    return value


class Place:
    def __init__(self, shards):
        self.lines = shards // 2
        self.rep, self.me = lax.axis_index("rep"), lax.axis_index("shard")
        self.far, self.core = self.rep // 2, self.rep % 2
        self.line, self.side = self.me // 2, self.me % 2

    def shard(self, hop, turn):
        return flip(self.line, hop) * 2 + flip(self.side, turn)

    def peer(self, hop, turn):
        return (self.rep, self.shard(hop, turn))

    def across(self):
        return ((1 - self.far) * 2 + self.core, self.me)

    def sibling(self):
        return (self.far * 2 + 1 - self.core, self.me)

    def others(self):
        return [(h, t) for h in range(self.lines) for t in range(2) if h or t]

    def meet(self, peers):
        barrier = pltpu.get_barrier_semaphore()
        for peer in peers:
            pl.semaphore_signal(barrier, inc=1, device_id=peer, device_id_type=MESH)
        pl.semaphore_wait(barrier, len(peers))


def aligned(start, size):
    return pl.ds(pl.multiple_of(start, 16), size)


def remote(src, dst, send, recv, peer):
    return pltpu.make_async_remote_copy(
        src_ref=src,
        dst_ref=dst,
        send_sem=send,
        recv_sem=recv,
        device_id=peer,
        device_id_type=MESH,
    )


class Gather:
    def __init__(self, place, own, full, send, recv, local):
        self.place, self.own, self.full = place, own, full
        self.send, self.recv, self.local = send, recv, local

    def rows(self, at, kind, far=None, core=None):
        count = self.own[at].shape[0]
        half, sixth = count // 2, count // 6
        far = self.place.far if far is None else far
        core = self.place.core if core is None else core
        if kind == "wide":
            return aligned(core * half + far * sixth, 2 * sixth)
        if kind == "edge":
            return aligned(core * half + 2 * far * sixth, sixth)
        return aligned(core * half, half)

    def copy(self, at, stage, hop, turn, arriving=False):
        place, lines = self.place, self.place.lines
        number = hop * 2 + turn
        far, core = place.far, place.core
        if stage == "line":
            slot, peer, kind = hop - 1, place.peer(hop, 0), "wide"
            shard = place.shard(hop if arriving else 0, 0)
        elif stage == "side":
            slot, peer, kind = lines - 1 + hop, place.peer(0, 1), "wide"
            shard = place.shard(hop, 1 if arriving else 0)
        elif stage == "far":
            slot, peer, kind = 2 * lines - 1 + number - 1, place.across(), "edge"
            shard = place.shard(hop, turn)
            far = 1 - far if arriving else far
        else:
            slot, peer, kind = 4 * lines - 2 + number - 1, place.sibling(), "half"
            shard = place.shard(hop, turn)
            core = 1 - core if arriving else core
        rows = self.rows(at, kind, far, core)
        target = self.full[at].at[shard, rows]
        mine = not arriving and hop == 0 if stage == "side" else not arriving and stage == "line"
        source = self.own[at].at[rows] if mine else target
        return remote(source, target, self.send.at[at, slot], self.recv.at[at, slot], peer)

    def start(self, at, stage, hop, turn=0):
        self.copy(at, stage, hop, turn).start()

    def got(self, at, stage, hop, turn=0):
        self.copy(at, stage, hop, turn, arriving=True).wait_recv()

    def keep(self, at):
        return pltpu.make_async_copy(
            self.own[at], self.full[at].at[self.place.me], self.local.at[at]
        )

    def first(self, at):
        for hop in reversed(range(1, self.place.lines)):
            self.start(at, "line", hop)

    def events(self, at):
        hops = range(1, self.place.lines)

        def line(hop):
            self.got(at, "line", hop)
            self.start(at, "side", hop)
            self.start(at, "far", hop, 0)

        def side(hop):
            self.got(at, "side", hop)
            self.start(at, "far", hop, 1)

        def far(hop, turn):
            self.got(at, "far", hop, turn)
            self.start(at, "core", hop, turn)

        todo = [partial(line, hop) for hop in hops]
        todo.insert(1, partial(side, 0))
        todo += [partial(far, 1, 0), partial(far, 0, 1)]
        for hop in hops:
            todo += [partial(side, hop)]
            if hop > 1:
                todo += [partial(far, hop, 0)]
            if hop > 1:
                todo += [partial(far, hop - 1, 1)]
        todo += [partial(far, self.place.lines - 1, 1)]
        return todo

    def last(self, at):
        for hop, turn in self.place.others():
            self.got(at, "core", hop, turn)

    def drain(self, at):
        for hop in range(1, self.place.lines):
            self.copy(at, "line", hop, 0).wait_send()
        for hop in range(self.place.lines):
            self.copy(at, "side", hop, 0).wait_send()
        for hop, turn in self.place.others():
            self.copy(at, "far", hop, turn).wait_send()
            self.copy(at, "core", hop, turn).wait_send()


def add_into(into, other):
    into[...] = (into[...].astype(f32) + other[...].astype(f32)).astype(bf16)


class Summed:
    STAGES = ("core", "far", "side", "line", "back", "pair")

    def __init__(self, place, grad, buffers, send, recv, local):
        self.place, self.grad = place, grad
        self.send, self.recv, self.local = send, recv, local
        (
            self.held,
            self.from_core,
            self.from_far,
            self.from_side,
            self.from_line,
            self.from_back,
            self.done,
        ) = buffers
        self.half, self.sixth = grad.shape[1] // 2, grad.shape[1] // 6
        self.wide = aligned(place.far * self.sixth, 2 * self.sixth)

    def edge(self, far):
        return aligned(2 * far * self.sixth, self.sixth)

    def both(self, hop, core):
        first = 2 * flip(self.place.line, hop)
        return self.grad.at[pl.ds(first, 2), aligned(core * self.half, self.half)]

    def copy(self, stage, hop=0):
        place, lines = self.place, self.place.lines
        side = place.side
        if stage == "core":
            slot, peer = hop, place.sibling()
            pair = self.both(hop, 1 - place.core), self.from_core.at[hop]
        elif stage == "far":
            slot, peer = lines + hop, place.across()
            pair = self.held.at[hop, :, self.edge(1 - place.far)], self.from_far.at[hop]
        elif stage == "side":
            slot, peer = 2 * lines + hop, place.peer(0, 1)
            pair = self.held.at[hop, 1 - side, self.wide], self.from_side.at[hop]
        elif stage == "line":
            slot, peer = 3 * lines + hop - 1, place.peer(hop, 0)
            pair = self.held.at[hop, side, self.wide], self.from_line.at[hop - 1]
        elif stage == "back":
            slot, peer = 4 * lines - 1, place.across()
            pair = self.held.at[0, side, self.wide], self.from_back
        else:
            slot, peer = 4 * lines, place.sibling()
            mine = self.done.at[aligned(place.core * self.half, self.half)]
            pair = mine, mine
        return remote(*pair, self.send.at[slot], self.recv.at[slot], peer)

    def load(self, hop):
        return pltpu.make_async_copy(
            self.both(hop, self.place.core), self.held.at[hop], self.local.at[hop]
        )

    def begin(self, hop):
        self.copy("core", hop).start()
        self.load(hop).start()

    def after_core(self, hop):
        self.copy("core", hop).wait_recv()
        self.load(hop).wait()
        for side in range(2):
            add_into(self.held.at[hop, side], self.from_core.at[hop, side])
        self.copy("far", hop).start()

    def after_far(self, hop):
        self.copy("far", hop).wait_recv()
        for side in range(2):
            add_into(
                self.held.at[hop, side, self.edge(self.place.far)], self.from_far.at[hop, side]
            )
        self.copy("side", hop).start()

    def after_side(self, hop):
        self.copy("side", hop).wait_recv()
        add_into(self.held.at[hop, self.place.side, self.wide], self.from_side.at[hop])
        if hop:
            self.copy("line", hop).start()

    def after_line(self):
        held = self.held.at[0, self.place.side, self.wide]
        sums = held[...].astype(f32)
        for hop in range(1, self.place.lines):
            self.copy("line", hop).wait_recv()
            sums = sums + self.from_line[hop - 1].astype(f32)
        held[...] = sums.astype(bf16)
        self.copy("back").start()

    def after_back(self):
        place = self.place
        self.copy("back").wait_recv()
        start = place.core * self.half
        rows = lambda offset: aligned(start + offset, self.sixth)
        far, sixth = place.far, self.sixth
        mine = self.held.at[0, place.side]
        self.done[rows(2 * far * sixth)] = mine[self.edge(far)]
        theirs = self.from_back
        self.done[rows(2 * (1 - far) * sixth)] = theirs[aligned((1 - far) * sixth, sixth)]
        middle = mine[sixth : 2 * sixth].astype(f32) + theirs[aligned(far * sixth, sixth)].astype(
            f32
        )
        self.done[rows(sixth)] = middle.astype(bf16)
        self.copy("pair").start()

    def finish(self):
        other = self.done.at[aligned((1 - self.place.core) * self.half, self.half)]
        peer, slot = self.place.sibling(), 4 * self.place.lines
        remote(other, other, self.send.at[slot], self.recv.at[slot], peer).wait_recv()

    def drain(self):
        for stage in ("core", "far", "side"):
            for hop in range(self.place.lines):
                self.copy(stage, hop).wait_send()
        for hop in range(1, self.place.lines):
            self.copy("line", hop).wait_send()
        self.copy("back").wait_send()
        self.copy("pair").wait_send()


def sum_buffers(lines, rows, columns):
    half, sixth = rows // 2, rows // 6
    return [
        pltpu.VMEM((lines, 2, half, columns), bf16),
        pltpu.VMEM((lines, 2, half, columns), bf16),
        pltpu.VMEM((lines, 2, sixth, columns), bf16),
        pltpu.VMEM((lines, 2 * sixth, columns), bf16),
        pltpu.VMEM((lines - 1, 2 * sixth, columns), bf16),
        pltpu.VMEM((2 * sixth, columns), bf16),
        pltpu.VMEM((rows, columns), bf16),
    ]


def project(tokens_ref, params_ref, w_qkv_ref, projected_ref, normed_ref, values_t_ref):
    length, width = tokens_ref.shape
    row = lambda at: params_ref[at : at + 1, :]
    for part, bias in enumerate((row(BIAS_Q), 0.0, row(BIAS_V))):
        columns = slice(part * width, (part + 1) * width)
        weights = w_qkv_ref[..., columns].reshape(width, width)
        projected_ref[:, columns] = (matmul(normed_ref[...], weights, NN) + bias).astype(bf16)
    values_t_ref[...] = jnp.transpose(projected_ref[:, 2 * width :])


def first_norm(tokens_ref, params_ref, normed_ref):
    length = tokens_ref.shape[0]
    row = lambda at: params_ref[at : at + 1, :]
    for at in range(0, length, ROW_CHUNK):
        norm, _ = normalized(tokens_ref[at : at + ROW_CHUNK].astype(f32))
        normed_ref[at : at + ROW_CHUNK] = (norm * row(GAIN1) + row(SHIFT1)).astype(bf16)


def forward_kernel(
    tokens_ref,
    segment_ref,
    params_ref,
    w_qkv_ref,
    projected_ref,
    attended_t_ref,
    lse_ref,
    mask_ref,
    normed_ref,
    values_t_ref,
):
    first_norm(tokens_ref, params_ref, normed_ref)
    project(tokens_ref, params_ref, w_qkv_ref, projected_ref, normed_ref, values_t_ref)
    build_mask(segment_ref, mask_ref)

    @pl.loop(0, tokens_ref.shape[1] // (2 * HEAD))
    def _(pair):
        attend_forward(pair, projected_ref, values_t_ref, mask_ref, attended_t_ref, lse_ref)


def spread(todo, steps):
    return [todo[len(todo) * k // steps : len(todo) * (k + 1) // steps] for k in range(steps)]


def at_step(step, parts):
    for number, part in enumerate(parts):
        if part:

            @pl.when(step == number)
            def _(part=part):
                for act in part:
                    act()


def gather_forward_kernel(
    shards,
    tokens_ref,
    segment_ref,
    own_params_ref,
    own_qkv_ref,
    own_out_ref,
    own_fc_ref,
    own_proj_ref,
    projected_ref,
    attended_t_ref,
    lse_ref,
    params_ref,
    full_qkv_ref,
    full_out_ref,
    full_fc_ref,
    full_proj_ref,
    mask_ref,
    normed_ref,
    values_t_ref,
    tables_ref,
    send_sem,
    recv_sem,
    local_sem,
    params_send_sem,
    params_recv_sem,
):
    place = Place(shards)
    others = place.others()
    gather = Gather(
        place,
        (own_qkv_ref, own_out_ref, own_fc_ref, own_proj_ref),
        (full_qkv_ref, full_out_ref, full_fc_ref, full_proj_ref),
        send_sem,
        recv_sem,
        local_sem,
    )
    place.meet([place.peer(*other) for other in others] + [place.across(), place.sibling()])

    def table(number, other, arriving):
        target = tables_ref.at[place.shard(*other) if arriving else place.me]
        return remote(
            target if arriving else own_params_ref,
            target,
            params_send_sem.at[number],
            params_recv_sem.at[number],
            place.peer(*other),
        )

    for number, other in enumerate(others):
        table(number, other, False).start()
    gather.first(0)
    gather.start(0, "side", 0)
    for at in range(4):
        gather.keep(at).start()
    tables_ref[place.me] = own_params_ref[...]
    build_mask(segment_ref, mask_ref)
    for number, other in enumerate(others):
        table(number, other, True).wait_recv()
    params_ref[...] = jnp.sum(tables_ref[...].astype(f32), axis=0)
    first_norm(tokens_ref, params_ref, normed_ref)
    todo = gather.events(0)
    for act in todo[:4]:
        act()
    for at in range(1, 4):
        gather.first(at)
    for act in todo[4:]:
        act()
    for at in range(1, 4):
        gather.start(at, "side", 0)
    gather.last(0)
    gather.keep(0).wait()
    project(tokens_ref, params_ref, full_qkv_ref, projected_ref, normed_ref, values_t_ref)
    todo = [act for at in range(1, 4) for act in gather.events(at)]
    pairs = tokens_ref.shape[1] // (2 * HEAD)
    beside = len(todo) * 3 // 4
    parts = spread(todo[:beside], pairs)

    @pl.loop(0, pairs)
    def _(pair):
        at_step(pair, parts)
        attend_forward(pair, projected_ref, values_t_ref, mask_ref, attended_t_ref, lse_ref)

    for act in todo[beside:]:
        act()
    for at in range(1, 4):
        gather.last(at)
        gather.keep(at).wait()
    for at in range(4):
        gather.drain(at)
    for number, other in enumerate(others):
        table(number, other, False).wait_send()


def hidden_kernel(
    attended_t_ref,
    tokens_ref,
    cotangent_ref,
    params_ref,
    w_out_ref,
    w_fc_ref,
    w_proj_ref,
    layer_out_ref,
    grad_middle_ref,
    grad_attended_ref,
    grad_w_out_ref,
    grad_w_fc_ref,
    grad_w_proj_t_ref,
    small_ref,
    middle_ref,
    normed_ref,
    normed_t_ref,
    cotangent_t_ref,
    mixed_ref,
    grad_normed_ref,
    activated_ref,
    grad_preact_ref,
):
    step, steps = pl.program_id(0), pl.num_programs(0)
    length, width = tokens_ref.shape
    row = lambda at: params_ref[at : at + 1, :]
    chunks = [slice(at, at + ROW_CHUNK) for at in range(0, length, ROW_CHUNK)]

    @pl.when(step == 0)
    def _():
        attended = jnp.transpose(attended_t_ref[...])
        middle_ref[...] = (
            tokens_ref[...].astype(f32) + matmul(attended, w_out_ref[...], NN) + row(BIAS_OUT)
        )
        for rows in chunks:
            norm, _ = normalized(middle_ref[rows])
            normed_ref[rows] = (norm * row(GAIN2) + row(SHIFT2)).astype(bf16)
        normed_t_ref[...] = jnp.transpose(normed_ref[...])
        cotangent_t_ref[...] = jnp.transpose(cotangent_ref[...])
        mixed_ref[...] = jnp.zeros_like(mixed_ref)
        grad_normed_ref[...] = jnp.zeros_like(grad_normed_ref)
        small_ref[...] = jnp.zeros_like(small_ref)

    bias_sum = 0.0
    bias_row = params_ref[pl.ds(BIAS_FC + step, 1), :]
    for rows in chunks:
        preact = matmul(normed_ref[rows], w_fc_ref[...], NN) + bias_row
        grad_act = matmul(cotangent_ref[rows], w_proj_ref[...], NT)
        square = preact * preact
        bend = jnp.tanh(GELU_SCALE * preact * (1.0 + GELU_CUBE * square))
        gate = 0.5 + 0.5 * bend
        activated_ref[rows] = (preact * gate).astype(bf16)
        slope = gate + (0.5 * GELU_SCALE) * preact * (1.0 - bend * bend) * (
            1.0 + (3 * GELU_CUBE) * square
        )
        grad_preact = (slope * grad_act).astype(bf16)
        grad_preact_ref[rows] = grad_preact
        bias_sum = bias_sum + total(grad_preact.astype(f32))
    small_ref[pl.ds(BIAS_FC + step, 1), :] = bias_sum
    mixed_ref[...] += matmul(activated_ref[...], w_proj_ref[...], NN)
    grad_w_proj_t = matmul(cotangent_t_ref[...], activated_ref[...], NN).astype(bf16)
    pieces, _, piece = grad_w_proj_t_ref.shape
    for at in range(pieces):
        grad_w_proj_t_ref[at] = grad_w_proj_t[:, at * piece : (at + 1) * piece]
    grad_w_fc_ref[...] = matmul(normed_t_ref[...], grad_preact_ref[...], NN).astype(bf16)
    grad_normed_ref[...] += matmul(grad_preact_ref[...], w_fc_ref[...], NT)

    @pl.when(step == steps - 1)
    def _():
        sums = [0.0] * 4
        for rows in chunks:
            middle = middle_ref[rows]
            layer_out_ref[rows] = (middle + mixed_ref[rows] + row(BIAS_PROJ)).astype(bf16)
            norm, inverse = normalized(middle)
            grad_normed = grad_normed_ref[rows]
            cotangent = cotangent_ref[rows].astype(f32)
            grad_middle = cotangent + norm_pull(grad_normed, row(GAIN2), norm, inverse)
            grad_middle_ref[rows] = grad_middle
            normed_ref[rows] = grad_middle.astype(bf16)
            terms = (grad_middle, grad_normed * norm, grad_normed, cotangent)
            sums = [a + total(b) for a, b in zip(sums, terms)]
        for at, value in zip((BIAS_OUT, GAIN2, SHIFT2, BIAS_PROJ), sums):
            small_ref[at : at + 1, :] = value
        grad_branch = normed_ref[...]
        grad_w_out_ref[...] = matmul(attended_t_ref[...], grad_branch, NN).astype(bf16)
        grad_attended_ref[...] = matmul(grad_branch, w_out_ref[...], NT).astype(bf16)


def backward_kernel(
    tokens_ref,
    segment_ref,
    params_ref,
    w_qkv_ref,
    projected_ref,
    attended_t_ref,
    lse_ref,
    grad_attended_ref,
    grad_middle_ref,
    small_in_ref,
    grad_tokens_ref,
    grad_w_qkv_ref,
    small_ref,
    mask_ref,
    wide_t_ref,
    grad_queries_t_ref,
    dots_ref,
    grad_projected_ref,
    grad_keys_ref,
    grad_values_ref,
):
    length, width = tokens_ref.shape
    build_mask(segment_ref, mask_ref)
    dot_rows(attended_t_ref, grad_attended_ref, wide_t_ref, dots_ref)
    wide_t_ref[...] = jnp.transpose(projected_ref[:, width : 2 * width])

    @pl.loop(0, width // (2 * HEAD))
    def _(pair):
        attend_backward(
            pair,
            projected_ref,
            wide_t_ref,
            grad_attended_ref,
            mask_ref,
            lse_ref,
            dots_ref,
            grad_queries_t_ref,
            grad_projected_ref,
            grad_keys_ref,
            grad_values_ref,
        )

    grad_projected_ref[:, 0:width] = jnp.transpose(grad_queries_t_ref[...])
    normed_transposed(tokens_ref, params_ref, wide_t_ref)
    small_ref[...] = small_in_ref[...]
    bias_sums(grad_projected_ref, small_ref)
    grad_w_qkv_ref[...] = matmul(wide_t_ref[...], grad_projected_ref[...], NN).astype(bf16)
    gain_sum = shift_sum = 0.0
    for at in range(0, length, ROW_CHUNK):
        gain_part, shift_part = token_rows(
            at,
            tokens_ref,
            params_ref,
            w_qkv_ref[...],
            grad_projected_ref,
            grad_middle_ref[at : at + ROW_CHUNK],
            grad_tokens_ref,
        )
        gain_sum, shift_sum = gain_sum + gain_part, shift_sum + shift_part
    small_ref[GAIN1 : GAIN1 + 1, :] = gain_sum
    small_ref[SHIFT1 : SHIFT1 + 1, :] = shift_sum


def dot_rows(attended_t_ref, grad_attended_ref, wide_t_ref, dots_ref):
    wide_t_ref[...] = jnp.transpose(grad_attended_ref[...])
    for head in range(wide_t_ref.shape[0] // HEAD):
        rows = slice(head * HEAD, (head + 1) * HEAD)
        dots_ref[head : head + 1, :] = total(
            wide_t_ref[rows].astype(f32) * attended_t_ref[rows].astype(f32)
        )


def normed_transposed(tokens_ref, params_ref, wide_t_ref):
    row = lambda at: params_ref[at : at + 1, :]
    for at in range(0, tokens_ref.shape[0], ROW_CHUNK):
        norm, _ = normalized(tokens_ref[at : at + ROW_CHUNK].astype(f32))
        normed = (norm * row(GAIN1) + row(SHIFT1)).astype(bf16)
        wide_t_ref[:, at : at + ROW_CHUNK] = jnp.transpose(normed)


def bias_sums(grad_projected_ref, small_ref):
    width = small_ref.shape[1]
    for at, part in ((BIAS_Q, 0), (BIAS_V, 2)):
        values = grad_projected_ref[:, part * width : (part + 1) * width]
        small_ref[at : at + 1, :] = total(values.astype(f32))


def token_rows(at, tokens_ref, params_ref, weights, grad_projected_ref, middle, grad_tokens_ref):
    rows = slice(at, at + ROW_CHUNK)
    grad_normed = matmul(grad_projected_ref[rows], weights, NT)
    norm, inverse = normalized(tokens_ref[rows].astype(f32))
    grad_rows = norm_pull(grad_normed, params_ref[GAIN1 : GAIN1 + 1, :], norm, inverse)
    grad_tokens_ref[rows] = (middle + grad_rows).astype(bf16)
    return total(grad_normed * norm), total(grad_normed)


def sum_backward_kernel(
    shards,
    tokens_ref,
    segment_ref,
    params_ref,
    attended_t_ref,
    lse_ref,
    grad_attended_ref,
    small_in_ref,
    projected_in_ref,
    w_qkv_in_ref,
    grad_middle_in_ref,
    grad_out_ref,
    grad_fc_ref,
    grad_proj_t_ref,
    grad_tokens_ref,
    sum_qkv_ref,
    sum_out_ref,
    sum_fc_ref,
    sum_proj_ref,
    small_ref,
    mask_ref,
    wide_t_ref,
    grad_queries_t_ref,
    dots_ref,
    projected_ref,
    grad_projected_ref,
    grad_keys_ref,
    grad_values_ref,
    grad_qkv_ref,
    *rest,
):
    buffers, rest = [rest[7 * k : 7 * k + 7] for k in range(4)], rest[28:]
    small_core_ref, small_far_ref, small_side_ref, small_line_ref, *rest = rest
    send_sem, recv_sem, local_sem, load_sem, small_send_sem, small_recv_sem = rest
    length, width = tokens_ref.shape
    place = Place(shards)
    lines = place.lines
    grads = (grad_qkv_ref, grad_out_ref, grad_fc_ref, grad_proj_t_ref)
    sums = [
        Summed(place, grads[k], buffers[k], send_sem.at[k], recv_sem.at[k], local_sem.at[k])
        for k in range(4)
    ]
    of_qkv, of_out, of_fc, of_proj = sums
    order = list(reversed(range(lines)))
    place.meet(
        [place.peer(hop, 0) for hop in range(1, lines)]
        + [place.peer(0, 1), place.across(), place.sibling()]
    )
    load_projected = pltpu.make_async_copy(projected_in_ref, projected_ref, load_sem.at[0])
    load_projected.start()
    groups = [[(item, hop)] for item in (of_proj, of_fc) for hop in order]
    groups.append([(of_out, hop) for hop in order])
    for group in groups:
        for item, hop in group:
            item.begin(hop)

    def stage(name, number):
        group = groups[number] if 0 <= number < len(groups) else []
        return [partial(getattr(item, name), hop) for item, hop in group]

    def write(item, out_ref, transposed=False):
        item.finish()
        values = item.done[...].astype(f32)
        out_ref[...] = jnp.transpose(values) if transposed else values

    ticks = [stage("after_core", 0) + stage("after_core", 1)]
    for number in range(1, len(groups) + 5):
        ticks.append(
            stage("after_core", number + 1)
            + stage("after_far", number - 1)
            + stage("after_side", number - 2)
        )
    tails = (
        (of_proj, lines, partial(write, of_proj, sum_proj_ref, True)),
        (of_fc, 2 * lines, partial(write, of_fc, sum_fc_ref)),
        (of_out, 2 * lines + 1, partial(write, of_out, sum_out_ref)),
    )
    for item, after, end in tails:
        for late, act in ((2, item.after_line), (3, item.after_back), (4, end)):
            ticks[after + late].append(act)

    build_mask(segment_ref, mask_ref)
    dot_rows(attended_t_ref, grad_attended_ref, wide_t_ref, dots_ref)
    for act in ticks[0]:
        act()
    load_projected.wait()
    wide_t_ref[...] = jnp.transpose(projected_ref[:, width : 2 * width])
    pairs = width // (2 * HEAD)

    @pl.loop(0, pairs)
    def _(pair):
        attend_backward(
            pair,
            projected_ref,
            wide_t_ref,
            grad_attended_ref,
            mask_ref,
            lse_ref,
            dots_ref,
            grad_queries_t_ref,
            grad_projected_ref,
            grad_keys_ref,
            grad_values_ref,
        )
        at_step(pair, ticks[1 : 1 + pairs])

    ticks = ticks[1 + pairs :]
    weights_ref = projected_ref.at[0:width]
    middle_ref = mask_ref.at[:, 0:width]
    load_weights = pltpu.make_async_copy(w_qkv_in_ref, weights_ref, load_sem.at[0])
    load_middle = pltpu.make_async_copy(grad_middle_in_ref, middle_ref, load_sem.at[1])
    load_weights.start()
    load_middle.start()
    grad_projected_ref[:, 0:width] = jnp.transpose(grad_queries_t_ref[...])
    normed_transposed(tokens_ref, params_ref, wide_t_ref)
    small_ref[...] = small_in_ref[...]
    rows = 2 * grad_qkv_ref.shape[1]
    for hop in order:
        line = flip(place.line, hop)
        grad_rows = matmul(wide_t_ref[aligned(line * rows, rows), :], grad_projected_ref[...], NN)
        grad_qkv_ref[pl.ds(2 * line, 2)] = grad_rows.astype(bf16).reshape(2, rows // 2, 3 * width)
        of_qkv.begin(hop)
        for act in ticks[0]:
            act()
        ticks = ticks[1:]
    bias_sums(grad_projected_ref, small_ref)
    load_weights.wait()
    load_middle.wait()
    own_ticks = [
        [partial(of_qkv.after_core, hop) for hop in order[0:2]],
        [partial(of_qkv.after_core, order[2]), partial(of_qkv.after_far, order[0])],
        [
            partial(of_qkv.after_core, order[3]),
            partial(of_qkv.after_far, order[1]),
            partial(of_qkv.after_side, order[0]),
        ],
        [partial(of_qkv.after_far, order[2]), partial(of_qkv.after_side, order[1])],
    ]
    gain_sum = shift_sum = 0.0
    for number, at in enumerate(range(0, length, ROW_CHUNK)):
        for act in own_ticks[number]:
            act()
        gain_part, shift_part = token_rows(
            at,
            tokens_ref,
            params_ref,
            projected_ref[0:width],
            grad_projected_ref,
            mask_ref[at : at + ROW_CHUNK, 0:width],
            grad_tokens_ref,
        )
        gain_sum, shift_sum = gain_sum + gain_part, shift_sum + shift_part
        if ticks:
            for act in ticks[0]:
                act()
            ticks = ticks[1:]
    small_ref[GAIN1 : GAIN1 + 1, :] = gain_sum
    small_ref[SHIFT1 : SHIFT1 + 1, :] = shift_sum

    def small_copy(slot, into_ref, peer):
        return remote(small_ref, into_ref, small_send_sem.at[slot], small_recv_sem.at[slot], peer)

    def exchange(slot, into_ref, peer):
        copy = small_copy(slot, into_ref, peer)
        copy.start()
        return copy

    copy = exchange(0, small_core_ref, place.sibling())
    of_qkv.after_far(order[3])
    copy.wait()
    small_ref[...] += small_core_ref[...]
    copy = exchange(1, small_far_ref, place.across())
    of_qkv.after_side(order[2])
    copy.wait()
    small_ref[...] += small_far_ref[...]
    copy = exchange(2, small_side_ref, place.peer(0, 1))
    of_qkv.after_side(order[3])
    copy.wait()
    small_ref[...] += small_side_ref[...]
    copies = [
        exchange(2 + hop, small_line_ref.at[hop - 1], place.peer(hop, 0))
        for hop in range(1, lines)
    ]
    for tick in ticks:
        for act in tick:
            act()
    of_qkv.after_line()
    for copy in copies:
        copy.wait()
    small = small_ref[...]
    for hop in range(1, lines):
        small = small + small_line_ref[hop - 1]
    small_ref[...] = small
    of_qkv.after_back()
    write(of_qkv, sum_qkv_ref)
    for item in sums:
        item.drain()


def kernel_params():
    return pltpu.CompilerParams(vmem_limit_bytes=VMEM_LIMIT)


def run_forward(tokens, segment, params, w_qkv):
    length, width = tokens.shape
    return pl.pallas_call(
        forward_kernel,
        in_specs=[WHOLE] * 4,
        out_specs=(WHOLE,) * 3,
        out_shape=(
            jax.ShapeDtypeStruct((length, 3 * width), bf16),
            jax.ShapeDtypeStruct((width, length), bf16),
            jax.ShapeDtypeStruct((16, length), f32),
        ),
        scratch_shapes=[
            pltpu.VMEM((length, length), f32),
            pltpu.VMEM((length, width), bf16),
            pltpu.VMEM((width, length), bf16),
        ],
        compiler_params=kernel_params(),
        name="forward",
    )(tokens, segment, params, w_qkv)


def run_hidden(attended_t, tokens, cotangent, params, w_out, w_fc, w_proj, piece):
    length, width = tokens.shape
    hidden = w_fc.shape[1]
    shape = jax.ShapeDtypeStruct
    columns = pl.BlockSpec((width, width), lambda step: (0, step))
    return pl.pallas_call(
        hidden_kernel,
        grid=(hidden // width,),
        in_specs=[WHOLE] * 5 + [columns, pl.BlockSpec((width, width), lambda step: (step, 0))],
        out_specs=(
            WHOLE,
            WHOLE,
            WHOLE,
            WHOLE,
            columns,
            pl.BlockSpec((width // piece, width, piece), lambda step: (step, 0, 0)),
            WHOLE,
        ),
        out_shape=(
            shape((length, width), bf16),
            shape((length, width), f32),
            shape((length, width), bf16),
            shape((width, width), bf16),
            shape((width, hidden), bf16),
            shape((hidden // piece, width, piece), bf16),
            shape((16, width), f32),
        ),
        scratch_shapes=[
            pltpu.VMEM((length, width), f32),
            pltpu.VMEM((length, width), bf16),
            pltpu.VMEM((width, length), bf16),
            pltpu.VMEM((width, length), bf16),
            pltpu.VMEM((length, width), f32),
            pltpu.VMEM((length, width), f32),
            pltpu.VMEM((length, width), bf16),
            pltpu.VMEM((length, width), bf16),
        ],
        compiler_params=kernel_params(),
        name="hidden",
    )(attended_t, tokens, cotangent, params, w_out, w_fc, w_proj)


def run_backward(
    tokens, segment, params, w_qkv, projected, attended_t, lse, grad_attended, grad_middle, small
):
    length, width = tokens.shape
    shape = jax.ShapeDtypeStruct
    return pl.pallas_call(
        backward_kernel,
        in_specs=[WHOLE] * 10,
        out_specs=(WHOLE,) * 3,
        out_shape=(
            shape((length, width), bf16),
            shape((width, 3 * width), bf16),
            shape((16, width), f32),
        ),
        scratch_shapes=[
            pltpu.VMEM((length, length), f32),
            pltpu.VMEM((width, length), bf16),
            pltpu.VMEM((width, length), bf16),
            pltpu.VMEM((16, length), f32),
            pltpu.VMEM((length, 3 * width), bf16),
            pltpu.VMEM((length, 2 * HEAD), f32),
            pltpu.VMEM((length, 2 * HEAD), f32),
        ],
        compiler_params=kernel_params(),
        name="backward",
    )(
        tokens,
        segment,
        params,
        w_qkv,
        projected,
        attended_t,
        lse,
        grad_attended,
        grad_middle,
        small,
    )


def link_params(number):
    return pltpu.CompilerParams(
        vmem_limit_bytes=VMEM_LIMIT, collective_id=number, has_side_effects=True
    )


def run_gather_forward(shards, tokens, segment, own_params, w_qkv, w_out, w_fc, w_proj):
    length, width = tokens.shape
    shape = jax.ShapeDtypeStruct
    copies = 3 * shards - 3
    weights = (w_qkv, w_out, w_fc, w_proj)
    return pl.pallas_call(
        partial(gather_forward_kernel, shards),
        in_specs=[WHOLE] * 3 + [HBM] * 4,
        out_specs=(WHOLE,) * 5 + (HBM,) * 3,
        out_shape=(
            shape((length, 3 * width), bf16),
            shape((width, length), bf16),
            shape((16, length), f32),
            shape(own_params.shape, f32),
        )
        + tuple(shape((shards,) + w.shape, bf16) for w in weights),
        scratch_shapes=[
            pltpu.VMEM((length, length), f32),
            pltpu.VMEM((length, width), bf16),
            pltpu.VMEM((width, length), bf16),
            pltpu.VMEM((shards,) + own_params.shape, bf16),
            pltpu.SemaphoreType.DMA((4, copies)),
            pltpu.SemaphoreType.DMA((4, copies)),
            pltpu.SemaphoreType.DMA((4,)),
            pltpu.SemaphoreType.DMA((shards - 1,)),
            pltpu.SemaphoreType.DMA((shards - 1,)),
        ],
        compiler_params=link_params(0),
        name="gather_forward",
    )(tokens, segment, own_params, *weights)


def run_sum_backward(
    shards,
    tokens,
    segment,
    params,
    attended_t,
    lse,
    grad_attended,
    small,
    projected,
    w_qkv,
    grad_middle,
    grad_out,
    grad_fc,
    grad_proj_t,
):
    length, width = tokens.shape
    shape = jax.ShapeDtypeStruct
    lines = shards // 2
    grads = (shape((shards, width // shards, 3 * width), bf16), grad_out, grad_fc, grad_proj_t)
    buffers = [ref for g in grads for ref in sum_buffers(lines, *g.shape[1:])]
    table = pltpu.VMEM(params.shape, f32)
    return pl.pallas_call(
        partial(sum_backward_kernel, shards),
        in_specs=[WHOLE] * 7 + [HBM] * 6,
        out_specs=(WHOLE,) * 6,
        out_shape=(shape((length, width), bf16),)
        + tuple(shape(g.shape[1:], f32) for g in grads[:3])
        + (shape(grad_proj_t.shape[:0:-1], f32), shape(params.shape, f32)),
        scratch_shapes=[
            pltpu.VMEM((length, length), f32),
            pltpu.VMEM((width, length), bf16),
            pltpu.VMEM((width, length), bf16),
            pltpu.VMEM((16, length), f32),
            pltpu.VMEM((length, 3 * width), bf16),
            pltpu.VMEM((length, 3 * width), bf16),
            pltpu.VMEM((length, 2 * HEAD), f32),
            pltpu.VMEM((length, 2 * HEAD), f32),
            pltpu.VMEM(grads[0].shape, bf16),
        ]
        + buffers
        + [table, table, table, pltpu.VMEM((lines - 1,) + params.shape, f32)]
        + [pltpu.SemaphoreType.DMA((4, 4 * lines + 1))] * 2
        + [
            pltpu.SemaphoreType.DMA((4, lines)),
            pltpu.SemaphoreType.DMA((2,)),
            pltpu.SemaphoreType.DMA((lines + 2,)),
            pltpu.SemaphoreType.DMA((lines + 2,)),
        ],
        compiler_params=link_params(1),
        name="sum_backward",
    )(
        tokens,
        segment,
        params,
        attended_t,
        lse,
        grad_attended,
        small,
        projected,
        w_qkv,
        grad_middle,
        grad_out,
        grad_fc,
        grad_proj_t,
    )


def on_device(
    replicas,
    shards,
    tokens,
    segment_ids,
    norm1_gain,
    norm1_shift,
    w_qkv,
    q_bias,
    v_bias,
    w_out,
    out_bias,
    norm2_gain,
    norm2_shift,
    w_fc,
    fc_bias,
    w_proj,
    proj_bias,
    cotangent,
):
    width, hidden = tokens.shape[1], w_fc.shape[1]
    vectors = (
        norm1_gain,
        norm1_shift,
        q_bias,
        v_bias,
        out_bias,
        norm2_gain,
        norm2_shift,
        proj_bias,
    )
    own, own_hidden = norm1_gain.shape[0], fc_bias.shape[0]
    me = lax.axis_index("shard")
    by_kernel = (
        replicas == 4 and shards & (shards - 1) == 0 and own % 96 == 0 and own_hidden % 128 == 0
    )
    piece = own_hidden if own_hidden % 128 == 0 else width
    mine = (lax.broadcasted_iota(jnp.int32, (1, shards, 1), 1) == me).astype(bf16)
    table = jnp.concatenate(
        [
            (jnp.stack(vectors)[:, None, :] * mine).reshape(8, width),
            (fc_bias[None, None, :] * mine).reshape(hidden // width, width),
        ]
    )
    table = jnp.pad(table, ((0, 16 - table.shape[0]), (0, 0)))
    if by_kernel:
        projected, attended_t, lse, params, *full = run_gather_forward(
            shards, tokens, segment_ids, table, w_qkv, w_out, w_fc, w_proj
        )
        full_qkv, full_out, full_fc, full_proj = (w.reshape(-1, w.shape[-1]) for w in full)
    else:
        gather = partial(lax.all_gather, axis_name="shard", axis=0, tiled=True)
        params = lax.psum(table.astype(f32), "shard")
        full_qkv, full_out, full_fc, full_proj = (gather(w) for w in (w_qkv, w_out, w_fc, w_proj))
        projected, attended_t, lse = run_forward(tokens, segment_ids, params, full_qkv)
    (
        layer_out,
        grad_middle,
        grad_attended,
        grad_w_out,
        grad_w_fc,
        grad_w_proj_t,
        small,
    ) = run_hidden(attended_t, tokens, cotangent, params, full_out, full_fc, full_proj, piece)
    if by_kernel:
        grad_tokens, sum_qkv, sum_out, sum_fc, sum_proj, small = run_sum_backward(
            shards,
            tokens,
            segment_ids,
            params,
            attended_t,
            lse,
            grad_attended,
            small,
            projected,
            full_qkv,
            grad_middle,
            grad_w_out.reshape((shards,) + w_out.shape),
            grad_w_fc.reshape((shards,) + w_fc.shape),
            grad_w_proj_t,
        )
    else:
        grad_tokens, grad_w_qkv, small = run_backward(
            tokens,
            segment_ids,
            params,
            full_qkv,
            projected,
            attended_t,
            lse,
            grad_attended,
            grad_middle,
            small,
        )

        def reduced(grad):
            own_sum = lax.psum_scatter(
                grad.astype(f32), "shard", scatter_dimension=0, tiled=True
            )
            return lax.psum(own_sum.astype(bf16), "rep").astype(f32)

        sum_proj = reduced(grad_w_proj_t.transpose(0, 2, 1).reshape(hidden, width))
        sum_fc, sum_out, sum_qkv = reduced(grad_w_fc), reduced(grad_w_out), reduced(grad_w_qkv)
        small = lax.psum(small, ("rep", "shard"))
    mine = lax.dynamic_slice_in_dim(small[:8], me * own, own, 1)
    hidden_rows = small[BIAS_FC : BIAS_FC + hidden // width].reshape(-1)
    mine_fc = lax.dynamic_slice_in_dim(hidden_rows, me * own_hidden, own_hidden, 0)
    return (
        layer_out,
        grad_tokens,
        mine[GAIN1],
        mine[SHIFT1],
        sum_qkv,
        mine[BIAS_Q],
        mine[BIAS_V],
        sum_out,
        mine[BIAS_OUT],
        mine[GAIN2],
        mine[SHIFT2],
        sum_fc,
        mine_fc,
        sum_proj,
        mine[BIAS_PROJ],
    )


def solution(mesh):
    rows, own, own_rows = P(("rep", "shard"), None), P("shard"), P("shard", None)
    in_specs = (
        rows,
        rows,
        own,
        own,
        own_rows,
        own,
        own,
        own_rows,
        own,
        own,
        own,
        own_rows,
        own,
        own_rows,
        own,
        rows,
    )
    out_specs = (
        rows,
        rows,
        own,
        own,
        own_rows,
        own,
        own,
        own_rows,
        own,
        own,
        own,
        own_rows,
        own,
        own_rows,
        own,
    )
    sizes = mesh.shape["rep"], mesh.shape["shard"]
    return jax.shard_map(
        partial(on_device, *sizes), mesh=mesh, in_specs=in_specs, out_specs=out_specs, check_vma=False
    )
```

```python
from functools import partial

import jax
import jax.numpy as jnp
from jax import lax
from jax.experimental import pallas as pl
from jax.experimental.pallas import tpu as pltpu
from jax.sharding import PartitionSpec as P

HEAD = 64
EPSILON = 1e-05
QUERY_BLOCK = 256
ROW_CHUNK = 256
MASKED = -1e30
GELU_SCALE = 0.7978845608028654
GELU_CUBE = 0.044715
VMEM_LIMIT = 62 << 20
NN = (((1,), (0,)), ((), ()))
NT = (((1,), (1,)), ((), ()))
f32 = jnp.float32
bf16 = jnp.bfloat16
WHOLE = pl.BlockSpec(memory_space=pltpu.VMEM)

GAIN1, SHIFT1, BIAS_Q, BIAS_V, BIAS_OUT, GAIN2, SHIFT2, BIAS_PROJ, BIAS_FC = range(9)


def matmul(left, right, dims):
    return lax.dot_general(left, right, dims, preferred_element_type=f32)


def normalized(values):
    centred = values - jnp.mean(values, axis=-1, keepdims=True)
    inverse = lax.rsqrt(jnp.mean(centred * centred, axis=-1, keepdims=True) + EPSILON)
    return centred * inverse, inverse


def norm_pull(grad_normed, gain_row, norm, inverse):
    scaled = grad_normed * gain_row
    return inverse * (
        scaled
        - jnp.mean(scaled, axis=-1, keepdims=True)
        - norm * jnp.mean(scaled * norm, axis=-1, keepdims=True)
    )


def total(values):
    return jnp.sum(values, axis=0, keepdims=True)


def block(index, size):
    return pl.ds(pl.multiple_of(index * size, size), size)


def build_mask(segment_ref, mask_ref):
    length = segment_ref.shape[1]
    query_seg = segment_ref[...].astype(f32)
    key_seg = jnp.transpose(jnp.broadcast_to(query_seg, (8, length)))[:, 0:1]
    for start in range(0, length, QUERY_BLOCK):
        stop = start + QUERY_BLOCK
        key_at = lax.broadcasted_iota(jnp.int32, (stop, QUERY_BLOCK), 0)
        query_at = lax.broadcasted_iota(jnp.int32, (stop, QUERY_BLOCK), 1) + start
        allowed = (key_seg[0:stop] == query_seg[:, start:stop]) & (key_at <= query_at)
        mask_ref[0:stop, start:stop] = jnp.where(allowed, 0.0, MASKED)


def half_lanes(which):
    lane = lax.broadcasted_iota(jnp.int32, (1, 2 * HEAD), 1)
    return (lane < HEAD) if which == 0 else (lane >= HEAD)


def keep_half(values, which):
    return jnp.where(half_lanes(which), values, jnp.zeros_like(values))


def attend_forward(
    pair, queries, keys, values_t_ref, mask_ref, attended_t_ref, lse_ref, tick=lambda number: None
):
    length = keys.shape[0]
    queries = queries * bf16(HEAD**-0.5)
    for which in range(2):
        tick(which)
        head_queries = keep_half(queries, which)
        rows = block(2 * pair + which, HEAD)
        values_t = values_t_ref[rows, :]
        for start in range(0, length, QUERY_BLOCK):
            stop = start + QUERY_BLOCK
            scores = matmul(keys[0:stop], head_queries[start:stop], NT)
            scores = scores + mask_ref[0:stop, start:stop]
            top = jnp.max(scores, axis=0, keepdims=True)
            terms = jnp.exp(scores - top)
            sums = jnp.sum(terms, axis=0, keepdims=True)
            mixed = matmul(values_t[:, 0:stop], terms.astype(bf16), NN)
            attended_t_ref[rows, start:stop] = (mixed * (1.0 / sums)).astype(bf16)
            lse_ref[pl.ds(2 * pair + which, 1), start:stop] = top + jnp.log(sums)


def attend_backward(
    pair,
    operands,
    keys_t_ref,
    mask_ref,
    lse_ref,
    dots_ref,
    grad_queries_t_ref,
    grad_keys_ref,
    grad_values_ref,
    tick=lambda number: None,
):
    queries, keys, values, grads = operands
    length, scale_by = keys.shape[0], HEAD**-0.5
    queries = queries * bf16(scale_by)
    for number, start in enumerate(reversed(range(0, length, QUERY_BLOCK))):
        tick(number)
        stop = start + QUERY_BLOCK
        grad_keys = grad_values = 0.0
        for which in range(2):
            head = pl.ds(2 * pair + which, 1)
            rows = block(2 * pair + which, HEAD)
            query_rows = keep_half(queries[start:stop], which)
            grad_rows = keep_half(grads[start:stop], which)
            scores = matmul(keys[0:stop], query_rows, NT)
            probs = jnp.exp(scores + mask_ref[0:stop, start:stop] - lse_ref[head, start:stop])
            grad_probs = matmul(values[0:stop], grad_rows, NT)
            grad_scores = (probs * (grad_probs - dots_ref[head, start:stop])).astype(bf16)
            grad_values = grad_values + matmul(probs.astype(bf16), grad_rows, NN)
            grad_keys = grad_keys + matmul(grad_scores, query_rows, NN)
            grad_queries_t_ref[rows, start:stop] = (
                matmul(keys_t_ref[rows, 0:stop], grad_scores, NN) * scale_by
            ).astype(bf16)
        if stop == length:
            grad_keys_ref[...] = grad_keys
            grad_values_ref[...] = grad_values
        else:
            grad_keys_ref[0:stop] += grad_keys
            grad_values_ref[0:stop] += grad_values


MESH = pl.DeviceIdType.MESH
HBM = pl.BlockSpec(memory_space=pl.ANY)


def flip(value, bits):
    bit = 1
    while bit <= bits:
        if bits & bit:
            value = value + bit - 2 * bit * ((value // bit) % 2)
        bit *= 2
    return value


class Place:
    def __init__(self, shards):
        self.lines = shards // 2
        self.rep, self.me = lax.axis_index("rep"), lax.axis_index("shard")
        self.far, self.core = self.rep // 2, self.rep % 2
        self.line, self.side = self.me // 2, self.me % 2

    def shard(self, hop, turn):
        return flip(self.line, hop) * 2 + flip(self.side, turn)

    def peer(self, hop, turn):
        return (self.rep, self.shard(hop, turn))

    def across(self):
        return ((1 - self.far) * 2 + self.core, self.me)

    def sibling(self):
        return (self.far * 2 + 1 - self.core, self.me)

    def others(self):
        return [(h, t) for h in range(self.lines) for t in range(2) if h or t]

    def meet(self, peers):
        barrier = pltpu.get_barrier_semaphore()
        for peer in peers:
            pl.semaphore_signal(barrier, inc=1, device_id=peer, device_id_type=MESH)
        pl.semaphore_wait(barrier, len(peers))


def aligned(start, size):
    return pl.ds(pl.multiple_of(start, 16), size)


def remote(src, dst, send, recv, peer):
    return pltpu.make_async_remote_copy(
        src_ref=src,
        dst_ref=dst,
        send_sem=send,
        recv_sem=recv,
        device_id=peer,
        device_id_type=MESH,
    )


def cut(count):
    half = count // 2
    return half // 3 // 16 * 16, half


class Gather:
    def __init__(self, place, own, full, send, recv, local):
        self.place, self.own, self.full = place, own, full
        self.send, self.recv, self.local = send, recv, local
        self.hops = range(1, place.lines)

    def rows(self, at, kind, far, core):
        edge, half = cut(self.own[at].shape[0])
        if kind == "wide":
            return aligned(core * half + far * edge, half - edge)
        if kind == "edge":
            return aligned(core * half + far * (half - edge), edge)
        return aligned(core * half, half)

    def copy(self, at, stage, hop, turn, arriving=False):
        place, lines = self.place, self.place.lines
        number = hop * 2 + turn
        far, core = place.far, place.core
        if stage == "line":
            slot, peer, kind = hop - 1, place.peer(hop, 0), "wide"
            shard = place.shard(hop if arriving else 0, 0)
        elif stage == "side":
            slot, peer, kind = lines - 1 + hop, place.peer(0, 1), "wide"
            shard = place.shard(hop, 1 if arriving else 0)
        elif stage == "far":
            slot, peer, kind = 2 * lines - 1 + number - 1, place.across(), "edge"
            shard = place.shard(hop, turn)
            far = 1 - far if arriving else far
        else:
            slot, peer, kind = 4 * lines - 2 + number - 1, place.sibling(), "half"
            shard = place.shard(hop, turn)
            core = 1 - core if arriving else core
        rows = self.rows(at, kind, far, core)
        target = self.full[at].at[shard, rows]
        mine = not arriving and (stage == "line" or (stage == "side" and hop == 0))
        source = self.own[at].at[rows] if mine else target
        return remote(source, target, self.send.at[at, slot], self.recv.at[at, slot], peer)

    def start(self, at, stage, hop, turn=0):
        self.copy(at, stage, hop, turn).start()

    def got(self, at, stage, hop, turn=0):
        self.copy(at, stage, hop, turn, arriving=True).wait_recv()

    def keep(self, at):
        return pltpu.make_async_copy(
            self.own[at], self.full[at].at[self.place.me], self.local.at[at]
        )

    def own_side(self, at):
        self.start(at, "side", 0)

    def first(self, at, hop):
        self.start(at, "line", hop)

    def line(self, at, hop):
        self.got(at, "line", hop)
        self.start(at, "side", hop)
        self.start(at, "far", hop, 0)

    def side(self, at, hop):
        self.got(at, "side", hop)
        self.start(at, "far", hop, 1)

    def far(self, at, hop, turn):
        self.got(at, "far", hop, turn)
        self.start(at, "core", hop, turn)

    def last(self, at):
        for hop, turn in self.place.others():
            self.got(at, "core", hop, turn)
        self.keep(at).wait()

    def drain(self, at):
        for hop in self.hops:
            self.copy(at, "line", hop, 0).wait_send()
        for hop in range(self.place.lines):
            self.copy(at, "side", hop, 0).wait_send()
        for hop, turn in self.place.others():
            self.copy(at, "far", hop, turn).wait_send()
            self.copy(at, "core", hop, turn).wait_send()


def add_into(into, other):
    into[...] = (into[...].astype(f32) + other[...].astype(f32)).astype(bf16)


class Summed:
    def __init__(self, place, grad, done, buffers, send, recv, source=None, load_sem=None):
        self.place, self.grad, self.done = place, grad, done
        self.send_sem, self.recv_sem = send, recv
        self.source = grad if source is None else source
        self.load_sem = load_sem
        (
            self.from_core,
            self.from_far,
            self.from_side,
            self.from_me,
            self.from_line,
            self.from_back,
        ) = buffers
        self.edge_size, self.half = cut(grad.shape[1])
        self.hops = range(1, place.lines)

    def rows(self, kind, far=None, core=None):
        far = self.place.far if far is None else far
        core = self.place.core if core is None else core
        edge, half = self.edge_size, self.half
        if kind == "wide":
            return aligned(core * half + far * edge, half - edge)
        if kind == "edge":
            return aligned(core * half + far * (half - edge), edge)
        return aligned(core * half, half)

    def pair_of(self, hop):
        return pl.ds(2 * flip(self.place.line, hop), 2)

    def copy(self, stage, hop=0):
        place, lines, grad = self.place, self.place.lines, self.grad
        if stage == "core":
            slot, peer = 0, place.sibling()
            pair = self.source.at[:, self.rows("half", core=1 - place.core)], self.from_core
        elif stage == "far":
            slot, peer = hop, place.across()
            pair = (
                grad.at[self.pair_of(hop), self.rows("edge", far=1 - place.far)],
                self.from_far.at[hop - 1],
            )
        elif stage == "side":
            slot, peer = lines + hop, place.peer(0, 1)
            source = grad.at[place.shard(hop, 1), self.rows("wide" if hop else "half")]
            pair = source, self.from_side.at[hop - 1] if hop else self.from_me
        elif stage == "line":
            slot, peer = 2 * lines + hop - 1, place.peer(hop, 0)
            pair = grad.at[place.shard(hop, 0), self.rows("wide")], self.from_line.at[hop - 1]
        elif stage == "back":
            slot, peer = 3 * lines - 1, place.across()
            pair = grad.at[place.me, self.rows("half")], self.from_back
        else:
            slot, peer = 3 * lines, place.sibling()
            mine = self.done.at[self.rows("half")]
            pair = mine, mine
        return remote(*pair, self.send_sem.at[slot], self.recv_sem.at[slot], peer)

    def load(self):
        rows = self.rows("half")
        return pltpu.make_async_copy(
            self.source.at[:, rows], self.grad.at[:, rows], self.load_sem
        )

    def begin(self):
        self.copy("core").start()
        if self.load_sem is not None:
            self.load().start()

    def core(self):
        self.copy("core").wait_recv()
        if self.load_sem is not None:
            self.load().wait()
        for shard in range(2 * self.place.lines):
            add_into(self.grad.at[shard, self.rows("half")], self.from_core.at[shard])

    def me0(self):
        self.copy("side", 0).start()

    def send(self, hop):
        self.copy("far", hop).start()

    def far(self, hop):
        self.copy("far", hop).wait_recv()
        add_into(self.grad.at[self.pair_of(hop), self.rows("edge")], self.from_far.at[hop - 1])
        self.copy("side", hop).start()

    def side(self, hop):
        self.copy("side", hop).wait_recv()
        mine = self.grad.at[self.place.shard(hop, 0), self.rows("wide")]
        add_into(mine, self.from_side.at[hop - 1])
        self.copy("line", hop).start()

    def me(self):
        self.copy("side", 0).wait_recv()
        add_into(self.grad.at[self.place.me, self.rows("half")], self.from_me)

    def lines(self):
        mine = self.grad.at[self.place.me, self.rows("wide")]
        sums = mine[...].astype(f32)
        for hop in self.hops:
            self.copy("line", hop).wait_recv()
            sums = sums + self.from_line[hop - 1].astype(f32)
        mine[...] = sums.astype(bf16)
        self.copy("back").start()

    def back(self):
        self.copy("back").wait_recv()
        mine = self.grad[self.place.me, self.rows("half")].astype(f32)
        self.done[self.rows("half")] = (mine + self.from_back[...].astype(f32)).astype(bf16)
        self.copy("pair").start()

    def finish(self):
        other = self.done.at[self.rows("half", core=1 - self.place.core)]
        slot = 3 * self.place.lines
        remote(
            other, other, self.send_sem.at[slot], self.recv_sem.at[slot], self.place.sibling()
        ).wait_recv()

    def drain(self):
        self.copy("core").wait_send()
        for hop in self.hops:
            self.copy("far", hop).wait_send()
            self.copy("line", hop).wait_send()
        for hop in range(self.place.lines):
            self.copy("side", hop).wait_send()
        self.copy("back").wait_send()
        self.copy("pair").wait_send()


SUM_BUFFERS = 6


def sum_buffers(lines, shards, rows, columns):
    edge, half = cut(rows)
    return [
        pltpu.VMEM((shards, half, columns), bf16),
        pltpu.VMEM((lines - 1, 2, edge, columns), bf16),
        pltpu.VMEM((lines - 1, half - edge, columns), bf16),
        pltpu.VMEM((half, columns), bf16),
        pltpu.VMEM((lines - 1, half - edge, columns), bf16),
        pltpu.VMEM((half, columns), bf16),
    ]


def sum_sems(lines, items):
    return [pltpu.SemaphoreType.DMA((items, 3 * lines + 1))] * 2


def first_norm(tokens_ref, params_ref, normed_ref):
    length, width = tokens_ref.shape
    row = lambda at: params_ref[at : at + 1, 0:width]
    for at in range(0, length, ROW_CHUNK):
        norm, _ = normalized(tokens_ref[at : at + ROW_CHUNK].astype(f32))
        normed_ref[at : at + ROW_CHUNK] = (norm * row(GAIN1) + row(SHIFT1)).astype(bf16)


def forward_kernel(
    tokens_ref,
    segment_ref,
    params_ref,
    w_qkv_ref,
    projected_ref,
    attended_t_ref,
    lse_ref,
    mask_ref,
    normed_ref,
    values_t_ref,
):
    length, width = tokens_ref.shape
    pairs = width // (2 * HEAD)
    row = lambda at: params_ref[at : at + 1, 0:width]
    first_norm(tokens_ref, params_ref, normed_ref)
    for part, bias in enumerate((row(BIAS_Q), 0.0, row(BIAS_V))):
        columns = slice(part * width, (part + 1) * width)
        projected_ref[:, columns] = (
            matmul(normed_ref[...], w_qkv_ref[:, columns], NN) + bias
        ).astype(bf16)
    values_t_ref[...] = jnp.transpose(projected_ref[:, 2 * width :])
    build_mask(segment_ref, mask_ref)

    @pl.loop(0, pairs)
    def _(pair):
        attend_forward(
            pair,
            projected_ref[:, block(pair, 2 * HEAD)],
            projected_ref[:, block(pairs + pair, 2 * HEAD)],
            values_t_ref,
            mask_ref,
            attended_t_ref,
            lse_ref,
        )


GROUP = 4 * HEAD
GATHERED_EARLY = 1
SUMMED_EARLY = 1


(
    OWN,
    FIRST,
    LINE,
    SIDE,
    FAR,
    LAST,
    BEGIN_SUM,
    CORE_SUM,
    ME0_SUM,
    SEND_SUM,
    FAR_SUM,
    SIDE_SUM,
    ME_SUM,
    LINES_SUM,
    BACK_SUM,
    FINISH_SUM,
) = range(16)
P0, P1, P2, H0, H1, H2, H3, E0, E1, E2, E3, B0, B1, B2, B3, NEED, END = range(100, 117)

FORWARD_PLAN = {P0: [(OWN, 0), (FIRST, 0, 1)],
 P1: [(FIRST, 0, 3), (OWN, 1)],
 P2: [(FIRST, 0, 2), (LINE, 0, 1), (SIDE, 0, 0)],
 END: [(LAST, 5)],
 NEED: {0: [(FIRST, 1, 1), (SIDE, 1, 0), (OWN, 2), (OWN, 3), (FIRST, 1, 3), (LINE, 0, 3), (FIRST, 1, 2),
            (FAR, 0, 1, 0), (FAR, 0, 0, 1), (FAR, 1, 0, 1), (OWN, 4), (SIDE, 0, 1), (FAR, 0, 3, 0),
            (FIRST, 2, 1), (LINE, 1, 1), (SIDE, 2, 0), (SIDE, 3, 0), (LINE, 0, 2), (FAR, 0, 1, 1),
            (FIRST, 2, 3), (SIDE, 0, 3), (FIRST, 2, 2), (OWN, 5), (FAR, 1, 1, 0), (FAR, 2, 0, 1),
            (LINE, 1, 3), (SIDE, 4, 0), (FIRST, 3, 1), (FAR, 3, 0, 1), (FAR, 0, 2, 0), (SIDE, 1, 1),
            (FAR, 0, 3, 1), (LINE, 1, 2), (FIRST, 3, 3), (SIDE, 0, 2), (LINE, 2, 1), (FIRST, 3, 2),
            (FAR, 1, 3, 0), (FAR, 4, 0, 1), (SIDE, 5, 0), (FAR, 1, 1, 1), (SIDE, 1, 3), (LINE, 2, 3),
            (FAR, 1, 2, 0), (FIRST, 4, 1), (LINE, 2, 2), (FAR, 0, 2, 1), (FAR, 2, 1, 0), (SIDE, 1, 2),
            (LINE, 3, 1), (SIDE, 2, 1), (FIRST, 4, 3), (FAR, 5, 0, 1), (LAST, 0)]},
 0: {0: [(FIRST, 4, 2)],
     1: [(LAST, 1), (LINE, 4, 1), (FIRST, 5, 3)],
     2: [(FAR, 2, 2, 1), (FAR, 2, 3, 1), (SIDE, 3, 2), (SIDE, 3, 3), (FAR, 3, 2, 0), (FAR, 3, 3, 0),
         (FAR, 3, 1, 1), (LINE, 4, 2), (SIDE, 4, 1), (FAR, 4, 1, 0), (FAR, 4, 3, 0)],
     3: [(SIDE, 4, 2), (LINE, 5, 2), (FAR, 3, 2, 1)],
     4: [(LAST, 3), (FAR, 4, 2, 1), (SIDE, 5, 2), (FAR, 5, 2, 0), (FAR, 5, 3, 0), (FAR, 5, 1, 1)],
     5: [(LAST, 4), (FAR, 5, 2, 1)]},
 1: {0: [(FAR, 1, 2, 1), (FAR, 1, 3, 1), (SIDE, 2, 2), (SIDE, 2, 3), (FAR, 2, 2, 0), (FAR, 2, 3, 0),
         (FAR, 2, 1, 1), (LINE, 3, 2), (SIDE, 3, 1), (FAR, 3, 1, 0), (LINE, 3, 3), (FIRST, 5, 1)],
     1: [(LINE, 4, 3), (FIRST, 5, 2)],
     2: [(SIDE, 4, 3), (LAST, 2), (LINE, 5, 1)],
     3: [(FAR, 3, 3, 1), (FAR, 4, 2, 0), (FAR, 4, 1, 1), (FAR, 4, 3, 1), (LINE, 5, 3), (FAR, 5, 1, 0),
         (SIDE, 5, 1)],
     4: [(SIDE, 5, 3)],
     5: [(FAR, 5, 3, 1)]}}

HIDDEN_PLAN = {H0: [(OWN, 0), (FIRST, 0, 1)],
 H1: [(FIRST, 0, 3), (OWN, 1)],
 H2: [(FIRST, 0, 2), (LINE, 0, 1), (SIDE, 0, 0)],
 H3: [(FIRST, 1, 1), (SIDE, 1, 0), (OWN, 2)],
 E1: [(LINES_SUM, 1)],
 END: [(BACK_SUM, 1), (FINISH_SUM, 1)],
 1: {0: [(FIRST, 1, 3), (OWN, 3)], 1: [(FAR, 2, 3, 0), (FAR_SUM, 0, 3), (SIDE, 2, 3)]},
 2: {0: [(LINE, 0, 3), (SIDE, 0, 1), (FAR, 0, 1, 0), (FAR, 0, 0, 1), (FIRST, 1, 2), (FAR, 1, 0, 1)],
     1: [(SIDE, 2, 2), (FAR, 2, 2, 0), (FAR, 2, 1, 1), (LINE, 3, 3), (FAR, 3, 1, 0)],
     2: [(SIDE_SUM, 1, 3), (LINES_SUM, 0)]},
 3: {0: [(LINE, 0, 2), (SIDE, 2, 0)], 1: [(LINE, 3, 2), (SIDE, 3, 1)], 2: [(SIDE_SUM, 1, 2)]},
 4: {0: [(LINE, 1, 1), (FIRST, 2, 1), (SIDE, 3, 0)],
     1: [(FAR, 2, 3, 1), (FAR_SUM, 0, 2), (SIDE_SUM, 0, 3), (FAR, 2, 2, 1), (FAR, 3, 3, 0),
         (SEND_SUM, 1, 3)]},
 5: {0: [(SIDE, 0, 3), (FAR, 0, 3, 0), (FAR, 0, 1, 1), (FIRST, 2, 3), (BEGIN_SUM, 0)],
     1: [(SIDE, 3, 3), (FAR, 3, 2, 0), (FAR, 3, 1, 1), (FAR_SUM, 0, 1), (SEND_SUM, 1, 2)],
     2: [(BACK_SUM, 0), (SIDE_SUM, 1, 1)]},
 6: {0: [(SIDE, 0, 2), (FAR, 0, 2, 0), (LINE, 1, 3), (FIRST, 2, 2), (FAR, 2, 0, 1), (BEGIN_SUM, 1)],
     1: [(LAST, 2), (SIDE, 3, 2), (ME0_SUM, 1), (SEND_SUM, 1, 1)]},
 7: {0: [(LINE, 1, 2), (FAR, 0, 3, 1), (SIDE, 1, 1), (FAR, 1, 1, 0), (FAR, 3, 0, 1)],
     1: [(SIDE_SUM, 0, 2), (FAR_SUM, 1, 3), (FAR, 3, 3, 1)],
     2: [(FINISH_SUM, 0)]},
 NEED: {1: [(FAR, 0, 2, 1), (FAR, 1, 3, 0), (LINE, 2, 1), (FIRST, 3, 1), (CORE_SUM, 0), (SIDE, 1, 3),
            (ME0_SUM, 0), (SEND_SUM, 0, 3), (CORE_SUM, 1), (FAR, 1, 2, 0), (FAR, 1, 1, 1), (FIRST, 3, 3),
            (LAST, 0), (SIDE, 1, 2), (SEND_SUM, 0, 2), (LINE, 2, 3), (FAR, 2, 1, 0), (FIRST, 3, 2),
            (FAR, 1, 3, 1), (SIDE, 2, 1), (LINE, 2, 2), (FAR, 1, 2, 1), (LINE, 3, 1), (SEND_SUM, 0, 1),
            (ME_SUM, 0), (LAST, 1)],
        2: [(FAR, 3, 2, 1), (SIDE_SUM, 0, 1), (FAR_SUM, 1, 2), (FAR_SUM, 1, 1), (ME_SUM, 1), (LAST, 3)]}}

BACKWARD_PLAN = {B0: [(BEGIN_SUM, 0), (BEGIN_SUM, 1), (BEGIN_SUM, 2), (BEGIN_SUM, 3), (BEGIN_SUM, 4)],
 E0: [(BACK_SUM, 1), (ME0_SUM, 5), (SEND_SUM, 6, 1), (BEGIN_SUM, 7)],
 E1: [(LINES_SUM, 2), (SIDE_SUM, 3, 1), (FAR_SUM, 5, 3)],
 E2: [(FINISH_SUM, 1), (SIDE_SUM, 4, 3), (FAR_SUM, 5, 2), (CORE_SUM, 7), (SIDE_SUM, 4, 2), (FAR_SUM, 5, 1),
      (ME_SUM, 5), (SEND_SUM, 7, 3)],
 E3: [(LINES_SUM, 3), (SIDE_SUM, 4, 1), (BACK_SUM, 2), (ME0_SUM, 6)],
 END: [(FINISH_SUM, 2), (SIDE_SUM, 5, 3), (FAR_SUM, 6, 3), (SEND_SUM, 7, 2), (SIDE_SUM, 5, 2),
       (FAR_SUM, 6, 2), (SEND_SUM, 7, 1), (FAR_SUM, 6, 1), (ME_SUM, 6), (BACK_SUM, 3), (LINES_SUM, 4),
       (SIDE_SUM, 5, 1), (ME0_SUM, 7), (FINISH_SUM, 3), (SIDE_SUM, 6, 3), (FAR_SUM, 7, 3), (SIDE_SUM, 6, 2),
       (FAR_SUM, 7, 2), (BACK_SUM, 4), (FAR_SUM, 7, 1), (SIDE_SUM, 6, 1), (LINES_SUM, 5), (FINISH_SUM, 4),
       (ME_SUM, 7), (SIDE_SUM, 7, 3), (SIDE_SUM, 7, 2), (BACK_SUM, 5), (LINES_SUM, 6), (SIDE_SUM, 7, 1),
       (FINISH_SUM, 5), (BACK_SUM, 6), (LINES_SUM, 7), (FINISH_SUM, 6), (BACK_SUM, 7), (FINISH_SUM, 7)],
 3: {0: [(CORE_SUM, 4), (ME0_SUM, 4), (SEND_SUM, 4, 3)],
     1: [(ME_SUM, 0), (SEND_SUM, 1, 2)],
     3: [(FAR_SUM, 2, 2), (SIDE_SUM, 1, 3), (SEND_SUM, 4, 2)],
     4: [(SIDE_SUM, 2, 2), (FAR_SUM, 3, 2), (SEND_SUM, 5, 2)],
     5: [(FINISH_SUM, 0), (SIDE_SUM, 3, 2), (FAR_SUM, 4, 1), (SEND_SUM, 6, 2)]},
 0: {1: [(CORE_SUM, 0), (ME0_SUM, 0), (SEND_SUM, 0, 3), (CORE_SUM, 1), (CORE_SUM, 2), (SEND_SUM, 0, 2),
         (CORE_SUM, 3)],
     2: [(FAR_SUM, 0, 3), (SEND_SUM, 1, 1), (BEGIN_SUM, 5)],
     3: [(FAR_SUM, 1, 2), (SEND_SUM, 3, 3)],
     4: [(SIDE_SUM, 1, 2), (FAR_SUM, 2, 1), (SEND_SUM, 4, 1), (BEGIN_SUM, 6)],
     5: [(SEND_SUM, 5, 1)]},
 1: {1: [(SEND_SUM, 0, 1), (ME0_SUM, 1)],
     2: [(FAR_SUM, 0, 2), (ME_SUM, 1), (SEND_SUM, 2, 3)],
     3: [(SIDE_SUM, 0, 2), (FAR_SUM, 1, 1), (SEND_SUM, 3, 2)],
     4: [(SIDE_SUM, 1, 1), (ME0_SUM, 3), (SEND_SUM, 5, 3), (LINES_SUM, 0)],
     5: [(FAR_SUM, 3, 1), (LINES_SUM, 1), (SIDE_SUM, 2, 1), (BACK_SUM, 0), (ME_SUM, 3), (FAR_SUM, 4, 3)]},
 2: {1: [(SEND_SUM, 1, 3), (ME0_SUM, 2), (ME_SUM, 4)],
     2: [(FAR_SUM, 0, 1), (SEND_SUM, 2, 2), (ME_SUM, 2), (CORE_SUM, 5), (SIDE_SUM, 0, 3), (FAR_SUM, 1, 3),
         (SEND_SUM, 2, 1)],
     3: [(SIDE_SUM, 0, 1), (FAR_SUM, 2, 3), (SEND_SUM, 3, 1)],
     4: [(SIDE_SUM, 2, 3), (FAR_SUM, 3, 3), (CORE_SUM, 6)],
     5: [(SIDE_SUM, 3, 3), (FAR_SUM, 4, 2), (SEND_SUM, 6, 3)]}}


class Runner:
    def __init__(self, plan, gather, sums):
        self.plan, self.gather, self.sums = plan, gather, sums

    def act(self, events):
        gather = self.gather
        for what, item, *where in events:
            if what >= BEGIN_SUM:
                one = self.sums[item]
                acts = (
                    one.begin,
                    one.core,
                    one.me0,
                    one.send,
                    one.far,
                    one.side,
                    one.me,
                    one.lines,
                    one.back,
                    one.finish,
                )
                acts[what - BEGIN_SUM](*where)
            else:
                acts = (
                    gather.own_side,
                    gather.first,
                    gather.line,
                    gather.side,
                    gather.far,
                    gather.last,
                )
                acts[what](item, *where)

    def do(self, key):
        self.act(self.plan.get(key, ()))

    def at_step(self, step, key):
        for number, events in self.plan.get(key, {}).items():

            @pl.when(step == number)
            def _(events=events):
                self.act(events)


def gather_forward_kernel(
    shards,
    tokens_ref,
    segment_ref,
    own_params_ref,
    own_qkv_ref,
    own_out_ref,
    own_fc_ref,
    own_proj_ref,
    projected_ref,
    attended_t_ref,
    lse_ref,
    params_ref,
    full_qkv_ref,
    full_out_ref,
    full_fc_ref,
    full_proj_ref,
    mask_ref,
    normed_ref,
    values_t_ref,
    held_ref,
    weights_ref,
    tables_ref,
    group_ref,
    own_block_ref,
    send_sem,
    recv_sem,
    local_sem,
    params_send_sem,
    params_recv_sem,
    load_sem,
    out_sem,
):
    length, width = tokens_ref.shape
    groups = width // GROUP
    blocks = full_fc_ref.shape[0]
    place = Place(shards)
    others = place.others()
    own = [group_ref.at[g] for g in range(groups)] + [own_out_ref]
    full = [weights_ref.at[g] for g in range(groups)] + [full_out_ref]
    for number in range(blocks):
        own += [own_block_ref.at[number], own_proj_ref.at[number * 128 : number * 128 + 128]]
        full += [full_fc_ref.at[number], full_proj_ref.at[number]]
    gather = Gather(place, own, full, send_sem, recv_sem, local_sem)

    def move(source, target, number):
        pltpu.make_async_copy(source, target, load_sem.at[number]).start()

    def moved(whole, number):
        pltpu.make_async_copy(whole, whole, load_sem.at[number]).wait()

    for g in range(groups):
        for part in range(3):
            start = part * width + g * GROUP
            move(
                own_qkv_ref.at[:, start : start + GROUP],
                group_ref.at[g, :, part * GROUP : (part + 1) * GROUP],
                g,
            )
    for number in range(blocks):
        take_block(
            move, own_fc_ref, number, shards, own_block_ref.at[number], groups + number
        )
    place.meet([place.peer(*other) for other in others] + [place.across(), place.sibling()])

    def table(number, other, arriving):
        target = tables_ref.at[place.shard(*other) if arriving else place.me]
        return remote(
            target if arriving else own_params_ref,
            target,
            params_send_sem.at[number],
            params_recv_sem.at[number],
            place.peer(*other),
        )

    for number, other in enumerate(others):
        table(number, other, False).start()
    for g in range(groups):
        moved(group_ref.at[g], g)
    runner = Runner(FORWARD_PLAN, gather, ())

    def outward(g):
        return (
            pltpu.make_async_copy(held_ref.at[g], projected_ref.at[g], out_sem.at[g, 0]),
            pltpu.make_async_copy(weights_ref.at[g], full_qkv_ref.at[g], out_sem.at[g, 1]),
        )

    runner.do(P0)
    for g in range(groups):
        gather.keep(g).start()
    for number in range(blocks):
        moved(own_block_ref.at[number], groups + number)
    for at in range(groups, groups + 1 + 2 * blocks):
        gather.keep(at).start()
    tables_ref[place.me] = own_params_ref[...]
    build_mask(segment_ref, mask_ref)
    runner.do(P1)
    for number, other in enumerate(others):
        table(number, other, True).wait_recv()
    params_ref[...] = jnp.sum(tables_ref[...].astype(f32), axis=0)
    first_norm(tokens_ref, params_ref, normed_ref)
    runner.do(P2)

    @pl.loop(0, 2 * groups)
    def _(pair):
        g, odd = pair // 2, pair % 2
        runner.at_step(pair, NEED)

        @pl.when(odd == 0)
        def _():
            part = block(g, GROUP)
            weights = weights_ref[g].reshape(width, 3 * GROUP)
            values = matmul(normed_ref[...], weights, NN)
            bias = jnp.concatenate(
                [
                    params_ref[BIAS_Q : BIAS_Q + 1, part],
                    jnp.zeros((1, GROUP), f32),
                    params_ref[BIAS_V : BIAS_V + 1, part],
                ],
                axis=1,
            )
            held_ref[g] = (values + bias).astype(bf16)
            values_t_ref[part, :] = jnp.transpose(held_ref[g, :, 2 * GROUP :])
            for copy in outward(g):
                copy.start()

        attend_forward(
            pair,
            held_ref[g, :, block(odd, 2 * HEAD)],
            held_ref[g, :, block(2 + odd, 2 * HEAD)],
            values_t_ref,
            mask_ref,
            attended_t_ref,
            lse_ref,
            lambda which: runner.at_step(pair, which),
        )

    runner.do(END)
    for g in range(groups):
        for copy in outward(g):
            copy.wait()
    for at in range(groups + 1 + 2 * blocks):
        gather.drain(at)
    for number, other in enumerate(others):
        table(number, other, False).wait_send()


def take_block(move, own_fc_ref, number, shards, target_ref, sem):
    own = own_fc_ref.shape[1] // shards
    for shard in range(shards):
        start = shard * own + number * 128
        move(
            own_fc_ref.at[:, start : start + 128],
            target_ref.at[:, shard * 128 : (shard + 1) * 128],
            sem,
        )


def hidden_kernel(
    attended_t_ref,
    tokens_ref,
    cotangent_ref,
    params_ref,
    w_out_ref,
    w_fc_ref,
    w_proj_ref,
    layer_out_ref,
    grad_middle_ref,
    grad_attended_ref,
    grad_w_out_ref,
    grad_w_fc_ref,
    grad_w_proj_t_ref,
    small_ref,
    middle_ref,
    normed_ref,
    normed_t_ref,
    cotangent_t_ref,
    mixed_ref,
    grad_normed_ref,
    activated_ref,
    grad_preact_ref,
):
    step, steps = pl.program_id(0), pl.num_programs(0)
    length, width = tokens_ref.shape
    row = lambda at: params_ref[at : at + 1, :]
    chunks = [slice(at, at + ROW_CHUNK) for at in range(0, length, ROW_CHUNK)]

    @pl.when(step == 0)
    def _():
        attended = jnp.transpose(attended_t_ref[...])
        middle_ref[...] = (
            tokens_ref[...].astype(f32) + matmul(attended, w_out_ref[...], NN) + row(BIAS_OUT)
        )
        for rows in chunks:
            norm, _ = normalized(middle_ref[rows])
            normed_ref[rows] = (norm * row(GAIN2) + row(SHIFT2)).astype(bf16)
        normed_t_ref[...] = jnp.transpose(normed_ref[...])
        cotangent_t_ref[...] = jnp.transpose(cotangent_ref[...])
        mixed_ref[...] = jnp.zeros_like(mixed_ref)
        grad_normed_ref[...] = jnp.zeros_like(grad_normed_ref)
        small_ref[...] = jnp.zeros_like(small_ref)

    bias_sum = 0.0
    bias_row = params_ref[pl.ds(BIAS_FC + step, 1), :]
    for rows in chunks:
        preact = matmul(normed_ref[rows], w_fc_ref[...], NN) + bias_row
        grad_act = matmul(cotangent_ref[rows], w_proj_ref[...], NT)
        square = preact * preact
        bend = jnp.tanh(GELU_SCALE * preact * (1.0 + GELU_CUBE * square))
        gate = 0.5 + 0.5 * bend
        activated_ref[rows] = (preact * gate).astype(bf16)
        slope = gate + (0.5 * GELU_SCALE) * preact * (1.0 - bend * bend) * (
            1.0 + (3 * GELU_CUBE) * square
        )
        grad_preact = (slope * grad_act).astype(bf16)
        grad_preact_ref[rows] = grad_preact
        bias_sum = bias_sum + total(grad_preact.astype(f32))
    small_ref[pl.ds(BIAS_FC + step, 1), :] = bias_sum
    mixed_ref[...] += matmul(activated_ref[...], w_proj_ref[...], NN)
    grad_w_proj_t = matmul(cotangent_t_ref[...], activated_ref[...], NN).astype(bf16)
    pieces, _, piece = grad_w_proj_t_ref.shape
    for at in range(pieces):
        grad_w_proj_t_ref[at] = grad_w_proj_t[:, at * piece : (at + 1) * piece]
    grad_w_fc_ref[...] = matmul(normed_t_ref[...], grad_preact_ref[...], NN).astype(bf16)
    grad_normed_ref[...] += matmul(grad_preact_ref[...], w_fc_ref[...], NT)

    @pl.when(step == steps - 1)
    def _():
        sums = [0.0] * 4
        for rows in chunks:
            middle = middle_ref[rows]
            layer_out_ref[rows] = (middle + mixed_ref[rows] + row(BIAS_PROJ)).astype(bf16)
            norm, inverse = normalized(middle)
            grad_normed = grad_normed_ref[rows]
            cotangent = cotangent_ref[rows].astype(f32)
            grad_middle = cotangent + norm_pull(grad_normed, row(GAIN2), norm, inverse)
            grad_middle_ref[rows] = grad_middle
            normed_ref[rows] = grad_middle.astype(bf16)
            terms = (grad_middle, grad_normed * norm, grad_normed, cotangent)
            sums = [a + total(b) for a, b in zip(sums, terms)]
        for at, value in zip((BIAS_OUT, GAIN2, SHIFT2, BIAS_PROJ), sums):
            small_ref[at : at + 1, :] = value
        grad_branch = normed_ref[...]
        grad_w_out_ref[...] = matmul(attended_t_ref[...], grad_branch, NN).astype(bf16)
        grad_attended_ref[...] = matmul(grad_branch, w_out_ref[...], NT).astype(bf16)


def sum_hidden_kernel(
    shards,
    attended_t_ref,
    tokens_ref,
    cotangent_ref,
    params_ref,
    w_out_ref,
    fc_in_ref,
    proj_in_ref,
    own_fc_ref,
    own_proj_ref,
    layer_out_ref,
    grad_middle_ref,
    grad_attended_ref,
    grad_out_ref,
    last_fc_ref,
    last_proj_ref,
    done_fc_ref,
    done_proj_ref,
    small_ref,
    middle_ref,
    normed_ref,
    normed_t_ref,
    cotangent_t_ref,
    mixed_ref,
    grad_normed_ref,
    activated_ref,
    grad_preact_ref,
    fc_ref,
    proj_ref,
    grad_fc_ref,
    grad_proj_ref,
    own_block_ref,
    *rest,
):
    length, width = tokens_ref.shape
    blocks = fc_ref.shape[0]
    units = fc_ref.shape[3]
    early = fc_in_ref.shape[0]
    summed = done_fc_ref.shape[0]
    buffers, rest = [rest[SUM_BUFFERS * k :][:SUM_BUFFERS] for k in range(2 * summed)], rest[
        SUM_BUFFERS * 2 * summed :
    ]
    send_sem, recv_sem, local_sem, load_sem, sum_send_sem, sum_recv_sem = rest
    row = lambda at: params_ref[at : at + 1, 0:width]
    chunks = [slice(at, at + ROW_CHUNK) for at in range(0, length, ROW_CHUNK)]
    place = Place(shards)

    def move(source, target, number):
        pltpu.make_async_copy(source, target, load_sem.at[number]).start()

    def moved(whole, number):
        pltpu.make_async_copy(whole, whole, load_sem.at[number]).wait()

    for number in range(early):
        move(fc_in_ref.at[number], fc_ref.at[number], number)
        move(proj_in_ref.at[number], proj_ref.at[number], blocks + number)
    own, full = [], []
    for number in range(early, blocks):
        own_block = own_block_ref.at[number - early]
        take_block(move, own_fc_ref, number, shards, own_block, number)
        own += [own_block, own_proj_ref.at[number * 128 : number * 128 + 128]]
        full += [fc_ref.at[number], proj_ref.at[number]]
    gather = Gather(place, own, full, send_sem, recv_sem, local_sem)
    sums = []
    for number in range(summed):
        for grad, done in ((grad_proj_ref, done_proj_ref), (grad_fc_ref, done_fc_ref)):
            k = len(sums)
            sums.append(
                Summed(
                    place,
                    grad.at[number],
                    done.at[number],
                    buffers[k],
                    sum_send_sem.at[k],
                    sum_recv_sem.at[k],
                )
            )
    runner = Runner(HIDDEN_PLAN, gather, sums)
    place.meet(
        [place.peer(hop, 0) for hop in range(1, place.lines)]
        + [place.peer(0, 1), place.across(), place.sibling()]
    )
    for number in range(early, blocks):
        moved(own_block_ref.at[number - early], number)
    runner.do(H0)
    for at in range(len(own)):
        gather.keep(at).start()

    attended = jnp.transpose(attended_t_ref[...])
    w_out = w_out_ref[...].reshape(width, width)
    middle_ref[...] = tokens_ref[...].astype(f32) + matmul(attended, w_out, NN) + row(BIAS_OUT)
    runner.do(H1)
    for rows in chunks:
        norm, _ = normalized(middle_ref[rows])
        normed_ref[rows] = (norm * row(GAIN2) + row(SHIFT2)).astype(bf16)
    runner.do(H2)
    normed_t_ref[...] = jnp.transpose(normed_ref[...])
    cotangent_t_ref[...] = jnp.transpose(cotangent_ref[...])
    mixed_ref[...] = jnp.zeros_like(mixed_ref)
    grad_normed_ref[...] = jnp.zeros_like(grad_normed_ref)
    small_ref[...] = jnp.zeros_like(small_ref)
    for number in range(early):
        moved(fc_ref.at[number], number)
        moved(proj_ref.at[number], blocks + number)
    runner.do(H3)

    @pl.loop(0, blocks)
    def _(step):
        runner.at_step(step, NEED)
        w_fc = fc_ref.at[step]
        w_proj = proj_ref.at[step]
        bias_sum = 0.0
        bias_row = params_ref[pl.ds(BIAS_FC + step, 1), 0:units]
        for tick, rows in enumerate(chunks):
            runner.at_step(step, tick)
            preact = matmul(normed_ref[rows], w_fc[...].reshape(width, units), NN) + bias_row
            grad_act = matmul(cotangent_ref[rows], w_proj[...].reshape(units, width), NT)
            square = preact * preact
            bend = jnp.tanh(GELU_SCALE * preact * (1.0 + GELU_CUBE * square))
            gate = 0.5 + 0.5 * bend
            activated_ref[rows] = (preact * gate).astype(bf16)
            slope = gate + (0.5 * GELU_SCALE) * preact * (1.0 - bend * bend) * (
                1.0 + (3 * GELU_CUBE) * square
            )
            grad_preact = (slope * grad_act).astype(bf16)
            grad_preact_ref[rows] = grad_preact
            bias_sum = bias_sum + total(grad_preact.astype(f32))
        small_ref[pl.ds(BIAS_FC + step, 1), 0:units] = bias_sum
        runner.at_step(step, len(chunks))
        grad_proj = matmul(cotangent_t_ref[...], activated_ref[...], NN).astype(bf16)
        for shard in range(shards):
            grad_proj_ref[step, shard] = grad_proj[:, shard * 128 : (shard + 1) * 128]
        runner.at_step(step, len(chunks) + 1)
        grad_fc = matmul(normed_t_ref[...], grad_preact_ref[...], NN).astype(bf16)
        grad_fc_ref[step] = grad_fc.reshape(grad_fc_ref.shape[1:])
        runner.at_step(step, len(chunks) + 2)
        mixed_ref[...] += matmul(activated_ref[...], w_proj[...].reshape(units, width), NN)
        runner.at_step(step, len(chunks) + 3)
        grad_normed_ref[...] += matmul(
            grad_preact_ref[...], w_fc[...].reshape(width, units), NT
        )

    hand_over = []

    def hand(source, target):
        copy = pltpu.make_async_copy(source, target, load_sem.at[len(hand_over)])
        copy.start()
        hand_over.append(copy)

    hand(grad_fc_ref.at[summed:blocks], last_fc_ref)
    hand(grad_proj_ref.at[summed:blocks], last_proj_ref)
    parts = [0.0] * 4
    for number, rows in enumerate(chunks):
        if number < 2:
            runner.do(E0 + number)
        middle = middle_ref[rows]
        layer_out_ref[rows] = (middle + mixed_ref[rows] + row(BIAS_PROJ)).astype(bf16)
        norm, inverse = normalized(middle)
        grad_normed = grad_normed_ref[rows]
        cotangent = cotangent_ref[rows].astype(f32)
        grad_middle = cotangent + norm_pull(grad_normed, row(GAIN2), norm, inverse)
        middle_ref[rows] = grad_middle
        normed_ref[rows] = grad_middle.astype(bf16)
        terms = (grad_middle, grad_normed * norm, grad_normed, cotangent)
        parts = [a + total(b) for a, b in zip(parts, terms)]
    for at, value in zip((BIAS_OUT, GAIN2, SHIFT2, BIAS_PROJ), parts):
        small_ref[at : at + 1, 0:width] = value
    hand(middle_ref, grad_middle_ref)
    runner.do(E2)
    grad_branch = normed_ref[...]
    grad_out = matmul(attended_t_ref[...], grad_branch, NN).astype(bf16)
    grad_out_ref[...] = grad_out.reshape(grad_out_ref.shape)
    runner.do(E3)
    grad_attended_ref[...] = matmul(grad_branch, w_out, NT).astype(bf16)
    runner.do(END)
    for copy in hand_over:
        copy.wait()
    for item in sums:
        item.drain()
    for at in range(len(own)):
        gather.drain(at)


def backward_kernel(
    tokens_ref,
    segment_ref,
    params_ref,
    w_qkv_ref,
    projected_ref,
    attended_t_ref,
    lse_ref,
    grad_attended_ref,
    grad_middle_ref,
    small_in_ref,
    grad_tokens_ref,
    grad_w_qkv_ref,
    small_ref,
    mask_ref,
    wide_t_ref,
    grad_queries_t_ref,
    dots_ref,
    grad_projected_ref,
    grad_keys_ref,
    grad_values_ref,
):
    length, width = tokens_ref.shape
    build_mask(segment_ref, mask_ref)
    dot_rows(attended_t_ref, grad_attended_ref, wide_t_ref, dots_ref)
    wide_t_ref[...] = jnp.transpose(projected_ref[:, width : 2 * width])

    pairs = width // (2 * HEAD)

    @pl.loop(0, pairs)
    def _(pair):
        parts = [projected_ref[:, block(k * pairs + pair, 2 * HEAD)] for k in range(3)]
        attend_backward(
            pair,
            parts + [grad_attended_ref[:, block(pair, 2 * HEAD)]],
            wide_t_ref,
            mask_ref,
            lse_ref,
            dots_ref,
            grad_queries_t_ref,
            grad_keys_ref,
            grad_values_ref,
        )
        for k, ref in ((1, grad_keys_ref), (2, grad_values_ref)):
            grad_projected_ref[:, block(k * pairs + pair, 2 * HEAD)] = ref[...].astype(bf16)

    grad_projected_ref[:, 0:width] = jnp.transpose(grad_queries_t_ref[...])
    normed_transposed(tokens_ref, params_ref, wide_t_ref)
    small_ref[...] = small_in_ref[...]
    bias_sums(grad_projected_ref, small_ref)
    grad_w_qkv_ref[...] = matmul(wide_t_ref[...], grad_projected_ref[...], NN).astype(bf16)
    gain_sum = shift_sum = 0.0
    for at in range(0, length, ROW_CHUNK):
        gain_part, shift_part = token_rows(
            at,
            tokens_ref,
            params_ref,
            matmul(grad_projected_ref[at : at + ROW_CHUNK], w_qkv_ref[...], NT),
            grad_middle_ref[at : at + ROW_CHUNK],
            grad_tokens_ref,
        )
        gain_sum, shift_sum = gain_sum + gain_part, shift_sum + shift_part
    small_ref[GAIN1 : GAIN1 + 1, :] = gain_sum
    small_ref[SHIFT1 : SHIFT1 + 1, :] = shift_sum


def dot_rows(attended_t_ref, grad_attended_ref, wide_t_ref, dots_ref):
    wide_t_ref[...] = jnp.transpose(grad_attended_ref[...])
    for head in range(wide_t_ref.shape[0] // HEAD):
        rows = slice(head * HEAD, (head + 1) * HEAD)
        dots_ref[head : head + 1, :] = total(
            wide_t_ref[rows].astype(f32) * attended_t_ref[rows].astype(f32)
        )


def normed_transposed(tokens_ref, params_ref, wide_t_ref):
    width = tokens_ref.shape[1]
    row = lambda at: params_ref[at : at + 1, 0:width]
    for at in range(0, tokens_ref.shape[0], ROW_CHUNK):
        norm, _ = normalized(tokens_ref[at : at + ROW_CHUNK].astype(f32))
        normed = (norm * row(GAIN1) + row(SHIFT1)).astype(bf16)
        wide_t_ref[:, at : at + ROW_CHUNK] = jnp.transpose(normed)


def bias_sums(grad_projected_ref, small_ref):
    width = small_ref.shape[1]
    for at, part in ((BIAS_Q, 0), (BIAS_V, 2)):
        values = grad_projected_ref[:, part * width : (part + 1) * width]
        small_ref[at : at + 1, :] = total(values.astype(f32))


def token_rows(at, tokens_ref, params_ref, grad_normed, middle, grad_tokens_ref):
    rows = slice(at, at + ROW_CHUNK)
    gain = params_ref[GAIN1 : GAIN1 + 1, 0 : tokens_ref.shape[1]]
    norm, inverse = normalized(tokens_ref[rows].astype(f32))
    grad_rows = norm_pull(grad_normed, gain, norm, inverse)
    grad_tokens_ref[rows] = (middle + grad_rows).astype(bf16)
    return total(grad_normed * norm), total(grad_normed)


def sum_backward_kernel(
    shards,
    tokens_ref,
    segment_ref,
    params_ref,
    attended_t_ref,
    lse_ref,
    grad_attended_ref,
    small_in_ref,
    projected_in_ref,
    w_qkv_in_ref,
    grad_middle_in_ref,
    grad_out_in_ref,
    grad_fc_in_ref,
    grad_proj_in_ref,
    grad_tokens_ref,
    done_qkv_ref,
    done_out_ref,
    done_fc_ref,
    done_proj_ref,
    small_ref,
    mask_ref,
    wide_t_ref,
    normed_t_ref,
    grad_queries_t_ref,
    dots_ref,
    projected_ref,
    grad_projected_ref,
    grad_keys_ref,
    grad_values_ref,
    grad_qkv_ref,
    grad_out_ref,
    grad_fc_ref,
    grad_proj_ref,
    weights_ref,
    *rest,
):
    length, width = tokens_ref.shape
    groups = width // GROUP
    late_blocks = grad_fc_ref.shape[0]
    items = 2 * late_blocks + 1 + groups
    buffers, rest = [rest[SUM_BUFFERS * k :][:SUM_BUFFERS] for k in range(items)], rest[
        SUM_BUFFERS * items :
    ]
    small_core_ref, small_far_ref, small_side_ref, small_line_ref, *rest = rest
    send_sem, recv_sem, load_sem, small_send_sem, small_recv_sem = rest
    place = Place(shards)
    lines = place.lines
    arrays = []
    for number in range(late_blocks):
        arrays += [
            (grad_proj_ref.at[number], done_proj_ref.at[number], grad_proj_in_ref.at[number]),
            (grad_fc_ref.at[number], done_fc_ref.at[number], grad_fc_in_ref.at[number]),
        ]
    arrays.append((grad_out_ref, done_out_ref, grad_out_in_ref))
    arrays += [(grad_qkv_ref.at[g], done_qkv_ref.at[g], None) for g in range(groups)]
    sums = [
        Summed(
            place,
            grad,
            done,
            buffers[k],
            send_sem.at[k],
            recv_sem.at[k],
            source,
            None if source is None else load_sem.at[k],
        )
        for k, (grad, done, source) in enumerate(arrays)
    ]
    runner = Runner(BACKWARD_PLAN, None, sums)
    load_projected = pltpu.make_async_copy(projected_in_ref, projected_ref, load_sem.at[items])
    load_projected.start()
    load_weights = pltpu.make_async_copy(w_qkv_in_ref, weights_ref, load_sem.at[items + 1])
    load_weights.start()
    place.meet(
        [place.peer(hop, 0) for hop in range(1, lines)]
        + [place.peer(0, 1), place.across(), place.sibling()]
    )
    runner.do(B0)
    build_mask(segment_ref, mask_ref)
    runner.do(B1)
    dot_rows(attended_t_ref, grad_attended_ref, wide_t_ref, dots_ref)
    runner.do(B2)
    normed_transposed(tokens_ref, params_ref, normed_t_ref)
    small_ref[...] = small_in_ref[...]
    load_projected.wait()
    for g in range(groups):
        wide_t_ref[g * GROUP : (g + 1) * GROUP] = jnp.transpose(
            projected_ref[g, :, GROUP : 2 * GROUP]
        )
    runner.do(B3)

    @pl.loop(0, 2 * groups)
    def _(pair):
        g, odd = pair // 2, pair % 2
        parts = [projected_ref[g, :, block(2 * k + odd, 2 * HEAD)] for k in range(3)]
        attend_backward(
            pair,
            parts + [grad_attended_ref[:, block(pair, 2 * HEAD)]],
            wide_t_ref,
            mask_ref,
            lse_ref,
            dots_ref,
            grad_queries_t_ref,
            grad_keys_ref,
            grad_values_ref,
            lambda number: runner.at_step(pair, number),
        )
        grad_queries = jnp.transpose(grad_queries_t_ref[block(pair, 2 * HEAD), :])
        grad_projected_ref[g, :, block(odd, 2 * HEAD)] = grad_queries
        for k, ref in ((1, grad_keys_ref), (2, grad_values_ref)):
            grad_projected_ref[g, :, block(2 * k + odd, 2 * HEAD)] = ref[...].astype(bf16)

        @pl.when(odd == 1)
        def _():
            grad_group = matmul(normed_t_ref[...], grad_projected_ref[g], NN).astype(bf16)
            grad_qkv_ref[g] = grad_group.reshape(grad_qkv_ref.shape[1:])

    middle_ref = mask_ref.at[:, 0:width]
    load_middle = pltpu.make_async_copy(grad_middle_in_ref, middle_ref, load_sem.at[items])
    load_middle.start()
    for g in range(groups):
        part = slice(g * GROUP, (g + 1) * GROUP)
        for at, k in ((BIAS_Q, 0), (BIAS_V, 2)):
            values = grad_projected_ref[g, :, k * GROUP : (k + 1) * GROUP]
            small_ref[at : at + 1, part] = total(values.astype(f32))
    load_weights.wait()
    load_middle.wait()
    gain_sum = shift_sum = 0.0
    for number, at in enumerate(range(0, length, ROW_CHUNK)):
        runner.do(E0 + number)
        rows = slice(at, at + ROW_CHUNK)
        grad_normed = 0.0
        for g in range(groups):
            weights = weights_ref[g].reshape(width, 3 * GROUP)
            grad_normed = grad_normed + matmul(grad_projected_ref[g, rows], weights, NT)
        gain_part, shift_part = token_rows(
            at, tokens_ref, params_ref, grad_normed, mask_ref[rows, 0:width], grad_tokens_ref
        )
        gain_sum, shift_sum = gain_sum + gain_part, shift_sum + shift_part
    small_ref[GAIN1 : GAIN1 + 1, 0:width] = gain_sum
    small_ref[SHIFT1 : SHIFT1 + 1, 0:width] = shift_sum

    def exchange(slot, into_ref, peer):
        copy = remote(small_ref, into_ref, small_send_sem.at[slot], small_recv_sem.at[slot], peer)
        copy.start()
        return copy

    todo = BACKWARD_PLAN.get(END, ())
    parts = [todo[len(todo) * k // 5 : len(todo) * (k + 1) // 5] for k in range(5)]
    for slot, into_ref, peer in (
        (0, small_core_ref, place.sibling()),
        (1, small_far_ref, place.across()),
        (2, small_side_ref, place.peer(0, 1)),
    ):
        copy = exchange(slot, into_ref, peer)
        runner.act(parts[slot])
        copy.wait()
        small_ref[...] += into_ref[...]
    copies = [
        exchange(2 + hop, small_line_ref.at[hop - 1], place.peer(hop, 0))
        for hop in range(1, lines)
    ]
    runner.act(parts[3] + parts[4])
    for copy in copies:
        copy.wait()
    small = small_ref[...]
    for hop in range(1, lines):
        small = small + small_line_ref[hop - 1]
    small_ref[...] = small
    for item in sums:
        item.drain()


def finish_kernel(
    shards,
    qkv_ref,
    out_ref,
    fc_early_ref,
    fc_last_ref,
    proj_early_ref,
    proj_last_ref,
    small_ref,
    sum_qkv_ref,
    sum_out_ref,
    sum_fc_ref,
    sum_proj_ref,
    mine_ref,
):
    groups, own, _ = qkv_ref.shape
    width = groups * GROUP
    for g in range(groups):
        for part in range(3):
            start = part * width + g * GROUP
            sum_qkv_ref[:, start : start + GROUP] = qkv_ref[
                g, :, part * GROUP : (part + 1) * GROUP
            ].astype(f32)
    sum_out_ref[...] = out_ref[...].astype(f32)
    early = fc_early_ref.shape[0]
    blocks = early + fc_last_ref.shape[0]
    for number in range(blocks):
        fc = fc_early_ref.at[number] if number < early else fc_last_ref.at[number - early]
        proj = proj_early_ref.at[number] if number < early else proj_last_ref.at[number - early]
        for shard in range(shards):
            start = (shard * blocks + number) * 128
            sum_fc_ref[:, start : start + 128] = fc[:, shard * 128 : (shard + 1) * 128].astype(f32)
        sum_proj_ref[number * 128 : (number + 1) * 128] = jnp.transpose(proj[...].astype(f32))
    me = lax.axis_index("shard")
    mine_ref[...] = jnp.zeros_like(mine_ref)
    for shard in range(shards):

        @pl.when(me == shard)
        def _(shard=shard):
            mine_ref[0:8, 0:own] = small_ref[0:8, shard * own : (shard + 1) * own]
            mine_ref[8:16, :] = small_ref[8:16, shard * 128 : (shard + 1) * 128]


def kernel_params():
    return pltpu.CompilerParams(vmem_limit_bytes=VMEM_LIMIT)


def run_forward(tokens, segment, params, w_qkv):
    length, width = tokens.shape
    return pl.pallas_call(
        forward_kernel,
        in_specs=[WHOLE] * 4,
        out_specs=(WHOLE,) * 3,
        out_shape=(
            jax.ShapeDtypeStruct((length, 3 * width), bf16),
            jax.ShapeDtypeStruct((width, length), bf16),
            jax.ShapeDtypeStruct((16, length), f32),
        ),
        scratch_shapes=[
            pltpu.VMEM((length, length), f32),
            pltpu.VMEM((length, width), bf16),
            pltpu.VMEM((width, length), bf16),
        ],
        compiler_params=kernel_params(),
        name="forward",
    )(tokens, segment, params, w_qkv)


def run_hidden(attended_t, tokens, cotangent, params, w_out, w_fc, w_proj, piece):
    length, width = tokens.shape
    hidden = w_fc.shape[1]
    shape = jax.ShapeDtypeStruct
    columns = pl.BlockSpec((width, width), lambda step: (0, step))
    return pl.pallas_call(
        hidden_kernel,
        grid=(hidden // width,),
        in_specs=[WHOLE] * 5 + [columns, pl.BlockSpec((width, width), lambda step: (step, 0))],
        out_specs=(
            WHOLE,
            WHOLE,
            WHOLE,
            WHOLE,
            columns,
            pl.BlockSpec((width // piece, width, piece), lambda step: (step, 0, 0)),
            WHOLE,
        ),
        out_shape=(
            shape((length, width), bf16),
            shape((length, width), f32),
            shape((length, width), bf16),
            shape((width, width), bf16),
            shape((width, hidden), bf16),
            shape((hidden // piece, width, piece), bf16),
            shape((16, width), f32),
        ),
        scratch_shapes=[
            pltpu.VMEM((length, width), f32),
            pltpu.VMEM((length, width), bf16),
            pltpu.VMEM((width, length), bf16),
            pltpu.VMEM((width, length), bf16),
            pltpu.VMEM((length, width), f32),
            pltpu.VMEM((length, width), f32),
            pltpu.VMEM((length, width), bf16),
            pltpu.VMEM((length, width), bf16),
        ],
        compiler_params=kernel_params(),
        name="hidden",
    )(attended_t, tokens, cotangent, params, w_out, w_fc, w_proj)


def run_backward(
    tokens, segment, params, w_qkv, projected, attended_t, lse, grad_attended, grad_middle, small
):
    length, width = tokens.shape
    shape = jax.ShapeDtypeStruct
    return pl.pallas_call(
        backward_kernel,
        in_specs=[WHOLE] * 10,
        out_specs=(WHOLE,) * 3,
        out_shape=(
            shape((length, width), bf16),
            shape((width, 3 * width), bf16),
            shape((16, width), f32),
        ),
        scratch_shapes=[
            pltpu.VMEM((length, length), f32),
            pltpu.VMEM((width, length), bf16),
            pltpu.VMEM((width, length), bf16),
            pltpu.VMEM((16, length), f32),
            pltpu.VMEM((length, 3 * width), bf16),
            pltpu.VMEM((length, 2 * HEAD), f32),
            pltpu.VMEM((length, 2 * HEAD), f32),
        ],
        compiler_params=kernel_params(),
        name="backward",
    )(
        tokens,
        segment,
        params,
        w_qkv,
        projected,
        attended_t,
        lse,
        grad_attended,
        grad_middle,
        small,
    )


def link_params(number):
    return pltpu.CompilerParams(
        vmem_limit_bytes=VMEM_LIMIT, collective_id=number, has_side_effects=True
    )


def run_gather_forward(shards, tokens, segment, own_params, w_qkv, w_out, w_fc, w_proj):
    length, width = tokens.shape
    own = w_qkv.shape[0]
    groups = width // GROUP
    blocks = GATHERED_EARLY
    items = groups + 1 + 2 * blocks
    shape = jax.ShapeDtypeStruct
    copies = 3 * shards - 3
    dma = pltpu.SemaphoreType.DMA
    return pl.pallas_call(
        partial(gather_forward_kernel, shards),
        in_specs=[WHOLE] * 3 + [HBM] * 4,
        out_specs=(HBM,) + (WHOLE,) * 3 + (HBM,) * 4,
        out_shape=(
            shape((groups, length, 3 * GROUP), bf16),
            shape((width, length), bf16),
            shape((16, length), f32),
            shape(own_params.shape, f32),
            shape((groups, shards, own, 3 * GROUP), bf16),
            shape((shards, own, width), bf16),
            shape((blocks, shards, own, shards * 128), bf16),
            shape((blocks, shards, 128, width), bf16),
        ),
        scratch_shapes=[
            pltpu.VMEM((length, length), f32),
            pltpu.VMEM((length, width), bf16),
            pltpu.VMEM((width, length), bf16),
            pltpu.VMEM((groups, length, 3 * GROUP), bf16),
            pltpu.VMEM((groups, shards, own, 3 * GROUP), bf16),
            pltpu.VMEM((shards,) + own_params.shape, bf16),
            pltpu.VMEM((groups, own, 3 * GROUP), bf16),
            pltpu.VMEM((blocks, own, shards * 128), bf16),
            dma((items, copies)),
            dma((items, copies)),
            dma((items,)),
            dma((shards - 1,)),
            dma((shards - 1,)),
            dma((groups + blocks,)),
            dma((groups, 2)),
        ],
        compiler_params=link_params(0),
        name="gather_forward",
    )(tokens, segment, own_params, w_qkv, w_out, w_fc, w_proj)


def run_sum_hidden(
    shards, attended_t, tokens, cotangent, params, full_out, full_fc, full_proj, w_fc, w_proj
):
    length, width = tokens.shape
    own, units = w_fc.shape[0], shards * 128
    blocks = w_proj.shape[0] // 128
    lines = shards // 2
    shape = jax.ShapeDtypeStruct
    dma = pltpu.SemaphoreType.DMA
    grads = ((shards, own, units), (shards, width, 128))
    late, early = blocks - full_fc.shape[0], SUMMED_EARLY
    buffers = [
        ref
        for _ in range(early)
        for grad in reversed(grads)
        for ref in sum_buffers(lines, *grad)
    ]
    return pl.pallas_call(
        partial(sum_hidden_kernel, shards),
        in_specs=[WHOLE] * 5 + [HBM] * 4,
        out_specs=(WHOLE, HBM, WHOLE, WHOLE, HBM, HBM) + (WHOLE,) * 3,
        out_shape=(
            shape((length, width), bf16),
            shape((length, width), f32),
            shape((length, width), bf16),
            shape((shards, own, width), bf16),
            shape((blocks - early,) + grads[0], bf16),
            shape((blocks - early,) + grads[1], bf16),
            shape((early, own, units), bf16),
            shape((early, width, 128), bf16),
            shape(params.shape, f32),
        ),
        scratch_shapes=[
            pltpu.VMEM((length, width), f32),
            pltpu.VMEM((length, width), bf16),
            pltpu.VMEM((width, length), bf16),
            pltpu.VMEM((width, length), bf16),
            pltpu.VMEM((length, width), f32),
            pltpu.VMEM((length, width), f32),
            pltpu.VMEM((length, units), bf16),
            pltpu.VMEM((length, units), bf16),
            pltpu.VMEM((blocks, shards, own, units), bf16),
            pltpu.VMEM((blocks, shards, 128, width), bf16),
            pltpu.VMEM((blocks,) + grads[0], bf16),
            pltpu.VMEM((blocks,) + grads[1], bf16),
            pltpu.VMEM((late, own, units), bf16),
        ]
        + buffers
        + [
            dma((2 * late, 3 * shards - 3)),
            dma((2 * late, 3 * shards - 3)),
            dma((2 * late,)),
            dma((2 * blocks,)),
        ]
        + sum_sems(lines, 2 * early),
        compiler_params=link_params(1),
        name="sum_hidden",
    )(attended_t, tokens, cotangent, params, full_out, full_fc, full_proj, w_fc, w_proj)


def run_sum_backward(
    shards,
    tokens,
    segment,
    params,
    attended_t,
    lse,
    grad_attended,
    small,
    projected,
    w_qkv,
    grad_middle,
    grad_out,
    grad_fc,
    grad_proj,
):
    length, width = tokens.shape
    shape = jax.ShapeDtypeStruct
    lines, groups = shards // 2, width // GROUP
    own = width // shards
    qkv = (shards, own, 3 * GROUP)
    late_blocks = grad_fc.shape[0]
    grads = [grad_proj.shape[1:], grad_fc.shape[1:]] * late_blocks
    grads += [grad_out.shape] + [qkv] * groups
    buffers = [ref for grad in grads for ref in sum_buffers(lines, *grad)]
    table = pltpu.VMEM(params.shape, f32)
    dma = pltpu.SemaphoreType.DMA
    items = len(grads)
    return pl.pallas_call(
        partial(sum_backward_kernel, shards),
        in_specs=[WHOLE] * 7 + [HBM] * 6,
        out_specs=(WHOLE,) * 6,
        out_shape=(
            shape((length, width), bf16),
            shape((groups,) + qkv[1:], bf16),
            shape(grad_out.shape[1:], bf16),
            shape((late_blocks,) + grad_fc.shape[2:], bf16),
            shape((late_blocks,) + grad_proj.shape[2:], bf16),
            shape(params.shape, f32),
        ),
        scratch_shapes=[
            pltpu.VMEM((length, length), f32),
            pltpu.VMEM((width, length), bf16),
            pltpu.VMEM((width, length), bf16),
            pltpu.VMEM((width, length), bf16),
            pltpu.VMEM((16, length), f32),
            pltpu.VMEM(projected.shape, bf16),
            pltpu.VMEM(projected.shape, bf16),
            pltpu.VMEM((length, 2 * HEAD), f32),
            pltpu.VMEM((length, 2 * HEAD), f32),
            pltpu.VMEM((groups,) + qkv, bf16),
            pltpu.VMEM(grad_out.shape, bf16),
            pltpu.VMEM(grad_fc.shape, bf16),
            pltpu.VMEM(grad_proj.shape, bf16),
            pltpu.VMEM(w_qkv.shape, bf16),
        ]
        + buffers
        + [table, table, table, pltpu.VMEM((lines - 1,) + params.shape, f32)]
        + sum_sems(lines, items)
        + [dma((items + 2,)), dma((lines + 2,)), dma((lines + 2,))],
        compiler_params=link_params(2),
        name="sum_backward",
    )(
        tokens,
        segment,
        params,
        attended_t,
        lse,
        grad_attended,
        small,
        projected,
        w_qkv,
        grad_middle,
        grad_out,
        grad_fc,
        grad_proj,
    )


def run_finish(shards, qkv, out, fc_early, fc_last, proj_early, proj_last, small):
    groups, own, _ = qkv.shape
    width = out.shape[1]
    blocks = fc_early.shape[0] + fc_last.shape[0]
    shape = jax.ShapeDtypeStruct
    return pl.pallas_call(
        partial(finish_kernel, shards),
        in_specs=[WHOLE] * 7,
        out_specs=(WHOLE,) * 5,
        out_shape=(
            shape((own, 3 * width), f32),
            shape((own, width), f32),
            shape((own, blocks * shards * 128), f32),
            shape((blocks * 128, width), f32),
            shape((16, 128), f32),
        ),
        compiler_params=kernel_params(),
        name="finish",
    )(qkv, out, fc_early, fc_last, proj_early, proj_last, small)


def by_kernels(
    shards, tokens, segment_ids, vectors, fc_bias, w_qkv, w_out, w_fc, w_proj, cotangent
):
    width, hidden = tokens.shape[1], w_fc.shape[1]
    blocks, units = w_proj.shape[0] // 128, shards * 128
    span = max(width, units)
    me = lax.axis_index("shard")
    mine = lax.broadcasted_iota(jnp.int32, (1, shards, 1), 1) == me
    zero = jnp.zeros((), bf16)
    rows = jnp.where(mine, jnp.stack(vectors)[:, None, :], zero).reshape(8, width)
    hidden_rows = jnp.where(mine, fc_bias.reshape(blocks, 1, 128), zero).reshape(blocks, units)
    table = jnp.concatenate(
        [
            jnp.pad(rows, ((0, 0), (0, span - width))),
            jnp.pad(hidden_rows, ((0, 8 - blocks), (0, span - units))),
        ]
    )
    projected, attended_t, lse, params, full_qkv, full_out, full_fc, full_proj = (
        run_gather_forward(shards, tokens, segment_ids, table, w_qkv, w_out, w_fc, w_proj)
    )
    (
        layer_out,
        grad_middle,
        grad_attended,
        grad_out,
        grad_fc,
        grad_proj,
        fc_early,
        proj_early,
        small,
    ) = run_sum_hidden(
        shards, attended_t, tokens, cotangent, params, full_out, full_fc, full_proj, w_fc, w_proj
    )
    grad_tokens, done_qkv, done_out, fc_last, proj_last, small = run_sum_backward(
        shards,
        tokens,
        segment_ids,
        params,
        attended_t,
        lse,
        grad_attended,
        small,
        projected,
        full_qkv,
        grad_middle,
        grad_out,
        grad_fc,
        grad_proj,
    )
    sum_qkv, sum_out, sum_fc, sum_proj, own_small = run_finish(
        shards, done_qkv, done_out, fc_early, fc_last, proj_early, proj_last, small
    )
    own = vectors[0].shape[0]
    pick = lambda at: own_small[at, 0:own]
    return (
        layer_out,
        grad_tokens,
        pick(GAIN1),
        pick(SHIFT1),
        sum_qkv,
        pick(BIAS_Q),
        pick(BIAS_V),
        sum_out,
        pick(BIAS_OUT),
        pick(GAIN2),
        pick(SHIFT2),
        sum_fc,
        own_small[BIAS_FC : BIAS_FC + blocks, 0:128].reshape(-1),
        sum_proj,
        pick(BIAS_PROJ),
    )


def on_device(
    replicas,
    shards,
    tokens,
    segment_ids,
    norm1_gain,
    norm1_shift,
    w_qkv,
    q_bias,
    v_bias,
    w_out,
    out_bias,
    norm2_gain,
    norm2_shift,
    w_fc,
    fc_bias,
    w_proj,
    proj_bias,
    cotangent,
):
    width, hidden = tokens.shape[1], w_fc.shape[1]
    vectors = (
        norm1_gain,
        norm1_shift,
        q_bias,
        v_bias,
        out_bias,
        norm2_gain,
        norm2_shift,
        proj_bias,
    )
    own, own_hidden = norm1_gain.shape[0], fc_bias.shape[0]
    if (
        replicas == 4
        and shards & (shards - 1) == 0
        and own % 96 == 0
        and own_hidden == 3 * 128
        and width == 3 * GROUP
    ):
        return by_kernels(
            shards, tokens, segment_ids, vectors, fc_bias, w_qkv, w_out, w_fc, w_proj, cotangent
        )
    me = lax.axis_index("shard")
    mine = (lax.broadcasted_iota(jnp.int32, (1, shards, 1), 1) == me).astype(bf16)
    table = jnp.concatenate(
        [
            (jnp.stack(vectors)[:, None, :] * mine).reshape(8, width),
            (fc_bias[None, None, :] * mine).reshape(hidden // width, width),
        ]
    )
    table = jnp.pad(table, ((0, 16 - table.shape[0]), (0, 0)))
    gather = partial(lax.all_gather, axis_name="shard", axis=0, tiled=True)
    params = lax.psum(table.astype(f32), "shard")
    full_qkv, full_out, full_fc, full_proj = (gather(w) for w in (w_qkv, w_out, w_fc, w_proj))
    projected, attended_t, lse = run_forward(tokens, segment_ids, params, full_qkv)
    (
        layer_out,
        grad_middle,
        grad_attended,
        grad_w_out,
        grad_w_fc,
        grad_w_proj_t,
        small,
    ) = run_hidden(attended_t, tokens, cotangent, params, full_out, full_fc, full_proj, width)
    grad_tokens, grad_w_qkv, small = run_backward(
        tokens,
        segment_ids,
        params,
        full_qkv,
        projected,
        attended_t,
        lse,
        grad_attended,
        grad_middle,
        small,
    )

    def reduced(grad):
        own_sum = lax.psum_scatter(grad.astype(f32), "shard", scatter_dimension=0, tiled=True)
        return lax.psum(own_sum.astype(bf16), "rep").astype(f32)

    sum_proj = reduced(grad_w_proj_t.transpose(0, 2, 1).reshape(hidden, width))
    sum_fc, sum_out, sum_qkv = reduced(grad_w_fc), reduced(grad_w_out), reduced(grad_w_qkv)
    small = lax.psum(small, ("rep", "shard"))
    mine = lax.dynamic_slice_in_dim(small[:8], me * own, own, 1)
    hidden_rows = small[BIAS_FC : BIAS_FC + hidden // width].reshape(-1)
    mine_fc = lax.dynamic_slice_in_dim(hidden_rows, me * own_hidden, own_hidden, 0)
    return (
        layer_out,
        grad_tokens,
        mine[GAIN1],
        mine[SHIFT1],
        sum_qkv,
        mine[BIAS_Q],
        mine[BIAS_V],
        sum_out,
        mine[BIAS_OUT],
        mine[GAIN2],
        mine[SHIFT2],
        sum_fc,
        mine_fc,
        sum_proj,
        mine[BIAS_PROJ],
    )


def solution(mesh):
    rows, own, own_rows = P(("rep", "shard"), None), P("shard"), P("shard", None)
    in_specs = (
        rows,
        rows,
        own,
        own,
        own_rows,
        own,
        own,
        own_rows,
        own,
        own,
        own,
        own_rows,
        own,
        own_rows,
        own,
        rows,
    )
    out_specs = (
        rows,
        rows,
        own,
        own,
        own_rows,
        own,
        own,
        own_rows,
        own,
        own,
        own,
        own_rows,
        own,
        own_rows,
        own,
    )
    sizes = mesh.shape["rep"], mesh.shape["shard"]
    return jax.shard_map(
        partial(on_device, *sizes), mesh=mesh, in_specs=in_specs, out_specs=out_specs, check_vma=False
    )
```

```python
from functools import partial

import jax
import jax.numpy as jnp
from jax import lax
from jax.experimental import pallas as pl
from jax.experimental.pallas import tpu as pltpu
from jax.sharding import PartitionSpec as P

HEAD = 64
EPSILON = 1e-05
QUERY_BLOCK = 256
ROW_CHUNK = 256
MASKED = -1e30
GELU_SCALE = 0.7978845608028654
GELU_CUBE = 0.044715
VMEM_LIMIT = 62 << 20
NN = (((1,), (0,)), ((), ()))
NT = (((1,), (1,)), ((), ()))
f32 = jnp.float32
bf16 = jnp.bfloat16
WHOLE = pl.BlockSpec(memory_space=pltpu.VMEM)

GAIN1, SHIFT1, BIAS_Q, BIAS_V, BIAS_OUT, GAIN2, SHIFT2, BIAS_PROJ, BIAS_FC = range(9)


def matmul(left, right, dims):
    return lax.dot_general(left, right, dims, preferred_element_type=f32)


def normalized(values):
    centred = values - jnp.mean(values, axis=-1, keepdims=True)
    inverse = lax.rsqrt(jnp.mean(centred * centred, axis=-1, keepdims=True) + EPSILON)
    return centred * inverse, inverse


def norm_pull(grad_normed, gain_row, norm, inverse):
    scaled = grad_normed * gain_row
    return inverse * (
        scaled
        - jnp.mean(scaled, axis=-1, keepdims=True)
        - norm * jnp.mean(scaled * norm, axis=-1, keepdims=True)
    )


def total(values):
    return jnp.sum(values, axis=0, keepdims=True)


def block(index, size):
    return pl.ds(pl.multiple_of(index * size, size), size)


def build_mask(segment_ref, mask_ref):
    length = segment_ref.shape[1]
    query_seg = segment_ref[...].astype(f32)
    key_seg = jnp.transpose(jnp.broadcast_to(query_seg, (8, length)))[:, 0:1]
    for start in range(0, length, QUERY_BLOCK):
        stop = start + QUERY_BLOCK
        key_at = lax.broadcasted_iota(jnp.int32, (stop, QUERY_BLOCK), 0)
        query_at = lax.broadcasted_iota(jnp.int32, (stop, QUERY_BLOCK), 1) + start
        allowed = (key_seg[0:stop] == query_seg[:, start:stop]) & (key_at <= query_at)
        mask_ref[0:stop, start:stop] = jnp.where(allowed, 0.0, MASKED)


def half_lanes(which):
    lane = lax.broadcasted_iota(jnp.int32, (1, 2 * HEAD), 1)
    return (lane < HEAD) if which == 0 else (lane >= HEAD)


def keep_half(values, which):
    return jnp.where(half_lanes(which), values, jnp.zeros_like(values))


def attend_forward(
    pair, queries, keys, values_t_ref, mask_ref, attended_t_ref, lse_ref, tick=lambda number: None
):
    length = keys.shape[0]
    queries = queries * bf16(HEAD**-0.5)
    for which in range(2):
        tick(which)
        head_queries = keep_half(queries, which)
        rows = block(2 * pair + which, HEAD)
        values_t = values_t_ref[rows, :]
        for start in range(0, length, QUERY_BLOCK):
            stop = start + QUERY_BLOCK
            scores = matmul(keys[0:stop], head_queries[start:stop], NT)
            scores = scores + mask_ref[0:stop, start:stop]
            top = jnp.max(scores, axis=0, keepdims=True)
            terms = jnp.exp(scores - top)
            sums = jnp.sum(terms, axis=0, keepdims=True)
            mixed = matmul(values_t[:, 0:stop], terms.astype(bf16), NN)
            attended_t_ref[rows, start:stop] = (mixed * (1.0 / sums)).astype(bf16)
            lse_ref[pl.ds(2 * pair + which, 1), start:stop] = top + jnp.log(sums)


def attend_backward(
    pair,
    operands,
    keys_t_ref,
    mask_ref,
    lse_ref,
    dots_ref,
    grad_queries_t_ref,
    grad_keys_ref,
    grad_values_ref,
    tick=lambda number: None,
):
    queries, keys, values, grads = operands
    length, scale_by = keys.shape[0], HEAD**-0.5
    queries = queries * bf16(scale_by)
    for number, start in enumerate(reversed(range(0, length, QUERY_BLOCK))):
        tick(number)
        stop = start + QUERY_BLOCK
        grad_keys = grad_values = 0.0
        for which in range(2):
            head = pl.ds(2 * pair + which, 1)
            rows = block(2 * pair + which, HEAD)
            query_rows = keep_half(queries[start:stop], which)
            grad_rows = keep_half(grads[start:stop], which)
            scores = matmul(keys[0:stop], query_rows, NT)
            probs = jnp.exp(scores + mask_ref[0:stop, start:stop] - lse_ref[head, start:stop])
            grad_probs = matmul(values[0:stop], grad_rows, NT)
            grad_scores = (probs * (grad_probs - dots_ref[head, start:stop])).astype(bf16)
            grad_values = grad_values + matmul(probs.astype(bf16), grad_rows, NN)
            grad_keys = grad_keys + matmul(grad_scores, query_rows, NN)
            grad_queries_t_ref[rows, start:stop] = (
                matmul(keys_t_ref[rows, 0:stop], grad_scores, NN) * scale_by
            ).astype(bf16)
        if stop == length:
            grad_keys_ref[...] = grad_keys
            grad_values_ref[...] = grad_values
        else:
            grad_keys_ref[0:stop] += grad_keys
            grad_values_ref[0:stop] += grad_values


MESH = pl.DeviceIdType.MESH
HBM = pl.BlockSpec(memory_space=pl.ANY)


def flip(value, bits):
    bit = 1
    while bit <= bits:
        if bits & bit:
            value = value + bit - 2 * bit * ((value // bit) % 2)
        bit *= 2
    return value


class Place:
    def __init__(self, shards):
        self.lines = shards // 2
        self.rep, self.me = lax.axis_index("rep"), lax.axis_index("shard")
        self.far, self.core = self.rep // 2, self.rep % 2
        self.line, self.side = self.me // 2, self.me % 2

    def shard(self, hop, turn):
        return flip(self.line, hop) * 2 + flip(self.side, turn)

    def peer(self, hop, turn):
        return (self.rep, self.shard(hop, turn))

    def across(self):
        return ((1 - self.far) * 2 + self.core, self.me)

    def sibling(self):
        return (self.far * 2 + 1 - self.core, self.me)

    def others(self):
        return [(h, t) for h in range(self.lines) for t in range(2) if h or t]

    def meet(self, peers):
        barrier = pltpu.get_barrier_semaphore()
        for peer in peers:
            pl.semaphore_signal(barrier, inc=1, device_id=peer, device_id_type=MESH)
        pl.semaphore_wait(barrier, len(peers))


def aligned(start, size):
    return pl.ds(pl.multiple_of(start, 16), size)


def remote(src, dst, send, recv, peer):
    return pltpu.make_async_remote_copy(
        src_ref=src,
        dst_ref=dst,
        send_sem=send,
        recv_sem=recv,
        device_id=peer,
        device_id_type=MESH,
    )


def cut(count):
    half = count // 2
    return half // 3 // 16 * 16, half


class Gather:
    def __init__(self, place, own, full, send, recv, local):
        self.place, self.own, self.full = place, own, full
        self.send, self.recv, self.local = send, recv, local
        self.hops = range(1, place.lines)

    def rows(self, at, kind, far, core):
        edge, half = cut(self.own[at].shape[0])
        if kind == "wide":
            return aligned(core * half + far * edge, half - edge)
        if kind == "edge":
            return aligned(core * half + far * (half - edge), edge)
        return aligned(core * half, half)

    def copy(self, at, stage, hop, turn, arriving=False):
        place, lines = self.place, self.place.lines
        number = hop * 2 + turn
        far, core = place.far, place.core
        if stage == "line":
            slot, peer, kind = hop - 1, place.peer(hop, 0), "wide"
            shard = place.shard(hop if arriving else 0, 0)
        elif stage == "side":
            slot, peer, kind = lines - 1 + hop, place.peer(0, 1), "wide"
            shard = place.shard(hop, 1 if arriving else 0)
        elif stage == "far":
            slot, peer, kind = 2 * lines - 1 + number - 1, place.across(), "edge"
            shard = place.shard(hop, turn)
            far = 1 - far if arriving else far
        else:
            slot, peer, kind = 4 * lines - 2 + number - 1, place.sibling(), "half"
            shard = place.shard(hop, turn)
            core = 1 - core if arriving else core
        rows = self.rows(at, kind, far, core)
        target = self.full[at].at[shard, rows]
        mine = not arriving and (stage == "line" or (stage == "side" and hop == 0))
        source = self.own[at].at[rows] if mine else target
        return remote(source, target, self.send.at[at, slot], self.recv.at[at, slot], peer)

    def start(self, at, stage, hop, turn=0):
        self.copy(at, stage, hop, turn).start()

    def got(self, at, stage, hop, turn=0):
        self.copy(at, stage, hop, turn, arriving=True).wait_recv()

    def keep(self, at):
        return pltpu.make_async_copy(
            self.own[at], self.full[at].at[self.place.me], self.local.at[at]
        )

    def own_side(self, at):
        self.start(at, "side", 0)

    def first(self, at, hop):
        self.start(at, "line", hop)

    def line(self, at, hop):
        self.got(at, "line", hop)
        self.start(at, "side", hop)
        self.start(at, "far", hop, 0)

    def side(self, at, hop):
        self.got(at, "side", hop)
        self.start(at, "far", hop, 1)

    def far(self, at, hop, turn):
        self.got(at, "far", hop, turn)
        self.start(at, "core", hop, turn)

    def last(self, at):
        for hop, turn in self.place.others():
            self.got(at, "core", hop, turn)
        self.keep(at).wait()

    def drain(self, at):
        for hop in self.hops:
            self.copy(at, "line", hop, 0).wait_send()
        for hop in range(self.place.lines):
            self.copy(at, "side", hop, 0).wait_send()
        for hop, turn in self.place.others():
            self.copy(at, "far", hop, turn).wait_send()
            self.copy(at, "core", hop, turn).wait_send()


def add_into(into, other):
    into[...] = (into[...].astype(f32) + other[...].astype(f32)).astype(bf16)


class Summed:
    def __init__(self, place, grad, done, buffers, send, recv, source=None, load_sem=None):
        self.place, self.grad, self.done = place, grad, done
        self.send_sem, self.recv_sem = send, recv
        self.source = grad if source is None else source
        self.load_sem = load_sem
        (
            self.from_core,
            self.from_far,
            self.from_side,
            self.from_me,
            self.from_line,
            self.from_back,
        ) = buffers
        self.edge_size, self.half = cut(grad.shape[1])
        self.hops = range(1, place.lines)

    def rows(self, kind, far=None, core=None):
        far = self.place.far if far is None else far
        core = self.place.core if core is None else core
        edge, half = self.edge_size, self.half
        if kind == "wide":
            return aligned(core * half + far * edge, half - edge)
        if kind == "edge":
            return aligned(core * half + far * (half - edge), edge)
        return aligned(core * half, half)

    def pair_of(self, hop):
        return pl.ds(2 * flip(self.place.line, hop), 2)

    def copy(self, stage, hop=0):
        place, lines, grad = self.place, self.place.lines, self.grad
        if stage == "core":
            slot, peer = 0, place.sibling()
            pair = self.source.at[:, self.rows("half", core=1 - place.core)], self.from_core
        elif stage == "far":
            slot, peer = hop, place.across()
            pair = (
                grad.at[self.pair_of(hop), self.rows("edge", far=1 - place.far)],
                self.from_far.at[hop - 1],
            )
        elif stage == "side":
            slot, peer = lines + hop, place.peer(0, 1)
            source = grad.at[place.shard(hop, 1), self.rows("wide" if hop else "half")]
            pair = source, self.from_side.at[hop - 1] if hop else self.from_me
        elif stage == "line":
            slot, peer = 2 * lines + hop - 1, place.peer(hop, 0)
            pair = grad.at[place.shard(hop, 0), self.rows("wide")], self.from_line.at[hop - 1]
        elif stage == "back":
            slot, peer = 3 * lines - 1, place.across()
            pair = grad.at[place.me, self.rows("half")], self.from_back
        else:
            slot, peer = 3 * lines, place.sibling()
            mine = self.done.at[self.rows("half")]
            pair = mine, mine
        return remote(*pair, self.send_sem.at[slot], self.recv_sem.at[slot], peer)

    def load(self):
        rows = self.rows("half")
        return pltpu.make_async_copy(
            self.source.at[:, rows], self.grad.at[:, rows], self.load_sem
        )

    def begin(self):
        self.copy("core").start()
        if self.load_sem is not None:
            self.load().start()

    def core(self):
        self.copy("core").wait_recv()
        if self.load_sem is not None:
            self.load().wait()
        for shard in range(2 * self.place.lines):
            add_into(self.grad.at[shard, self.rows("half")], self.from_core.at[shard])

    def me0(self):
        self.copy("side", 0).start()

    def send(self, hop):
        self.copy("far", hop).start()

    def far(self, hop):
        self.copy("far", hop).wait_recv()
        add_into(self.grad.at[self.pair_of(hop), self.rows("edge")], self.from_far.at[hop - 1])
        self.copy("side", hop).start()

    def side(self, hop):
        self.copy("side", hop).wait_recv()
        mine = self.grad.at[self.place.shard(hop, 0), self.rows("wide")]
        add_into(mine, self.from_side.at[hop - 1])
        self.copy("line", hop).start()

    def me(self):
        self.copy("side", 0).wait_recv()
        add_into(self.grad.at[self.place.me, self.rows("half")], self.from_me)

    def lines(self):
        mine = self.grad.at[self.place.me, self.rows("wide")]
        sums = mine[...].astype(f32)
        for hop in self.hops:
            self.copy("line", hop).wait_recv()
            sums = sums + self.from_line[hop - 1].astype(f32)
        mine[...] = sums.astype(bf16)
        self.copy("back").start()

    def back(self):
        self.copy("back").wait_recv()
        mine = self.grad[self.place.me, self.rows("half")].astype(f32)
        self.done[self.rows("half")] = (mine + self.from_back[...].astype(f32)).astype(bf16)
        self.copy("pair").start()

    def finish(self):
        other = self.done.at[self.rows("half", core=1 - self.place.core)]
        slot = 3 * self.place.lines
        remote(
            other, other, self.send_sem.at[slot], self.recv_sem.at[slot], self.place.sibling()
        ).wait_recv()

    def drain(self):
        self.copy("core").wait_send()
        for hop in self.hops:
            self.copy("far", hop).wait_send()
            self.copy("line", hop).wait_send()
        for hop in range(self.place.lines):
            self.copy("side", hop).wait_send()
        self.copy("back").wait_send()
        self.copy("pair").wait_send()


SUM_BUFFERS = 6


def sum_buffers(lines, shards, rows, columns):
    edge, half = cut(rows)
    return [
        pltpu.VMEM((shards, half, columns), bf16),
        pltpu.VMEM((lines - 1, 2, edge, columns), bf16),
        pltpu.VMEM((lines - 1, half - edge, columns), bf16),
        pltpu.VMEM((half, columns), bf16),
        pltpu.VMEM((lines - 1, half - edge, columns), bf16),
        pltpu.VMEM((half, columns), bf16),
    ]


def sum_sems(lines, items):
    return [pltpu.SemaphoreType.DMA((items, 3 * lines + 1))] * 2


def first_norm(tokens_ref, params_ref, normed_ref):
    length, width = tokens_ref.shape
    row = lambda at: params_ref[at : at + 1, 0:width]
    for at in range(0, length, ROW_CHUNK):
        norm, _ = normalized(tokens_ref[at : at + ROW_CHUNK].astype(f32))
        normed_ref[at : at + ROW_CHUNK] = (norm * row(GAIN1) + row(SHIFT1)).astype(bf16)


def forward_kernel(
    tokens_ref,
    segment_ref,
    params_ref,
    w_qkv_ref,
    projected_ref,
    attended_t_ref,
    lse_ref,
    mask_ref,
    normed_ref,
    values_t_ref,
):
    length, width = tokens_ref.shape
    pairs = width // (2 * HEAD)
    row = lambda at: params_ref[at : at + 1, 0:width]
    first_norm(tokens_ref, params_ref, normed_ref)
    for part, bias in enumerate((row(BIAS_Q), 0.0, row(BIAS_V))):
        columns = slice(part * width, (part + 1) * width)
        projected_ref[:, columns] = (
            matmul(normed_ref[...], w_qkv_ref[:, columns], NN) + bias
        ).astype(bf16)
    values_t_ref[...] = jnp.transpose(projected_ref[:, 2 * width :])
    build_mask(segment_ref, mask_ref)

    @pl.loop(0, pairs)
    def _(pair):
        attend_forward(
            pair,
            projected_ref[:, block(pair, 2 * HEAD)],
            projected_ref[:, block(pairs + pair, 2 * HEAD)],
            values_t_ref,
            mask_ref,
            attended_t_ref,
            lse_ref,
        )


GROUP = 4 * HEAD
GATHERED_EARLY = 1
SUMMED_EARLY = 1


(
    OWN,
    FIRST,
    LINE,
    SIDE,
    FAR,
    LAST,
    BEGIN_SUM,
    CORE_SUM,
    ME0_SUM,
    SEND_SUM,
    FAR_SUM,
    SIDE_SUM,
    ME_SUM,
    LINES_SUM,
    BACK_SUM,
    FINISH_SUM,
) = range(16)
P0, P1, P2, H0, H1, H2, H3, E0, E1, E2, E3, B0, B1, B2, B3, NEED, END = range(100, 117)

FORWARD_PLAN = {P0: [(OWN, 0), (FIRST, 0, 1)],
 P1: [(FIRST, 0, 3), (OWN, 1)],
 P2: [(FIRST, 0, 2), (LINE, 0, 1), (SIDE, 0, 0)],
 END: [(LAST, 5)],
 NEED: {0: [(FIRST, 1, 1), (SIDE, 1, 0), (OWN, 2), (OWN, 3), (FIRST, 1, 3), (LINE, 0, 3), (FIRST, 1, 2),
            (FAR, 0, 1, 0), (FAR, 0, 0, 1), (FAR, 1, 0, 1), (OWN, 4), (SIDE, 0, 1), (FAR, 0, 3, 0),
            (FIRST, 2, 1), (LINE, 1, 1), (SIDE, 2, 0), (SIDE, 3, 0), (LINE, 0, 2), (FAR, 0, 1, 1),
            (FIRST, 2, 3), (SIDE, 0, 3), (FIRST, 2, 2), (OWN, 5), (FAR, 1, 1, 0), (FAR, 2, 0, 1),
            (LINE, 1, 3), (SIDE, 4, 0), (FIRST, 3, 1), (FAR, 3, 0, 1), (FAR, 0, 2, 0), (SIDE, 1, 1),
            (FAR, 0, 3, 1), (LINE, 1, 2), (FIRST, 3, 3), (SIDE, 0, 2), (LINE, 2, 1), (FIRST, 3, 2),
            (FAR, 1, 3, 0), (FAR, 4, 0, 1), (SIDE, 5, 0), (FAR, 1, 1, 1), (SIDE, 1, 3), (LINE, 2, 3),
            (FAR, 1, 2, 0), (FIRST, 4, 1), (LINE, 2, 2), (FAR, 0, 2, 1), (FAR, 2, 1, 0), (SIDE, 1, 2),
            (LINE, 3, 1), (SIDE, 2, 1), (FIRST, 4, 3), (FAR, 5, 0, 1), (LAST, 0)]},
 0: {0: [(FIRST, 4, 2)],
     1: [(LAST, 1), (LINE, 4, 1), (FIRST, 5, 3)],
     2: [(FAR, 2, 2, 1), (FAR, 2, 3, 1), (SIDE, 3, 2), (SIDE, 3, 3), (FAR, 3, 2, 0), (FAR, 3, 3, 0),
         (FAR, 3, 1, 1), (LINE, 4, 2), (SIDE, 4, 1), (FAR, 4, 1, 0), (FAR, 4, 3, 0)],
     3: [(SIDE, 4, 2), (LINE, 5, 2), (FAR, 3, 2, 1)],
     4: [(LAST, 3), (FAR, 4, 2, 1), (SIDE, 5, 2), (FAR, 5, 2, 0), (FAR, 5, 3, 0), (FAR, 5, 1, 1)],
     5: [(LAST, 4), (FAR, 5, 2, 1)]},
 1: {0: [(FAR, 1, 2, 1), (FAR, 1, 3, 1), (SIDE, 2, 2), (SIDE, 2, 3), (FAR, 2, 2, 0), (FAR, 2, 3, 0),
         (FAR, 2, 1, 1), (LINE, 3, 2), (SIDE, 3, 1), (FAR, 3, 1, 0), (LINE, 3, 3), (FIRST, 5, 1)],
     1: [(LINE, 4, 3), (FIRST, 5, 2)],
     2: [(SIDE, 4, 3), (LAST, 2), (LINE, 5, 1)],
     3: [(FAR, 3, 3, 1), (FAR, 4, 2, 0), (FAR, 4, 1, 1), (FAR, 4, 3, 1), (LINE, 5, 3), (FAR, 5, 1, 0),
         (SIDE, 5, 1)],
     4: [(SIDE, 5, 3)],
     5: [(FAR, 5, 3, 1)]}}

HIDDEN_PLAN = {H0: [(OWN, 0), (FIRST, 0, 1)],
 H1: [(FIRST, 0, 3), (OWN, 1)],
 H2: [(FIRST, 0, 2), (LINE, 0, 1), (SIDE, 0, 0)],
 H3: [(FIRST, 1, 1), (SIDE, 1, 0), (OWN, 2)],
 E1: [(LINES_SUM, 1)],
 END: [(BACK_SUM, 1), (FINISH_SUM, 1)],
 1: {0: [(FIRST, 1, 3), (OWN, 3)], 1: [(FAR, 2, 3, 0), (FAR_SUM, 0, 3), (SIDE, 2, 3)]},
 2: {0: [(LINE, 0, 3), (SIDE, 0, 1), (FAR, 0, 1, 0), (FAR, 0, 0, 1), (FIRST, 1, 2), (FAR, 1, 0, 1)],
     1: [(SIDE, 2, 2), (FAR, 2, 2, 0), (FAR, 2, 1, 1), (LINE, 3, 3), (FAR, 3, 1, 0)],
     2: [(SIDE_SUM, 1, 3), (LINES_SUM, 0)]},
 3: {0: [(LINE, 0, 2), (SIDE, 2, 0)], 1: [(LINE, 3, 2), (SIDE, 3, 1)], 2: [(SIDE_SUM, 1, 2)]},
 4: {0: [(LINE, 1, 1), (FIRST, 2, 1), (SIDE, 3, 0)],
     1: [(FAR, 2, 3, 1), (FAR_SUM, 0, 2), (SIDE_SUM, 0, 3), (FAR, 2, 2, 1), (FAR, 3, 3, 0),
         (SEND_SUM, 1, 3)]},
 5: {0: [(SIDE, 0, 3), (FAR, 0, 3, 0), (FAR, 0, 1, 1), (FIRST, 2, 3), (BEGIN_SUM, 0)],
     1: [(SIDE, 3, 3), (FAR, 3, 2, 0), (FAR, 3, 1, 1), (FAR_SUM, 0, 1), (SEND_SUM, 1, 2)],
     2: [(BACK_SUM, 0), (SIDE_SUM, 1, 1)]},
 6: {0: [(SIDE, 0, 2), (FAR, 0, 2, 0), (LINE, 1, 3), (FIRST, 2, 2), (FAR, 2, 0, 1), (BEGIN_SUM, 1)],
     1: [(LAST, 2), (SIDE, 3, 2), (ME0_SUM, 1), (SEND_SUM, 1, 1)]},
 7: {0: [(LINE, 1, 2), (FAR, 0, 3, 1), (SIDE, 1, 1), (FAR, 1, 1, 0), (FAR, 3, 0, 1)],
     1: [(SIDE_SUM, 0, 2), (FAR_SUM, 1, 3), (FAR, 3, 3, 1)],
     2: [(FINISH_SUM, 0)]},
 NEED: {1: [(FAR, 0, 2, 1), (FAR, 1, 3, 0), (LINE, 2, 1), (FIRST, 3, 1), (CORE_SUM, 0), (SIDE, 1, 3),
            (ME0_SUM, 0), (SEND_SUM, 0, 3), (CORE_SUM, 1), (FAR, 1, 2, 0), (FAR, 1, 1, 1), (FIRST, 3, 3),
            (LAST, 0), (SIDE, 1, 2), (SEND_SUM, 0, 2), (LINE, 2, 3), (FAR, 2, 1, 0), (FIRST, 3, 2),
            (FAR, 1, 3, 1), (SIDE, 2, 1), (LINE, 2, 2), (FAR, 1, 2, 1), (LINE, 3, 1), (SEND_SUM, 0, 1),
            (ME_SUM, 0), (LAST, 1)],
        2: [(FAR, 3, 2, 1), (SIDE_SUM, 0, 1), (FAR_SUM, 1, 2), (FAR_SUM, 1, 1), (ME_SUM, 1), (LAST, 3)]}}

BACKWARD_PLAN = {B0: [(BEGIN_SUM, 0), (BEGIN_SUM, 1), (BEGIN_SUM, 2), (BEGIN_SUM, 3), (BEGIN_SUM, 4)],
 B2: [(CORE_SUM, 0), (ME0_SUM, 0), (SEND_SUM, 0, 3), (SEND_SUM, 0, 2)],
 B3: [(SEND_SUM, 0, 1), (CORE_SUM, 1), (ME0_SUM, 1)],
 E0: [(SIDE_SUM, 4, 1), (FAR_SUM, 6, 3), (FAR_SUM, 6, 2), (BEGIN_SUM, 7)],
 E1: [(BACK_SUM, 2), (SIDE_SUM, 5, 3), (FAR_SUM, 6, 1)],
 E2: [(FINISH_SUM, 2), (LINES_SUM, 3), (SIDE_SUM, 5, 2), (ME_SUM, 6), (CORE_SUM, 7), (ME0_SUM, 7),
      (SEND_SUM, 7, 3)],
 E3: [(SIDE_SUM, 5, 1), (SEND_SUM, 7, 2)],
 END: [(SIDE_SUM, 6, 3), (SEND_SUM, 7, 1), (BACK_SUM, 3), (ME_SUM, 7), (LINES_SUM, 4), (SIDE_SUM, 6, 2),
       (FAR_SUM, 7, 3), (FINISH_SUM, 3), (FAR_SUM, 7, 2), (SIDE_SUM, 6, 1), (FAR_SUM, 7, 1), (SIDE_SUM, 7, 3),
       (BACK_SUM, 4), (SIDE_SUM, 7, 2), (LINES_SUM, 5), (FINISH_SUM, 4), (SIDE_SUM, 7, 1), (BACK_SUM, 5),
       (FINISH_SUM, 5), (LINES_SUM, 6), (LINES_SUM, 7), (BACK_SUM, 6), (FINISH_SUM, 6), (BACK_SUM, 7),
       (FINISH_SUM, 7)],
 1: {0: [(FAR_SUM, 0, 3), (SEND_SUM, 1, 3), (CORE_SUM, 2), (ME_SUM, 0), (SEND_SUM, 1, 2), (ME0_SUM, 2),
         (CORE_SUM, 3)],
     1: [(FAR_SUM, 0, 1), (FAR_SUM, 1, 3), (SEND_SUM, 2, 2)],
     2: [(SIDE_SUM, 1, 3), (SIDE_SUM, 1, 2), (FAR_SUM, 2, 2), (SEND_SUM, 3, 1), (SEND_SUM, 4, 3)],
     3: [(SIDE_SUM, 2, 3), (FAR_SUM, 3, 3), (SEND_SUM, 4, 1)],
     4: [(FINISH_SUM, 0), (LINES_SUM, 1), (SIDE_SUM, 3, 3), (FAR_SUM, 4, 3), (FAR_SUM, 4, 2)],
     5: [(BACK_SUM, 1), (SIDE_SUM, 3, 1), (FAR_SUM, 5, 3), (FAR_SUM, 5, 2)]},
 2: {0: [(SEND_SUM, 1, 1), (CORE_SUM, 4), (ME_SUM, 1), (FAR_SUM, 0, 2)],
     1: [(FAR_SUM, 1, 2), (SEND_SUM, 2, 1), (ME_SUM, 2)],
     2: [(FAR_SUM, 2, 1), (SEND_SUM, 4, 2), (CORE_SUM, 5), (SIDE_SUM, 1, 1)],
     3: [(FAR_SUM, 3, 2), (SEND_SUM, 5, 3)],
     4: [(FAR_SUM, 4, 1), (CORE_SUM, 6), (SEND_SUM, 6, 3), (SEND_SUM, 6, 2), (SIDE_SUM, 3, 2)],
     5: [(FINISH_SUM, 1), (LINES_SUM, 2), (SIDE_SUM, 4, 3), (FAR_SUM, 5, 1)]},
 3: {0: [(SEND_SUM, 2, 3)],
     1: [(SIDE_SUM, 0, 2), (SEND_SUM, 3, 3)],
     2: [(LINES_SUM, 0), (ME0_SUM, 3)],
     3: [(SIDE_SUM, 2, 2), (FAR_SUM, 3, 1), (SEND_SUM, 5, 2)],
     4: [(ME_SUM, 4), (ME0_SUM, 5), (SEND_SUM, 6, 1)],
     5: [(ME_SUM, 5), (SIDE_SUM, 4, 2), (ME0_SUM, 6)]},
 0: {1: [(SIDE_SUM, 0, 3)],
     2: [(SIDE_SUM, 0, 1), (FAR_SUM, 1, 1), (FAR_SUM, 2, 3), (SEND_SUM, 3, 2), (BEGIN_SUM, 5)],
     4: [(BACK_SUM, 0), (SIDE_SUM, 2, 1), (ME_SUM, 3), (ME0_SUM, 4), (SEND_SUM, 5, 1), (BEGIN_SUM, 6)]}}


class Runner:
    def __init__(self, plan, gather, sums):
        self.plan, self.gather, self.sums = plan, gather, sums

    def act(self, events):
        gather = self.gather
        for what, item, *where in events:
            if what >= BEGIN_SUM:
                one = self.sums[item]
                acts = (
                    one.begin,
                    one.core,
                    one.me0,
                    one.send,
                    one.far,
                    one.side,
                    one.me,
                    one.lines,
                    one.back,
                    one.finish,
                )
                acts[what - BEGIN_SUM](*where)
            else:
                acts = (
                    gather.own_side,
                    gather.first,
                    gather.line,
                    gather.side,
                    gather.far,
                    gather.last,
                )
                acts[what](item, *where)

    def do(self, key):
        self.act(self.plan.get(key, ()))

    def at_step(self, step, key):
        for number, events in self.plan.get(key, {}).items():

            @pl.when(step == number)
            def _(events=events):
                self.act(events)


def gather_forward_kernel(
    shards,
    tokens_ref,
    segment_ref,
    own_params_ref,
    own_qkv_ref,
    own_out_ref,
    own_fc_ref,
    own_proj_ref,
    projected_ref,
    attended_t_ref,
    lse_ref,
    params_ref,
    full_qkv_ref,
    full_out_ref,
    full_fc_ref,
    full_proj_ref,
    mask_ref,
    normed_ref,
    values_t_ref,
    held_ref,
    weights_ref,
    tables_ref,
    group_ref,
    own_block_ref,
    send_sem,
    recv_sem,
    local_sem,
    params_send_sem,
    params_recv_sem,
    load_sem,
    out_sem,
):
    length, width = tokens_ref.shape
    groups = width // GROUP
    blocks = full_fc_ref.shape[0]
    place = Place(shards)
    others = place.others()
    own = [group_ref.at[g] for g in range(groups)] + [own_out_ref]
    full = [weights_ref.at[g] for g in range(groups)] + [full_out_ref]
    for number in range(blocks):
        own += [own_block_ref.at[number], own_proj_ref.at[number * 128 : number * 128 + 128]]
        full += [full_fc_ref.at[number], full_proj_ref.at[number]]
    gather = Gather(place, own, full, send_sem, recv_sem, local_sem)

    def move(source, target, number):
        pltpu.make_async_copy(source, target, load_sem.at[number]).start()

    def moved(whole, number):
        pltpu.make_async_copy(whole, whole, load_sem.at[number]).wait()

    for g in range(groups):
        for part in range(3):
            start = part * width + g * GROUP
            move(
                own_qkv_ref.at[:, start : start + GROUP],
                group_ref.at[g, :, part * GROUP : (part + 1) * GROUP],
                g,
            )
    for number in range(blocks):
        take_block(
            move, own_fc_ref, number, shards, own_block_ref.at[number], groups + number
        )
    place.meet([place.peer(*other) for other in others] + [place.across(), place.sibling()])

    def table(number, other, arriving):
        target = tables_ref.at[place.shard(*other) if arriving else place.me]
        return remote(
            target if arriving else own_params_ref,
            target,
            params_send_sem.at[number],
            params_recv_sem.at[number],
            place.peer(*other),
        )

    for number, other in enumerate(others):
        table(number, other, False).start()
    for g in range(groups):
        moved(group_ref.at[g], g)
    runner = Runner(FORWARD_PLAN, gather, ())

    def outward(g):
        return (
            pltpu.make_async_copy(held_ref.at[g], projected_ref.at[g], out_sem.at[g, 0]),
            pltpu.make_async_copy(weights_ref.at[g], full_qkv_ref.at[g], out_sem.at[g, 1]),
        )

    runner.do(P0)
    for g in range(groups):
        gather.keep(g).start()
    for number in range(blocks):
        moved(own_block_ref.at[number], groups + number)
    for at in range(groups, groups + 1 + 2 * blocks):
        gather.keep(at).start()
    tables_ref[place.me] = own_params_ref[...]
    build_mask(segment_ref, mask_ref)
    runner.do(P1)
    for number, other in enumerate(others):
        table(number, other, True).wait_recv()
    spread_params(shards, width // shards, tables_ref, params_ref)
    first_norm(tokens_ref, params_ref, normed_ref)
    runner.do(P2)

    @pl.loop(0, 2 * groups)
    def _(pair):
        g, odd = pair // 2, pair % 2
        runner.at_step(pair, NEED)

        @pl.when(odd == 0)
        def _():
            part = block(g, GROUP)
            weights = weights_ref[g].reshape(width, 3 * GROUP)
            values = matmul(normed_ref[...], weights, NN)
            bias = jnp.concatenate(
                [
                    params_ref[BIAS_Q : BIAS_Q + 1, part],
                    jnp.zeros((1, GROUP), f32),
                    params_ref[BIAS_V : BIAS_V + 1, part],
                ],
                axis=1,
            )
            held_ref[g] = (values + bias).astype(bf16)
            values_t_ref[part, :] = jnp.transpose(held_ref[g, :, 2 * GROUP :])
            for copy in outward(g):
                copy.start()

        attend_forward(
            pair,
            held_ref[g, :, block(odd, 2 * HEAD)],
            held_ref[g, :, block(2 + odd, 2 * HEAD)],
            values_t_ref,
            mask_ref,
            attended_t_ref,
            lse_ref,
            lambda which: runner.at_step(pair, which),
        )

    runner.do(END)
    for g in range(groups):
        for copy in outward(g):
            copy.wait()
    for at in range(groups + 1 + 2 * blocks):
        gather.drain(at)
    for number, other in enumerate(others):
        table(number, other, False).wait_send()


def spread_params(shards, own, tables_ref, params_ref):
    span = params_ref.shape[1]
    lane = lax.broadcasted_iota(jnp.int32, (128, span), 0)
    column = lax.broadcasted_iota(jnp.int32, (128, span), 1)
    narrow = wide = 0.0
    for shard in range(shards):
        values = tables_ref[shard]
        place = (column == lane + shard * own) & (lane < own)
        narrow = narrow + matmul(values, place.astype(f32).astype(bf16), NN)
        place = column == lane + shard * 128
        wide = wide + matmul(values, place.astype(f32).astype(bf16), NN)
    params_ref[0:8] = narrow[0:8]
    params_ref[8:16] = wide[8:16]


def take_block(move, own_fc_ref, number, shards, target_ref, sem):
    own = own_fc_ref.shape[1] // shards
    for shard in range(shards):
        start = shard * own + number * 128
        move(
            own_fc_ref.at[:, start : start + 128],
            target_ref.at[:, shard * 128 : (shard + 1) * 128],
            sem,
        )


def hidden_kernel(
    attended_t_ref,
    tokens_ref,
    cotangent_ref,
    params_ref,
    w_out_ref,
    w_fc_ref,
    w_proj_ref,
    layer_out_ref,
    grad_middle_ref,
    grad_attended_ref,
    grad_w_out_ref,
    grad_w_fc_ref,
    grad_w_proj_t_ref,
    small_ref,
    middle_ref,
    normed_ref,
    normed_t_ref,
    cotangent_t_ref,
    mixed_ref,
    grad_normed_ref,
    activated_ref,
    grad_preact_ref,
):
    step, steps = pl.program_id(0), pl.num_programs(0)
    length, width = tokens_ref.shape
    row = lambda at: params_ref[at : at + 1, :]
    chunks = [slice(at, at + ROW_CHUNK) for at in range(0, length, ROW_CHUNK)]

    @pl.when(step == 0)
    def _():
        attended = jnp.transpose(attended_t_ref[...])
        middle_ref[...] = (
            tokens_ref[...].astype(f32) + matmul(attended, w_out_ref[...], NN) + row(BIAS_OUT)
        )
        for rows in chunks:
            norm, _ = normalized(middle_ref[rows])
            normed_ref[rows] = (norm * row(GAIN2) + row(SHIFT2)).astype(bf16)
        normed_t_ref[...] = jnp.transpose(normed_ref[...])
        cotangent_t_ref[...] = jnp.transpose(cotangent_ref[...])
        mixed_ref[...] = jnp.zeros_like(mixed_ref)
        grad_normed_ref[...] = jnp.zeros_like(grad_normed_ref)
        small_ref[...] = jnp.zeros_like(small_ref)

    bias_sum = 0.0
    bias_row = params_ref[pl.ds(BIAS_FC + step, 1), :]
    for rows in chunks:
        preact = matmul(normed_ref[rows], w_fc_ref[...], NN) + bias_row
        grad_act = matmul(cotangent_ref[rows], w_proj_ref[...], NT)
        square = preact * preact
        bend = jnp.tanh(GELU_SCALE * preact * (1.0 + GELU_CUBE * square))
        gate = 0.5 + 0.5 * bend
        activated_ref[rows] = (preact * gate).astype(bf16)
        slope = gate + (0.5 * GELU_SCALE) * preact * (1.0 - bend * bend) * (
            1.0 + (3 * GELU_CUBE) * square
        )
        grad_preact = (slope * grad_act).astype(bf16)
        grad_preact_ref[rows] = grad_preact
        bias_sum = bias_sum + total(grad_preact.astype(f32))
    small_ref[pl.ds(BIAS_FC + step, 1), :] = bias_sum
    mixed_ref[...] += matmul(activated_ref[...], w_proj_ref[...], NN)
    grad_w_proj_t = matmul(cotangent_t_ref[...], activated_ref[...], NN).astype(bf16)
    pieces, _, piece = grad_w_proj_t_ref.shape
    for at in range(pieces):
        grad_w_proj_t_ref[at] = grad_w_proj_t[:, at * piece : (at + 1) * piece]
    grad_w_fc_ref[...] = matmul(normed_t_ref[...], grad_preact_ref[...], NN).astype(bf16)
    grad_normed_ref[...] += matmul(grad_preact_ref[...], w_fc_ref[...], NT)

    @pl.when(step == steps - 1)
    def _():
        sums = [0.0] * 4
        for rows in chunks:
            middle = middle_ref[rows]
            layer_out_ref[rows] = (middle + mixed_ref[rows] + row(BIAS_PROJ)).astype(bf16)
            norm, inverse = normalized(middle)
            grad_normed = grad_normed_ref[rows]
            cotangent = cotangent_ref[rows].astype(f32)
            grad_middle = cotangent + norm_pull(grad_normed, row(GAIN2), norm, inverse)
            grad_middle_ref[rows] = grad_middle
            normed_ref[rows] = grad_middle.astype(bf16)
            terms = (grad_middle, grad_normed * norm, grad_normed, cotangent)
            sums = [a + total(b) for a, b in zip(sums, terms)]
        for at, value in zip((BIAS_OUT, GAIN2, SHIFT2, BIAS_PROJ), sums):
            small_ref[at : at + 1, :] = value
        grad_branch = normed_ref[...]
        grad_w_out_ref[...] = matmul(attended_t_ref[...], grad_branch, NN).astype(bf16)
        grad_attended_ref[...] = matmul(grad_branch, w_out_ref[...], NT).astype(bf16)


def sum_hidden_kernel(
    shards,
    attended_t_in_ref,
    tokens_in_ref,
    cotangent_in_ref,
    params_ref,
    w_out_in_ref,
    fc_in_ref,
    proj_in_ref,
    own_fc_ref,
    own_proj_ref,
    layer_out_ref,
    grad_middle_ref,
    grad_attended_ref,
    grad_out_ref,
    last_fc_ref,
    last_proj_ref,
    done_fc_ref,
    done_proj_ref,
    small_ref,
    middle_ref,
    normed_ref,
    normed_t_ref,
    cotangent_t_ref,
    mixed_ref,
    grad_normed_ref,
    activated_ref,
    grad_preact_ref,
    fc_ref,
    proj_ref,
    grad_fc_ref,
    grad_proj_ref,
    own_block_ref,
    attended_t_ref,
    tokens_ref,
    cotangent_ref,
    w_out_ref,
    *rest,
):
    length, width = tokens_ref.shape
    blocks = fc_ref.shape[0]
    units = fc_ref.shape[3]
    early = fc_in_ref.shape[0]
    summed = done_fc_ref.shape[0]
    buffers, rest = [rest[SUM_BUFFERS * k :][:SUM_BUFFERS] for k in range(2 * summed)], rest[
        SUM_BUFFERS * 2 * summed :
    ]
    send_sem, recv_sem, local_sem, load_sem, sum_send_sem, sum_recv_sem = rest
    row = lambda at: params_ref[at : at + 1, 0:width]
    chunks = [slice(at, at + ROW_CHUNK) for at in range(0, length, ROW_CHUNK)]
    place = Place(shards)

    def move(source, target, number):
        pltpu.make_async_copy(source, target, load_sem.at[number]).start()

    def moved(whole, number):
        pltpu.make_async_copy(whole, whole, load_sem.at[number]).wait()

    own, full = [], []
    for number in range(early, blocks):
        own_block = own_block_ref.at[number - early]
        take_block(move, own_fc_ref, number, shards, own_block, number)
        own += [own_block, own_proj_ref.at[number * 128 : number * 128 + 128]]
        full += [fc_ref.at[number], proj_ref.at[number]]
    inputs = (
        (attended_t_in_ref, attended_t_ref),
        (w_out_in_ref, w_out_ref),
        (tokens_in_ref, tokens_ref),
        (cotangent_in_ref, cotangent_ref),
    )
    for number, pair in enumerate(inputs):
        move(*pair, 2 * blocks + number)
    for number in range(early):
        move(fc_in_ref.at[number], fc_ref.at[number], number)
        move(proj_in_ref.at[number], proj_ref.at[number], blocks + number)
    gather = Gather(place, own, full, send_sem, recv_sem, local_sem)
    sums = []
    for number in range(summed):
        for grad, done in ((grad_proj_ref, done_proj_ref), (grad_fc_ref, done_fc_ref)):
            k = len(sums)
            sums.append(
                Summed(
                    place,
                    grad.at[number],
                    done.at[number],
                    buffers[k],
                    sum_send_sem.at[k],
                    sum_recv_sem.at[k],
                )
            )
    runner = Runner(HIDDEN_PLAN, gather, sums)
    place.meet(
        [place.peer(hop, 0) for hop in range(1, place.lines)]
        + [place.peer(0, 1), place.across(), place.sibling()]
    )
    for number in range(early, blocks):
        moved(own_block_ref.at[number - early], number)
    runner.do(H0)
    for at in range(len(own)):
        gather.keep(at).start()

    for number, pair in enumerate(inputs):
        moved(pair[1], 2 * blocks + number)
    attended = jnp.transpose(attended_t_ref[...])
    w_out = w_out_ref[...].reshape(width, width)
    middle_ref[...] = tokens_ref[...].astype(f32) + matmul(attended, w_out, NN) + row(BIAS_OUT)
    runner.do(H1)
    for rows in chunks:
        norm, _ = normalized(middle_ref[rows])
        normed_ref[rows] = (norm * row(GAIN2) + row(SHIFT2)).astype(bf16)
    runner.do(H2)
    normed_t_ref[...] = jnp.transpose(normed_ref[...])
    cotangent_t_ref[...] = jnp.transpose(cotangent_ref[...])
    mixed_ref[...] = jnp.zeros_like(mixed_ref)
    grad_normed_ref[...] = jnp.zeros_like(grad_normed_ref)
    small_ref[...] = jnp.zeros_like(small_ref)
    for number in range(early):
        moved(fc_ref.at[number], number)
        moved(proj_ref.at[number], blocks + number)
    runner.do(H3)

    @pl.loop(0, blocks)
    def _(step):
        runner.at_step(step, NEED)
        w_fc = fc_ref.at[step]
        w_proj = proj_ref.at[step]
        bias_sum = 0.0
        bias_row = params_ref[pl.ds(BIAS_FC + step, 1), 0:units]
        for tick, rows in enumerate(chunks):
            runner.at_step(step, tick)
            preact = matmul(normed_ref[rows], w_fc[...].reshape(width, units), NN) + bias_row
            grad_act = matmul(cotangent_ref[rows], w_proj[...].reshape(units, width), NT)
            square = preact * preact
            bend = jnp.tanh(GELU_SCALE * preact * (1.0 + GELU_CUBE * square))
            gate = 0.5 + 0.5 * bend
            activated_ref[rows] = (preact * gate).astype(bf16)
            slope = gate + (0.5 * GELU_SCALE) * preact * (1.0 - bend * bend) * (
                1.0 + (3 * GELU_CUBE) * square
            )
            grad_preact = (slope * grad_act).astype(bf16)
            grad_preact_ref[rows] = grad_preact
            bias_sum = bias_sum + total(grad_preact.astype(f32))
        small_ref[pl.ds(BIAS_FC + step, 1), 0:units] = bias_sum
        runner.at_step(step, len(chunks))
        grad_proj = matmul(cotangent_t_ref[...], activated_ref[...], NN).astype(bf16)
        for shard in range(shards):
            grad_proj_ref[step, shard] = grad_proj[:, shard * 128 : (shard + 1) * 128]
        runner.at_step(step, len(chunks) + 1)
        grad_fc = matmul(normed_t_ref[...], grad_preact_ref[...], NN).astype(bf16)
        grad_fc_ref[step] = grad_fc.reshape(grad_fc_ref.shape[1:])
        runner.at_step(step, len(chunks) + 2)
        mixed_ref[...] += matmul(activated_ref[...], w_proj[...].reshape(units, width), NN)
        runner.at_step(step, len(chunks) + 3)
        grad_normed_ref[...] += matmul(
            grad_preact_ref[...], w_fc[...].reshape(width, units), NT
        )

    hand_over = []

    def hand(source, target):
        copy = pltpu.make_async_copy(source, target, load_sem.at[len(hand_over)])
        copy.start()
        hand_over.append(copy)

    hand(grad_fc_ref.at[summed:blocks], last_fc_ref)
    hand(grad_proj_ref.at[summed:blocks], last_proj_ref)
    parts = [0.0] * 4
    for number, rows in enumerate(chunks):
        if number < 2:
            runner.do(E0 + number)
        middle = middle_ref[rows]
        layer_out_ref[rows] = (middle + mixed_ref[rows] + row(BIAS_PROJ)).astype(bf16)
        norm, inverse = normalized(middle)
        grad_normed = grad_normed_ref[rows]
        cotangent = cotangent_ref[rows].astype(f32)
        grad_middle = cotangent + norm_pull(grad_normed, row(GAIN2), norm, inverse)
        middle_ref[rows] = grad_middle
        normed_ref[rows] = grad_middle.astype(bf16)
        terms = (grad_middle, grad_normed * norm, grad_normed, cotangent)
        parts = [a + total(b) for a, b in zip(parts, terms)]
    for at, value in zip((BIAS_OUT, GAIN2, SHIFT2, BIAS_PROJ), parts):
        small_ref[at : at + 1, 0:width] = value
    hand(middle_ref, grad_middle_ref)
    runner.do(E2)
    grad_branch = normed_ref[...]
    grad_out = matmul(attended_t_ref[...], grad_branch, NN).astype(bf16)
    grad_out_ref[...] = grad_out.reshape(grad_out_ref.shape)
    runner.do(E3)
    grad_attended_ref[...] = matmul(grad_branch, w_out, NT).astype(bf16)
    runner.do(END)
    for copy in hand_over:
        copy.wait()
    for item in sums:
        item.drain()
    for at in range(len(own)):
        gather.drain(at)


def backward_kernel(
    tokens_ref,
    segment_ref,
    params_ref,
    w_qkv_ref,
    projected_ref,
    attended_t_ref,
    lse_ref,
    grad_attended_ref,
    grad_middle_ref,
    small_in_ref,
    grad_tokens_ref,
    grad_w_qkv_ref,
    small_ref,
    mask_ref,
    wide_t_ref,
    grad_queries_t_ref,
    dots_ref,
    grad_projected_ref,
    grad_keys_ref,
    grad_values_ref,
):
    length, width = tokens_ref.shape
    build_mask(segment_ref, mask_ref)
    dot_rows(attended_t_ref, grad_attended_ref, wide_t_ref, dots_ref)
    wide_t_ref[...] = jnp.transpose(projected_ref[:, width : 2 * width])

    pairs = width // (2 * HEAD)

    @pl.loop(0, pairs)
    def _(pair):
        parts = [projected_ref[:, block(k * pairs + pair, 2 * HEAD)] for k in range(3)]
        attend_backward(
            pair,
            parts + [grad_attended_ref[:, block(pair, 2 * HEAD)]],
            wide_t_ref,
            mask_ref,
            lse_ref,
            dots_ref,
            grad_queries_t_ref,
            grad_keys_ref,
            grad_values_ref,
        )
        for k, ref in ((1, grad_keys_ref), (2, grad_values_ref)):
            grad_projected_ref[:, block(k * pairs + pair, 2 * HEAD)] = ref[...].astype(bf16)

    grad_projected_ref[:, 0:width] = jnp.transpose(grad_queries_t_ref[...])
    normed_transposed(tokens_ref, params_ref, wide_t_ref)
    small_ref[...] = small_in_ref[...]
    bias_sums(grad_projected_ref, small_ref)
    grad_w_qkv_ref[...] = matmul(wide_t_ref[...], grad_projected_ref[...], NN).astype(bf16)
    gain_sum = shift_sum = 0.0
    for at in range(0, length, ROW_CHUNK):
        gain_part, shift_part = token_rows(
            at,
            tokens_ref,
            params_ref,
            matmul(grad_projected_ref[at : at + ROW_CHUNK], w_qkv_ref[...], NT),
            grad_middle_ref[at : at + ROW_CHUNK],
            grad_tokens_ref,
        )
        gain_sum, shift_sum = gain_sum + gain_part, shift_sum + shift_part
    small_ref[GAIN1 : GAIN1 + 1, :] = gain_sum
    small_ref[SHIFT1 : SHIFT1 + 1, :] = shift_sum


def dot_rows(attended_t_ref, grad_attended_ref, wide_t_ref, dots_ref):
    wide_t_ref[...] = jnp.transpose(grad_attended_ref[...])
    for head in range(wide_t_ref.shape[0] // HEAD):
        rows = slice(head * HEAD, (head + 1) * HEAD)
        dots_ref[head : head + 1, :] = total(
            wide_t_ref[rows].astype(f32) * attended_t_ref[rows].astype(f32)
        )


def normed_transposed(tokens_ref, params_ref, wide_t_ref):
    width = tokens_ref.shape[1]
    row = lambda at: params_ref[at : at + 1, 0:width]
    for at in range(0, tokens_ref.shape[0], ROW_CHUNK):
        norm, _ = normalized(tokens_ref[at : at + ROW_CHUNK].astype(f32))
        normed = (norm * row(GAIN1) + row(SHIFT1)).astype(bf16)
        wide_t_ref[:, at : at + ROW_CHUNK] = jnp.transpose(normed)


def bias_sums(grad_projected_ref, small_ref):
    width = small_ref.shape[1]
    for at, part in ((BIAS_Q, 0), (BIAS_V, 2)):
        values = grad_projected_ref[:, part * width : (part + 1) * width]
        small_ref[at : at + 1, :] = total(values.astype(f32))


def token_rows(at, tokens_ref, params_ref, grad_normed, middle, grad_tokens_ref):
    rows = slice(at, at + ROW_CHUNK)
    gain = params_ref[GAIN1 : GAIN1 + 1, 0 : tokens_ref.shape[1]]
    norm, inverse = normalized(tokens_ref[rows].astype(f32))
    grad_rows = norm_pull(grad_normed, gain, norm, inverse)
    grad_tokens_ref[rows] = (middle + grad_rows).astype(bf16)
    return total(grad_normed * norm), total(grad_normed)


def sum_backward_kernel(
    shards,
    tokens_in_ref,
    segment_ref,
    params_ref,
    attended_t_in_ref,
    lse_ref,
    grad_attended_in_ref,
    small_in_ref,
    projected_in_ref,
    w_qkv_in_ref,
    grad_middle_in_ref,
    grad_out_in_ref,
    grad_fc_in_ref,
    grad_proj_in_ref,
    grad_tokens_ref,
    done_qkv_ref,
    done_out_ref,
    done_fc_ref,
    done_proj_ref,
    small_ref,
    mask_ref,
    wide_t_ref,
    normed_t_ref,
    grad_queries_t_ref,
    dots_ref,
    projected_ref,
    grad_projected_ref,
    grad_keys_ref,
    grad_values_ref,
    grad_qkv_ref,
    grad_out_ref,
    grad_fc_ref,
    grad_proj_ref,
    weights_ref,
    tokens_ref,
    attended_t_ref,
    grad_attended_ref,
    *rest,
):
    length, width = tokens_ref.shape
    groups = width // GROUP
    late_blocks = grad_fc_ref.shape[0]
    items = 2 * late_blocks + 1 + groups
    buffers, rest = [rest[SUM_BUFFERS * k :][:SUM_BUFFERS] for k in range(items)], rest[
        SUM_BUFFERS * items :
    ]
    small_core_ref, small_far_ref, small_side_ref, small_line_ref, *rest = rest
    send_sem, recv_sem, load_sem, small_send_sem, small_recv_sem = rest
    place = Place(shards)
    lines = place.lines
    arrays = []
    for number in range(late_blocks):
        arrays += [
            (grad_proj_ref.at[number], done_proj_ref.at[number], grad_proj_in_ref.at[number]),
            (grad_fc_ref.at[number], done_fc_ref.at[number], grad_fc_in_ref.at[number]),
        ]
    arrays.append((grad_out_ref, done_out_ref, grad_out_in_ref))
    arrays += [(grad_qkv_ref.at[g], done_qkv_ref.at[g], None) for g in range(groups)]
    sums = [
        Summed(
            place,
            grad,
            done,
            buffers[k],
            send_sem.at[k],
            recv_sem.at[k],
            source,
            None if source is None else load_sem.at[k],
        )
        for k, (grad, done, source) in enumerate(arrays)
    ]
    runner = Runner(BACKWARD_PLAN, None, sums)
    load_projected = pltpu.make_async_copy(projected_in_ref, projected_ref, load_sem.at[items])
    load_projected.start()
    inputs = [
        pltpu.make_async_copy(source, target, load_sem.at[items + 2 + number])
        for number, (source, target) in enumerate(
            (
                (attended_t_in_ref, attended_t_ref),
                (grad_attended_in_ref, grad_attended_ref),
                (tokens_in_ref, tokens_ref),
            )
        )
    ]
    for copy in inputs:
        copy.start()
    load_weights = pltpu.make_async_copy(w_qkv_in_ref, weights_ref, load_sem.at[items + 1])
    load_weights.start()
    place.meet(
        [place.peer(hop, 0) for hop in range(1, lines)]
        + [place.peer(0, 1), place.across(), place.sibling()]
    )
    runner.do(B0)
    build_mask(segment_ref, mask_ref)
    runner.do(B1)
    for copy in inputs:
        copy.wait()
    dot_rows(attended_t_ref, grad_attended_ref, wide_t_ref, dots_ref)
    runner.do(B2)
    normed_transposed(tokens_ref, params_ref, normed_t_ref)
    small_ref[...] = small_in_ref[...]
    load_projected.wait()
    for g in range(groups):
        wide_t_ref[g * GROUP : (g + 1) * GROUP] = jnp.transpose(
            projected_ref[g, :, GROUP : 2 * GROUP]
        )
    runner.do(B3)

    @pl.loop(0, 2 * groups)
    def _(pair):
        g, odd = pair // 2, pair % 2
        parts = [projected_ref[g, :, block(2 * k + odd, 2 * HEAD)] for k in range(3)]
        attend_backward(
            pair,
            parts + [grad_attended_ref[:, block(pair, 2 * HEAD)]],
            wide_t_ref,
            mask_ref,
            lse_ref,
            dots_ref,
            grad_queries_t_ref,
            grad_keys_ref,
            grad_values_ref,
            lambda number: runner.at_step(pair, number),
        )
        grad_queries = jnp.transpose(grad_queries_t_ref[block(pair, 2 * HEAD), :])
        grad_projected_ref[g, :, block(odd, 2 * HEAD)] = grad_queries
        for k, ref in ((1, grad_keys_ref), (2, grad_values_ref)):
            grad_projected_ref[g, :, block(2 * k + odd, 2 * HEAD)] = ref[...].astype(bf16)

        @pl.when(odd == 1)
        def _():
            grad_group = matmul(normed_t_ref[...], grad_projected_ref[g], NN).astype(bf16)
            grad_qkv_ref[g] = grad_group.reshape(grad_qkv_ref.shape[1:])

    middle_ref = mask_ref.at[:, 0:width]
    load_middle = pltpu.make_async_copy(grad_middle_in_ref, middle_ref, load_sem.at[items])
    load_middle.start()
    for g in range(groups):
        part = slice(g * GROUP, (g + 1) * GROUP)
        for at, k in ((BIAS_Q, 0), (BIAS_V, 2)):
            values = grad_projected_ref[g, :, k * GROUP : (k + 1) * GROUP]
            small_ref[at : at + 1, part] = total(values.astype(f32))
    load_weights.wait()
    load_middle.wait()
    gain_sum = shift_sum = 0.0
    for number, at in enumerate(range(0, length, ROW_CHUNK)):
        runner.do(E0 + number)
        rows = slice(at, at + ROW_CHUNK)
        grad_normed = 0.0
        for g in range(groups):
            weights = weights_ref[g].reshape(width, 3 * GROUP)
            grad_normed = grad_normed + matmul(grad_projected_ref[g, rows], weights, NT)
        gain_part, shift_part = token_rows(
            at, tokens_ref, params_ref, grad_normed, mask_ref[rows, 0:width], grad_tokens_ref
        )
        gain_sum, shift_sum = gain_sum + gain_part, shift_sum + shift_part
    small_ref[GAIN1 : GAIN1 + 1, 0:width] = gain_sum
    small_ref[SHIFT1 : SHIFT1 + 1, 0:width] = shift_sum

    def exchange(slot, into_ref, peer):
        copy = remote(small_ref, into_ref, small_send_sem.at[slot], small_recv_sem.at[slot], peer)
        copy.start()
        return copy

    todo = BACKWARD_PLAN.get(END, ())
    parts = [todo[len(todo) * k // 5 : len(todo) * (k + 1) // 5] for k in range(5)]
    for slot, into_ref, peer in (
        (0, small_core_ref, place.sibling()),
        (1, small_far_ref, place.across()),
        (2, small_side_ref, place.peer(0, 1)),
    ):
        copy = exchange(slot, into_ref, peer)
        runner.act(parts[slot])
        copy.wait()
        small_ref[...] += into_ref[...]
    copies = [
        exchange(2 + hop, small_line_ref.at[hop - 1], place.peer(hop, 0))
        for hop in range(1, lines)
    ]
    runner.act(parts[3] + parts[4])
    for copy in copies:
        copy.wait()
    small = small_ref[...]
    for hop in range(1, lines):
        small = small + small_line_ref[hop - 1]
    small_ref[...] = small
    for item in sums:
        item.drain()


def finish_kernel(
    shards,
    qkv_ref,
    out_ref,
    fc_early_ref,
    fc_last_ref,
    proj_early_ref,
    proj_last_ref,
    small_ref,
    layer_in_ref,
    tokens_in_ref,
    sum_qkv_ref,
    sum_out_ref,
    sum_fc_ref,
    sum_proj_ref,
    mine_ref,
    layer_out_ref,
    grad_tokens_ref,
    copy_sem,
):
    copies = [
        pltpu.make_async_copy(source, target, copy_sem.at[k])
        for k, (source, target) in enumerate(
            ((layer_in_ref, layer_out_ref), (tokens_in_ref, grad_tokens_ref))
        )
    ]
    for copy in copies:
        copy.start()
    groups, own, _ = qkv_ref.shape
    width = groups * GROUP
    for g in range(groups):
        for part in range(3):
            start = part * width + g * GROUP
            sum_qkv_ref[:, start : start + GROUP] = qkv_ref[
                g, :, part * GROUP : (part + 1) * GROUP
            ].astype(f32)
    sum_out_ref[...] = out_ref[...].astype(f32)
    early = fc_early_ref.shape[0]
    blocks = early + fc_last_ref.shape[0]
    for number in range(blocks):
        fc = fc_early_ref.at[number] if number < early else fc_last_ref.at[number - early]
        proj = proj_early_ref.at[number] if number < early else proj_last_ref.at[number - early]
        for shard in range(shards):
            start = (shard * blocks + number) * 128
            sum_fc_ref[:, start : start + 128] = fc[:, shard * 128 : (shard + 1) * 128].astype(f32)
        sum_proj_ref[number * 128 : (number + 1) * 128] = jnp.transpose(proj[...].astype(f32))
    me = lax.axis_index("shard")
    mine_ref[...] = jnp.zeros_like(mine_ref)
    for shard in range(shards):

        @pl.when(me == shard)
        def _(shard=shard):
            mine_ref[0:8, 0:own] = small_ref[0:8, shard * own : (shard + 1) * own]
            mine_ref[8:16, :] = small_ref[8:16, shard * 128 : (shard + 1) * 128]

    for copy in copies:
        copy.wait()


def kernel_params():
    return pltpu.CompilerParams(vmem_limit_bytes=VMEM_LIMIT)


def run_forward(tokens, segment, params, w_qkv):
    length, width = tokens.shape
    return pl.pallas_call(
        forward_kernel,
        in_specs=[WHOLE] * 4,
        out_specs=(WHOLE,) * 3,
        out_shape=(
            jax.ShapeDtypeStruct((length, 3 * width), bf16),
            jax.ShapeDtypeStruct((width, length), bf16),
            jax.ShapeDtypeStruct((16, length), f32),
        ),
        scratch_shapes=[
            pltpu.VMEM((length, length), f32),
            pltpu.VMEM((length, width), bf16),
            pltpu.VMEM((width, length), bf16),
        ],
        compiler_params=kernel_params(),
        name="forward",
    )(tokens, segment, params, w_qkv)


def run_hidden(attended_t, tokens, cotangent, params, w_out, w_fc, w_proj, piece):
    length, width = tokens.shape
    hidden = w_fc.shape[1]
    shape = jax.ShapeDtypeStruct
    columns = pl.BlockSpec((width, width), lambda step: (0, step))
    return pl.pallas_call(
        hidden_kernel,
        grid=(hidden // width,),
        in_specs=[WHOLE] * 5 + [columns, pl.BlockSpec((width, width), lambda step: (step, 0))],
        out_specs=(
            WHOLE,
            WHOLE,
            WHOLE,
            WHOLE,
            columns,
            pl.BlockSpec((width // piece, width, piece), lambda step: (step, 0, 0)),
            WHOLE,
        ),
        out_shape=(
            shape((length, width), bf16),
            shape((length, width), f32),
            shape((length, width), bf16),
            shape((width, width), bf16),
            shape((width, hidden), bf16),
            shape((hidden // piece, width, piece), bf16),
            shape((16, width), f32),
        ),
        scratch_shapes=[
            pltpu.VMEM((length, width), f32),
            pltpu.VMEM((length, width), bf16),
            pltpu.VMEM((width, length), bf16),
            pltpu.VMEM((width, length), bf16),
            pltpu.VMEM((length, width), f32),
            pltpu.VMEM((length, width), f32),
            pltpu.VMEM((length, width), bf16),
            pltpu.VMEM((length, width), bf16),
        ],
        compiler_params=kernel_params(),
        name="hidden",
    )(attended_t, tokens, cotangent, params, w_out, w_fc, w_proj)


def run_backward(
    tokens, segment, params, w_qkv, projected, attended_t, lse, grad_attended, grad_middle, small
):
    length, width = tokens.shape
    shape = jax.ShapeDtypeStruct
    return pl.pallas_call(
        backward_kernel,
        in_specs=[WHOLE] * 10,
        out_specs=(WHOLE,) * 3,
        out_shape=(
            shape((length, width), bf16),
            shape((width, 3 * width), bf16),
            shape((16, width), f32),
        ),
        scratch_shapes=[
            pltpu.VMEM((length, length), f32),
            pltpu.VMEM((width, length), bf16),
            pltpu.VMEM((width, length), bf16),
            pltpu.VMEM((16, length), f32),
            pltpu.VMEM((length, 3 * width), bf16),
            pltpu.VMEM((length, 2 * HEAD), f32),
            pltpu.VMEM((length, 2 * HEAD), f32),
        ],
        compiler_params=kernel_params(),
        name="backward",
    )(
        tokens,
        segment,
        params,
        w_qkv,
        projected,
        attended_t,
        lse,
        grad_attended,
        grad_middle,
        small,
    )


def link_params(number):
    return pltpu.CompilerParams(
        vmem_limit_bytes=VMEM_LIMIT, collective_id=number, has_side_effects=True
    )


def run_gather_forward(
    shards, span, tokens, segment, own_params, w_qkv, w_out, w_fc, w_proj
):
    length, width = tokens.shape
    own = w_qkv.shape[0]
    groups = width // GROUP
    blocks = GATHERED_EARLY
    items = groups + 1 + 2 * blocks
    shape = jax.ShapeDtypeStruct
    copies = 3 * shards - 3
    dma = pltpu.SemaphoreType.DMA
    return pl.pallas_call(
        partial(gather_forward_kernel, shards),
        in_specs=[WHOLE] * 3 + [HBM] * 4,
        out_specs=(HBM,) + (WHOLE,) * 3 + (HBM,) * 4,
        out_shape=(
            shape((groups, length, 3 * GROUP), bf16),
            shape((width, length), bf16),
            shape((16, length), f32),
            shape((own_params.shape[0], span), f32),
            shape((groups, shards, own, 3 * GROUP), bf16),
            shape((shards, own, width), bf16),
            shape((blocks, shards, own, shards * 128), bf16),
            shape((blocks, shards, 128, width), bf16),
        ),
        scratch_shapes=[
            pltpu.VMEM((length, length), f32),
            pltpu.VMEM((length, width), bf16),
            pltpu.VMEM((width, length), bf16),
            pltpu.VMEM((groups, length, 3 * GROUP), bf16),
            pltpu.VMEM((groups, shards, own, 3 * GROUP), bf16),
            pltpu.VMEM((shards,) + own_params.shape, bf16),
            pltpu.VMEM((groups, own, 3 * GROUP), bf16),
            pltpu.VMEM((blocks, own, shards * 128), bf16),
            dma((items, copies)),
            dma((items, copies)),
            dma((items,)),
            dma((shards - 1,)),
            dma((shards - 1,)),
            dma((groups + blocks,)),
            dma((groups, 2)),
        ],
        compiler_params=link_params(0),
        name="gather_forward",
    )(tokens, segment, own_params, w_qkv, w_out, w_fc, w_proj)


def run_sum_hidden(
    shards, attended_t, tokens, cotangent, params, full_out, full_fc, full_proj, w_fc, w_proj
):
    length, width = tokens.shape
    own, units = w_fc.shape[0], shards * 128
    blocks = w_proj.shape[0] // 128
    lines = shards // 2
    shape = jax.ShapeDtypeStruct
    dma = pltpu.SemaphoreType.DMA
    grads = ((shards, own, units), (shards, width, 128))
    late, early = blocks - full_fc.shape[0], SUMMED_EARLY
    buffers = [
        ref
        for _ in range(early)
        for grad in reversed(grads)
        for ref in sum_buffers(lines, *grad)
    ]
    return pl.pallas_call(
        partial(sum_hidden_kernel, shards),
        in_specs=[HBM] * 3 + [WHOLE] + [HBM] * 5,
        out_specs=(WHOLE, HBM, WHOLE, WHOLE, HBM, HBM) + (WHOLE,) * 3,
        out_shape=(
            shape((length, width), bf16),
            shape((length, width), f32),
            shape((length, width), bf16),
            shape((shards, own, width), bf16),
            shape((blocks - early,) + grads[0], bf16),
            shape((blocks - early,) + grads[1], bf16),
            shape((early, own, units), bf16),
            shape((early, width, 128), bf16),
            shape(params.shape, f32),
        ),
        scratch_shapes=[
            pltpu.VMEM((length, width), f32),
            pltpu.VMEM((length, width), bf16),
            pltpu.VMEM((width, length), bf16),
            pltpu.VMEM((width, length), bf16),
            pltpu.VMEM((length, width), f32),
            pltpu.VMEM((length, width), f32),
            pltpu.VMEM((length, units), bf16),
            pltpu.VMEM((length, units), bf16),
            pltpu.VMEM((blocks, shards, own, units), bf16),
            pltpu.VMEM((blocks, shards, 128, width), bf16),
            pltpu.VMEM((blocks,) + grads[0], bf16),
            pltpu.VMEM((blocks,) + grads[1], bf16),
            pltpu.VMEM((late, own, units), bf16),
            pltpu.VMEM((width, length), bf16),
            pltpu.VMEM((length, width), bf16),
            pltpu.VMEM((length, width), bf16),
            pltpu.VMEM((shards, own, width), bf16),
        ]
        + buffers
        + [
            dma((2 * late, 3 * shards - 3)),
            dma((2 * late, 3 * shards - 3)),
            dma((2 * late,)),
            dma((2 * blocks + 4,)),
        ]
        + sum_sems(lines, 2 * early),
        compiler_params=link_params(1),
        name="sum_hidden",
    )(attended_t, tokens, cotangent, params, full_out, full_fc, full_proj, w_fc, w_proj)


def run_sum_backward(
    shards,
    tokens,
    segment,
    params,
    attended_t,
    lse,
    grad_attended,
    small,
    projected,
    w_qkv,
    grad_middle,
    grad_out,
    grad_fc,
    grad_proj,
):
    length, width = tokens.shape
    shape = jax.ShapeDtypeStruct
    lines, groups = shards // 2, width // GROUP
    own = width // shards
    qkv = (shards, own, 3 * GROUP)
    late_blocks = grad_fc.shape[0]
    grads = [grad_proj.shape[1:], grad_fc.shape[1:]] * late_blocks
    grads += [grad_out.shape] + [qkv] * groups
    buffers = [ref for grad in grads for ref in sum_buffers(lines, *grad)]
    table = pltpu.VMEM(params.shape, f32)
    dma = pltpu.SemaphoreType.DMA
    items = len(grads)
    return pl.pallas_call(
        partial(sum_backward_kernel, shards),
        in_specs=[HBM, WHOLE, WHOLE, HBM, WHOLE, HBM, WHOLE] + [HBM] * 6,
        out_specs=(WHOLE,) * 6,
        out_shape=(
            shape((length, width), bf16),
            shape((groups,) + qkv[1:], bf16),
            shape(grad_out.shape[1:], bf16),
            shape((late_blocks,) + grad_fc.shape[2:], bf16),
            shape((late_blocks,) + grad_proj.shape[2:], bf16),
            shape(params.shape, f32),
        ),
        scratch_shapes=[
            pltpu.VMEM((length, length), f32),
            pltpu.VMEM((width, length), bf16),
            pltpu.VMEM((width, length), bf16),
            pltpu.VMEM((width, length), bf16),
            pltpu.VMEM((16, length), f32),
            pltpu.VMEM(projected.shape, bf16),
            pltpu.VMEM(projected.shape, bf16),
            pltpu.VMEM((length, 2 * HEAD), f32),
            pltpu.VMEM((length, 2 * HEAD), f32),
            pltpu.VMEM((groups,) + qkv, bf16),
            pltpu.VMEM(grad_out.shape, bf16),
            pltpu.VMEM(grad_fc.shape, bf16),
            pltpu.VMEM(grad_proj.shape, bf16),
            pltpu.VMEM(w_qkv.shape, bf16),
            pltpu.VMEM((length, width), bf16),
            pltpu.VMEM((width, length), bf16),
            pltpu.VMEM((length, width), bf16),
        ]
        + buffers
        + [table, table, table, pltpu.VMEM((lines - 1,) + params.shape, f32)]
        + sum_sems(lines, items)
        + [dma((items + 5,)), dma((lines + 2,)), dma((lines + 2,))],
        compiler_params=link_params(2),
        name="sum_backward",
    )(
        tokens,
        segment,
        params,
        attended_t,
        lse,
        grad_attended,
        small,
        projected,
        w_qkv,
        grad_middle,
        grad_out,
        grad_fc,
        grad_proj,
    )


def run_finish(
    shards, qkv, out, fc_early, fc_last, proj_early, proj_last, small, layer_out, grad_tokens
):
    groups, own, _ = qkv.shape
    width = out.shape[1]
    blocks = fc_early.shape[0] + fc_last.shape[0]
    shape = jax.ShapeDtypeStruct
    return pl.pallas_call(
        partial(finish_kernel, shards),
        in_specs=[WHOLE] * 9,
        out_specs=(WHOLE,) * 5 + (HBM,) * 2,
        out_shape=(
            shape((own, 3 * width), f32),
            shape((own, width), f32),
            shape((own, blocks * shards * 128), f32),
            shape((blocks * 128, width), f32),
            shape((16, 128), f32),
            shape(layer_out.shape, bf16),
            shape(grad_tokens.shape, bf16),
        ),
        scratch_shapes=[pltpu.SemaphoreType.DMA((2,))],
        compiler_params=kernel_params(),
        name="finish",
    )(qkv, out, fc_early, fc_last, proj_early, proj_last, small, layer_out, grad_tokens)


def by_kernels(
    shards, tokens, segment_ids, vectors, fc_bias, w_qkv, w_out, w_fc, w_proj, cotangent
):
    width, hidden = tokens.shape[1], w_fc.shape[1]
    blocks, units = w_proj.shape[0] // 128, shards * 128
    span = max(width, units)
    rows = jnp.pad(jnp.stack(vectors), ((0, 0), (0, 128 - vectors[0].shape[0])))
    table = jnp.concatenate(
        [rows, jnp.pad(fc_bias.reshape(blocks, 128), ((0, 8 - blocks), (0, 0)))]
    )
    projected, attended_t, lse, params, full_qkv, full_out, full_fc, full_proj = (
        run_gather_forward(shards, span, tokens, segment_ids, table, w_qkv, w_out, w_fc, w_proj)
    )
    (
        layer_out,
        grad_middle,
        grad_attended,
        grad_out,
        grad_fc,
        grad_proj,
        fc_early,
        proj_early,
        small,
    ) = run_sum_hidden(
        shards, attended_t, tokens, cotangent, params, full_out, full_fc, full_proj, w_fc, w_proj
    )
    grad_tokens, done_qkv, done_out, fc_last, proj_last, small = run_sum_backward(
        shards,
        tokens,
        segment_ids,
        params,
        attended_t,
        lse,
        grad_attended,
        small,
        projected,
        full_qkv,
        grad_middle,
        grad_out,
        grad_fc,
        grad_proj,
    )
    sum_qkv, sum_out, sum_fc, sum_proj, own_small, layer_out, grad_tokens = run_finish(
        shards,
        done_qkv,
        done_out,
        fc_early,
        fc_last,
        proj_early,
        proj_last,
        small,
        layer_out,
        grad_tokens,
    )
    own = vectors[0].shape[0]
    pick = lambda at: own_small[at, 0:own]
    return (
        layer_out,
        grad_tokens,
        pick(GAIN1),
        pick(SHIFT1),
        sum_qkv,
        pick(BIAS_Q),
        pick(BIAS_V),
        sum_out,
        pick(BIAS_OUT),
        pick(GAIN2),
        pick(SHIFT2),
        sum_fc,
        own_small[BIAS_FC : BIAS_FC + blocks, 0:128].reshape(-1),
        sum_proj,
        pick(BIAS_PROJ),
    )


def on_device(
    replicas,
    shards,
    tokens,
    segment_ids,
    norm1_gain,
    norm1_shift,
    w_qkv,
    q_bias,
    v_bias,
    w_out,
    out_bias,
    norm2_gain,
    norm2_shift,
    w_fc,
    fc_bias,
    w_proj,
    proj_bias,
    cotangent,
):
    width, hidden = tokens.shape[1], w_fc.shape[1]
    vectors = (
        norm1_gain,
        norm1_shift,
        q_bias,
        v_bias,
        out_bias,
        norm2_gain,
        norm2_shift,
        proj_bias,
    )
    own, own_hidden = norm1_gain.shape[0], fc_bias.shape[0]
    if (
        replicas == 4
        and shards & (shards - 1) == 0
        and own % 96 == 0
        and own_hidden == 3 * 128
        and width == 3 * GROUP
    ):
        return by_kernels(
            shards, tokens, segment_ids, vectors, fc_bias, w_qkv, w_out, w_fc, w_proj, cotangent
        )
    me = lax.axis_index("shard")
    mine = (lax.broadcasted_iota(jnp.int32, (1, shards, 1), 1) == me).astype(bf16)
    table = jnp.concatenate(
        [
            (jnp.stack(vectors)[:, None, :] * mine).reshape(8, width),
            (fc_bias[None, None, :] * mine).reshape(hidden // width, width),
        ]
    )
    table = jnp.pad(table, ((0, 16 - table.shape[0]), (0, 0)))
    gather = partial(lax.all_gather, axis_name="shard", axis=0, tiled=True)
    params = lax.psum(table.astype(f32), "shard")
    full_qkv, full_out, full_fc, full_proj = (gather(w) for w in (w_qkv, w_out, w_fc, w_proj))
    projected, attended_t, lse = run_forward(tokens, segment_ids, params, full_qkv)
    (
        layer_out,
        grad_middle,
        grad_attended,
        grad_w_out,
        grad_w_fc,
        grad_w_proj_t,
        small,
    ) = run_hidden(attended_t, tokens, cotangent, params, full_out, full_fc, full_proj, width)
    grad_tokens, grad_w_qkv, small = run_backward(
        tokens,
        segment_ids,
        params,
        full_qkv,
        projected,
        attended_t,
        lse,
        grad_attended,
        grad_middle,
        small,
    )

    def reduced(grad):
        own_sum = lax.psum_scatter(grad.astype(f32), "shard", scatter_dimension=0, tiled=True)
        return lax.psum(own_sum.astype(bf16), "rep").astype(f32)

    sum_proj = reduced(grad_w_proj_t.transpose(0, 2, 1).reshape(hidden, width))
    sum_fc, sum_out, sum_qkv = reduced(grad_w_fc), reduced(grad_w_out), reduced(grad_w_qkv)
    small = lax.psum(small, ("rep", "shard"))
    mine = lax.dynamic_slice_in_dim(small[:8], me * own, own, 1)
    hidden_rows = small[BIAS_FC : BIAS_FC + hidden // width].reshape(-1)
    mine_fc = lax.dynamic_slice_in_dim(hidden_rows, me * own_hidden, own_hidden, 0)
    return (
        layer_out,
        grad_tokens,
        mine[GAIN1],
        mine[SHIFT1],
        sum_qkv,
        mine[BIAS_Q],
        mine[BIAS_V],
        sum_out,
        mine[BIAS_OUT],
        mine[GAIN2],
        mine[SHIFT2],
        sum_fc,
        mine_fc,
        sum_proj,
        mine[BIAS_PROJ],
    )


def solution(mesh):
    rows, own, own_rows = P(("rep", "shard"), None), P("shard"), P("shard", None)
    in_specs = (
        rows,
        rows,
        own,
        own,
        own_rows,
        own,
        own,
        own_rows,
        own,
        own,
        own,
        own_rows,
        own,
        own_rows,
        own,
        rows,
    )
    out_specs = (
        rows,
        rows,
        own,
        own,
        own_rows,
        own,
        own,
        own_rows,
        own,
        own,
        own,
        own_rows,
        own,
        own_rows,
        own,
    )
    sizes = mesh.shape["rep"], mesh.shape["shard"]
    return jax.shard_map(
        partial(on_device, *sizes), mesh=mesh, in_specs=in_specs, out_specs=out_specs, check_vma=False
    )
```

```python
from functools import partial

import jax
import jax.numpy as jnp
from jax import lax
from jax.experimental import pallas as pl
from jax.experimental.pallas import tpu as pltpu
from jax.sharding import PartitionSpec as P

HEAD = 64
EPSILON = 1e-05
QUERY_BLOCK = 256
ROW_CHUNK = 256
MASKED = -1e30
GELU_SCALE = 0.7978845608028654
GELU_CUBE = 0.044715
VMEM_LIMIT = 62 << 20
NN = (((1,), (0,)), ((), ()))
NT = (((1,), (1,)), ((), ()))
f32 = jnp.float32
bf16 = jnp.bfloat16
WHOLE = pl.BlockSpec(memory_space=pltpu.VMEM)

GAIN1, SHIFT1, BIAS_Q, BIAS_V, BIAS_OUT, GAIN2, SHIFT2, BIAS_PROJ, BIAS_FC = range(9)


def matmul(left, right, dims):
    return lax.dot_general(left, right, dims, preferred_element_type=f32)


def normalized(values):
    centred = values - jnp.mean(values, axis=-1, keepdims=True)
    inverse = lax.rsqrt(jnp.mean(centred * centred, axis=-1, keepdims=True) + EPSILON)
    return centred * inverse, inverse


def norm_pull(grad_normed, gain_row, norm, inverse):
    scaled = grad_normed * gain_row
    return inverse * (
        scaled
        - jnp.mean(scaled, axis=-1, keepdims=True)
        - norm * jnp.mean(scaled * norm, axis=-1, keepdims=True)
    )


def total(values):
    return jnp.sum(values, axis=0, keepdims=True)


def block(index, size):
    return pl.ds(pl.multiple_of(index * size, size), size)


def build_mask(segment_ref, mask_ref):
    length = segment_ref.shape[1]
    query_seg = segment_ref[...].astype(f32)
    key_seg = jnp.transpose(jnp.broadcast_to(query_seg, (8, length)))[:, 0:1]
    for start in range(0, length, QUERY_BLOCK):
        stop = start + QUERY_BLOCK
        key_at = lax.broadcasted_iota(jnp.int32, (stop, QUERY_BLOCK), 0)
        query_at = lax.broadcasted_iota(jnp.int32, (stop, QUERY_BLOCK), 1) + start
        allowed = (key_seg[0:stop] == query_seg[:, start:stop]) & (key_at <= query_at)
        mask_ref[0:stop, start:stop] = jnp.where(allowed, 0.0, MASKED)


def half_lanes(which):
    lane = lax.broadcasted_iota(jnp.int32, (1, 2 * HEAD), 1)
    return (lane < HEAD) if which == 0 else (lane >= HEAD)


def keep_half(values, which):
    return jnp.where(half_lanes(which), values, jnp.zeros_like(values))


def attend_forward(
    pair, queries, keys, values_t_ref, mask_ref, attended_t_ref, lse_ref, tick=lambda number: None
):
    length = keys.shape[0]
    queries = queries * bf16(HEAD**-0.5)
    for which in range(2):
        tick(which)
        head_queries = keep_half(queries, which)
        rows = block(2 * pair + which, HEAD)
        values_t = values_t_ref[rows, :]
        for start in range(0, length, QUERY_BLOCK):
            stop = start + QUERY_BLOCK
            scores = matmul(keys[0:stop], head_queries[start:stop], NT)
            scores = scores + mask_ref[0:stop, start:stop]
            top = jnp.max(scores, axis=0, keepdims=True)
            terms = jnp.exp(scores - top)
            sums = jnp.sum(terms, axis=0, keepdims=True)
            mixed = matmul(values_t[:, 0:stop], terms.astype(bf16), NN)
            attended_t_ref[rows, start:stop] = (mixed * (1.0 / sums)).astype(bf16)
            lse_ref[pl.ds(2 * pair + which, 1), start:stop] = top + jnp.log(sums)


def attend_backward(
    pair,
    operands,
    keys_t_ref,
    mask_ref,
    lse_ref,
    dots_ref,
    grad_queries_t_ref,
    grad_keys_ref,
    grad_values_ref,
    tick=lambda number: None,
):
    queries, keys, values, grads = operands
    length, scale_by = keys.shape[0], HEAD**-0.5
    queries = queries * bf16(scale_by)
    for number, start in enumerate(reversed(range(0, length, QUERY_BLOCK))):
        tick(number)
        stop = start + QUERY_BLOCK
        grad_keys = grad_values = 0.0
        for which in range(2):
            head = pl.ds(2 * pair + which, 1)
            rows = block(2 * pair + which, HEAD)
            query_rows = keep_half(queries[start:stop], which)
            grad_rows = keep_half(grads[start:stop], which)
            scores = matmul(keys[0:stop], query_rows, NT)
            probs = jnp.exp(scores + mask_ref[0:stop, start:stop] - lse_ref[head, start:stop])
            grad_probs = matmul(values[0:stop], grad_rows, NT)
            grad_scores = (probs * (grad_probs - dots_ref[head, start:stop])).astype(bf16)
            grad_values = grad_values + matmul(probs.astype(bf16), grad_rows, NN)
            grad_keys = grad_keys + matmul(grad_scores, query_rows, NN)
            grad_queries_t_ref[rows, start:stop] = (
                matmul(keys_t_ref[rows, 0:stop], grad_scores, NN) * scale_by
            ).astype(bf16)
        if stop == length:
            grad_keys_ref[...] = grad_keys
            grad_values_ref[...] = grad_values
        else:
            grad_keys_ref[0:stop] += grad_keys
            grad_values_ref[0:stop] += grad_values


MESH = pl.DeviceIdType.MESH
HBM = pl.BlockSpec(memory_space=pl.ANY)


def flip(value, bits):
    bit = 1
    while bit <= bits:
        if bits & bit:
            value = value + bit - 2 * bit * ((value // bit) % 2)
        bit *= 2
    return value


class Place:
    def __init__(self, shards):
        self.lines = shards // 2
        self.rep, self.me = lax.axis_index("rep"), lax.axis_index("shard")
        self.far, self.core = self.rep // 2, self.rep % 2
        self.line, self.side = self.me // 2, self.me % 2

    def shard(self, hop, turn):
        return flip(self.line, hop) * 2 + flip(self.side, turn)

    def peer(self, hop, turn):
        return (self.rep, self.shard(hop, turn))

    def across(self):
        return ((1 - self.far) * 2 + self.core, self.me)

    def sibling(self):
        return (self.far * 2 + 1 - self.core, self.me)

    def others(self):
        return [(h, t) for h in range(self.lines) for t in range(2) if h or t]

    def meet(self, peers):
        barrier = pltpu.get_barrier_semaphore()
        for peer in peers:
            pl.semaphore_signal(barrier, inc=1, device_id=peer, device_id_type=MESH)
        pl.semaphore_wait(barrier, len(peers))


def aligned(start, size):
    return pl.ds(pl.multiple_of(start, 16), size)


def remote(src, dst, send, recv, peer):
    return pltpu.make_async_remote_copy(
        src_ref=src,
        dst_ref=dst,
        send_sem=send,
        recv_sem=recv,
        device_id=peer,
        device_id_type=MESH,
    )


def cut(count):
    half = count // 2
    return half // 3 // 16 * 16, half


class Gather:
    def __init__(self, place, own, full, send, recv, local):
        self.place, self.own, self.full = place, own, full
        self.send, self.recv, self.local = send, recv, local
        self.hops = range(1, place.lines)

    def rows(self, at, kind, far, core):
        edge, half = cut(self.own[at].shape[0])
        if kind == "wide":
            return aligned(core * half + far * edge, half - edge)
        if kind == "edge":
            return aligned(core * half + far * (half - edge), edge)
        return aligned(core * half, half)

    def copy(self, at, stage, hop, turn, arriving=False):
        place, lines = self.place, self.place.lines
        number = hop * 2 + turn
        far, core = place.far, place.core
        if stage == "line":
            slot, peer, kind = hop - 1, place.peer(hop, 0), "wide"
            shard = place.shard(hop if arriving else 0, 0)
        elif stage == "side":
            slot, peer, kind = lines - 1 + hop, place.peer(0, 1), "wide"
            shard = place.shard(hop, 1 if arriving else 0)
        elif stage == "far":
            slot, peer, kind = 2 * lines - 1 + number - 1, place.across(), "edge"
            shard = place.shard(hop, turn)
            far = 1 - far if arriving else far
        else:
            slot, peer, kind = 4 * lines - 2 + number - 1, place.sibling(), "half"
            shard = place.shard(hop, turn)
            core = 1 - core if arriving else core
        rows = self.rows(at, kind, far, core)
        target = self.full[at].at[shard, rows]
        mine = not arriving and (stage == "line" or (stage == "side" and hop == 0))
        source = self.own[at].at[rows] if mine else target
        return remote(source, target, self.send.at[at, slot], self.recv.at[at, slot], peer)

    def start(self, at, stage, hop, turn=0):
        self.copy(at, stage, hop, turn).start()

    def got(self, at, stage, hop, turn=0):
        self.copy(at, stage, hop, turn, arriving=True).wait_recv()

    def keep(self, at):
        return pltpu.make_async_copy(
            self.own[at], self.full[at].at[self.place.me], self.local.at[at]
        )

    def own_side(self, at):
        self.start(at, "side", 0)

    def first(self, at, hop):
        self.start(at, "line", hop)

    def line(self, at, hop):
        self.got(at, "line", hop)
        self.start(at, "side", hop)
        self.start(at, "far", hop, 0)

    def side(self, at, hop):
        self.got(at, "side", hop)
        self.start(at, "far", hop, 1)

    def far(self, at, hop, turn):
        self.got(at, "far", hop, turn)
        self.start(at, "core", hop, turn)

    def last(self, at):
        for hop, turn in self.place.others():
            self.got(at, "core", hop, turn)
        self.keep(at).wait()

    def drain(self, at):
        for hop in self.hops:
            self.copy(at, "line", hop, 0).wait_send()
        for hop in range(self.place.lines):
            self.copy(at, "side", hop, 0).wait_send()
        for hop, turn in self.place.others():
            self.copy(at, "far", hop, turn).wait_send()
            self.copy(at, "core", hop, turn).wait_send()


def add_into(into, other):
    into[...] = (into[...].astype(f32) + other[...].astype(f32)).astype(bf16)


class Summed:
    def __init__(self, place, grad, done, buffers, send, recv, source=None, load_sem=None):
        self.place, self.grad, self.done = place, grad, done
        self.send_sem, self.recv_sem = send, recv
        self.source = grad if source is None else source
        self.load_sem = load_sem
        (
            self.from_core,
            self.from_far,
            self.from_side,
            self.from_me,
            self.from_line,
            self.from_back,
        ) = buffers
        self.edge_size, self.half = cut(grad.shape[1])
        self.hops = range(1, place.lines)

    def rows(self, kind, far=None, core=None):
        far = self.place.far if far is None else far
        core = self.place.core if core is None else core
        edge, half = self.edge_size, self.half
        if kind == "wide":
            return aligned(core * half + far * edge, half - edge)
        if kind == "edge":
            return aligned(core * half + far * (half - edge), edge)
        return aligned(core * half, half)

    def pair_of(self, hop):
        return pl.ds(2 * flip(self.place.line, hop), 2)

    def copy(self, stage, hop=0):
        place, lines, grad = self.place, self.place.lines, self.grad
        if stage == "core":
            slot, peer = 0, place.sibling()
            pair = self.source.at[:, self.rows("half", core=1 - place.core)], self.from_core
        elif stage == "far":
            slot, peer = hop, place.across()
            pair = (
                grad.at[self.pair_of(hop), self.rows("edge", far=1 - place.far)],
                self.from_far.at[hop - 1],
            )
        elif stage == "side":
            slot, peer = lines + hop, place.peer(0, 1)
            source = grad.at[place.shard(hop, 1), self.rows("wide" if hop else "half")]
            pair = source, self.from_side.at[hop - 1] if hop else self.from_me
        elif stage == "line":
            slot, peer = 2 * lines + hop - 1, place.peer(hop, 0)
            pair = grad.at[place.shard(hop, 0), self.rows("wide")], self.from_line.at[hop - 1]
        elif stage == "back":
            slot, peer = 3 * lines - 1, place.across()
            pair = grad.at[place.me, self.rows("half")], self.from_back
        else:
            slot, peer = 3 * lines, place.sibling()
            mine = self.done.at[self.rows("half")]
            pair = mine, mine
        return remote(*pair, self.send_sem.at[slot], self.recv_sem.at[slot], peer)

    def load(self):
        rows = self.rows("half")
        return pltpu.make_async_copy(
            self.source.at[:, rows], self.grad.at[:, rows], self.load_sem
        )

    def begin(self):
        self.copy("core").start()
        if self.load_sem is not None:
            self.load().start()

    def core(self):
        self.copy("core").wait_recv()
        if self.load_sem is not None:
            self.load().wait()
        for shard in range(2 * self.place.lines):
            add_into(self.grad.at[shard, self.rows("half")], self.from_core.at[shard])

    def me0(self):
        self.copy("side", 0).start()

    def send(self, hop):
        self.copy("far", hop).start()

    def far(self, hop):
        self.copy("far", hop).wait_recv()
        add_into(self.grad.at[self.pair_of(hop), self.rows("edge")], self.from_far.at[hop - 1])
        self.copy("side", hop).start()

    def side(self, hop):
        self.copy("side", hop).wait_recv()
        mine = self.grad.at[self.place.shard(hop, 0), self.rows("wide")]
        add_into(mine, self.from_side.at[hop - 1])
        self.copy("line", hop).start()

    def me(self):
        self.copy("side", 0).wait_recv()
        add_into(self.grad.at[self.place.me, self.rows("half")], self.from_me)

    def lines(self):
        mine = self.grad.at[self.place.me, self.rows("wide")]
        sums = mine[...].astype(f32)
        for hop in self.hops:
            self.copy("line", hop).wait_recv()
            sums = sums + self.from_line[hop - 1].astype(f32)
        mine[...] = sums.astype(bf16)
        self.copy("back").start()

    def back(self):
        self.copy("back").wait_recv()
        mine = self.grad[self.place.me, self.rows("half")].astype(f32)
        self.done[self.rows("half")] = (mine + self.from_back[...].astype(f32)).astype(bf16)
        self.copy("pair").start()

    def finish(self):
        other = self.done.at[self.rows("half", core=1 - self.place.core)]
        slot = 3 * self.place.lines
        remote(
            other, other, self.send_sem.at[slot], self.recv_sem.at[slot], self.place.sibling()
        ).wait_recv()

    def drain(self):
        self.copy("core").wait_send()
        for hop in self.hops:
            self.copy("far", hop).wait_send()
            self.copy("line", hop).wait_send()
        for hop in range(self.place.lines):
            self.copy("side", hop).wait_send()
        self.copy("back").wait_send()
        self.copy("pair").wait_send()


SUM_BUFFERS = 6


def sum_buffers(lines, shards, rows, columns):
    edge, half = cut(rows)
    return [
        pltpu.VMEM((shards, half, columns), bf16),
        pltpu.VMEM((lines - 1, 2, edge, columns), bf16),
        pltpu.VMEM((lines - 1, half - edge, columns), bf16),
        pltpu.VMEM((half, columns), bf16),
        pltpu.VMEM((lines - 1, half - edge, columns), bf16),
        pltpu.VMEM((half, columns), bf16),
    ]


def sum_sems(lines, items):
    return [pltpu.SemaphoreType.DMA((items, 3 * lines + 1))] * 2


def first_norm(tokens_ref, params_ref, normed_ref):
    length, width = tokens_ref.shape
    row = lambda at: params_ref[at : at + 1, 0:width]
    for at in range(0, length, ROW_CHUNK):
        norm, _ = normalized(tokens_ref[at : at + ROW_CHUNK].astype(f32))
        normed_ref[at : at + ROW_CHUNK] = (norm * row(GAIN1) + row(SHIFT1)).astype(bf16)


def forward_kernel(
    tokens_ref,
    segment_ref,
    params_ref,
    w_qkv_ref,
    projected_ref,
    attended_t_ref,
    lse_ref,
    mask_ref,
    normed_ref,
    values_t_ref,
):
    length, width = tokens_ref.shape
    pairs = width // (2 * HEAD)
    row = lambda at: params_ref[at : at + 1, 0:width]
    first_norm(tokens_ref, params_ref, normed_ref)
    for part, bias in enumerate((row(BIAS_Q), 0.0, row(BIAS_V))):
        columns = slice(part * width, (part + 1) * width)
        projected_ref[:, columns] = (
            matmul(normed_ref[...], w_qkv_ref[:, columns], NN) + bias
        ).astype(bf16)
    values_t_ref[...] = jnp.transpose(projected_ref[:, 2 * width :])
    build_mask(segment_ref, mask_ref)

    @pl.loop(0, pairs)
    def _(pair):
        attend_forward(
            pair,
            projected_ref[:, block(pair, 2 * HEAD)],
            projected_ref[:, block(pairs + pair, 2 * HEAD)],
            values_t_ref,
            mask_ref,
            attended_t_ref,
            lse_ref,
        )


GROUP = 4 * HEAD
GATHERED_EARLY = 1
SUMMED_EARLY = 1


(
    OWN,
    FIRST,
    LINE,
    SIDE,
    FAR,
    LAST,
    BEGIN_SUM,
    CORE_SUM,
    ME0_SUM,
    SEND_SUM,
    FAR_SUM,
    SIDE_SUM,
    ME_SUM,
    LINES_SUM,
    BACK_SUM,
    FINISH_SUM,
) = range(16)
P0, P1, P2, H0, H1, H2, H3, E0, E1, E2, E3, B0, B1, B2, B3, NEED, END = range(100, 117)

FORWARD_PLAN = {P0: [(OWN, 0), (FIRST, 0, 1)],
 P1: [(FIRST, 0, 3), (OWN, 1)],
 P2: [(FIRST, 0, 2), (LINE, 0, 1), (SIDE, 0, 0)],
 END: [(LAST, 5)],
 NEED: {0: [(FIRST, 1, 1), (SIDE, 1, 0), (OWN, 2), (OWN, 3), (FIRST, 1, 3), (LINE, 0, 3), (FIRST, 1, 2),
            (FAR, 0, 1, 0), (FAR, 0, 0, 1), (FAR, 1, 0, 1), (OWN, 4), (SIDE, 0, 1), (FAR, 0, 3, 0),
            (FIRST, 2, 1), (LINE, 1, 1), (SIDE, 2, 0), (SIDE, 3, 0), (LINE, 0, 2), (FAR, 0, 1, 1),
            (FIRST, 2, 3), (SIDE, 0, 3), (FIRST, 2, 2), (OWN, 5), (FAR, 1, 1, 0), (FAR, 2, 0, 1),
            (LINE, 1, 3), (SIDE, 4, 0), (FIRST, 3, 1), (FAR, 3, 0, 1), (FAR, 0, 2, 0), (SIDE, 1, 1),
            (FAR, 0, 3, 1), (LINE, 1, 2), (FIRST, 3, 3), (SIDE, 0, 2), (LINE, 2, 1), (FIRST, 3, 2),
            (FAR, 1, 3, 0), (FAR, 4, 0, 1), (SIDE, 5, 0), (FAR, 1, 1, 1), (SIDE, 1, 3), (LINE, 2, 3),
            (FAR, 1, 2, 0), (FIRST, 4, 1), (LINE, 2, 2), (FAR, 0, 2, 1), (FAR, 2, 1, 0), (SIDE, 1, 2),
            (LINE, 3, 1), (SIDE, 2, 1), (FIRST, 4, 3), (FAR, 5, 0, 1), (LAST, 0)]},
 0: {0: [(FIRST, 4, 2)],
     1: [(LAST, 1), (LINE, 4, 1), (FIRST, 5, 3)],
     2: [(FAR, 2, 2, 1), (FAR, 2, 3, 1), (SIDE, 3, 2), (SIDE, 3, 3), (FAR, 3, 2, 0), (FAR, 3, 3, 0),
         (FAR, 3, 1, 1), (LINE, 4, 2), (SIDE, 4, 1), (FAR, 4, 1, 0), (FAR, 4, 3, 0)],
     3: [(SIDE, 4, 2), (LINE, 5, 2), (FAR, 3, 2, 1)],
     4: [(LAST, 3), (FAR, 4, 2, 1), (SIDE, 5, 2), (FAR, 5, 2, 0), (FAR, 5, 3, 0), (FAR, 5, 1, 1)],
     5: [(LAST, 4), (FAR, 5, 2, 1)]},
 1: {0: [(FAR, 1, 2, 1), (FAR, 1, 3, 1), (SIDE, 2, 2), (SIDE, 2, 3), (FAR, 2, 2, 0), (FAR, 2, 3, 0),
         (FAR, 2, 1, 1), (LINE, 3, 2), (SIDE, 3, 1), (FAR, 3, 1, 0), (LINE, 3, 3), (FIRST, 5, 1)],
     1: [(LINE, 4, 3), (FIRST, 5, 2)],
     2: [(SIDE, 4, 3), (LAST, 2), (LINE, 5, 1)],
     3: [(FAR, 3, 3, 1), (FAR, 4, 2, 0), (FAR, 4, 1, 1), (FAR, 4, 3, 1), (LINE, 5, 3), (FAR, 5, 1, 0),
         (SIDE, 5, 1)],
     4: [(SIDE, 5, 3)],
     5: [(FAR, 5, 3, 1)]}}

HIDDEN_PLAN = {H0: [(OWN, 0), (FIRST, 0, 1), (FIRST, 0, 3)],
 H1: [(FIRST, 0, 2), (OWN, 1)],
 H2: [(LINE, 0, 1), (SIDE, 0, 0), (FIRST, 1, 1)],
 H3: [(FIRST, 1, 3), (OWN, 2)],
 E0: [(FINISH_SUM, 0)],
 E3: [(BACK_SUM, 1)],
 END: [(FINISH_SUM, 1)],
 1: {0: [(LINE, 0, 3), (FAR, 0, 1, 0), (FIRST, 1, 2), (SIDE, 1, 0)],
     1: [(SIDE, 2, 2), (FAR, 2, 2, 0), (LINE, 3, 3), (SEND_SUM, 1, 3)]},
 2: {0: [(LINE, 0, 2), (SIDE, 0, 1), (FAR, 0, 0, 1)],
     1: [(LINE, 3, 2), (SIDE, 3, 1)],
     2: [(LINES_SUM, 0), (SIDE_SUM, 1, 2), (SIDE_SUM, 1, 1)]},
 3: {0: [(FAR, 0, 3, 0), (LINE, 1, 1), (FIRST, 2, 1), (SIDE, 2, 0)],
     1: [(FAR, 2, 2, 1), (FAR, 2, 3, 1), (FAR, 3, 1, 0), (FAR_SUM, 0, 2), (SIDE_SUM, 0, 3),
         (SEND_SUM, 1, 2)]},
 4: {0: [(SIDE, 0, 3), (FAR, 0, 2, 0), (FAR, 1, 0, 1), (FIRST, 2, 3), (OWN, 3)],
     1: [(SIDE, 3, 3), (FAR, 3, 3, 0), (FAR_SUM, 0, 1), (SEND_SUM, 1, 1)]},
 5: {0: [(SIDE, 0, 2), (FAR, 0, 1, 1), (FAR, 1, 1, 0), (FIRST, 2, 2), (BEGIN_SUM, 0)],
     1: [(LAST, 2), (SIDE, 3, 2), (FAR, 3, 2, 0), (FAR, 3, 1, 1), (ME0_SUM, 1)]},
 6: {0: [(LINE, 1, 3), (SIDE, 1, 1), (FAR, 2, 0, 1), (FIRST, 3, 1), (BEGIN_SUM, 1)],
     1: [(SIDE_SUM, 0, 2), (FAR_SUM, 1, 3)],
     2: [(BACK_SUM, 0)]},
 7: {0: [(FAR, 0, 3, 1), (LINE, 1, 2), (SIDE, 3, 0)],
     1: [(FAR, 3, 3, 1), (SIDE_SUM, 0, 1), (FAR_SUM, 1, 2)],
     2: [(LINES_SUM, 1)]},
 NEED: {1: [(FAR, 0, 2, 1), (FAR, 1, 3, 0), (FAR, 1, 1, 1), (LINE, 2, 1), (FIRST, 3, 3), (CORE_SUM, 0),
            (SEND_SUM, 0, 3), (CORE_SUM, 1), (SIDE, 1, 3), (FAR, 1, 2, 0), (ME0_SUM, 0), (LAST, 0),
            (FAR, 3, 0, 1), (SEND_SUM, 0, 2), (SIDE, 1, 2), (FAR, 2, 1, 0), (FIRST, 3, 2), (LINE, 2, 3),
            (SIDE, 2, 1), (FAR, 1, 3, 1), (LINE, 2, 2), (SEND_SUM, 0, 1), (ME_SUM, 0), (LINE, 3, 1),
            (FAR, 1, 2, 1), (SIDE, 2, 3), (FAR, 2, 3, 0), (FAR_SUM, 0, 3), (LAST, 1), (FAR, 2, 1, 1)],
        2: [(FAR, 3, 2, 1), (FAR_SUM, 1, 1), (ME_SUM, 1), (SIDE_SUM, 1, 3), (LAST, 3)]}}

BACKWARD_PLAN = {B0: [(BEGIN_SUM, 0), (BEGIN_SUM, 1), (BEGIN_SUM, 2), (BEGIN_SUM, 3), (BEGIN_SUM, 4)],
 B2: [(CORE_SUM, 0), (ME0_SUM, 0), (SEND_SUM, 0, 3), (SEND_SUM, 0, 2)],
 B3: [(SEND_SUM, 0, 1), (CORE_SUM, 1), (ME0_SUM, 1)],
 E0: [(SIDE_SUM, 4, 1), (FAR_SUM, 6, 3), (FAR_SUM, 6, 2), (BEGIN_SUM, 7)],
 E1: [(BACK_SUM, 2), (SIDE_SUM, 5, 3), (FAR_SUM, 6, 1)],
 E2: [(FINISH_SUM, 2), (LINES_SUM, 3), (SIDE_SUM, 5, 2), (ME_SUM, 6), (CORE_SUM, 7), (ME0_SUM, 7),
      (SEND_SUM, 7, 3)],
 E3: [(SIDE_SUM, 5, 1), (SEND_SUM, 7, 2)],
 END: [(SIDE_SUM, 6, 3), (SEND_SUM, 7, 1), (BACK_SUM, 3), (ME_SUM, 7), (LINES_SUM, 4), (SIDE_SUM, 6, 2),
       (FAR_SUM, 7, 3), (FINISH_SUM, 3), (FAR_SUM, 7, 2), (SIDE_SUM, 6, 1), (FAR_SUM, 7, 1), (SIDE_SUM, 7, 3),
       (BACK_SUM, 4), (SIDE_SUM, 7, 2), (LINES_SUM, 5), (FINISH_SUM, 4), (SIDE_SUM, 7, 1), (BACK_SUM, 5),
       (FINISH_SUM, 5), (LINES_SUM, 6), (LINES_SUM, 7), (BACK_SUM, 6), (FINISH_SUM, 6), (BACK_SUM, 7),
       (FINISH_SUM, 7)],
 1: {0: [(FAR_SUM, 0, 3), (SEND_SUM, 1, 3), (CORE_SUM, 2), (ME_SUM, 0), (SEND_SUM, 1, 2), (ME0_SUM, 2),
         (CORE_SUM, 3)],
     1: [(FAR_SUM, 0, 1), (FAR_SUM, 1, 3), (SEND_SUM, 2, 2)],
     2: [(SIDE_SUM, 1, 3), (SIDE_SUM, 1, 2), (FAR_SUM, 2, 2), (SEND_SUM, 3, 1), (SEND_SUM, 4, 3)],
     3: [(SIDE_SUM, 2, 3), (FAR_SUM, 3, 3), (SEND_SUM, 4, 1)],
     4: [(FINISH_SUM, 0), (LINES_SUM, 1), (SIDE_SUM, 3, 3), (FAR_SUM, 4, 3), (FAR_SUM, 4, 2)],
     5: [(BACK_SUM, 1), (SIDE_SUM, 3, 1), (FAR_SUM, 5, 3), (FAR_SUM, 5, 2)]},
 2: {0: [(SEND_SUM, 1, 1), (CORE_SUM, 4), (ME_SUM, 1), (FAR_SUM, 0, 2)],
     1: [(FAR_SUM, 1, 2), (SEND_SUM, 2, 1), (ME_SUM, 2)],
     2: [(FAR_SUM, 2, 1), (SEND_SUM, 4, 2), (CORE_SUM, 5), (SIDE_SUM, 1, 1)],
     3: [(FAR_SUM, 3, 2), (SEND_SUM, 5, 3)],
     4: [(FAR_SUM, 4, 1), (CORE_SUM, 6), (SEND_SUM, 6, 3), (SEND_SUM, 6, 2), (SIDE_SUM, 3, 2)],
     5: [(FINISH_SUM, 1), (LINES_SUM, 2), (SIDE_SUM, 4, 3), (FAR_SUM, 5, 1)]},
 3: {0: [(SEND_SUM, 2, 3)],
     1: [(SIDE_SUM, 0, 2), (SEND_SUM, 3, 3)],
     2: [(LINES_SUM, 0), (ME0_SUM, 3)],
     3: [(SIDE_SUM, 2, 2), (FAR_SUM, 3, 1), (SEND_SUM, 5, 2)],
     4: [(ME_SUM, 4), (ME0_SUM, 5), (SEND_SUM, 6, 1)],
     5: [(ME_SUM, 5), (SIDE_SUM, 4, 2), (ME0_SUM, 6)]},
 0: {1: [(SIDE_SUM, 0, 3)],
     2: [(SIDE_SUM, 0, 1), (FAR_SUM, 1, 1), (FAR_SUM, 2, 3), (SEND_SUM, 3, 2), (BEGIN_SUM, 5)],
     4: [(BACK_SUM, 0), (SIDE_SUM, 2, 1), (ME_SUM, 3), (ME0_SUM, 4), (SEND_SUM, 5, 1), (BEGIN_SUM, 6)]}}


class Runner:
    def __init__(self, plan, gather, sums):
        self.plan, self.gather, self.sums = plan, gather, sums

    def act(self, events):
        gather = self.gather
        for what, item, *where in events:
            if what >= BEGIN_SUM:
                one = self.sums[item]
                acts = (
                    one.begin,
                    one.core,
                    one.me0,
                    one.send,
                    one.far,
                    one.side,
                    one.me,
                    one.lines,
                    one.back,
                    one.finish,
                )
                acts[what - BEGIN_SUM](*where)
            else:
                acts = (
                    gather.own_side,
                    gather.first,
                    gather.line,
                    gather.side,
                    gather.far,
                    gather.last,
                )
                acts[what](item, *where)

    def do(self, key):
        self.act(self.plan.get(key, ()))

    def at_step(self, step, key):
        for number, events in self.plan.get(key, {}).items():

            @pl.when(step == number)
            def _(events=events):
                self.act(events)


def gather_forward_kernel(
    shards,
    tokens_ref,
    segment_ref,
    own_params_ref,
    own_qkv_ref,
    own_out_ref,
    own_fc_ref,
    own_proj_ref,
    projected_ref,
    attended_t_ref,
    lse_ref,
    params_ref,
    full_qkv_ref,
    full_out_ref,
    full_fc_ref,
    full_proj_ref,
    mask_ref,
    normed_ref,
    values_t_ref,
    held_ref,
    weights_ref,
    tables_ref,
    group_ref,
    own_block_ref,
    own_rows_ref,
    own_units_ref,
    send_sem,
    recv_sem,
    local_sem,
    params_send_sem,
    params_recv_sem,
    load_sem,
    out_sem,
):
    length, width = tokens_ref.shape
    groups = width // GROUP
    blocks = full_fc_ref.shape[0]
    place = Place(shards)
    others = place.others()
    own = [group_ref.at[g] for g in range(groups)] + [own_rows_ref]
    full = [weights_ref.at[g] for g in range(groups)] + [full_out_ref]
    for number in range(blocks):
        own += [own_block_ref.at[number], own_units_ref.at[number * 128 : number * 128 + 128]]
        full += [full_fc_ref.at[number], full_proj_ref.at[number]]
    gather = Gather(place, own, full, send_sem, recv_sem, local_sem)

    def move(source, target, number):
        pltpu.make_async_copy(source, target, load_sem.at[number]).start()

    def moved(whole, number):
        pltpu.make_async_copy(whole, whole, load_sem.at[number]).wait()

    for g in range(groups):
        for part in range(3):
            start = part * width + g * GROUP
            move(
                own_qkv_ref.at[:, start : start + GROUP],
                group_ref.at[g, :, part * GROUP : (part + 1) * GROUP],
                g,
            )
    for number in range(blocks):
        take_block(
            move, own_fc_ref, number, shards, own_block_ref.at[number], groups + number
        )
    move(own_out_ref, own_rows_ref, groups + blocks)
    move(own_proj_ref.at[0 : blocks * 128], own_units_ref, groups + blocks + 1)
    place.meet([place.peer(*other) for other in others] + [place.across(), place.sibling()])

    def table(number, other, arriving):
        target = tables_ref.at[place.shard(*other) if arriving else place.me]
        return remote(
            target if arriving else own_params_ref,
            target,
            params_send_sem.at[number],
            params_recv_sem.at[number],
            place.peer(*other),
        )

    for number, other in enumerate(others):
        table(number, other, False).start()
    runner = Runner(FORWARD_PLAN, gather, ())

    def outward(g):
        return (
            pltpu.make_async_copy(held_ref.at[g], projected_ref.at[g], out_sem.at[g, 0]),
            pltpu.make_async_copy(weights_ref.at[g], full_qkv_ref.at[g], out_sem.at[g, 1]),
        )

    for g in range(groups):
        moved(group_ref.at[g], g)
        runner.act([event for event in FORWARD_PLAN[P0] if event[1] == g])
    moved(own_rows_ref, groups + blocks)
    moved(own_units_ref, groups + blocks + 1)
    runner.act([event for event in FORWARD_PLAN[P0] if event[1] >= groups])
    for g in range(groups):
        gather.keep(g).start()
    for number in range(blocks):
        moved(own_block_ref.at[number], groups + number)
    for at in range(groups, groups + 1 + 2 * blocks):
        gather.keep(at).start()
    tables_ref[place.me] = own_params_ref[...]
    build_mask(segment_ref, mask_ref)
    runner.do(P1)
    for number, other in enumerate(others):
        table(number, other, True).wait_recv()
    spread_params(shards, width // shards, tables_ref, params_ref)
    first_norm(tokens_ref, params_ref, normed_ref)
    runner.do(P2)

    @pl.loop(0, 2 * groups)
    def _(pair):
        g, odd = pair // 2, pair % 2
        runner.at_step(pair, NEED)

        @pl.when(odd == 0)
        def _():
            part = block(g, GROUP)
            weights = weights_ref[g].reshape(width, 3 * GROUP)
            values = matmul(normed_ref[...], weights, NN)
            bias = jnp.concatenate(
                [
                    params_ref[BIAS_Q : BIAS_Q + 1, part],
                    jnp.zeros((1, GROUP), f32),
                    params_ref[BIAS_V : BIAS_V + 1, part],
                ],
                axis=1,
            )
            held_ref[g] = (values + bias).astype(bf16)
            values_t_ref[part, :] = jnp.transpose(held_ref[g, :, 2 * GROUP :])
            for copy in outward(g):
                copy.start()

        attend_forward(
            pair,
            held_ref[g, :, block(odd, 2 * HEAD)],
            held_ref[g, :, block(2 + odd, 2 * HEAD)],
            values_t_ref,
            mask_ref,
            attended_t_ref,
            lse_ref,
            lambda which: runner.at_step(pair, which),
        )

    runner.do(END)
    for g in range(groups):
        for copy in outward(g):
            copy.wait()
    for at in range(groups + 1 + 2 * blocks):
        gather.drain(at)
    for number, other in enumerate(others):
        table(number, other, False).wait_send()


def spread_params(shards, own, tables_ref, params_ref):
    span = params_ref.shape[1]
    lane = lax.broadcasted_iota(jnp.int32, (128, span), 0)
    column = lax.broadcasted_iota(jnp.int32, (128, span), 1)
    narrow = wide = 0.0
    for shard in range(shards):
        values = tables_ref[shard]
        place = (column == lane + shard * own) & (lane < own)
        narrow = narrow + matmul(values, place.astype(f32).astype(bf16), NN)
        place = column == lane + shard * 128
        wide = wide + matmul(values, place.astype(f32).astype(bf16), NN)
    params_ref[0:8] = narrow[0:8]
    params_ref[8:16] = wide[8:16]


def take_block(move, own_fc_ref, number, shards, target_ref, sem):
    own = own_fc_ref.shape[1] // shards
    for shard in range(shards):
        start = shard * own + number * 128
        move(
            own_fc_ref.at[:, start : start + 128],
            target_ref.at[:, shard * 128 : (shard + 1) * 128],
            sem,
        )


def hidden_kernel(
    attended_t_ref,
    tokens_ref,
    cotangent_ref,
    params_ref,
    w_out_ref,
    w_fc_ref,
    w_proj_ref,
    layer_out_ref,
    grad_middle_ref,
    grad_attended_ref,
    grad_w_out_ref,
    grad_w_fc_ref,
    grad_w_proj_t_ref,
    small_ref,
    middle_ref,
    normed_ref,
    normed_t_ref,
    cotangent_t_ref,
    mixed_ref,
    grad_normed_ref,
    activated_ref,
    grad_preact_ref,
):
    step, steps = pl.program_id(0), pl.num_programs(0)
    length, width = tokens_ref.shape
    row = lambda at: params_ref[at : at + 1, :]
    chunks = [slice(at, at + ROW_CHUNK) for at in range(0, length, ROW_CHUNK)]

    @pl.when(step == 0)
    def _():
        attended = jnp.transpose(attended_t_ref[...])
        middle_ref[...] = (
            tokens_ref[...].astype(f32) + matmul(attended, w_out_ref[...], NN) + row(BIAS_OUT)
        )
        for rows in chunks:
            norm, _ = normalized(middle_ref[rows])
            normed_ref[rows] = (norm * row(GAIN2) + row(SHIFT2)).astype(bf16)
        normed_t_ref[...] = jnp.transpose(normed_ref[...])
        cotangent_t_ref[...] = jnp.transpose(cotangent_ref[...])
        mixed_ref[...] = jnp.zeros_like(mixed_ref)
        grad_normed_ref[...] = jnp.zeros_like(grad_normed_ref)
        small_ref[...] = jnp.zeros_like(small_ref)

    bias_sum = 0.0
    bias_row = params_ref[pl.ds(BIAS_FC + step, 1), :]
    for rows in chunks:
        preact = matmul(normed_ref[rows], w_fc_ref[...], NN) + bias_row
        grad_act = matmul(cotangent_ref[rows], w_proj_ref[...], NT)
        square = preact * preact
        bend = jnp.tanh(GELU_SCALE * preact * (1.0 + GELU_CUBE * square))
        gate = 0.5 + 0.5 * bend
        activated_ref[rows] = (preact * gate).astype(bf16)
        slope = gate + (0.5 * GELU_SCALE) * preact * (1.0 - bend * bend) * (
            1.0 + (3 * GELU_CUBE) * square
        )
        grad_preact = (slope * grad_act).astype(bf16)
        grad_preact_ref[rows] = grad_preact
        bias_sum = bias_sum + total(grad_preact.astype(f32))
    small_ref[pl.ds(BIAS_FC + step, 1), :] = bias_sum
    mixed_ref[...] += matmul(activated_ref[...], w_proj_ref[...], NN)
    grad_w_proj_t = matmul(cotangent_t_ref[...], activated_ref[...], NN).astype(bf16)
    pieces, _, piece = grad_w_proj_t_ref.shape
    for at in range(pieces):
        grad_w_proj_t_ref[at] = grad_w_proj_t[:, at * piece : (at + 1) * piece]
    grad_w_fc_ref[...] = matmul(normed_t_ref[...], grad_preact_ref[...], NN).astype(bf16)
    grad_normed_ref[...] += matmul(grad_preact_ref[...], w_fc_ref[...], NT)

    @pl.when(step == steps - 1)
    def _():
        sums = [0.0] * 4
        for rows in chunks:
            middle = middle_ref[rows]
            layer_out_ref[rows] = (middle + mixed_ref[rows] + row(BIAS_PROJ)).astype(bf16)
            norm, inverse = normalized(middle)
            grad_normed = grad_normed_ref[rows]
            cotangent = cotangent_ref[rows].astype(f32)
            grad_middle = cotangent + norm_pull(grad_normed, row(GAIN2), norm, inverse)
            grad_middle_ref[rows] = grad_middle
            normed_ref[rows] = grad_middle.astype(bf16)
            terms = (grad_middle, grad_normed * norm, grad_normed, cotangent)
            sums = [a + total(b) for a, b in zip(sums, terms)]
        for at, value in zip((BIAS_OUT, GAIN2, SHIFT2, BIAS_PROJ), sums):
            small_ref[at : at + 1, :] = value
        grad_branch = normed_ref[...]
        grad_w_out_ref[...] = matmul(attended_t_ref[...], grad_branch, NN).astype(bf16)
        grad_attended_ref[...] = matmul(grad_branch, w_out_ref[...], NT).astype(bf16)


def sum_hidden_kernel(
    shards,
    attended_t_in_ref,
    tokens_in_ref,
    cotangent_in_ref,
    params_ref,
    w_out_in_ref,
    fc_in_ref,
    proj_in_ref,
    own_fc_ref,
    own_proj_ref,
    layer_out_ref,
    grad_middle_ref,
    grad_attended_ref,
    grad_out_ref,
    last_fc_ref,
    last_proj_ref,
    done_fc_ref,
    done_proj_ref,
    small_ref,
    middle_ref,
    normed_ref,
    normed_t_ref,
    cotangent_t_ref,
    mixed_ref,
    grad_normed_ref,
    activated_ref,
    grad_preact_ref,
    fc_ref,
    proj_ref,
    grad_fc_ref,
    grad_proj_ref,
    own_block_ref,
    attended_t_ref,
    tokens_ref,
    cotangent_ref,
    w_out_ref,
    layer_ref,
    *rest,
):
    length, width = tokens_ref.shape
    blocks = fc_ref.shape[0]
    units = fc_ref.shape[3]
    early = fc_in_ref.shape[0]
    summed = done_fc_ref.shape[0]
    buffers, rest = [rest[SUM_BUFFERS * k :][:SUM_BUFFERS] for k in range(2 * summed)], rest[
        SUM_BUFFERS * 2 * summed :
    ]
    send_sem, recv_sem, local_sem, load_sem, sum_send_sem, sum_recv_sem = rest
    row = lambda at: params_ref[at : at + 1, 0:width]
    chunks = [slice(at, at + ROW_CHUNK) for at in range(0, length, ROW_CHUNK)]
    place = Place(shards)

    def move(source, target, number):
        pltpu.make_async_copy(source, target, load_sem.at[number]).start()

    def moved(whole, number):
        pltpu.make_async_copy(whole, whole, load_sem.at[number]).wait()

    own, full = [], []
    for number in range(early, blocks):
        own_block = own_block_ref.at[number - early]
        take_block(move, own_fc_ref, number, shards, own_block, number)
        own += [own_block, own_proj_ref.at[number * 128 : number * 128 + 128]]
        full += [fc_ref.at[number], proj_ref.at[number]]
    inputs = (
        (attended_t_in_ref, attended_t_ref),
        (w_out_in_ref, w_out_ref),
        (tokens_in_ref, tokens_ref),
        (cotangent_in_ref, cotangent_ref),
    )
    for number, pair in enumerate(inputs):
        move(*pair, 2 * blocks + number)
    for number in range(early):
        move(fc_in_ref.at[number], fc_ref.at[number], number)
        move(proj_in_ref.at[number], proj_ref.at[number], blocks + number)
    gather = Gather(place, own, full, send_sem, recv_sem, local_sem)
    sums = []
    for number in range(summed):
        for grad, done in ((grad_proj_ref, done_proj_ref), (grad_fc_ref, done_fc_ref)):
            k = len(sums)
            sums.append(
                Summed(
                    place,
                    grad.at[number],
                    done.at[number],
                    buffers[k],
                    sum_send_sem.at[k],
                    sum_recv_sem.at[k],
                )
            )
    runner = Runner(HIDDEN_PLAN, gather, sums)
    place.meet(
        [place.peer(hop, 0) for hop in range(1, place.lines)]
        + [place.peer(0, 1), place.across(), place.sibling()]
    )
    for number in range(early, blocks):
        moved(own_block_ref.at[number - early], number)
    runner.do(H0)
    for at in range(len(own)):
        gather.keep(at).start()

    for number, pair in enumerate(inputs):
        moved(pair[1], 2 * blocks + number)
    attended = jnp.transpose(attended_t_ref[...])
    w_out = w_out_ref[...].reshape(width, width)
    middle_ref[...] = tokens_ref[...].astype(f32) + matmul(attended, w_out, NN) + row(BIAS_OUT)
    runner.do(H1)
    for rows in chunks:
        norm, _ = normalized(middle_ref[rows])
        normed_ref[rows] = (norm * row(GAIN2) + row(SHIFT2)).astype(bf16)
    runner.do(H2)
    normed_t_ref[...] = jnp.transpose(normed_ref[...])
    cotangent_t_ref[...] = jnp.transpose(cotangent_ref[...])
    mixed_ref[...] = jnp.zeros_like(mixed_ref)
    grad_normed_ref[...] = jnp.zeros_like(grad_normed_ref)
    small_ref[...] = jnp.zeros_like(small_ref)
    for number in range(early):
        moved(fc_ref.at[number], number)
        moved(proj_ref.at[number], blocks + number)
    runner.do(H3)

    @pl.loop(0, blocks)
    def _(step):
        runner.at_step(step, NEED)
        w_fc = fc_ref.at[step]
        w_proj = proj_ref.at[step]
        bias_sum = 0.0
        bias_row = params_ref[pl.ds(BIAS_FC + step, 1), 0:units]
        for tick, rows in enumerate(chunks):
            runner.at_step(step, tick)
            preact = matmul(normed_ref[rows], w_fc[...].reshape(width, units), NN) + bias_row
            grad_act = matmul(cotangent_ref[rows], w_proj[...].reshape(units, width), NT)
            square = preact * preact
            bend = jnp.tanh(GELU_SCALE * preact * (1.0 + GELU_CUBE * square))
            gate = 0.5 + 0.5 * bend
            activated_ref[rows] = (preact * gate).astype(bf16)
            slope = gate + (0.5 * GELU_SCALE) * preact * (1.0 - bend * bend) * (
                1.0 + (3 * GELU_CUBE) * square
            )
            grad_preact = (slope * grad_act).astype(bf16)
            grad_preact_ref[rows] = grad_preact
            bias_sum = bias_sum + total(grad_preact.astype(f32))
        small_ref[pl.ds(BIAS_FC + step, 1), 0:units] = bias_sum
        runner.at_step(step, len(chunks))
        grad_proj = matmul(cotangent_t_ref[...], activated_ref[...], NN).astype(bf16)
        for shard in range(shards):
            grad_proj_ref[step, shard] = grad_proj[:, shard * 128 : (shard + 1) * 128]
        runner.at_step(step, len(chunks) + 1)
        grad_fc = matmul(normed_t_ref[...], grad_preact_ref[...], NN).astype(bf16)
        grad_fc_ref[step] = grad_fc.reshape(grad_fc_ref.shape[1:])
        runner.at_step(step, len(chunks) + 2)
        mixed_ref[...] += matmul(activated_ref[...], w_proj[...].reshape(units, width), NN)
        runner.at_step(step, len(chunks) + 3)
        grad_normed_ref[...] += matmul(
            grad_preact_ref[...], w_fc[...].reshape(width, units), NT
        )

    hand_over = []

    def hand(source, target):
        copy = pltpu.make_async_copy(source, target, load_sem.at[len(hand_over)])
        copy.start()
        hand_over.append(copy)

    hand(grad_fc_ref.at[summed:blocks], last_fc_ref)
    hand(grad_proj_ref.at[summed:blocks], last_proj_ref)
    parts = [0.0] * 4
    for number, rows in enumerate(chunks):
        if number < 2:
            runner.do(E0 + number)
        middle = middle_ref[rows]
        layer_ref[rows] = (middle + mixed_ref[rows] + row(BIAS_PROJ)).astype(bf16)
        norm, inverse = normalized(middle)
        grad_normed = grad_normed_ref[rows]
        cotangent = cotangent_ref[rows].astype(f32)
        grad_middle = cotangent + norm_pull(grad_normed, row(GAIN2), norm, inverse)
        middle_ref[rows] = grad_middle
        normed_ref[rows] = grad_middle.astype(bf16)
        terms = (grad_middle, grad_normed * norm, grad_normed, cotangent)
        parts = [a + total(b) for a, b in zip(parts, terms)]
    for at, value in zip((BIAS_OUT, GAIN2, SHIFT2, BIAS_PROJ), parts):
        small_ref[at : at + 1, 0:width] = value
    hand(middle_ref, grad_middle_ref)
    hand(layer_ref, layer_out_ref)
    runner.do(E2)
    grad_branch = normed_ref[...]
    grad_out = matmul(attended_t_ref[...], grad_branch, NN).astype(bf16)
    grad_out_ref[...] = grad_out.reshape(grad_out_ref.shape)
    runner.do(E3)
    grad_attended_ref[...] = matmul(grad_branch, w_out, NT).astype(bf16)
    runner.do(END)
    for copy in hand_over:
        copy.wait()
    for item in sums:
        item.drain()
    for at in range(len(own)):
        gather.drain(at)


def backward_kernel(
    tokens_ref,
    segment_ref,
    params_ref,
    w_qkv_ref,
    projected_ref,
    attended_t_ref,
    lse_ref,
    grad_attended_ref,
    grad_middle_ref,
    small_in_ref,
    grad_tokens_ref,
    grad_w_qkv_ref,
    small_ref,
    mask_ref,
    wide_t_ref,
    grad_queries_t_ref,
    dots_ref,
    grad_projected_ref,
    grad_keys_ref,
    grad_values_ref,
):
    length, width = tokens_ref.shape
    build_mask(segment_ref, mask_ref)
    dot_rows(attended_t_ref, grad_attended_ref, wide_t_ref, dots_ref)
    wide_t_ref[...] = jnp.transpose(projected_ref[:, width : 2 * width])

    pairs = width // (2 * HEAD)

    @pl.loop(0, pairs)
    def _(pair):
        parts = [projected_ref[:, block(k * pairs + pair, 2 * HEAD)] for k in range(3)]
        attend_backward(
            pair,
            parts + [grad_attended_ref[:, block(pair, 2 * HEAD)]],
            wide_t_ref,
            mask_ref,
            lse_ref,
            dots_ref,
            grad_queries_t_ref,
            grad_keys_ref,
            grad_values_ref,
        )
        for k, ref in ((1, grad_keys_ref), (2, grad_values_ref)):
            grad_projected_ref[:, block(k * pairs + pair, 2 * HEAD)] = ref[...].astype(bf16)

    grad_projected_ref[:, 0:width] = jnp.transpose(grad_queries_t_ref[...])
    normed_transposed(tokens_ref, params_ref, wide_t_ref)
    small_ref[...] = small_in_ref[...]
    bias_sums(grad_projected_ref, small_ref)
    grad_w_qkv_ref[...] = matmul(wide_t_ref[...], grad_projected_ref[...], NN).astype(bf16)
    gain_sum = shift_sum = 0.0
    for at in range(0, length, ROW_CHUNK):
        gain_part, shift_part = token_rows(
            at,
            tokens_ref,
            params_ref,
            matmul(grad_projected_ref[at : at + ROW_CHUNK], w_qkv_ref[...], NT),
            grad_middle_ref[at : at + ROW_CHUNK],
            grad_tokens_ref,
        )
        gain_sum, shift_sum = gain_sum + gain_part, shift_sum + shift_part
    small_ref[GAIN1 : GAIN1 + 1, :] = gain_sum
    small_ref[SHIFT1 : SHIFT1 + 1, :] = shift_sum


def dot_rows(attended_t_ref, grad_attended_ref, wide_t_ref, dots_ref):
    wide_t_ref[...] = jnp.transpose(grad_attended_ref[...])
    for head in range(wide_t_ref.shape[0] // HEAD):
        rows = slice(head * HEAD, (head + 1) * HEAD)
        dots_ref[head : head + 1, :] = total(
            wide_t_ref[rows].astype(f32) * attended_t_ref[rows].astype(f32)
        )


def normed_transposed(tokens_ref, params_ref, wide_t_ref):
    width = tokens_ref.shape[1]
    row = lambda at: params_ref[at : at + 1, 0:width]
    for at in range(0, tokens_ref.shape[0], ROW_CHUNK):
        norm, _ = normalized(tokens_ref[at : at + ROW_CHUNK].astype(f32))
        normed = (norm * row(GAIN1) + row(SHIFT1)).astype(bf16)
        wide_t_ref[:, at : at + ROW_CHUNK] = jnp.transpose(normed)


def bias_sums(grad_projected_ref, small_ref):
    width = small_ref.shape[1]
    for at, part in ((BIAS_Q, 0), (BIAS_V, 2)):
        values = grad_projected_ref[:, part * width : (part + 1) * width]
        small_ref[at : at + 1, :] = total(values.astype(f32))


def token_rows(at, tokens_ref, params_ref, grad_normed, middle, grad_tokens_ref):
    rows = slice(at, at + ROW_CHUNK)
    gain = params_ref[GAIN1 : GAIN1 + 1, 0 : tokens_ref.shape[1]]
    norm, inverse = normalized(tokens_ref[rows].astype(f32))
    grad_rows = norm_pull(grad_normed, gain, norm, inverse)
    grad_tokens_ref[rows] = (middle + grad_rows).astype(bf16)
    return total(grad_normed * norm), total(grad_normed)


def sum_backward_kernel(
    shards,
    tokens_in_ref,
    segment_ref,
    params_ref,
    attended_t_in_ref,
    lse_ref,
    grad_attended_in_ref,
    small_in_ref,
    projected_in_ref,
    w_qkv_in_ref,
    grad_middle_in_ref,
    grad_out_in_ref,
    grad_fc_in_ref,
    grad_proj_in_ref,
    grad_tokens_ref,
    done_qkv_ref,
    done_out_ref,
    done_fc_ref,
    done_proj_ref,
    own_small_ref,
    mask_ref,
    wide_t_ref,
    normed_t_ref,
    grad_queries_t_ref,
    dots_ref,
    projected_ref,
    grad_projected_ref,
    grad_keys_ref,
    grad_values_ref,
    grad_qkv_ref,
    grad_out_ref,
    grad_fc_ref,
    grad_proj_ref,
    weights_ref,
    tokens_ref,
    attended_t_ref,
    grad_attended_ref,
    *rest,
):
    length, width = tokens_ref.shape
    groups = width // GROUP
    late_blocks = grad_fc_ref.shape[0]
    items = 2 * late_blocks + 1 + groups
    buffers, rest = [rest[SUM_BUFFERS * k :][:SUM_BUFFERS] for k in range(items)], rest[
        SUM_BUFFERS * items :
    ]
    small_ref, parts_ref, core_parts_ref, far_parts_ref, side_parts_ref, line_parts_ref, *rest = rest
    send_sem, recv_sem, load_sem, small_send_sem, small_recv_sem = rest
    place = Place(shards)
    lines = place.lines
    arrays = []
    for number in range(late_blocks):
        arrays += [
            (grad_proj_ref.at[number], done_proj_ref.at[number], grad_proj_in_ref.at[number]),
            (grad_fc_ref.at[number], done_fc_ref.at[number], grad_fc_in_ref.at[number]),
        ]
    arrays.append((grad_out_ref, done_out_ref, grad_out_in_ref))
    arrays += [(grad_qkv_ref.at[g], done_qkv_ref.at[g], None) for g in range(groups)]
    sums = [
        Summed(
            place,
            grad,
            done,
            buffers[k],
            send_sem.at[k],
            recv_sem.at[k],
            source,
            None if source is None else load_sem.at[k],
        )
        for k, (grad, done, source) in enumerate(arrays)
    ]
    runner = Runner(BACKWARD_PLAN, None, sums)
    load_projected = pltpu.make_async_copy(projected_in_ref, projected_ref, load_sem.at[items])
    load_projected.start()
    inputs = [
        pltpu.make_async_copy(source, target, load_sem.at[items + 2 + number])
        for number, (source, target) in enumerate(
            (
                (attended_t_in_ref, attended_t_ref),
                (grad_attended_in_ref, grad_attended_ref),
                (tokens_in_ref, tokens_ref),
            )
        )
    ]
    for copy in inputs:
        copy.start()
    load_weights = pltpu.make_async_copy(w_qkv_in_ref, weights_ref, load_sem.at[items + 1])
    load_weights.start()
    place.meet(
        [place.peer(hop, 0) for hop in range(1, lines)]
        + [place.peer(0, 1), place.across(), place.sibling()]
    )
    runner.do(B0)
    build_mask(segment_ref, mask_ref)
    runner.do(B1)
    for copy in inputs:
        copy.wait()
    dot_rows(attended_t_ref, grad_attended_ref, wide_t_ref, dots_ref)
    runner.do(B2)
    normed_transposed(tokens_ref, params_ref, normed_t_ref)
    small_ref[...] = small_in_ref[...]
    parts_ref[...] = jnp.zeros_like(parts_ref)
    load_projected.wait()
    for g in range(groups):
        wide_t_ref[g * GROUP : (g + 1) * GROUP] = jnp.transpose(
            projected_ref[g, :, GROUP : 2 * GROUP]
        )
    runner.do(B3)

    @pl.loop(0, 2 * groups)
    def _(pair):
        g, odd = pair // 2, pair % 2
        parts = [projected_ref[g, :, block(2 * k + odd, 2 * HEAD)] for k in range(3)]
        attend_backward(
            pair,
            parts + [grad_attended_ref[:, block(pair, 2 * HEAD)]],
            wide_t_ref,
            mask_ref,
            lse_ref,
            dots_ref,
            grad_queries_t_ref,
            grad_keys_ref,
            grad_values_ref,
            lambda number: runner.at_step(pair, number),
        )
        grad_queries = jnp.transpose(grad_queries_t_ref[block(pair, 2 * HEAD), :])
        grad_projected_ref[g, :, block(odd, 2 * HEAD)] = grad_queries
        for k, ref in ((1, grad_keys_ref), (2, grad_values_ref)):
            grad_projected_ref[g, :, block(2 * k + odd, 2 * HEAD)] = ref[...].astype(bf16)

        @pl.when(odd == 1)
        def _():
            grad_group = matmul(normed_t_ref[...], grad_projected_ref[g], NN).astype(bf16)
            grad_qkv_ref[g] = grad_group.reshape(grad_qkv_ref.shape[1:])

    middle_ref = mask_ref.at[:, 0:width]
    load_middle = pltpu.make_async_copy(grad_middle_in_ref, middle_ref, load_sem.at[items])
    load_middle.start()
    for g in range(groups):
        part = slice(g * GROUP, (g + 1) * GROUP)
        for at, k in ((BIAS_Q, 0), (BIAS_V, 2)):
            values = grad_projected_ref[g, :, k * GROUP : (k + 1) * GROUP]
            small_ref[at : at + 1, part] = total(values.astype(f32))
    load_weights.wait()
    load_middle.wait()
    gain_sum = shift_sum = 0.0
    for number, at in enumerate(range(0, length, ROW_CHUNK)):
        runner.do(E0 + number)
        rows = slice(at, at + ROW_CHUNK)
        grad_normed = 0.0
        for g in range(groups):
            weights = weights_ref[g].reshape(width, 3 * GROUP)
            grad_normed = grad_normed + matmul(grad_projected_ref[g, rows], weights, NT)
        gain_part, shift_part = token_rows(
            at, tokens_ref, params_ref, grad_normed, mask_ref[rows, 0:width], grad_tokens_ref
        )
        gain_sum, shift_sum = gain_sum + gain_part, shift_sum + shift_part
    small_ref[GAIN1 : GAIN1 + 1, 0:width] = gain_sum
    small_ref[SHIFT1 : SHIFT1 + 1, 0:width] = shift_sum

    own = width // shards
    for shard in range(shards):
        into = parts_ref.at[shard // 2, shard % 2]
        into[0:8, 0:own] = small_ref[0:8, shard * own : (shard + 1) * own]
        into[8:16, :] = small_ref[8:16, shard * 128 : (shard + 1) * 128]

    def exchange(slot, source, into, peer):
        copy = remote(source, into, small_send_sem.at[slot], small_recv_sem.at[slot], peer)
        copy.start()
        return copy

    line, side = place.line, place.side
    todo = BACKWARD_PLAN.get(END, ())
    portions = [todo[len(todo) * k // 5 : len(todo) * (k + 1) // 5] for k in range(5)]
    copy = exchange(0, parts_ref, core_parts_ref, place.sibling())
    runner.act(portions[0])
    copy.wait()
    parts_ref[...] += core_parts_ref[...]
    copy = exchange(1, parts_ref, far_parts_ref, place.across())
    runner.act(portions[1])
    copy.wait()
    parts_ref[...] += far_parts_ref[...]
    copy = exchange(2, parts_ref.at[:, 1 - side], side_parts_ref, place.peer(0, 1))
    runner.act(portions[2])
    copy.wait()
    parts_ref[:, side] += side_parts_ref[...]
    copies = [
        exchange(
            2 + hop,
            parts_ref.at[flip(line, hop), side],
            line_parts_ref.at[hop - 1],
            place.peer(hop, 0),
        )
        for hop in range(1, lines)
    ]
    runner.act(portions[3] + portions[4])
    for copy in copies:
        copy.wait()
    small = parts_ref[line, side]
    for hop in range(1, lines):
        small = small + line_parts_ref[hop - 1]
    own_small_ref[...] = small
    for item in sums:
        item.drain()


def finish_kernel(
    shards,
    qkv_ref,
    out_ref,
    fc_early_ref,
    fc_last_ref,
    proj_early_ref,
    proj_last_ref,
    small_ref,
    layer_in_ref,
    tokens_in_ref,
    sum_qkv_ref,
    sum_out_ref,
    sum_fc_ref,
    sum_proj_ref,
    layer_out_ref,
    grad_tokens_ref,
    *rest,
):
    *vector_refs, fc_bias_ref, copy_sem = rest
    copies = [
        pltpu.make_async_copy(source, target, copy_sem.at[k])
        for k, (source, target) in enumerate(
            ((layer_in_ref, layer_out_ref), (tokens_in_ref, grad_tokens_ref))
        )
    ]
    for copy in copies:
        copy.start()
    groups, own, _ = qkv_ref.shape
    width = groups * GROUP
    for g in range(groups):
        for part in range(3):
            start = part * width + g * GROUP
            sum_qkv_ref[:, start : start + GROUP] = qkv_ref[
                g, :, part * GROUP : (part + 1) * GROUP
            ].astype(f32)
    sum_out_ref[...] = out_ref[...].astype(f32)
    early = fc_early_ref.shape[0]
    blocks = early + fc_last_ref.shape[0]
    for number in range(blocks):
        fc = fc_early_ref.at[number] if number < early else fc_last_ref.at[number - early]
        proj = proj_early_ref.at[number] if number < early else proj_last_ref.at[number - early]
        for shard in range(shards):
            start = (shard * blocks + number) * 128
            sum_fc_ref[:, start : start + 128] = fc[:, shard * 128 : (shard + 1) * 128].astype(f32)
        sum_proj_ref[number * 128 : (number + 1) * 128] = jnp.transpose(proj[...].astype(f32))
    for at, vector_ref in enumerate(vector_refs):
        vector_ref[...] = small_ref[at, 0:own]
    for number in range(blocks):
        fc_bias_ref[number * 128 : (number + 1) * 128] = small_ref[BIAS_FC + number, :]
    for copy in copies:
        copy.wait()


def kernel_params():
    return pltpu.CompilerParams(vmem_limit_bytes=VMEM_LIMIT)


def run_forward(tokens, segment, params, w_qkv):
    length, width = tokens.shape
    return pl.pallas_call(
        forward_kernel,
        in_specs=[WHOLE] * 4,
        out_specs=(WHOLE,) * 3,
        out_shape=(
            jax.ShapeDtypeStruct((length, 3 * width), bf16),
            jax.ShapeDtypeStruct((width, length), bf16),
            jax.ShapeDtypeStruct((16, length), f32),
        ),
        scratch_shapes=[
            pltpu.VMEM((length, length), f32),
            pltpu.VMEM((length, width), bf16),
            pltpu.VMEM((width, length), bf16),
        ],
        compiler_params=kernel_params(),
        name="forward",
    )(tokens, segment, params, w_qkv)


def run_hidden(attended_t, tokens, cotangent, params, w_out, w_fc, w_proj, piece):
    length, width = tokens.shape
    hidden = w_fc.shape[1]
    shape = jax.ShapeDtypeStruct
    columns = pl.BlockSpec((width, width), lambda step: (0, step))
    return pl.pallas_call(
        hidden_kernel,
        grid=(hidden // width,),
        in_specs=[WHOLE] * 5 + [columns, pl.BlockSpec((width, width), lambda step: (step, 0))],
        out_specs=(
            WHOLE,
            WHOLE,
            WHOLE,
            WHOLE,
            columns,
            pl.BlockSpec((width // piece, width, piece), lambda step: (step, 0, 0)),
            WHOLE,
        ),
        out_shape=(
            shape((length, width), bf16),
            shape((length, width), f32),
            shape((length, width), bf16),
            shape((width, width), bf16),
            shape((width, hidden), bf16),
            shape((hidden // piece, width, piece), bf16),
            shape((16, width), f32),
        ),
        scratch_shapes=[
            pltpu.VMEM((length, width), f32),
            pltpu.VMEM((length, width), bf16),
            pltpu.VMEM((width, length), bf16),
            pltpu.VMEM((width, length), bf16),
            pltpu.VMEM((length, width), f32),
            pltpu.VMEM((length, width), f32),
            pltpu.VMEM((length, width), bf16),
            pltpu.VMEM((length, width), bf16),
        ],
        compiler_params=kernel_params(),
        name="hidden",
    )(attended_t, tokens, cotangent, params, w_out, w_fc, w_proj)


def run_backward(
    tokens, segment, params, w_qkv, projected, attended_t, lse, grad_attended, grad_middle, small
):
    length, width = tokens.shape
    shape = jax.ShapeDtypeStruct
    return pl.pallas_call(
        backward_kernel,
        in_specs=[WHOLE] * 10,
        out_specs=(WHOLE,) * 3,
        out_shape=(
            shape((length, width), bf16),
            shape((width, 3 * width), bf16),
            shape((16, width), f32),
        ),
        scratch_shapes=[
            pltpu.VMEM((length, length), f32),
            pltpu.VMEM((width, length), bf16),
            pltpu.VMEM((width, length), bf16),
            pltpu.VMEM((16, length), f32),
            pltpu.VMEM((length, 3 * width), bf16),
            pltpu.VMEM((length, 2 * HEAD), f32),
            pltpu.VMEM((length, 2 * HEAD), f32),
        ],
        compiler_params=kernel_params(),
        name="backward",
    )(
        tokens,
        segment,
        params,
        w_qkv,
        projected,
        attended_t,
        lse,
        grad_attended,
        grad_middle,
        small,
    )


def link_params(number):
    return pltpu.CompilerParams(
        vmem_limit_bytes=VMEM_LIMIT, collective_id=number, has_side_effects=True
    )


def run_gather_forward(
    shards, span, tokens, segment, own_params, w_qkv, w_out, w_fc, w_proj
):
    length, width = tokens.shape
    own = w_qkv.shape[0]
    groups = width // GROUP
    blocks = GATHERED_EARLY
    items = groups + 1 + 2 * blocks
    shape = jax.ShapeDtypeStruct
    copies = 3 * shards - 3
    dma = pltpu.SemaphoreType.DMA
    return pl.pallas_call(
        partial(gather_forward_kernel, shards),
        in_specs=[WHOLE] * 3 + [HBM] * 4,
        out_specs=(HBM,) + (WHOLE,) * 3 + (HBM,) * 4,
        out_shape=(
            shape((groups, length, 3 * GROUP), bf16),
            shape((width, length), bf16),
            shape((16, length), f32),
            shape((own_params.shape[0], span), f32),
            shape((groups, shards, own, 3 * GROUP), bf16),
            shape((shards, own, width), bf16),
            shape((blocks, shards, own, shards * 128), bf16),
            shape((blocks, shards, 128, width), bf16),
        ),
        scratch_shapes=[
            pltpu.VMEM((length, length), f32),
            pltpu.VMEM((length, width), bf16),
            pltpu.VMEM((width, length), bf16),
            pltpu.VMEM((groups, length, 3 * GROUP), bf16),
            pltpu.VMEM((groups, shards, own, 3 * GROUP), bf16),
            pltpu.VMEM((shards,) + own_params.shape, bf16),
            pltpu.VMEM((groups, own, 3 * GROUP), bf16),
            pltpu.VMEM((blocks, own, shards * 128), bf16),
            pltpu.VMEM((own, width), bf16),
            pltpu.VMEM((blocks * 128, width), bf16),
            dma((items, copies)),
            dma((items, copies)),
            dma((items,)),
            dma((shards - 1,)),
            dma((shards - 1,)),
            dma((groups + blocks + 2,)),
            dma((groups, 2)),
        ],
        compiler_params=link_params(0),
        name="gather_forward",
    )(tokens, segment, own_params, w_qkv, w_out, w_fc, w_proj)


def run_sum_hidden(
    shards, attended_t, tokens, cotangent, params, full_out, full_fc, full_proj, w_fc, w_proj
):
    length, width = tokens.shape
    own, units = w_fc.shape[0], shards * 128
    blocks = w_proj.shape[0] // 128
    lines = shards // 2
    shape = jax.ShapeDtypeStruct
    dma = pltpu.SemaphoreType.DMA
    grads = ((shards, own, units), (shards, width, 128))
    late, early = blocks - full_fc.shape[0], SUMMED_EARLY
    buffers = [
        ref
        for _ in range(early)
        for grad in reversed(grads)
        for ref in sum_buffers(lines, *grad)
    ]
    return pl.pallas_call(
        partial(sum_hidden_kernel, shards),
        in_specs=[HBM] * 3 + [WHOLE] + [HBM] * 5,
        out_specs=(HBM, HBM, WHOLE, WHOLE, HBM, HBM) + (WHOLE,) * 3,
        out_shape=(
            shape((length, width), bf16),
            shape((length, width), f32),
            shape((length, width), bf16),
            shape((shards, own, width), bf16),
            shape((blocks - early,) + grads[0], bf16),
            shape((blocks - early,) + grads[1], bf16),
            shape((early, own, units), bf16),
            shape((early, width, 128), bf16),
            shape(params.shape, f32),
        ),
        scratch_shapes=[
            pltpu.VMEM((length, width), f32),
            pltpu.VMEM((length, width), bf16),
            pltpu.VMEM((width, length), bf16),
            pltpu.VMEM((width, length), bf16),
            pltpu.VMEM((length, width), f32),
            pltpu.VMEM((length, width), f32),
            pltpu.VMEM((length, units), bf16),
            pltpu.VMEM((length, units), bf16),
            pltpu.VMEM((blocks, shards, own, units), bf16),
            pltpu.VMEM((blocks, shards, 128, width), bf16),
            pltpu.VMEM((blocks,) + grads[0], bf16),
            pltpu.VMEM((blocks,) + grads[1], bf16),
            pltpu.VMEM((late, own, units), bf16),
            pltpu.VMEM((width, length), bf16),
            pltpu.VMEM((length, width), bf16),
            pltpu.VMEM((length, width), bf16),
            pltpu.VMEM((shards, own, width), bf16),
            pltpu.VMEM((length, width), bf16),
        ]
        + buffers
        + [
            dma((2 * late, 3 * shards - 3)),
            dma((2 * late, 3 * shards - 3)),
            dma((2 * late,)),
            dma((2 * blocks + 4,)),
        ]
        + sum_sems(lines, 2 * early),
        compiler_params=link_params(1),
        name="sum_hidden",
    )(attended_t, tokens, cotangent, params, full_out, full_fc, full_proj, w_fc, w_proj)


def run_sum_backward(
    shards,
    tokens,
    segment,
    params,
    attended_t,
    lse,
    grad_attended,
    small,
    projected,
    w_qkv,
    grad_middle,
    grad_out,
    grad_fc,
    grad_proj,
):
    length, width = tokens.shape
    shape = jax.ShapeDtypeStruct
    lines, groups = shards // 2, width // GROUP
    own = width // shards
    qkv = (shards, own, 3 * GROUP)
    late_blocks = grad_fc.shape[0]
    grads = [grad_proj.shape[1:], grad_fc.shape[1:]] * late_blocks
    grads += [grad_out.shape] + [qkv] * groups
    buffers = [ref for grad in grads for ref in sum_buffers(lines, *grad)]
    parts = pltpu.VMEM((lines, 2, 16, 128), f32)
    dma = pltpu.SemaphoreType.DMA
    items = len(grads)
    return pl.pallas_call(
        partial(sum_backward_kernel, shards),
        in_specs=[HBM, WHOLE, WHOLE, HBM, WHOLE, HBM, WHOLE] + [HBM] * 6,
        out_specs=(WHOLE,) * 6,
        out_shape=(
            shape((length, width), bf16),
            shape((groups,) + qkv[1:], bf16),
            shape(grad_out.shape[1:], bf16),
            shape((late_blocks,) + grad_fc.shape[2:], bf16),
            shape((late_blocks,) + grad_proj.shape[2:], bf16),
            shape((16, 128), f32),
        ),
        scratch_shapes=[
            pltpu.VMEM((length, length), f32),
            pltpu.VMEM((width, length), bf16),
            pltpu.VMEM((width, length), bf16),
            pltpu.VMEM((width, length), bf16),
            pltpu.VMEM((16, length), f32),
            pltpu.VMEM(projected.shape, bf16),
            pltpu.VMEM(projected.shape, bf16),
            pltpu.VMEM((length, 2 * HEAD), f32),
            pltpu.VMEM((length, 2 * HEAD), f32),
            pltpu.VMEM((groups,) + qkv, bf16),
            pltpu.VMEM(grad_out.shape, bf16),
            pltpu.VMEM(grad_fc.shape, bf16),
            pltpu.VMEM(grad_proj.shape, bf16),
            pltpu.VMEM(w_qkv.shape, bf16),
            pltpu.VMEM((length, width), bf16),
            pltpu.VMEM((width, length), bf16),
            pltpu.VMEM((length, width), bf16),
        ]
        + buffers
        + [pltpu.VMEM(params.shape, f32), parts, parts, parts]
        + [pltpu.VMEM((lines, 16, 128), f32), pltpu.VMEM((lines - 1, 16, 128), f32)]
        + sum_sems(lines, items)
        + [dma((items + 5,)), dma((lines + 2,)), dma((lines + 2,))],
        compiler_params=link_params(2),
        name="sum_backward",
    )(
        tokens,
        segment,
        params,
        attended_t,
        lse,
        grad_attended,
        small,
        projected,
        w_qkv,
        grad_middle,
        grad_out,
        grad_fc,
        grad_proj,
    )


def run_finish(
    shards, qkv, out, fc_early, fc_last, proj_early, proj_last, small, layer_out, grad_tokens
):
    groups, own, _ = qkv.shape
    width = out.shape[1]
    blocks = fc_early.shape[0] + fc_last.shape[0]
    shape = jax.ShapeDtypeStruct
    return pl.pallas_call(
        partial(finish_kernel, shards),
        in_specs=[WHOLE] * 9,
        out_specs=(WHOLE,) * 4 + (HBM,) * 2 + (WHOLE,) * 9,
        out_shape=(
            shape((own, 3 * width), f32),
            shape((own, width), f32),
            shape((own, blocks * shards * 128), f32),
            shape((blocks * 128, width), f32),
            shape(layer_out.shape, bf16),
            shape(grad_tokens.shape, bf16),
        )
        + (shape((own,), f32),) * 8
        + (shape((blocks * 128,), f32),),
        scratch_shapes=[pltpu.SemaphoreType.DMA((2,))],
        compiler_params=kernel_params(),
        name="finish",
    )(qkv, out, fc_early, fc_last, proj_early, proj_last, small, layer_out, grad_tokens)


def by_kernels(
    shards, tokens, segment_ids, vectors, fc_bias, w_qkv, w_out, w_fc, w_proj, cotangent
):
    width, hidden = tokens.shape[1], w_fc.shape[1]
    blocks, units = w_proj.shape[0] // 128, shards * 128
    span = max(width, units)
    rows = jnp.pad(jnp.stack(vectors), ((0, 0), (0, 128 - vectors[0].shape[0])))
    table = jnp.concatenate(
        [rows, jnp.pad(fc_bias.reshape(blocks, 128), ((0, 8 - blocks), (0, 0)))]
    )
    projected, attended_t, lse, params, full_qkv, full_out, full_fc, full_proj = (
        run_gather_forward(shards, span, tokens, segment_ids, table, w_qkv, w_out, w_fc, w_proj)
    )
    (
        layer_out,
        grad_middle,
        grad_attended,
        grad_out,
        grad_fc,
        grad_proj,
        fc_early,
        proj_early,
        small,
    ) = run_sum_hidden(
        shards, attended_t, tokens, cotangent, params, full_out, full_fc, full_proj, w_fc, w_proj
    )
    grad_tokens, done_qkv, done_out, fc_last, proj_last, small = run_sum_backward(
        shards,
        tokens,
        segment_ids,
        params,
        attended_t,
        lse,
        grad_attended,
        small,
        projected,
        full_qkv,
        grad_middle,
        grad_out,
        grad_fc,
        grad_proj,
    )
    sum_qkv, sum_out, sum_fc, sum_proj, layer_out, grad_tokens, *own_vectors = run_finish(
        shards,
        done_qkv,
        done_out,
        fc_early,
        fc_last,
        proj_early,
        proj_last,
        small,
        layer_out,
        grad_tokens,
    )
    pick = lambda at: own_vectors[at]
    return (
        layer_out,
        grad_tokens,
        pick(GAIN1),
        pick(SHIFT1),
        sum_qkv,
        pick(BIAS_Q),
        pick(BIAS_V),
        sum_out,
        pick(BIAS_OUT),
        pick(GAIN2),
        pick(SHIFT2),
        sum_fc,
        pick(BIAS_FC),
        sum_proj,
        pick(BIAS_PROJ),
    )


def on_device(
    replicas,
    shards,
    tokens,
    segment_ids,
    norm1_gain,
    norm1_shift,
    w_qkv,
    q_bias,
    v_bias,
    w_out,
    out_bias,
    norm2_gain,
    norm2_shift,
    w_fc,
    fc_bias,
    w_proj,
    proj_bias,
    cotangent,
):
    width, hidden = tokens.shape[1], w_fc.shape[1]
    vectors = (
        norm1_gain,
        norm1_shift,
        q_bias,
        v_bias,
        out_bias,
        norm2_gain,
        norm2_shift,
        proj_bias,
    )
    own, own_hidden = norm1_gain.shape[0], fc_bias.shape[0]
    if (
        replicas == 4
        and shards & (shards - 1) == 0
        and own % 96 == 0
        and own_hidden == 3 * 128
        and width == 3 * GROUP
    ):
        return by_kernels(
            shards, tokens, segment_ids, vectors, fc_bias, w_qkv, w_out, w_fc, w_proj, cotangent
        )
    me = lax.axis_index("shard")
    mine = (lax.broadcasted_iota(jnp.int32, (1, shards, 1), 1) == me).astype(bf16)
    table = jnp.concatenate(
        [
            (jnp.stack(vectors)[:, None, :] * mine).reshape(8, width),
            (fc_bias[None, None, :] * mine).reshape(hidden // width, width),
        ]
    )
    table = jnp.pad(table, ((0, 16 - table.shape[0]), (0, 0)))
    gather = partial(lax.all_gather, axis_name="shard", axis=0, tiled=True)
    params = lax.psum(table.astype(f32), "shard")
    full_qkv, full_out, full_fc, full_proj = (gather(w) for w in (w_qkv, w_out, w_fc, w_proj))
    projected, attended_t, lse = run_forward(tokens, segment_ids, params, full_qkv)
    (
        layer_out,
        grad_middle,
        grad_attended,
        grad_w_out,
        grad_w_fc,
        grad_w_proj_t,
        small,
    ) = run_hidden(attended_t, tokens, cotangent, params, full_out, full_fc, full_proj, width)
    grad_tokens, grad_w_qkv, small = run_backward(
        tokens,
        segment_ids,
        params,
        full_qkv,
        projected,
        attended_t,
        lse,
        grad_attended,
        grad_middle,
        small,
    )

    def reduced(grad):
        own_sum = lax.psum_scatter(grad.astype(f32), "shard", scatter_dimension=0, tiled=True)
        return lax.psum(own_sum.astype(bf16), "rep").astype(f32)

    sum_proj = reduced(grad_w_proj_t.transpose(0, 2, 1).reshape(hidden, width))
    sum_fc, sum_out, sum_qkv = reduced(grad_w_fc), reduced(grad_w_out), reduced(grad_w_qkv)
    small = lax.psum(small, ("rep", "shard"))
    mine = lax.dynamic_slice_in_dim(small[:8], me * own, own, 1)
    hidden_rows = small[BIAS_FC : BIAS_FC + hidden // width].reshape(-1)
    mine_fc = lax.dynamic_slice_in_dim(hidden_rows, me * own_hidden, own_hidden, 0)
    return (
        layer_out,
        grad_tokens,
        mine[GAIN1],
        mine[SHIFT1],
        sum_qkv,
        mine[BIAS_Q],
        mine[BIAS_V],
        sum_out,
        mine[BIAS_OUT],
        mine[GAIN2],
        mine[SHIFT2],
        sum_fc,
        mine_fc,
        sum_proj,
        mine[BIAS_PROJ],
    )


def solution(mesh):
    rows, own, own_rows = P(("rep", "shard"), None), P("shard"), P("shard", None)
    in_specs = (
        rows,
        rows,
        own,
        own,
        own_rows,
        own,
        own,
        own_rows,
        own,
        own,
        own,
        own_rows,
        own,
        own_rows,
        own,
        rows,
    )
    out_specs = (
        rows,
        rows,
        own,
        own,
        own_rows,
        own,
        own,
        own_rows,
        own,
        own,
        own,
        own_rows,
        own,
        own_rows,
        own,
    )
    sizes = mesh.shape["rep"], mesh.shape["shard"]
    return jax.shard_map(
        partial(on_device, *sizes), mesh=mesh, in_specs=in_specs, out_specs=out_specs, check_vma=False
    )
```

```python
from functools import partial

import jax
import jax.numpy as jnp
from jax import lax
from jax.experimental import pallas as pl
from jax.experimental.pallas import tpu as pltpu
from jax.sharding import PartitionSpec as P

HEAD = 64
EPSILON = 1e-05
QUERY_BLOCK = 256
ROW_CHUNK = 256
MASKED = -1e30
GELU_SCALE = 0.7978845608028654
GELU_CUBE = 0.044715
VMEM_LIMIT = 62 << 20
NN = (((1,), (0,)), ((), ()))
NT = (((1,), (1,)), ((), ()))
f32 = jnp.float32
bf16 = jnp.bfloat16
WHOLE = pl.BlockSpec(memory_space=pltpu.VMEM)

GAIN1, SHIFT1, BIAS_Q, BIAS_V, BIAS_OUT, GAIN2, SHIFT2, BIAS_PROJ, BIAS_FC = range(9)


def matmul(left, right, dims):
    return lax.dot_general(left, right, dims, preferred_element_type=f32)


def normalized(values):
    centred = values - jnp.mean(values, axis=-1, keepdims=True)
    inverse = lax.rsqrt(jnp.mean(centred * centred, axis=-1, keepdims=True) + EPSILON)
    return centred * inverse, inverse


def norm_pull(grad_normed, gain_row, norm, inverse):
    scaled = grad_normed * gain_row
    return inverse * (
        scaled
        - jnp.mean(scaled, axis=-1, keepdims=True)
        - norm * jnp.mean(scaled * norm, axis=-1, keepdims=True)
    )


def chunk(number):
    return pl.ds(pl.multiple_of(number * ROW_CHUNK, ROW_CHUNK), ROW_CHUNK)


def total(values):
    return jnp.sum(values, axis=0, keepdims=True)


def block(index, size):
    return pl.ds(pl.multiple_of(index * size, size), size)


def build_mask(segment_ref, mask_ref):
    length = segment_ref.shape[1]
    query_seg = segment_ref[...].astype(f32)
    key_seg = jnp.transpose(jnp.broadcast_to(query_seg, (8, length)))[:, 0:1]
    for start in range(0, length, QUERY_BLOCK):
        stop = start + QUERY_BLOCK
        key_at = lax.broadcasted_iota(jnp.int32, (stop, QUERY_BLOCK), 0)
        query_at = lax.broadcasted_iota(jnp.int32, (stop, QUERY_BLOCK), 1) + start
        allowed = (key_seg[0:stop] == query_seg[:, start:stop]) & (key_at <= query_at)
        mask_ref[0:stop, start:stop] = jnp.where(allowed, 0.0, MASKED)


def half_lanes(which):
    lane = lax.broadcasted_iota(jnp.int32, (1, 2 * HEAD), 1)
    return (lane < HEAD) if which == 0 else (lane >= HEAD)


def keep_half(values, which):
    return jnp.where(half_lanes(which), values, jnp.zeros_like(values))


def attend_forward(
    pair, queries, keys, values_t_ref, mask_ref, attended_t_ref, lse_ref, tick=lambda number: None
):
    length = keys.shape[0]
    queries = queries * bf16(HEAD**-0.5)
    for which in range(2):
        tick(which)
        head_queries = keep_half(queries, which)
        rows = block(2 * pair + which, HEAD)
        values_t = values_t_ref[rows, :]
        for start in range(0, length, QUERY_BLOCK):
            stop = start + QUERY_BLOCK
            scores = matmul(keys[0:stop], head_queries[start:stop], NT)
            scores = scores + mask_ref[0:stop, start:stop]
            top = jnp.max(scores, axis=0, keepdims=True)
            terms = jnp.exp(scores - top)
            sums = jnp.sum(terms, axis=0, keepdims=True)
            mixed = matmul(values_t[:, 0:stop], terms.astype(bf16), NN)
            attended_t_ref[rows, start:stop] = (mixed * (1.0 / sums)).astype(bf16)
            lse_ref[pl.ds(2 * pair + which, 1), start:stop] = top + jnp.log(sums)


def attend_backward(
    pair,
    operands,
    keys_t_ref,
    mask_ref,
    lse_ref,
    dots_ref,
    grad_queries_t_ref,
    grad_keys_ref,
    grad_values_ref,
    tick=lambda number: None,
):
    queries, keys, values, grads = operands
    length, scale_by = keys.shape[0], HEAD**-0.5
    queries = queries * bf16(scale_by)
    for number, start in enumerate(reversed(range(0, length, QUERY_BLOCK))):
        tick(number)
        stop = start + QUERY_BLOCK
        grad_keys = grad_values = 0.0
        for which in range(2):
            head = pl.ds(2 * pair + which, 1)
            rows = block(2 * pair + which, HEAD)
            query_rows = keep_half(queries[start:stop], which)
            grad_rows = keep_half(grads[start:stop], which)
            scores = matmul(keys[0:stop], query_rows, NT)
            probs = jnp.exp(scores + mask_ref[0:stop, start:stop] - lse_ref[head, start:stop])
            grad_probs = matmul(values[0:stop], grad_rows, NT)
            grad_scores = (probs * (grad_probs - dots_ref[head, start:stop])).astype(bf16)
            grad_values = grad_values + matmul(probs.astype(bf16), grad_rows, NN)
            grad_keys = grad_keys + matmul(grad_scores, query_rows, NN)
            grad_queries_t_ref[rows, start:stop] = (
                matmul(keys_t_ref[rows, 0:stop], grad_scores, NN) * scale_by
            ).astype(bf16)
        if stop == length:
            grad_keys_ref[...] = grad_keys
            grad_values_ref[...] = grad_values
        else:
            grad_keys_ref[0:stop] += grad_keys
            grad_values_ref[0:stop] += grad_values


MESH = pl.DeviceIdType.MESH
HBM = pl.BlockSpec(memory_space=pl.ANY)


def flip(value, bits):
    bit = 1
    while bit <= bits:
        if bits & bit:
            value = value + bit - 2 * bit * ((value // bit) % 2)
        bit *= 2
    return value


class Place:
    def __init__(self, shards):
        self.lines = shards // 2
        self.rep, self.me = lax.axis_index("rep"), lax.axis_index("shard")
        self.far, self.core = self.rep // 2, self.rep % 2
        self.line, self.side = self.me // 2, self.me % 2

    def shard(self, hop, turn):
        return flip(self.line, hop) * 2 + flip(self.side, turn)

    def peer(self, hop, turn):
        return (self.rep, self.shard(hop, turn))

    def across(self):
        return ((1 - self.far) * 2 + self.core, self.me)

    def sibling(self):
        return (self.far * 2 + 1 - self.core, self.me)

    def others(self):
        return [(h, t) for h in range(self.lines) for t in range(2) if h or t]

    def meet(self, peers):
        barrier = pltpu.get_barrier_semaphore()
        for peer in peers:
            pl.semaphore_signal(barrier, inc=1, device_id=peer, device_id_type=MESH)
        pl.semaphore_wait(barrier, len(peers))


def aligned(start, size):
    return pl.ds(pl.multiple_of(start, 16), size)


def remote(src, dst, send, recv, peer):
    return pltpu.make_async_remote_copy(
        src_ref=src,
        dst_ref=dst,
        send_sem=send,
        recv_sem=recv,
        device_id=peer,
        device_id_type=MESH,
    )


def cut(count):
    half = count // 2
    return half // 3 // 16 * 16, half


class Gather:
    def __init__(self, place, own, full, send, recv, local):
        self.place, self.own, self.full = place, own, full
        self.send, self.recv, self.local = send, recv, local
        self.hops = range(1, place.lines)

    def rows(self, at, kind, far, core):
        edge, half = cut(self.own[at].shape[0])
        if kind == "wide":
            return aligned(core * half + far * edge, half - edge)
        if kind == "edge":
            return aligned(core * half + far * (half - edge), edge)
        return aligned(core * half, half)

    def copy(self, at, stage, hop, turn, arriving=False):
        place, lines = self.place, self.place.lines
        number = hop * 2 + turn
        far, core = place.far, place.core
        if stage == "line":
            slot, peer, kind = hop - 1, place.peer(hop, 0), "wide"
            shard = place.shard(hop if arriving else 0, 0)
        elif stage == "side":
            slot, peer, kind = lines - 1 + hop, place.peer(0, 1), "wide"
            shard = place.shard(hop, 1 if arriving else 0)
        elif stage == "far":
            slot, peer, kind = 2 * lines - 1 + number - 1, place.across(), "edge"
            shard = place.shard(hop, turn)
            far = 1 - far if arriving else far
        else:
            slot, peer, kind = 4 * lines - 2 + number - 1, place.sibling(), "half"
            shard = place.shard(hop, turn)
            core = 1 - core if arriving else core
        rows = self.rows(at, kind, far, core)
        target = self.full[at].at[shard, rows]
        mine = not arriving and (stage == "line" or (stage == "side" and hop == 0))
        source = self.own[at].at[rows] if mine else target
        return remote(source, target, self.send.at[at, slot], self.recv.at[at, slot], peer)

    def start(self, at, stage, hop, turn=0):
        self.copy(at, stage, hop, turn).start()

    def got(self, at, stage, hop, turn=0):
        self.copy(at, stage, hop, turn, arriving=True).wait_recv()

    def keep(self, at):
        return pltpu.make_async_copy(
            self.own[at], self.full[at].at[self.place.me], self.local.at[at]
        )

    def own_side(self, at):
        self.start(at, "side", 0)

    def first(self, at, hop):
        self.start(at, "line", hop)

    def line(self, at, hop):
        self.got(at, "line", hop)
        self.start(at, "side", hop)
        self.start(at, "far", hop, 0)

    def side(self, at, hop):
        self.got(at, "side", hop)
        self.start(at, "far", hop, 1)

    def far(self, at, hop, turn):
        self.got(at, "far", hop, turn)
        self.start(at, "core", hop, turn)

    def last(self, at):
        for hop, turn in self.place.others():
            self.got(at, "core", hop, turn)
        self.keep(at).wait()

    def drain(self, at):
        for hop in self.hops:
            self.copy(at, "line", hop, 0).wait_send()
        for hop in range(self.place.lines):
            self.copy(at, "side", hop, 0).wait_send()
        for hop, turn in self.place.others():
            self.copy(at, "far", hop, turn).wait_send()
            self.copy(at, "core", hop, turn).wait_send()


def add_into(into, other):
    into[...] = (into[...].astype(f32) + other[...].astype(f32)).astype(bf16)


class Summed:
    def __init__(self, place, grad, done, buffers, send, recv, source=None, load_sem=None):
        self.place, self.grad, self.done = place, grad, done
        self.send_sem, self.recv_sem = send, recv
        self.source = grad if source is None else source
        self.load_sem = load_sem
        (
            self.from_core,
            self.from_far,
            self.from_side,
            self.from_me,
            self.from_line,
            self.from_back,
        ) = buffers
        self.edge_size, self.half = cut(grad.shape[1])
        self.hops = range(1, place.lines)

    def rows(self, kind, far=None, core=None):
        far = self.place.far if far is None else far
        core = self.place.core if core is None else core
        edge, half = self.edge_size, self.half
        if kind == "wide":
            return aligned(core * half + far * edge, half - edge)
        if kind == "edge":
            return aligned(core * half + far * (half - edge), edge)
        return aligned(core * half, half)

    def pair_of(self, hop):
        return pl.ds(2 * flip(self.place.line, hop), 2)

    def copy(self, stage, hop=0):
        place, lines, grad = self.place, self.place.lines, self.grad
        if stage == "core":
            slot, peer = 0, place.sibling()
            pair = self.source.at[:, self.rows("half", core=1 - place.core)], self.from_core
        elif stage == "far":
            slot, peer = hop, place.across()
            pair = (
                grad.at[self.pair_of(hop), self.rows("edge", far=1 - place.far)],
                self.from_far.at[hop - 1],
            )
        elif stage == "side":
            slot, peer = lines + hop, place.peer(0, 1)
            source = grad.at[place.shard(hop, 1), self.rows("wide" if hop else "half")]
            pair = source, self.from_side.at[hop - 1] if hop else self.from_me
        elif stage == "line":
            slot, peer = 2 * lines + hop - 1, place.peer(hop, 0)
            pair = grad.at[place.shard(hop, 0), self.rows("wide")], self.from_line.at[hop - 1]
        elif stage == "back":
            slot, peer = 3 * lines - 1, place.across()
            pair = grad.at[place.me, self.rows("half")], self.from_back
        else:
            slot, peer = 3 * lines, place.sibling()
            mine = self.done.at[self.rows("half")]
            pair = mine, mine
        return remote(*pair, self.send_sem.at[slot], self.recv_sem.at[slot], peer)

    def load(self):
        rows = self.rows("half")
        return pltpu.make_async_copy(
            self.source.at[:, rows], self.grad.at[:, rows], self.load_sem
        )

    def begin(self):
        self.copy("core").start()
        if self.load_sem is not None:
            self.load().start()

    def core(self):
        self.copy("core").wait_recv()
        if self.load_sem is not None:
            self.load().wait()
        for shard in range(2 * self.place.lines):
            add_into(self.grad.at[shard, self.rows("half")], self.from_core.at[shard])

    def me0(self):
        self.copy("side", 0).start()

    def send(self, hop):
        self.copy("far", hop).start()

    def far(self, hop):
        self.copy("far", hop).wait_recv()
        add_into(self.grad.at[self.pair_of(hop), self.rows("edge")], self.from_far.at[hop - 1])
        self.copy("side", hop).start()

    def side(self, hop):
        self.copy("side", hop).wait_recv()
        mine = self.grad.at[self.place.shard(hop, 0), self.rows("wide")]
        add_into(mine, self.from_side.at[hop - 1])
        self.copy("line", hop).start()

    def me(self):
        self.copy("side", 0).wait_recv()
        add_into(self.grad.at[self.place.me, self.rows("half")], self.from_me)

    def lines(self):
        mine = self.grad.at[self.place.me, self.rows("wide")]
        sums = mine[...].astype(f32)
        for hop in self.hops:
            self.copy("line", hop).wait_recv()
            sums = sums + self.from_line[hop - 1].astype(f32)
        mine[...] = sums.astype(bf16)
        self.copy("back").start()

    def back(self):
        self.copy("back").wait_recv()
        mine = self.grad[self.place.me, self.rows("half")].astype(f32)
        self.done[self.rows("half")] = (mine + self.from_back[...].astype(f32)).astype(bf16)
        self.copy("pair").start()

    def finish(self):
        other = self.done.at[self.rows("half", core=1 - self.place.core)]
        slot = 3 * self.place.lines
        remote(
            other, other, self.send_sem.at[slot], self.recv_sem.at[slot], self.place.sibling()
        ).wait_recv()

    def drain(self):
        self.copy("core").wait_send()
        for hop in self.hops:
            self.copy("far", hop).wait_send()
            self.copy("line", hop).wait_send()
        for hop in range(self.place.lines):
            self.copy("side", hop).wait_send()
        self.copy("back").wait_send()
        self.copy("pair").wait_send()


SUM_BUFFERS = 6


def sum_buffers(lines, shards, rows, columns):
    edge, half = cut(rows)
    return [
        pltpu.VMEM((shards, half, columns), bf16),
        pltpu.VMEM((lines - 1, 2, edge, columns), bf16),
        pltpu.VMEM((lines - 1, half - edge, columns), bf16),
        pltpu.VMEM((half, columns), bf16),
        pltpu.VMEM((lines - 1, half - edge, columns), bf16),
        pltpu.VMEM((half, columns), bf16),
    ]


def sum_sems(lines, items):
    return [pltpu.SemaphoreType.DMA((items, 3 * lines + 1))] * 2


def first_norm(tokens_ref, params_ref, normed_ref):
    length, width = tokens_ref.shape
    row = lambda at: params_ref[at : at + 1, 0:width]

    @pl.loop(0, length // ROW_CHUNK)
    def _(number):
        norm, _ = normalized(tokens_ref[chunk(number)].astype(f32))
        normed_ref[chunk(number)] = (norm * row(GAIN1) + row(SHIFT1)).astype(bf16)


def forward_kernel(
    tokens_ref,
    segment_ref,
    params_ref,
    w_qkv_ref,
    projected_ref,
    attended_t_ref,
    lse_ref,
    mask_ref,
    normed_ref,
    values_t_ref,
):
    length, width = tokens_ref.shape
    pairs = width // (2 * HEAD)
    row = lambda at: params_ref[at : at + 1, 0:width]
    first_norm(tokens_ref, params_ref, normed_ref)
    for part, bias in enumerate((row(BIAS_Q), 0.0, row(BIAS_V))):
        columns = slice(part * width, (part + 1) * width)
        projected_ref[:, columns] = (
            matmul(normed_ref[...], w_qkv_ref[:, columns], NN) + bias
        ).astype(bf16)
    values_t_ref[...] = jnp.transpose(projected_ref[:, 2 * width :])
    build_mask(segment_ref, mask_ref)

    @pl.loop(0, pairs)
    def _(pair):
        attend_forward(
            pair,
            projected_ref[:, block(pair, 2 * HEAD)],
            projected_ref[:, block(pairs + pair, 2 * HEAD)],
            values_t_ref,
            mask_ref,
            attended_t_ref,
            lse_ref,
        )


GROUP = 4 * HEAD
GATHERED_EARLY = 1
SUMMED_EARLY = 1


(
    OWN,
    FIRST,
    LINE,
    SIDE,
    FAR,
    LAST,
    BEGIN_SUM,
    CORE_SUM,
    ME0_SUM,
    SEND_SUM,
    FAR_SUM,
    SIDE_SUM,
    ME_SUM,
    LINES_SUM,
    BACK_SUM,
    FINISH_SUM,
) = range(16)
P0, P1, P2, H0, H1, H2, H3, E0, E1, E2, E3, B0, B1, B2, B3, NEED, END = range(100, 117)

FORWARD_PLAN = {P0: [(OWN, 0), (FIRST, 0, 1)],
 P1: [(FIRST, 0, 3), (OWN, 1)],
 P2: [(FIRST, 0, 2), (LINE, 0, 1), (SIDE, 0, 0)],
 END: [(LAST, 5)],
 NEED: {0: [(FIRST, 1, 1), (SIDE, 1, 0), (OWN, 2), (OWN, 3), (FIRST, 1, 3), (LINE, 0, 3), (FIRST, 1, 2),
            (FAR, 0, 1, 0), (FAR, 0, 0, 1), (FAR, 1, 0, 1), (OWN, 4), (SIDE, 0, 1), (FAR, 0, 3, 0),
            (FIRST, 2, 1), (LINE, 1, 1), (SIDE, 2, 0), (SIDE, 3, 0), (LINE, 0, 2), (FAR, 0, 1, 1),
            (FIRST, 2, 3), (SIDE, 0, 3), (FIRST, 2, 2), (OWN, 5), (FAR, 1, 1, 0), (FAR, 2, 0, 1),
            (LINE, 1, 3), (SIDE, 4, 0), (FIRST, 3, 1), (FAR, 3, 0, 1), (FAR, 0, 2, 0), (SIDE, 1, 1),
            (FAR, 0, 3, 1), (LINE, 1, 2), (FIRST, 3, 3), (SIDE, 0, 2), (LINE, 2, 1), (FIRST, 3, 2),
            (FAR, 1, 3, 0), (FAR, 4, 0, 1), (SIDE, 5, 0), (FAR, 1, 1, 1), (SIDE, 1, 3), (LINE, 2, 3),
            (FAR, 1, 2, 0), (FIRST, 4, 1), (LINE, 2, 2), (FAR, 0, 2, 1), (FAR, 2, 1, 0), (SIDE, 1, 2),
            (LINE, 3, 1), (SIDE, 2, 1), (FIRST, 4, 3), (FAR, 5, 0, 1), (LAST, 0)]},
 0: {0: [(FIRST, 4, 2)],
     1: [(LAST, 1), (LINE, 4, 1), (FIRST, 5, 3)],
     2: [(FAR, 2, 2, 1), (FAR, 2, 3, 1), (SIDE, 3, 2), (SIDE, 3, 3), (FAR, 3, 2, 0), (FAR, 3, 3, 0),
         (FAR, 3, 1, 1), (LINE, 4, 2), (SIDE, 4, 1), (FAR, 4, 1, 0), (FAR, 4, 3, 0)],
     3: [(SIDE, 4, 2), (LINE, 5, 2), (FAR, 3, 2, 1)],
     4: [(LAST, 3), (FAR, 4, 2, 1), (SIDE, 5, 2), (FAR, 5, 2, 0), (FAR, 5, 3, 0), (FAR, 5, 1, 1)],
     5: [(LAST, 4), (FAR, 5, 2, 1)]},
 1: {0: [(FAR, 1, 2, 1), (FAR, 1, 3, 1), (SIDE, 2, 2), (SIDE, 2, 3), (FAR, 2, 2, 0), (FAR, 2, 3, 0),
         (FAR, 2, 1, 1), (LINE, 3, 2), (SIDE, 3, 1), (FAR, 3, 1, 0), (LINE, 3, 3), (FIRST, 5, 1)],
     1: [(LINE, 4, 3), (FIRST, 5, 2)],
     2: [(SIDE, 4, 3), (LAST, 2), (LINE, 5, 1)],
     3: [(FAR, 3, 3, 1), (FAR, 4, 2, 0), (FAR, 4, 1, 1), (FAR, 4, 3, 1), (LINE, 5, 3), (FAR, 5, 1, 0),
         (SIDE, 5, 1)],
     4: [(SIDE, 5, 3)],
     5: [(FAR, 5, 3, 1)]}}

HIDDEN_PLAN = {H0: [(OWN, 0), (FIRST, 0, 1), (FIRST, 0, 3)],
 H1: [(FIRST, 0, 2), (OWN, 1)],
 H2: [(LINE, 0, 1), (SIDE, 0, 0), (FIRST, 1, 1)],
 H3: [(FIRST, 1, 3), (OWN, 2)],
 E0: [(FINISH_SUM, 0)],
 E3: [(BACK_SUM, 1)],
 END: [(FINISH_SUM, 1)],
 1: {0: [(LINE, 0, 3), (FAR, 0, 1, 0), (FIRST, 1, 2), (SIDE, 1, 0)],
     1: [(SIDE, 2, 2), (FAR, 2, 2, 0), (LINE, 3, 3), (SEND_SUM, 1, 3)]},
 2: {0: [(LINE, 0, 2), (SIDE, 0, 1), (FAR, 0, 0, 1)],
     1: [(LINE, 3, 2), (SIDE, 3, 1)],
     2: [(LINES_SUM, 0), (SIDE_SUM, 1, 2), (SIDE_SUM, 1, 1)]},
 3: {0: [(FAR, 0, 3, 0), (LINE, 1, 1), (FIRST, 2, 1), (SIDE, 2, 0)],
     1: [(FAR, 2, 2, 1), (FAR, 2, 3, 1), (FAR, 3, 1, 0), (FAR_SUM, 0, 2), (SIDE_SUM, 0, 3),
         (SEND_SUM, 1, 2)]},
 4: {0: [(SIDE, 0, 3), (FAR, 0, 2, 0), (FAR, 1, 0, 1), (FIRST, 2, 3), (OWN, 3)],
     1: [(SIDE, 3, 3), (FAR, 3, 3, 0), (FAR_SUM, 0, 1), (SEND_SUM, 1, 1)]},
 5: {0: [(SIDE, 0, 2), (FAR, 0, 1, 1), (FAR, 1, 1, 0), (FIRST, 2, 2), (BEGIN_SUM, 0)],
     1: [(LAST, 2), (SIDE, 3, 2), (FAR, 3, 2, 0), (FAR, 3, 1, 1), (ME0_SUM, 1)]},
 6: {0: [(LINE, 1, 3), (SIDE, 1, 1), (FAR, 2, 0, 1), (FIRST, 3, 1), (BEGIN_SUM, 1)],
     1: [(SIDE_SUM, 0, 2), (FAR_SUM, 1, 3)],
     2: [(BACK_SUM, 0)]},
 7: {0: [(FAR, 0, 3, 1), (LINE, 1, 2), (SIDE, 3, 0)],
     1: [(FAR, 3, 3, 1), (SIDE_SUM, 0, 1), (FAR_SUM, 1, 2)],
     2: [(LINES_SUM, 1)]},
 NEED: {1: [(FAR, 0, 2, 1), (FAR, 1, 3, 0), (FAR, 1, 1, 1), (LINE, 2, 1), (FIRST, 3, 3), (CORE_SUM, 0),
            (SEND_SUM, 0, 3), (CORE_SUM, 1), (SIDE, 1, 3), (FAR, 1, 2, 0), (ME0_SUM, 0), (LAST, 0),
            (FAR, 3, 0, 1), (SEND_SUM, 0, 2), (SIDE, 1, 2), (FAR, 2, 1, 0), (FIRST, 3, 2), (LINE, 2, 3),
            (SIDE, 2, 1), (FAR, 1, 3, 1), (LINE, 2, 2), (SEND_SUM, 0, 1), (ME_SUM, 0), (LINE, 3, 1),
            (FAR, 1, 2, 1), (SIDE, 2, 3), (FAR, 2, 3, 0), (FAR_SUM, 0, 3), (LAST, 1), (FAR, 2, 1, 1)],
        2: [(FAR, 3, 2, 1), (FAR_SUM, 1, 1), (ME_SUM, 1), (SIDE_SUM, 1, 3), (LAST, 3)]}}

BACKWARD_PLAN = {B0: [(BEGIN_SUM, 0), (BEGIN_SUM, 1), (BEGIN_SUM, 2), (BEGIN_SUM, 3), (BEGIN_SUM, 4)],
 B2: [(CORE_SUM, 0), (ME0_SUM, 0), (SEND_SUM, 0, 3), (SEND_SUM, 0, 2)],
 B3: [(SEND_SUM, 0, 1), (CORE_SUM, 1), (ME0_SUM, 1)],
 E0: [(SIDE_SUM, 4, 1), (FAR_SUM, 6, 3), (FAR_SUM, 6, 2), (BEGIN_SUM, 7)],
 E1: [(BACK_SUM, 2), (SIDE_SUM, 5, 3), (FAR_SUM, 6, 1)],
 E2: [(FINISH_SUM, 2), (LINES_SUM, 3), (SIDE_SUM, 5, 2), (ME_SUM, 6), (CORE_SUM, 7), (ME0_SUM, 7),
      (SEND_SUM, 7, 3)],
 E3: [(SIDE_SUM, 5, 1), (SEND_SUM, 7, 2)],
 END: [(SIDE_SUM, 6, 3), (SEND_SUM, 7, 1), (BACK_SUM, 3), (ME_SUM, 7), (LINES_SUM, 4), (SIDE_SUM, 6, 2),
       (FAR_SUM, 7, 3), (FINISH_SUM, 3), (FAR_SUM, 7, 2), (SIDE_SUM, 6, 1), (FAR_SUM, 7, 1), (SIDE_SUM, 7, 3),
       (BACK_SUM, 4), (SIDE_SUM, 7, 2), (LINES_SUM, 5), (FINISH_SUM, 4), (SIDE_SUM, 7, 1), (BACK_SUM, 5),
       (FINISH_SUM, 5), (LINES_SUM, 6), (LINES_SUM, 7), (BACK_SUM, 6), (FINISH_SUM, 6), (BACK_SUM, 7),
       (FINISH_SUM, 7)],
 1: {0: [(FAR_SUM, 0, 3), (SEND_SUM, 1, 3), (CORE_SUM, 2), (ME_SUM, 0), (SEND_SUM, 1, 2), (ME0_SUM, 2),
         (CORE_SUM, 3)],
     1: [(FAR_SUM, 0, 1), (FAR_SUM, 1, 3), (SEND_SUM, 2, 2)],
     2: [(SIDE_SUM, 1, 3), (SIDE_SUM, 1, 2), (FAR_SUM, 2, 2), (SEND_SUM, 3, 1), (SEND_SUM, 4, 3)],
     3: [(SIDE_SUM, 2, 3), (FAR_SUM, 3, 3), (SEND_SUM, 4, 1)],
     4: [(FINISH_SUM, 0), (LINES_SUM, 1), (SIDE_SUM, 3, 3), (FAR_SUM, 4, 3), (FAR_SUM, 4, 2)],
     5: [(BACK_SUM, 1), (SIDE_SUM, 3, 1), (FAR_SUM, 5, 3), (FAR_SUM, 5, 2)]},
 2: {0: [(SEND_SUM, 1, 1), (CORE_SUM, 4), (ME_SUM, 1), (FAR_SUM, 0, 2)],
     1: [(FAR_SUM, 1, 2), (SEND_SUM, 2, 1), (ME_SUM, 2)],
     2: [(FAR_SUM, 2, 1), (SEND_SUM, 4, 2), (CORE_SUM, 5), (SIDE_SUM, 1, 1)],
     3: [(FAR_SUM, 3, 2), (SEND_SUM, 5, 3)],
     4: [(FAR_SUM, 4, 1), (CORE_SUM, 6), (SEND_SUM, 6, 3), (SEND_SUM, 6, 2), (SIDE_SUM, 3, 2)],
     5: [(FINISH_SUM, 1), (LINES_SUM, 2), (SIDE_SUM, 4, 3), (FAR_SUM, 5, 1)]},
 3: {0: [(SEND_SUM, 2, 3)],
     1: [(SIDE_SUM, 0, 2), (SEND_SUM, 3, 3)],
     2: [(LINES_SUM, 0), (ME0_SUM, 3)],
     3: [(SIDE_SUM, 2, 2), (FAR_SUM, 3, 1), (SEND_SUM, 5, 2)],
     4: [(ME_SUM, 4), (ME0_SUM, 5), (SEND_SUM, 6, 1)],
     5: [(ME_SUM, 5), (SIDE_SUM, 4, 2), (ME0_SUM, 6)]},
 0: {1: [(SIDE_SUM, 0, 3)],
     2: [(SIDE_SUM, 0, 1), (FAR_SUM, 1, 1), (FAR_SUM, 2, 3), (SEND_SUM, 3, 2), (BEGIN_SUM, 5)],
     4: [(BACK_SUM, 0), (SIDE_SUM, 2, 1), (ME_SUM, 3), (ME0_SUM, 4), (SEND_SUM, 5, 1), (BEGIN_SUM, 6)]}}


class Runner:
    def __init__(self, plan, gather, sums):
        self.plan, self.gather, self.sums = plan, gather, sums

    def act(self, events):
        gather = self.gather
        for what, item, *where in events:
            if what >= BEGIN_SUM:
                one = self.sums[item]
                acts = (
                    one.begin,
                    one.core,
                    one.me0,
                    one.send,
                    one.far,
                    one.side,
                    one.me,
                    one.lines,
                    one.back,
                    one.finish,
                )
                acts[what - BEGIN_SUM](*where)
            else:
                acts = (
                    gather.own_side,
                    gather.first,
                    gather.line,
                    gather.side,
                    gather.far,
                    gather.last,
                )
                acts[what](item, *where)

    def do(self, key):
        self.act(self.plan.get(key, ()))

    def at_step(self, step, key):
        self.on(step, self.plan.get(key, {}))

    def on(self, step, table):
        for number, events in table.items():

            @pl.when(step == number)
            def _(events=events):
                self.act(events)


def gather_forward_kernel(
    shards,
    tokens_ref,
    segment_ref,
    own_params_ref,
    own_qkv_ref,
    own_out_ref,
    own_fc_ref,
    own_proj_ref,
    projected_ref,
    attended_t_ref,
    lse_ref,
    params_ref,
    full_qkv_ref,
    full_out_ref,
    full_fc_ref,
    full_proj_ref,
    mask_ref,
    normed_ref,
    values_t_ref,
    held_ref,
    weights_ref,
    tables_ref,
    group_ref,
    own_block_ref,
    own_rows_ref,
    own_units_ref,
    send_sem,
    recv_sem,
    local_sem,
    params_send_sem,
    params_recv_sem,
    load_sem,
    out_sem,
):
    length, width = tokens_ref.shape
    groups = width // GROUP
    blocks = full_fc_ref.shape[0]
    place = Place(shards)
    others = place.others()
    own = [group_ref.at[g] for g in range(groups)] + [own_rows_ref]
    full = [weights_ref.at[g] for g in range(groups)] + [full_out_ref]
    for number in range(blocks):
        own += [own_block_ref.at[number], own_units_ref.at[number * 128 : number * 128 + 128]]
        full += [full_fc_ref.at[number], full_proj_ref.at[number]]
    gather = Gather(place, own, full, send_sem, recv_sem, local_sem)

    def move(source, target, number):
        pltpu.make_async_copy(source, target, load_sem.at[number]).start()

    def moved(whole, number):
        pltpu.make_async_copy(whole, whole, load_sem.at[number]).wait()

    for g in range(groups):
        for part in range(3):
            start = part * width + g * GROUP
            move(
                own_qkv_ref.at[:, start : start + GROUP],
                group_ref.at[g, :, part * GROUP : (part + 1) * GROUP],
                g,
            )
    for number in range(blocks):
        take_block(
            move, own_fc_ref, number, shards, own_block_ref.at[number], groups + number
        )
    move(own_out_ref, own_rows_ref, groups + blocks)
    move(own_proj_ref.at[0 : blocks * 128], own_units_ref, groups + blocks + 1)
    place.meet([place.peer(*other) for other in others] + [place.across(), place.sibling()])

    def table(number, other, arriving):
        target = tables_ref.at[place.shard(*other) if arriving else place.me]
        return remote(
            target if arriving else own_params_ref,
            target,
            params_send_sem.at[number],
            params_recv_sem.at[number],
            place.peer(*other),
        )

    for number, other in enumerate(others):
        table(number, other, False).start()
    runner = Runner(FORWARD_PLAN, gather, ())

    def outward(g):
        return (
            pltpu.make_async_copy(held_ref.at[g], projected_ref.at[g], out_sem.at[g, 0]),
            pltpu.make_async_copy(weights_ref.at[g], full_qkv_ref.at[g], out_sem.at[g, 1]),
        )

    for g in range(groups):
        moved(group_ref.at[g], g)
        runner.act([event for event in FORWARD_PLAN[P0] if event[1] == g])
    moved(own_rows_ref, groups + blocks)
    moved(own_units_ref, groups + blocks + 1)
    runner.act([event for event in FORWARD_PLAN[P0] if event[1] >= groups])
    for g in range(groups):
        gather.keep(g).start()
    for number in range(blocks):
        moved(own_block_ref.at[number], groups + number)
    for at in range(groups, groups + 1 + 2 * blocks):
        gather.keep(at).start()
    tables_ref[place.me] = own_params_ref[...]
    build_mask(segment_ref, mask_ref)
    runner.do(P1)
    for number, other in enumerate(others):
        table(number, other, True).wait_recv()
    spread_params(shards, width // shards, tables_ref, params_ref)
    first_norm(tokens_ref, params_ref, normed_ref)
    runner.do(P2)

    @pl.loop(0, 2 * groups)
    def _(pair):
        g, odd = pair // 2, pair % 2
        runner.at_step(pair, NEED)

        @pl.when(odd == 0)
        def _():
            part = block(g, GROUP)
            weights = weights_ref[g].reshape(width, 3 * GROUP)
            values = matmul(normed_ref[...], weights, NN)
            bias = jnp.concatenate(
                [
                    params_ref[BIAS_Q : BIAS_Q + 1, part],
                    jnp.zeros((1, GROUP), f32),
                    params_ref[BIAS_V : BIAS_V + 1, part],
                ],
                axis=1,
            )
            held_ref[g] = (values + bias).astype(bf16)
            values_t_ref[part, :] = jnp.transpose(held_ref[g, :, 2 * GROUP :])
            for copy in outward(g):
                copy.start()

        attend_forward(
            pair,
            held_ref[g, :, block(odd, 2 * HEAD)],
            held_ref[g, :, block(2 + odd, 2 * HEAD)],
            values_t_ref,
            mask_ref,
            attended_t_ref,
            lse_ref,
            lambda which: runner.at_step(pair, which),
        )

    runner.do(END)
    for g in range(groups):
        for copy in outward(g):
            copy.wait()
    for at in range(groups + 1 + 2 * blocks):
        gather.drain(at)
    for number, other in enumerate(others):
        table(number, other, False).wait_send()


def spread_params(shards, own, tables_ref, params_ref):
    span = params_ref.shape[1]
    lane = lax.broadcasted_iota(jnp.int32, (128, span), 0)
    column = lax.broadcasted_iota(jnp.int32, (128, span), 1)
    narrow = wide = 0.0
    for shard in range(shards):
        values = tables_ref[shard]
        place = (column == lane + shard * own) & (lane < own)
        narrow = narrow + matmul(values, place.astype(f32).astype(bf16), NN)
        place = column == lane + shard * 128
        wide = wide + matmul(values, place.astype(f32).astype(bf16), NN)
    params_ref[0:8] = narrow[0:8]
    params_ref[8:16] = wide[8:16]


def take_block(move, own_fc_ref, number, shards, target_ref, sem):
    own = own_fc_ref.shape[1] // shards
    for shard in range(shards):
        start = shard * own + number * 128
        move(
            own_fc_ref.at[:, start : start + 128],
            target_ref.at[:, shard * 128 : (shard + 1) * 128],
            sem,
        )


def hidden_kernel(
    attended_t_ref,
    tokens_ref,
    cotangent_ref,
    params_ref,
    w_out_ref,
    w_fc_ref,
    w_proj_ref,
    layer_out_ref,
    grad_middle_ref,
    grad_attended_ref,
    grad_w_out_ref,
    grad_w_fc_ref,
    grad_w_proj_t_ref,
    small_ref,
    middle_ref,
    normed_ref,
    normed_t_ref,
    cotangent_t_ref,
    mixed_ref,
    grad_normed_ref,
    activated_ref,
    grad_preact_ref,
):
    step, steps = pl.program_id(0), pl.num_programs(0)
    length, width = tokens_ref.shape
    row = lambda at: params_ref[at : at + 1, :]
    chunks = [slice(at, at + ROW_CHUNK) for at in range(0, length, ROW_CHUNK)]

    @pl.when(step == 0)
    def _():
        attended = jnp.transpose(attended_t_ref[...])
        middle_ref[...] = (
            tokens_ref[...].astype(f32) + matmul(attended, w_out_ref[...], NN) + row(BIAS_OUT)
        )
        for rows in chunks:
            norm, _ = normalized(middle_ref[rows])
            normed_ref[rows] = (norm * row(GAIN2) + row(SHIFT2)).astype(bf16)
        normed_t_ref[...] = jnp.transpose(normed_ref[...])
        cotangent_t_ref[...] = jnp.transpose(cotangent_ref[...])
        mixed_ref[...] = jnp.zeros_like(mixed_ref)
        grad_normed_ref[...] = jnp.zeros_like(grad_normed_ref)
        small_ref[...] = jnp.zeros_like(small_ref)

    bias_sum = 0.0
    bias_row = params_ref[pl.ds(BIAS_FC + step, 1), :]
    for rows in chunks:
        preact = matmul(normed_ref[rows], w_fc_ref[...], NN) + bias_row
        grad_act = matmul(cotangent_ref[rows], w_proj_ref[...], NT)
        square = preact * preact
        bend = jnp.tanh(GELU_SCALE * preact * (1.0 + GELU_CUBE * square))
        gate = 0.5 + 0.5 * bend
        activated_ref[rows] = (preact * gate).astype(bf16)
        slope = gate + (0.5 * GELU_SCALE) * preact * (1.0 - bend * bend) * (
            1.0 + (3 * GELU_CUBE) * square
        )
        grad_preact = (slope * grad_act).astype(bf16)
        grad_preact_ref[rows] = grad_preact
        bias_sum = bias_sum + total(grad_preact.astype(f32))
    small_ref[pl.ds(BIAS_FC + step, 1), :] = bias_sum
    mixed_ref[...] += matmul(activated_ref[...], w_proj_ref[...], NN)
    grad_w_proj_t = matmul(cotangent_t_ref[...], activated_ref[...], NN).astype(bf16)
    pieces, _, piece = grad_w_proj_t_ref.shape
    for at in range(pieces):
        grad_w_proj_t_ref[at] = grad_w_proj_t[:, at * piece : (at + 1) * piece]
    grad_w_fc_ref[...] = matmul(normed_t_ref[...], grad_preact_ref[...], NN).astype(bf16)
    grad_normed_ref[...] += matmul(grad_preact_ref[...], w_fc_ref[...], NT)

    @pl.when(step == steps - 1)
    def _():
        sums = [0.0] * 4
        for rows in chunks:
            middle = middle_ref[rows]
            layer_out_ref[rows] = (middle + mixed_ref[rows] + row(BIAS_PROJ)).astype(bf16)
            norm, inverse = normalized(middle)
            grad_normed = grad_normed_ref[rows]
            cotangent = cotangent_ref[rows].astype(f32)
            grad_middle = cotangent + norm_pull(grad_normed, row(GAIN2), norm, inverse)
            grad_middle_ref[rows] = grad_middle
            normed_ref[rows] = grad_middle.astype(bf16)
            terms = (grad_middle, grad_normed * norm, grad_normed, cotangent)
            sums = [a + total(b) for a, b in zip(sums, terms)]
        for at, value in zip((BIAS_OUT, GAIN2, SHIFT2, BIAS_PROJ), sums):
            small_ref[at : at + 1, :] = value
        grad_branch = normed_ref[...]
        grad_w_out_ref[...] = matmul(attended_t_ref[...], grad_branch, NN).astype(bf16)
        grad_attended_ref[...] = matmul(grad_branch, w_out_ref[...], NT).astype(bf16)


def sum_hidden_kernel(
    shards,
    attended_t_in_ref,
    tokens_in_ref,
    cotangent_in_ref,
    params_ref,
    w_out_in_ref,
    fc_in_ref,
    proj_in_ref,
    own_fc_ref,
    own_proj_ref,
    layer_out_ref,
    grad_middle_ref,
    grad_attended_ref,
    grad_out_ref,
    last_fc_ref,
    last_proj_ref,
    done_fc_ref,
    done_proj_ref,
    small_ref,
    middle_ref,
    normed_ref,
    normed_t_ref,
    cotangent_t_ref,
    mixed_ref,
    grad_normed_ref,
    activated_ref,
    grad_preact_ref,
    fc_ref,
    proj_ref,
    grad_fc_ref,
    grad_proj_ref,
    own_block_ref,
    attended_t_ref,
    tokens_ref,
    cotangent_ref,
    w_out_ref,
    layer_ref,
    *rest,
):
    length, width = tokens_ref.shape
    blocks = fc_ref.shape[0]
    units = fc_ref.shape[3]
    early = fc_in_ref.shape[0]
    summed = done_fc_ref.shape[0]
    buffers, rest = [rest[SUM_BUFFERS * k :][:SUM_BUFFERS] for k in range(2 * summed)], rest[
        SUM_BUFFERS * 2 * summed :
    ]
    send_sem, recv_sem, local_sem, load_sem, sum_send_sem, sum_recv_sem = rest
    row = lambda at: params_ref[at : at + 1, 0:width]
    chunks = [slice(at, at + ROW_CHUNK) for at in range(0, length, ROW_CHUNK)]
    place = Place(shards)

    def move(source, target, number):
        pltpu.make_async_copy(source, target, load_sem.at[number]).start()

    def moved(whole, number):
        pltpu.make_async_copy(whole, whole, load_sem.at[number]).wait()

    own, full = [], []
    for number in range(early, blocks):
        own_block = own_block_ref.at[number - early]
        take_block(move, own_fc_ref, number, shards, own_block, number)
        own += [own_block, own_proj_ref.at[number * 128 : number * 128 + 128]]
        full += [fc_ref.at[number], proj_ref.at[number]]
    inputs = (
        (attended_t_in_ref, attended_t_ref),
        (w_out_in_ref, w_out_ref),
        (tokens_in_ref, tokens_ref),
        (cotangent_in_ref, cotangent_ref),
    )
    for number, pair in enumerate(inputs):
        move(*pair, 2 * blocks + number)
    for number in range(early):
        move(fc_in_ref.at[number], fc_ref.at[number], number)
        move(proj_in_ref.at[number], proj_ref.at[number], blocks + number)
    gather = Gather(place, own, full, send_sem, recv_sem, local_sem)
    sums = []
    for number in range(summed):
        for grad, done in ((grad_proj_ref, done_proj_ref), (grad_fc_ref, done_fc_ref)):
            k = len(sums)
            sums.append(
                Summed(
                    place,
                    grad.at[number],
                    done.at[number],
                    buffers[k],
                    sum_send_sem.at[k],
                    sum_recv_sem.at[k],
                )
            )
    runner = Runner(HIDDEN_PLAN, gather, sums)
    place.meet(
        [place.peer(hop, 0) for hop in range(1, place.lines)]
        + [place.peer(0, 1), place.across(), place.sibling()]
    )
    for number in range(early, blocks):
        moved(own_block_ref.at[number - early], number)
    runner.do(H0)
    for at in range(len(own)):
        gather.keep(at).start()

    for number, pair in enumerate(inputs):
        moved(pair[1], 2 * blocks + number)
    attended = jnp.transpose(attended_t_ref[...])
    w_out = w_out_ref[...].reshape(width, width)
    middle_ref[...] = tokens_ref[...].astype(f32) + matmul(attended, w_out, NN) + row(BIAS_OUT)
    runner.do(H1)

    @pl.loop(0, len(chunks))
    def _(number):
        norm, _ = normalized(middle_ref[chunk(number)])
        normed_ref[chunk(number)] = (norm * row(GAIN2) + row(SHIFT2)).astype(bf16)

    runner.do(H2)
    normed_t_ref[...] = jnp.transpose(normed_ref[...])
    cotangent_t_ref[...] = jnp.transpose(cotangent_ref[...])
    mixed_ref[...] = jnp.zeros_like(mixed_ref)
    grad_normed_ref[...] = jnp.zeros_like(grad_normed_ref)
    small_ref[...] = jnp.zeros_like(small_ref)
    for number in range(early):
        moved(fc_ref.at[number], number)
        moved(proj_ref.at[number], blocks + number)
    runner.do(H3)

    table = {
        step * len(chunks) + tick: events
        for tick in range(len(chunks))
        for step, events in HIDDEN_PLAN.get(tick, {}).items()
    }

    @pl.loop(0, blocks)
    def _(step):
        runner.at_step(step, NEED)
        w_fc = fc_ref.at[step]
        w_proj = proj_ref.at[step]
        bias_row = params_ref[pl.ds(BIAS_FC + step, 1), 0:units]

        @pl.loop(0, len(chunks))
        def _(number):
            runner.on(step * len(chunks) + number, table)
            rows = chunk(number)
            preact = matmul(normed_ref[rows], w_fc[...].reshape(width, units), NN) + bias_row
            grad_act = matmul(cotangent_ref[rows], w_proj[...].reshape(units, width), NT)
            square = preact * preact
            bend = jnp.tanh(GELU_SCALE * preact * (1.0 + GELU_CUBE * square))
            gate = 0.5 + 0.5 * bend
            activated_ref[rows] = (preact * gate).astype(bf16)
            slope = gate + (0.5 * GELU_SCALE) * preact * (1.0 - bend * bend) * (
                1.0 + (3 * GELU_CUBE) * square
            )
            grad_preact = (slope * grad_act).astype(bf16)
            grad_preact_ref[rows] = grad_preact
            small_ref[pl.ds(BIAS_FC + step, 1), 0:units] += total(grad_preact.astype(f32))

        runner.at_step(step, len(chunks))
        grad_proj = matmul(cotangent_t_ref[...], activated_ref[...], NN).astype(bf16)
        for shard in range(shards):
            grad_proj_ref[step, shard] = grad_proj[:, shard * 128 : (shard + 1) * 128]
        runner.at_step(step, len(chunks) + 1)
        grad_fc = matmul(normed_t_ref[...], grad_preact_ref[...], NN).astype(bf16)
        grad_fc_ref[step] = grad_fc.reshape(grad_fc_ref.shape[1:])
        runner.at_step(step, len(chunks) + 2)
        mixed_ref[...] += matmul(activated_ref[...], w_proj[...].reshape(units, width), NN)
        runner.at_step(step, len(chunks) + 3)
        grad_normed_ref[...] += matmul(
            grad_preact_ref[...], w_fc[...].reshape(width, units), NT
        )

    hand_over = []

    def hand(source, target):
        copy = pltpu.make_async_copy(source, target, load_sem.at[len(hand_over)])
        copy.start()
        hand_over.append(copy)

    hand(grad_fc_ref.at[summed:blocks], last_fc_ref)
    hand(grad_proj_ref.at[summed:blocks], last_proj_ref)
    runner.do(E0)

    @pl.loop(0, len(chunks))
    def _(number):
        rows = chunk(number)
        middle = middle_ref[rows]
        layer_ref[rows] = (middle + mixed_ref[rows] + row(BIAS_PROJ)).astype(bf16)
        norm, inverse = normalized(middle)
        grad_normed = grad_normed_ref[rows]
        cotangent = cotangent_ref[rows].astype(f32)
        grad_middle = cotangent + norm_pull(grad_normed, row(GAIN2), norm, inverse)
        middle_ref[rows] = grad_middle
        normed_ref[rows] = grad_middle.astype(bf16)
        terms = (grad_middle, grad_normed * norm, grad_normed, cotangent)
        for at, term in zip((BIAS_OUT, GAIN2, SHIFT2, BIAS_PROJ), terms):
            small_ref[at : at + 1, 0:width] += total(term)

    runner.do(E1)
    hand(middle_ref, grad_middle_ref)
    hand(layer_ref, layer_out_ref)
    runner.do(E2)
    grad_branch = normed_ref[...]
    grad_out = matmul(attended_t_ref[...], grad_branch, NN).astype(bf16)
    grad_out_ref[...] = grad_out.reshape(grad_out_ref.shape)
    runner.do(E3)
    grad_attended_ref[...] = matmul(grad_branch, w_out, NT).astype(bf16)
    runner.do(END)
    for copy in hand_over:
        copy.wait()
    for item in sums:
        item.drain()
    for at in range(len(own)):
        gather.drain(at)


def backward_kernel(
    tokens_ref,
    segment_ref,
    params_ref,
    w_qkv_ref,
    projected_ref,
    attended_t_ref,
    lse_ref,
    grad_attended_ref,
    grad_middle_ref,
    small_in_ref,
    grad_tokens_ref,
    grad_w_qkv_ref,
    small_ref,
    mask_ref,
    wide_t_ref,
    grad_queries_t_ref,
    dots_ref,
    grad_projected_ref,
    grad_keys_ref,
    grad_values_ref,
):
    length, width = tokens_ref.shape
    build_mask(segment_ref, mask_ref)
    dot_rows(attended_t_ref, grad_attended_ref, wide_t_ref, dots_ref)
    wide_t_ref[...] = jnp.transpose(projected_ref[:, width : 2 * width])

    pairs = width // (2 * HEAD)

    @pl.loop(0, pairs)
    def _(pair):
        parts = [projected_ref[:, block(k * pairs + pair, 2 * HEAD)] for k in range(3)]
        attend_backward(
            pair,
            parts + [grad_attended_ref[:, block(pair, 2 * HEAD)]],
            wide_t_ref,
            mask_ref,
            lse_ref,
            dots_ref,
            grad_queries_t_ref,
            grad_keys_ref,
            grad_values_ref,
        )
        for k, ref in ((1, grad_keys_ref), (2, grad_values_ref)):
            grad_projected_ref[:, block(k * pairs + pair, 2 * HEAD)] = ref[...].astype(bf16)

    grad_projected_ref[:, 0:width] = jnp.transpose(grad_queries_t_ref[...])
    normed_transposed(tokens_ref, params_ref, wide_t_ref)
    small_ref[...] = small_in_ref[...]
    bias_sums(grad_projected_ref, small_ref)
    grad_w_qkv_ref[...] = matmul(wide_t_ref[...], grad_projected_ref[...], NN).astype(bf16)
    gain_sum = shift_sum = 0.0
    for at in range(0, length, ROW_CHUNK):
        gain_part, shift_part = token_rows(
            slice(at, at + ROW_CHUNK),
            tokens_ref,
            params_ref,
            matmul(grad_projected_ref[at : at + ROW_CHUNK], w_qkv_ref[...], NT),
            grad_middle_ref[at : at + ROW_CHUNK],
            grad_tokens_ref,
        )
        gain_sum, shift_sum = gain_sum + gain_part, shift_sum + shift_part
    small_ref[GAIN1 : GAIN1 + 1, :] = gain_sum
    small_ref[SHIFT1 : SHIFT1 + 1, :] = shift_sum


def dot_rows(attended_t_ref, grad_attended_ref, wide_t_ref, dots_ref):
    wide_t_ref[...] = jnp.transpose(grad_attended_ref[...])
    for head in range(wide_t_ref.shape[0] // HEAD):
        rows = slice(head * HEAD, (head + 1) * HEAD)
        dots_ref[head : head + 1, :] = total(
            wide_t_ref[rows].astype(f32) * attended_t_ref[rows].astype(f32)
        )


def normed_transposed(tokens_ref, params_ref, wide_t_ref):
    width = tokens_ref.shape[1]
    row = lambda at: params_ref[at : at + 1, 0:width]

    @pl.loop(0, tokens_ref.shape[0] // ROW_CHUNK)
    def _(number):
        norm, _ = normalized(tokens_ref[chunk(number)].astype(f32))
        normed = (norm * row(GAIN1) + row(SHIFT1)).astype(bf16)
        wide_t_ref[:, chunk(number)] = jnp.transpose(normed)


def bias_sums(grad_projected_ref, small_ref):
    width = small_ref.shape[1]
    for at, part in ((BIAS_Q, 0), (BIAS_V, 2)):
        values = grad_projected_ref[:, part * width : (part + 1) * width]
        small_ref[at : at + 1, :] = total(values.astype(f32))


def token_rows(rows, tokens_ref, params_ref, grad_normed, middle, grad_tokens_ref):
    gain = params_ref[GAIN1 : GAIN1 + 1, 0 : tokens_ref.shape[1]]
    norm, inverse = normalized(tokens_ref[rows].astype(f32))
    grad_rows = norm_pull(grad_normed, gain, norm, inverse)
    grad_tokens_ref[rows] = (middle + grad_rows).astype(bf16)
    return total(grad_normed * norm), total(grad_normed)


def sum_backward_kernel(
    shards,
    tokens_in_ref,
    segment_ref,
    params_ref,
    attended_t_in_ref,
    lse_ref,
    grad_attended_in_ref,
    small_in_ref,
    projected_in_ref,
    w_qkv_in_ref,
    grad_middle_in_ref,
    grad_out_in_ref,
    grad_fc_in_ref,
    grad_proj_in_ref,
    grad_tokens_ref,
    done_qkv_ref,
    done_out_ref,
    done_fc_ref,
    done_proj_ref,
    own_small_ref,
    mask_ref,
    wide_t_ref,
    normed_t_ref,
    grad_queries_t_ref,
    dots_ref,
    projected_ref,
    grad_projected_ref,
    grad_keys_ref,
    grad_values_ref,
    grad_qkv_ref,
    grad_out_ref,
    grad_fc_ref,
    grad_proj_ref,
    weights_ref,
    tokens_ref,
    attended_t_ref,
    grad_attended_ref,
    *rest,
):
    length, width = tokens_ref.shape
    groups = width // GROUP
    late_blocks = grad_fc_ref.shape[0]
    items = 2 * late_blocks + 1 + groups
    buffers, rest = [rest[SUM_BUFFERS * k :][:SUM_BUFFERS] for k in range(items)], rest[
        SUM_BUFFERS * items :
    ]
    small_ref, parts_ref, core_parts_ref, far_parts_ref, side_parts_ref, line_parts_ref, *rest = rest
    send_sem, recv_sem, load_sem, small_send_sem, small_recv_sem = rest
    place = Place(shards)
    lines = place.lines
    arrays = []
    for number in range(late_blocks):
        arrays += [
            (grad_proj_ref.at[number], done_proj_ref.at[number], grad_proj_in_ref.at[number]),
            (grad_fc_ref.at[number], done_fc_ref.at[number], grad_fc_in_ref.at[number]),
        ]
    arrays.append((grad_out_ref, done_out_ref, grad_out_in_ref))
    arrays += [(grad_qkv_ref.at[g], done_qkv_ref.at[g], None) for g in range(groups)]
    sums = [
        Summed(
            place,
            grad,
            done,
            buffers[k],
            send_sem.at[k],
            recv_sem.at[k],
            source,
            None if source is None else load_sem.at[k],
        )
        for k, (grad, done, source) in enumerate(arrays)
    ]
    runner = Runner(BACKWARD_PLAN, None, sums)
    load_projected = pltpu.make_async_copy(projected_in_ref, projected_ref, load_sem.at[items])
    load_projected.start()
    inputs = [
        pltpu.make_async_copy(source, target, load_sem.at[items + 2 + number])
        for number, (source, target) in enumerate(
            (
                (attended_t_in_ref, attended_t_ref),
                (grad_attended_in_ref, grad_attended_ref),
                (tokens_in_ref, tokens_ref),
            )
        )
    ]
    for copy in inputs:
        copy.start()
    load_weights = pltpu.make_async_copy(w_qkv_in_ref, weights_ref, load_sem.at[items + 1])
    load_weights.start()
    place.meet(
        [place.peer(hop, 0) for hop in range(1, lines)]
        + [place.peer(0, 1), place.across(), place.sibling()]
    )
    runner.do(B0)
    build_mask(segment_ref, mask_ref)
    runner.do(B1)
    for copy in inputs:
        copy.wait()
    dot_rows(attended_t_ref, grad_attended_ref, wide_t_ref, dots_ref)
    runner.do(B2)
    normed_transposed(tokens_ref, params_ref, normed_t_ref)
    small_ref[...] = small_in_ref[...]
    parts_ref[...] = jnp.zeros_like(parts_ref)
    load_projected.wait()
    for g in range(groups):
        wide_t_ref[g * GROUP : (g + 1) * GROUP] = jnp.transpose(
            projected_ref[g, :, GROUP : 2 * GROUP]
        )
    runner.do(B3)

    @pl.loop(0, 2 * groups)
    def _(pair):
        g, odd = pair // 2, pair % 2
        parts = [projected_ref[g, :, block(2 * k + odd, 2 * HEAD)] for k in range(3)]
        attend_backward(
            pair,
            parts + [grad_attended_ref[:, block(pair, 2 * HEAD)]],
            wide_t_ref,
            mask_ref,
            lse_ref,
            dots_ref,
            grad_queries_t_ref,
            grad_keys_ref,
            grad_values_ref,
            lambda number: runner.at_step(pair, number),
        )
        grad_queries = jnp.transpose(grad_queries_t_ref[block(pair, 2 * HEAD), :])
        grad_projected_ref[g, :, block(odd, 2 * HEAD)] = grad_queries
        for k, ref in ((1, grad_keys_ref), (2, grad_values_ref)):
            grad_projected_ref[g, :, block(2 * k + odd, 2 * HEAD)] = ref[...].astype(bf16)

        @pl.when(odd == 1)
        def _():
            grad_group = matmul(normed_t_ref[...], grad_projected_ref[g], NN).astype(bf16)
            grad_qkv_ref[g] = grad_group.reshape(grad_qkv_ref.shape[1:])

    middle_ref = mask_ref.at[:, 0:width]
    load_middle = pltpu.make_async_copy(grad_middle_in_ref, middle_ref, load_sem.at[items])
    load_middle.start()
    for g in range(groups):
        part = slice(g * GROUP, (g + 1) * GROUP)
        for at, k in ((BIAS_Q, 0), (BIAS_V, 2)):
            values = grad_projected_ref[g, :, k * GROUP : (k + 1) * GROUP]
            small_ref[at : at + 1, part] = total(values.astype(f32))
    load_weights.wait()
    load_middle.wait()
    table = {k: BACKWARD_PLAN.get(E0 + k, ()) for k in range(length // ROW_CHUNK)}

    @pl.loop(0, length // ROW_CHUNK)
    def _(number):
        runner.on(number, table)
        rows = chunk(number)
        grad_normed = 0.0
        for g in range(groups):
            weights = weights_ref[g].reshape(width, 3 * GROUP)
            grad_normed = grad_normed + matmul(grad_projected_ref[g, rows], weights, NT)
        gain_part, shift_part = token_rows(
            rows, tokens_ref, params_ref, grad_normed, mask_ref[rows, 0:width], grad_tokens_ref
        )
        small_ref[GAIN1 : GAIN1 + 1, 0:width] += gain_part
        small_ref[SHIFT1 : SHIFT1 + 1, 0:width] += shift_part

    own = width // shards
    for shard in range(shards):
        into = parts_ref.at[shard // 2, shard % 2]
        into[0:8, 0:own] = small_ref[0:8, shard * own : (shard + 1) * own]
        into[8:16, :] = small_ref[8:16, shard * 128 : (shard + 1) * 128]

    def exchange(slot, source, into, peer):
        copy = remote(source, into, small_send_sem.at[slot], small_recv_sem.at[slot], peer)
        copy.start()
        return copy

    line, side = place.line, place.side
    todo = BACKWARD_PLAN.get(END, ())
    portions = [todo[len(todo) * k // 5 : len(todo) * (k + 1) // 5] for k in range(5)]
    copy = exchange(0, parts_ref, core_parts_ref, place.sibling())
    runner.act(portions[0])
    copy.wait()
    parts_ref[...] += core_parts_ref[...]
    copy = exchange(1, parts_ref, far_parts_ref, place.across())
    runner.act(portions[1])
    copy.wait()
    parts_ref[...] += far_parts_ref[...]
    copy = exchange(2, parts_ref.at[:, 1 - side], side_parts_ref, place.peer(0, 1))
    runner.act(portions[2])
    copy.wait()
    parts_ref[:, side] += side_parts_ref[...]
    copies = [
        exchange(
            2 + hop,
            parts_ref.at[flip(line, hop), side],
            line_parts_ref.at[hop - 1],
            place.peer(hop, 0),
        )
        for hop in range(1, lines)
    ]
    runner.act(portions[3] + portions[4])
    for copy in copies:
        copy.wait()
    small = parts_ref[line, side]
    for hop in range(1, lines):
        small = small + line_parts_ref[hop - 1]
    own_small_ref[...] = small
    for item in sums:
        item.drain()


def finish_kernel(
    shards,
    qkv_ref,
    out_ref,
    fc_early_ref,
    fc_last_ref,
    proj_early_ref,
    proj_last_ref,
    small_ref,
    layer_in_ref,
    tokens_in_ref,
    sum_qkv_ref,
    sum_out_ref,
    sum_fc_ref,
    sum_proj_ref,
    layer_out_ref,
    grad_tokens_ref,
    *rest,
):
    *vector_refs, fc_bias_ref, copy_sem = rest
    copies = [
        pltpu.make_async_copy(source, target, copy_sem.at[k])
        for k, (source, target) in enumerate(
            ((layer_in_ref, layer_out_ref), (tokens_in_ref, grad_tokens_ref))
        )
    ]
    for copy in copies:
        copy.start()
    groups, own, _ = qkv_ref.shape
    width = groups * GROUP
    for g in range(groups):
        for part in range(3):
            start = part * width + g * GROUP
            sum_qkv_ref[:, start : start + GROUP] = qkv_ref[
                g, :, part * GROUP : (part + 1) * GROUP
            ].astype(f32)
    sum_out_ref[...] = out_ref[...].astype(f32)
    early = fc_early_ref.shape[0]
    blocks = early + fc_last_ref.shape[0]
    for number in range(blocks):
        fc = fc_early_ref.at[number] if number < early else fc_last_ref.at[number - early]
        proj = proj_early_ref.at[number] if number < early else proj_last_ref.at[number - early]
        for shard in range(shards):
            start = (shard * blocks + number) * 128
            sum_fc_ref[:, start : start + 128] = fc[:, shard * 128 : (shard + 1) * 128].astype(f32)
        sum_proj_ref[number * 128 : (number + 1) * 128] = jnp.transpose(proj[...].astype(f32))
    for at, vector_ref in enumerate(vector_refs):
        vector_ref[...] = small_ref[at, 0:own]
    for number in range(blocks):
        fc_bias_ref[number * 128 : (number + 1) * 128] = small_ref[BIAS_FC + number, :]
    for copy in copies:
        copy.wait()


def kernel_params():
    return pltpu.CompilerParams(vmem_limit_bytes=VMEM_LIMIT)


def run_forward(tokens, segment, params, w_qkv):
    length, width = tokens.shape
    return pl.pallas_call(
        forward_kernel,
        in_specs=[WHOLE] * 4,
        out_specs=(WHOLE,) * 3,
        out_shape=(
            jax.ShapeDtypeStruct((length, 3 * width), bf16),
            jax.ShapeDtypeStruct((width, length), bf16),
            jax.ShapeDtypeStruct((16, length), f32),
        ),
        scratch_shapes=[
            pltpu.VMEM((length, length), f32),
            pltpu.VMEM((length, width), bf16),
            pltpu.VMEM((width, length), bf16),
        ],
        compiler_params=kernel_params(),
        name="forward",
    )(tokens, segment, params, w_qkv)


def run_hidden(attended_t, tokens, cotangent, params, w_out, w_fc, w_proj, piece):
    length, width = tokens.shape
    hidden = w_fc.shape[1]
    shape = jax.ShapeDtypeStruct
    columns = pl.BlockSpec((width, width), lambda step: (0, step))
    return pl.pallas_call(
        hidden_kernel,
        grid=(hidden // width,),
        in_specs=[WHOLE] * 5 + [columns, pl.BlockSpec((width, width), lambda step: (step, 0))],
        out_specs=(
            WHOLE,
            WHOLE,
            WHOLE,
            WHOLE,
            columns,
            pl.BlockSpec((width // piece, width, piece), lambda step: (step, 0, 0)),
            WHOLE,
        ),
        out_shape=(
            shape((length, width), bf16),
            shape((length, width), f32),
            shape((length, width), bf16),
            shape((width, width), bf16),
            shape((width, hidden), bf16),
            shape((hidden // piece, width, piece), bf16),
            shape((16, width), f32),
        ),
        scratch_shapes=[
            pltpu.VMEM((length, width), f32),
            pltpu.VMEM((length, width), bf16),
            pltpu.VMEM((width, length), bf16),
            pltpu.VMEM((width, length), bf16),
            pltpu.VMEM((length, width), f32),
            pltpu.VMEM((length, width), f32),
            pltpu.VMEM((length, width), bf16),
            pltpu.VMEM((length, width), bf16),
        ],
        compiler_params=kernel_params(),
        name="hidden",
    )(attended_t, tokens, cotangent, params, w_out, w_fc, w_proj)


def run_backward(
    tokens, segment, params, w_qkv, projected, attended_t, lse, grad_attended, grad_middle, small
):
    length, width = tokens.shape
    shape = jax.ShapeDtypeStruct
    return pl.pallas_call(
        backward_kernel,
        in_specs=[WHOLE] * 10,
        out_specs=(WHOLE,) * 3,
        out_shape=(
            shape((length, width), bf16),
            shape((width, 3 * width), bf16),
            shape((16, width), f32),
        ),
        scratch_shapes=[
            pltpu.VMEM((length, length), f32),
            pltpu.VMEM((width, length), bf16),
            pltpu.VMEM((width, length), bf16),
            pltpu.VMEM((16, length), f32),
            pltpu.VMEM((length, 3 * width), bf16),
            pltpu.VMEM((length, 2 * HEAD), f32),
            pltpu.VMEM((length, 2 * HEAD), f32),
        ],
        compiler_params=kernel_params(),
        name="backward",
    )(
        tokens,
        segment,
        params,
        w_qkv,
        projected,
        attended_t,
        lse,
        grad_attended,
        grad_middle,
        small,
    )


def link_params(number):
    return pltpu.CompilerParams(
        vmem_limit_bytes=VMEM_LIMIT, collective_id=number, has_side_effects=True
    )


def run_gather_forward(
    shards, span, tokens, segment, own_params, w_qkv, w_out, w_fc, w_proj
):
    length, width = tokens.shape
    own = w_qkv.shape[0]
    groups = width // GROUP
    blocks = GATHERED_EARLY
    items = groups + 1 + 2 * blocks
    shape = jax.ShapeDtypeStruct
    copies = 3 * shards - 3
    dma = pltpu.SemaphoreType.DMA
    return pl.pallas_call(
        partial(gather_forward_kernel, shards),
        in_specs=[WHOLE] * 3 + [HBM] * 4,
        out_specs=(HBM,) + (WHOLE,) * 3 + (HBM,) * 4,
        out_shape=(
            shape((groups, length, 3 * GROUP), bf16),
            shape((width, length), bf16),
            shape((16, length), f32),
            shape((own_params.shape[0], span), f32),
            shape((groups, shards, own, 3 * GROUP), bf16),
            shape((shards, own, width), bf16),
            shape((blocks, shards, own, shards * 128), bf16),
            shape((blocks, shards, 128, width), bf16),
        ),
        scratch_shapes=[
            pltpu.VMEM((length, length), f32),
            pltpu.VMEM((length, width), bf16),
            pltpu.VMEM((width, length), bf16),
            pltpu.VMEM((groups, length, 3 * GROUP), bf16),
            pltpu.VMEM((groups, shards, own, 3 * GROUP), bf16),
            pltpu.VMEM((shards,) + own_params.shape, bf16),
            pltpu.VMEM((groups, own, 3 * GROUP), bf16),
            pltpu.VMEM((blocks, own, shards * 128), bf16),
            pltpu.VMEM((own, width), bf16),
            pltpu.VMEM((blocks * 128, width), bf16),
            dma((items, copies)),
            dma((items, copies)),
            dma((items,)),
            dma((shards - 1,)),
            dma((shards - 1,)),
            dma((groups + blocks + 2,)),
            dma((groups, 2)),
        ],
        compiler_params=link_params(0),
        name="gather_forward",
    )(tokens, segment, own_params, w_qkv, w_out, w_fc, w_proj)


def run_sum_hidden(
    shards, attended_t, tokens, cotangent, params, full_out, full_fc, full_proj, w_fc, w_proj
):
    length, width = tokens.shape
    own, units = w_fc.shape[0], shards * 128
    blocks = w_proj.shape[0] // 128
    lines = shards // 2
    shape = jax.ShapeDtypeStruct
    dma = pltpu.SemaphoreType.DMA
    grads = ((shards, own, units), (shards, width, 128))
    late, early = blocks - full_fc.shape[0], SUMMED_EARLY
    buffers = [
        ref
        for _ in range(early)
        for grad in reversed(grads)
        for ref in sum_buffers(lines, *grad)
    ]
    return pl.pallas_call(
        partial(sum_hidden_kernel, shards),
        in_specs=[HBM] * 3 + [WHOLE] + [HBM] * 5,
        out_specs=(HBM, HBM, WHOLE, WHOLE, HBM, HBM) + (WHOLE,) * 3,
        out_shape=(
            shape((length, width), bf16),
            shape((length, width), f32),
            shape((length, width), bf16),
            shape((shards, own, width), bf16),
            shape((blocks - early,) + grads[0], bf16),
            shape((blocks - early,) + grads[1], bf16),
            shape((early, own, units), bf16),
            shape((early, width, 128), bf16),
            shape(params.shape, f32),
        ),
        scratch_shapes=[
            pltpu.VMEM((length, width), f32),
            pltpu.VMEM((length, width), bf16),
            pltpu.VMEM((width, length), bf16),
            pltpu.VMEM((width, length), bf16),
            pltpu.VMEM((length, width), f32),
            pltpu.VMEM((length, width), f32),
            pltpu.VMEM((length, units), bf16),
            pltpu.VMEM((length, units), bf16),
            pltpu.VMEM((blocks, shards, own, units), bf16),
            pltpu.VMEM((blocks, shards, 128, width), bf16),
            pltpu.VMEM((blocks,) + grads[0], bf16),
            pltpu.VMEM((blocks,) + grads[1], bf16),
            pltpu.VMEM((late, own, units), bf16),
            pltpu.VMEM((width, length), bf16),
            pltpu.VMEM((length, width), bf16),
            pltpu.VMEM((length, width), bf16),
            pltpu.VMEM((shards, own, width), bf16),
            pltpu.VMEM((length, width), bf16),
        ]
        + buffers
        + [
            dma((2 * late, 3 * shards - 3)),
            dma((2 * late, 3 * shards - 3)),
            dma((2 * late,)),
            dma((2 * blocks + 4,)),
        ]
        + sum_sems(lines, 2 * early),
        compiler_params=link_params(1),
        name="sum_hidden",
    )(attended_t, tokens, cotangent, params, full_out, full_fc, full_proj, w_fc, w_proj)


def run_sum_backward(
    shards,
    tokens,
    segment,
    params,
    attended_t,
    lse,
    grad_attended,
    small,
    projected,
    w_qkv,
    grad_middle,
    grad_out,
    grad_fc,
    grad_proj,
):
    length, width = tokens.shape
    shape = jax.ShapeDtypeStruct
    lines, groups = shards // 2, width // GROUP
    own = width // shards
    qkv = (shards, own, 3 * GROUP)
    late_blocks = grad_fc.shape[0]
    grads = [grad_proj.shape[1:], grad_fc.shape[1:]] * late_blocks
    grads += [grad_out.shape] + [qkv] * groups
    buffers = [ref for grad in grads for ref in sum_buffers(lines, *grad)]
    parts = pltpu.VMEM((lines, 2, 16, 128), f32)
    dma = pltpu.SemaphoreType.DMA
    items = len(grads)
    return pl.pallas_call(
        partial(sum_backward_kernel, shards),
        in_specs=[HBM, WHOLE, WHOLE, HBM, WHOLE, HBM, WHOLE] + [HBM] * 6,
        out_specs=(WHOLE,) * 6,
        out_shape=(
            shape((length, width), bf16),
            shape((groups,) + qkv[1:], bf16),
            shape(grad_out.shape[1:], bf16),
            shape((late_blocks,) + grad_fc.shape[2:], bf16),
            shape((late_blocks,) + grad_proj.shape[2:], bf16),
            shape((16, 128), f32),
        ),
        scratch_shapes=[
            pltpu.VMEM((length, length), f32),
            pltpu.VMEM((width, length), bf16),
            pltpu.VMEM((width, length), bf16),
            pltpu.VMEM((width, length), bf16),
            pltpu.VMEM((16, length), f32),
            pltpu.VMEM(projected.shape, bf16),
            pltpu.VMEM(projected.shape, bf16),
            pltpu.VMEM((length, 2 * HEAD), f32),
            pltpu.VMEM((length, 2 * HEAD), f32),
            pltpu.VMEM((groups,) + qkv, bf16),
            pltpu.VMEM(grad_out.shape, bf16),
            pltpu.VMEM(grad_fc.shape, bf16),
            pltpu.VMEM(grad_proj.shape, bf16),
            pltpu.VMEM(w_qkv.shape, bf16),
            pltpu.VMEM((length, width), bf16),
            pltpu.VMEM((width, length), bf16),
            pltpu.VMEM((length, width), bf16),
        ]
        + buffers
        + [pltpu.VMEM(params.shape, f32), parts, parts, parts]
        + [pltpu.VMEM((lines, 16, 128), f32), pltpu.VMEM((lines - 1, 16, 128), f32)]
        + sum_sems(lines, items)
        + [dma((items + 5,)), dma((lines + 2,)), dma((lines + 2,))],
        compiler_params=link_params(2),
        name="sum_backward",
    )(
        tokens,
        segment,
        params,
        attended_t,
        lse,
        grad_attended,
        small,
        projected,
        w_qkv,
        grad_middle,
        grad_out,
        grad_fc,
        grad_proj,
    )


def run_finish(
    shards, qkv, out, fc_early, fc_last, proj_early, proj_last, small, layer_out, grad_tokens
):
    groups, own, _ = qkv.shape
    width = out.shape[1]
    blocks = fc_early.shape[0] + fc_last.shape[0]
    shape = jax.ShapeDtypeStruct
    return pl.pallas_call(
        partial(finish_kernel, shards),
        in_specs=[WHOLE] * 9,
        out_specs=(WHOLE,) * 4 + (HBM,) * 2 + (WHOLE,) * 9,
        out_shape=(
            shape((own, 3 * width), f32),
            shape((own, width), f32),
            shape((own, blocks * shards * 128), f32),
            shape((blocks * 128, width), f32),
            shape(layer_out.shape, bf16),
            shape(grad_tokens.shape, bf16),
        )
        + (shape((own,), f32),) * 8
        + (shape((blocks * 128,), f32),),
        scratch_shapes=[pltpu.SemaphoreType.DMA((2,))],
        compiler_params=kernel_params(),
        name="finish",
    )(qkv, out, fc_early, fc_last, proj_early, proj_last, small, layer_out, grad_tokens)


def by_kernels(
    shards, tokens, segment_ids, vectors, fc_bias, w_qkv, w_out, w_fc, w_proj, cotangent
):
    width, hidden = tokens.shape[1], w_fc.shape[1]
    blocks, units = w_proj.shape[0] // 128, shards * 128
    span = max(width, units)
    rows = jnp.pad(jnp.stack(vectors), ((0, 0), (0, 128 - vectors[0].shape[0])))
    table = jnp.concatenate(
        [rows, jnp.pad(fc_bias.reshape(blocks, 128), ((0, 8 - blocks), (0, 0)))]
    )
    projected, attended_t, lse, params, full_qkv, full_out, full_fc, full_proj = (
        run_gather_forward(shards, span, tokens, segment_ids, table, w_qkv, w_out, w_fc, w_proj)
    )
    (
        layer_out,
        grad_middle,
        grad_attended,
        grad_out,
        grad_fc,
        grad_proj,
        fc_early,
        proj_early,
        small,
    ) = run_sum_hidden(
        shards, attended_t, tokens, cotangent, params, full_out, full_fc, full_proj, w_fc, w_proj
    )
    grad_tokens, done_qkv, done_out, fc_last, proj_last, small = run_sum_backward(
        shards,
        tokens,
        segment_ids,
        params,
        attended_t,
        lse,
        grad_attended,
        small,
        projected,
        full_qkv,
        grad_middle,
        grad_out,
        grad_fc,
        grad_proj,
    )
    sum_qkv, sum_out, sum_fc, sum_proj, layer_out, grad_tokens, *own_vectors = run_finish(
        shards,
        done_qkv,
        done_out,
        fc_early,
        fc_last,
        proj_early,
        proj_last,
        small,
        layer_out,
        grad_tokens,
    )
    pick = lambda at: own_vectors[at]
    return (
        layer_out,
        grad_tokens,
        pick(GAIN1),
        pick(SHIFT1),
        sum_qkv,
        pick(BIAS_Q),
        pick(BIAS_V),
        sum_out,
        pick(BIAS_OUT),
        pick(GAIN2),
        pick(SHIFT2),
        sum_fc,
        pick(BIAS_FC),
        sum_proj,
        pick(BIAS_PROJ),
    )


def on_device(
    replicas,
    shards,
    tokens,
    segment_ids,
    norm1_gain,
    norm1_shift,
    w_qkv,
    q_bias,
    v_bias,
    w_out,
    out_bias,
    norm2_gain,
    norm2_shift,
    w_fc,
    fc_bias,
    w_proj,
    proj_bias,
    cotangent,
):
    width, hidden = tokens.shape[1], w_fc.shape[1]
    vectors = (
        norm1_gain,
        norm1_shift,
        q_bias,
        v_bias,
        out_bias,
        norm2_gain,
        norm2_shift,
        proj_bias,
    )
    own, own_hidden = norm1_gain.shape[0], fc_bias.shape[0]
    if (
        replicas == 4
        and shards & (shards - 1) == 0
        and own % 96 == 0
        and own_hidden == 3 * 128
        and width == 3 * GROUP
    ):
        return by_kernels(
            shards, tokens, segment_ids, vectors, fc_bias, w_qkv, w_out, w_fc, w_proj, cotangent
        )
    me = lax.axis_index("shard")
    mine = (lax.broadcasted_iota(jnp.int32, (1, shards, 1), 1) == me).astype(bf16)
    table = jnp.concatenate(
        [
            (jnp.stack(vectors)[:, None, :] * mine).reshape(8, width),
            (fc_bias[None, None, :] * mine).reshape(hidden // width, width),
        ]
    )
    table = jnp.pad(table, ((0, 16 - table.shape[0]), (0, 0)))
    gather = partial(lax.all_gather, axis_name="shard", axis=0, tiled=True)
    params = lax.psum(table.astype(f32), "shard")
    full_qkv, full_out, full_fc, full_proj = (gather(w) for w in (w_qkv, w_out, w_fc, w_proj))
    projected, attended_t, lse = run_forward(tokens, segment_ids, params, full_qkv)
    (
        layer_out,
        grad_middle,
        grad_attended,
        grad_w_out,
        grad_w_fc,
        grad_w_proj_t,
        small,
    ) = run_hidden(attended_t, tokens, cotangent, params, full_out, full_fc, full_proj, width)
    grad_tokens, grad_w_qkv, small = run_backward(
        tokens,
        segment_ids,
        params,
        full_qkv,
        projected,
        attended_t,
        lse,
        grad_attended,
        grad_middle,
        small,
    )

    def reduced(grad):
        own_sum = lax.psum_scatter(grad.astype(f32), "shard", scatter_dimension=0, tiled=True)
        return lax.psum(own_sum.astype(bf16), "rep").astype(f32)

    sum_proj = reduced(grad_w_proj_t.transpose(0, 2, 1).reshape(hidden, width))
    sum_fc, sum_out, sum_qkv = reduced(grad_w_fc), reduced(grad_w_out), reduced(grad_w_qkv)
    small = lax.psum(small, ("rep", "shard"))
    mine = lax.dynamic_slice_in_dim(small[:8], me * own, own, 1)
    hidden_rows = small[BIAS_FC : BIAS_FC + hidden // width].reshape(-1)
    mine_fc = lax.dynamic_slice_in_dim(hidden_rows, me * own_hidden, own_hidden, 0)
    return (
        layer_out,
        grad_tokens,
        mine[GAIN1],
        mine[SHIFT1],
        sum_qkv,
        mine[BIAS_Q],
        mine[BIAS_V],
        sum_out,
        mine[BIAS_OUT],
        mine[GAIN2],
        mine[SHIFT2],
        sum_fc,
        mine_fc,
        sum_proj,
        mine[BIAS_PROJ],
    )


def solution(mesh):
    rows, own, own_rows = P(("rep", "shard"), None), P("shard"), P("shard", None)
    in_specs = (
        rows,
        rows,
        own,
        own,
        own_rows,
        own,
        own,
        own_rows,
        own,
        own,
        own,
        own_rows,
        own,
        own_rows,
        own,
        rows,
    )
    out_specs = (
        rows,
        rows,
        own,
        own,
        own_rows,
        own,
        own,
        own_rows,
        own,
        own,
        own,
        own_rows,
        own,
        own_rows,
        own,
    )
    sizes = mesh.shape["rep"], mesh.shape["shard"]
    return jax.shard_map(
        partial(on_device, *sizes), mesh=mesh, in_specs=in_specs, out_specs=out_specs, check_vma=False
    )
```

```python
from functools import partial

import jax
import jax.numpy as jnp
from jax import lax
from jax.experimental import pallas as pl
from jax.experimental.pallas import tpu as pltpu
from jax.sharding import PartitionSpec as P

HEAD = 64
EPSILON = 1e-05
QUERY_BLOCK = 256
ROW_CHUNK = 256
MASKED = -1e30
GELU_SCALE = 0.7978845608028654
GELU_CUBE = 0.044715
VMEM_LIMIT = 62 << 20
NN = (((1,), (0,)), ((), ()))
NT = (((1,), (1,)), ((), ()))
f32 = jnp.float32
bf16 = jnp.bfloat16
WHOLE = pl.BlockSpec(memory_space=pltpu.VMEM)

GAIN1, SHIFT1, BIAS_Q, BIAS_V, BIAS_OUT, GAIN2, SHIFT2, BIAS_PROJ, BIAS_FC = range(9)


def matmul(left, right, dims):
    return lax.dot_general(left, right, dims, preferred_element_type=f32)


def normalized(values):
    centred = values - jnp.mean(values, axis=-1, keepdims=True)
    inverse = lax.rsqrt(jnp.mean(centred * centred, axis=-1, keepdims=True) + EPSILON)
    return centred * inverse, inverse


def norm_pull(grad_normed, gain_row, norm, inverse):
    scaled = grad_normed * gain_row
    return inverse * (
        scaled
        - jnp.mean(scaled, axis=-1, keepdims=True)
        - norm * jnp.mean(scaled * norm, axis=-1, keepdims=True)
    )


def chunk(number):
    return pl.ds(pl.multiple_of(number * ROW_CHUNK, ROW_CHUNK), ROW_CHUNK)


def total(values):
    return jnp.sum(values, axis=0, keepdims=True)


def block(index, size):
    return pl.ds(pl.multiple_of(index * size, size), size)


def build_mask(segment_ref, mask_ref):
    length = segment_ref.shape[1]
    query_seg = segment_ref[...].astype(f32)
    key_seg = jnp.transpose(jnp.broadcast_to(query_seg, (8, length)))[:, 0:1]
    for start in range(0, length, QUERY_BLOCK):
        stop = start + QUERY_BLOCK
        key_at = lax.broadcasted_iota(jnp.int32, (stop, QUERY_BLOCK), 0)
        query_at = lax.broadcasted_iota(jnp.int32, (stop, QUERY_BLOCK), 1) + start
        allowed = (key_seg[0:stop] == query_seg[:, start:stop]) & (key_at <= query_at)
        mask_ref[0:stop, start:stop] = jnp.where(allowed, 0.0, MASKED)


def half_lanes(which):
    lane = lax.broadcasted_iota(jnp.int32, (1, 2 * HEAD), 1)
    return (lane < HEAD) if which == 0 else (lane >= HEAD)


def keep_half(values, which):
    return jnp.where(half_lanes(which), values, jnp.zeros_like(values))


def attend_forward(
    pair, queries, keys, values_t_ref, mask_ref, attended_t_ref, lse_ref, tick=lambda number: None
):
    length = keys.shape[0]
    queries = queries * bf16(HEAD**-0.5)
    for which in range(2):
        tick(which)
        head_queries = keep_half(queries, which)
        rows = block(2 * pair + which, HEAD)
        values_t = values_t_ref[rows, :]
        for start in range(0, length, QUERY_BLOCK):
            stop = start + QUERY_BLOCK
            scores = matmul(keys[0:stop], head_queries[start:stop], NT)
            scores = scores + mask_ref[0:stop, start:stop]
            top = jnp.max(scores, axis=0, keepdims=True)
            terms = jnp.exp(scores - top)
            sums = jnp.sum(terms, axis=0, keepdims=True)
            mixed = matmul(values_t[:, 0:stop], terms.astype(bf16), NN)
            attended_t_ref[rows, start:stop] = (mixed * (1.0 / sums)).astype(bf16)
            lse_ref[pl.ds(2 * pair + which, 1), start:stop] = top + jnp.log(sums)


def attend_backward(
    pair,
    operands,
    keys_t_ref,
    mask_ref,
    lse_ref,
    dots_ref,
    grad_queries_t_ref,
    grad_keys_ref,
    grad_values_ref,
    tick=lambda number: None,
):
    queries, keys, values, grads = operands
    length, scale_by = keys.shape[0], HEAD**-0.5
    queries = queries * bf16(scale_by)
    for number, start in enumerate(reversed(range(0, length, QUERY_BLOCK))):
        tick(number)
        stop = start + QUERY_BLOCK
        grad_keys = grad_values = 0.0
        for which in range(2):
            head = pl.ds(2 * pair + which, 1)
            rows = block(2 * pair + which, HEAD)
            query_rows = keep_half(queries[start:stop], which)
            grad_rows = keep_half(grads[start:stop], which)
            scores = matmul(keys[0:stop], query_rows, NT)
            probs = jnp.exp(scores + mask_ref[0:stop, start:stop] - lse_ref[head, start:stop])
            grad_probs = matmul(values[0:stop], grad_rows, NT)
            grad_scores = (probs * (grad_probs - dots_ref[head, start:stop])).astype(bf16)
            grad_values = grad_values + matmul(probs.astype(bf16), grad_rows, NN)
            grad_keys = grad_keys + matmul(grad_scores, query_rows, NN)
            grad_queries_t_ref[rows, start:stop] = (
                matmul(keys_t_ref[rows, 0:stop], grad_scores, NN) * scale_by
            ).astype(bf16)
        if stop == length:
            grad_keys_ref[...] = grad_keys
            grad_values_ref[...] = grad_values
        else:
            grad_keys_ref[0:stop] += grad_keys
            grad_values_ref[0:stop] += grad_values


MESH = pl.DeviceIdType.MESH
HBM = pl.BlockSpec(memory_space=pl.ANY)


def flip(value, bits):
    bit = 1
    while bit <= bits:
        if bits & bit:
            value = value + bit - 2 * bit * ((value // bit) % 2)
        bit *= 2
    return value


class Place:
    def __init__(self, shards):
        self.lines = shards // 2
        self.rep, self.me = lax.axis_index("rep"), lax.axis_index("shard")
        self.far, self.core = self.rep // 2, self.rep % 2
        self.line, self.side = self.me // 2, self.me % 2

    def shard(self, hop, turn):
        return flip(self.line, hop) * 2 + flip(self.side, turn)

    def peer(self, hop, turn):
        return (self.rep, self.shard(hop, turn))

    def across(self):
        return ((1 - self.far) * 2 + self.core, self.me)

    def sibling(self):
        return (self.far * 2 + 1 - self.core, self.me)

    def others(self):
        return [(h, t) for h in range(self.lines) for t in range(2) if h or t]

    def meet(self, peers):
        barrier = pltpu.get_barrier_semaphore()
        for peer in peers:
            pl.semaphore_signal(barrier, inc=1, device_id=peer, device_id_type=MESH)
        pl.semaphore_wait(barrier, len(peers))


def aligned(start, size):
    return pl.ds(pl.multiple_of(start, 16), size)


def remote(src, dst, send, recv, peer):
    return pltpu.make_async_remote_copy(
        src_ref=src,
        dst_ref=dst,
        send_sem=send,
        recv_sem=recv,
        device_id=peer,
        device_id_type=MESH,
    )


def cut(count):
    half = count // 2
    return half // 3 // 16 * 16, half


class Gather:
    def __init__(self, place, own, full, send, recv, local):
        self.place, self.own, self.full = place, own, full
        self.send, self.recv, self.local = send, recv, local
        self.hops = range(1, place.lines)

    def rows(self, at, kind, far, core):
        edge, half = cut(self.own[at].shape[0])
        if kind == "wide":
            return aligned(core * half + far * edge, half - edge)
        if kind == "edge":
            return aligned(core * half + far * (half - edge), edge)
        return aligned(core * half, half)

    def copy(self, at, stage, hop, turn, arriving=False):
        place, lines = self.place, self.place.lines
        number = hop * 2 + turn
        far, core = place.far, place.core
        if stage == "line":
            slot, peer, kind = hop - 1, place.peer(hop, 0), "wide"
            shard = place.shard(hop if arriving else 0, 0)
        elif stage == "side":
            slot, peer, kind = lines - 1 + hop, place.peer(0, 1), "wide"
            shard = place.shard(hop, 1 if arriving else 0)
        elif stage == "far":
            slot, peer, kind = 2 * lines - 1 + number - 1, place.across(), "edge"
            shard = place.shard(hop, turn)
            far = 1 - far if arriving else far
        else:
            slot, peer, kind = 4 * lines - 2 + number - 1, place.sibling(), "half"
            shard = place.shard(hop, turn)
            core = 1 - core if arriving else core
        rows = self.rows(at, kind, far, core)
        target = self.full[at].at[shard, rows]
        mine = not arriving and (stage == "line" or (stage == "side" and hop == 0))
        source = self.own[at].at[rows] if mine else target
        return remote(source, target, self.send.at[at, slot], self.recv.at[at, slot], peer)

    def start(self, at, stage, hop, turn=0):
        self.copy(at, stage, hop, turn).start()

    def got(self, at, stage, hop, turn=0):
        self.copy(at, stage, hop, turn, arriving=True).wait_recv()

    def keep(self, at):
        return pltpu.make_async_copy(
            self.own[at], self.full[at].at[self.place.me], self.local.at[at]
        )

    def own_side(self, at):
        self.start(at, "side", 0)

    def first(self, at, hop):
        self.start(at, "line", hop)

    def line(self, at, hop):
        self.got(at, "line", hop)
        self.start(at, "side", hop)
        self.start(at, "far", hop, 0)

    def side(self, at, hop):
        self.got(at, "side", hop)
        self.start(at, "far", hop, 1)

    def far(self, at, hop, turn):
        self.got(at, "far", hop, turn)
        self.start(at, "core", hop, turn)

    def last(self, at):
        for hop, turn in self.place.others():
            self.got(at, "core", hop, turn)
        self.keep(at).wait()

    def drain(self, at):
        for hop in self.hops:
            self.copy(at, "line", hop, 0).wait_send()
        for hop in range(self.place.lines):
            self.copy(at, "side", hop, 0).wait_send()
        for hop, turn in self.place.others():
            self.copy(at, "far", hop, turn).wait_send()
            self.copy(at, "core", hop, turn).wait_send()


def add_into(into, other):
    into[...] = (into[...].astype(f32) + other[...].astype(f32)).astype(bf16)


class Summed:
    def __init__(self, place, grad, done, buffers, send, recv, source=None, load_sem=None):
        self.place, self.grad, self.done = place, grad, done
        self.send_sem, self.recv_sem = send, recv
        self.source = grad if source is None else source
        self.load_sem = load_sem
        (
            self.from_core,
            self.from_far,
            self.from_side,
            self.from_me,
            self.from_line,
            self.from_back,
        ) = buffers
        self.edge_size, self.half = cut(grad.shape[1])
        self.hops = range(1, place.lines)

    def rows(self, kind, far=None, core=None):
        far = self.place.far if far is None else far
        core = self.place.core if core is None else core
        edge, half = self.edge_size, self.half
        if kind == "wide":
            return aligned(core * half + far * edge, half - edge)
        if kind == "edge":
            return aligned(core * half + far * (half - edge), edge)
        return aligned(core * half, half)

    def pair_of(self, hop):
        return pl.ds(2 * flip(self.place.line, hop), 2)

    def copy(self, stage, hop=0):
        place, lines, grad = self.place, self.place.lines, self.grad
        if stage == "core":
            slot, peer = 0, place.sibling()
            pair = self.source.at[:, self.rows("half", core=1 - place.core)], self.from_core
        elif stage == "far":
            slot, peer = hop, place.across()
            pair = (
                grad.at[self.pair_of(hop), self.rows("edge", far=1 - place.far)],
                self.from_far.at[hop - 1],
            )
        elif stage == "side":
            slot, peer = lines + hop, place.peer(0, 1)
            source = grad.at[place.shard(hop, 1), self.rows("wide" if hop else "half")]
            pair = source, self.from_side.at[hop - 1] if hop else self.from_me
        elif stage == "line":
            slot, peer = 2 * lines + hop - 1, place.peer(hop, 0)
            pair = grad.at[place.shard(hop, 0), self.rows("wide")], self.from_line.at[hop - 1]
        elif stage == "back":
            slot, peer = 3 * lines - 1, place.across()
            pair = grad.at[place.me, self.rows("half")], self.from_back
        else:
            slot, peer = 3 * lines, place.sibling()
            mine = self.done.at[self.rows("half")]
            pair = mine, mine
        return remote(*pair, self.send_sem.at[slot], self.recv_sem.at[slot], peer)

    def load(self):
        rows = self.rows("half")
        return pltpu.make_async_copy(
            self.source.at[:, rows], self.grad.at[:, rows], self.load_sem
        )

    def begin(self):
        self.copy("core").start()
        if self.load_sem is not None:
            self.load().start()

    def core(self):
        self.copy("core").wait_recv()
        if self.load_sem is not None:
            self.load().wait()
        for shard in range(2 * self.place.lines):
            add_into(self.grad.at[shard, self.rows("half")], self.from_core.at[shard])

    def me0(self):
        self.copy("side", 0).start()

    def send(self, hop):
        self.copy("far", hop).start()

    def far(self, hop):
        self.copy("far", hop).wait_recv()
        add_into(self.grad.at[self.pair_of(hop), self.rows("edge")], self.from_far.at[hop - 1])
        self.copy("side", hop).start()

    def side(self, hop):
        self.copy("side", hop).wait_recv()
        mine = self.grad.at[self.place.shard(hop, 0), self.rows("wide")]
        add_into(mine, self.from_side.at[hop - 1])
        self.copy("line", hop).start()

    def me(self):
        self.copy("side", 0).wait_recv()
        add_into(self.grad.at[self.place.me, self.rows("half")], self.from_me)

    def lines(self):
        mine = self.grad.at[self.place.me, self.rows("wide")]
        sums = mine[...].astype(f32)
        for hop in self.hops:
            self.copy("line", hop).wait_recv()
            sums = sums + self.from_line[hop - 1].astype(f32)
        mine[...] = sums.astype(bf16)
        self.copy("back").start()

    def back(self):
        self.copy("back").wait_recv()
        mine = self.grad[self.place.me, self.rows("half")].astype(f32)
        self.done[self.rows("half")] = (mine + self.from_back[...].astype(f32)).astype(bf16)
        self.copy("pair").start()

    def finish(self):
        other = self.done.at[self.rows("half", core=1 - self.place.core)]
        slot = 3 * self.place.lines
        remote(
            other, other, self.send_sem.at[slot], self.recv_sem.at[slot], self.place.sibling()
        ).wait_recv()

    def drain(self):
        self.copy("core").wait_send()
        for hop in self.hops:
            self.copy("far", hop).wait_send()
            self.copy("line", hop).wait_send()
        for hop in range(self.place.lines):
            self.copy("side", hop).wait_send()
        self.copy("back").wait_send()
        self.copy("pair").wait_send()


SUM_BUFFERS = 6


def sum_buffers(lines, shards, rows, columns):
    edge, half = cut(rows)
    return [
        pltpu.VMEM((shards, half, columns), bf16),
        pltpu.VMEM((lines - 1, 2, edge, columns), bf16),
        pltpu.VMEM((lines - 1, half - edge, columns), bf16),
        pltpu.VMEM((half, columns), bf16),
        pltpu.VMEM((lines - 1, half - edge, columns), bf16),
        pltpu.VMEM((half, columns), bf16),
    ]


def sum_sems(lines, items):
    return [pltpu.SemaphoreType.DMA((items, 3 * lines + 1))] * 2


def first_norm(tokens_ref, params_ref, normed_ref):
    length, width = tokens_ref.shape
    row = lambda at: params_ref[at : at + 1, 0:width]

    @pl.loop(0, length // ROW_CHUNK)
    def _(number):
        norm, _ = normalized(tokens_ref[chunk(number)].astype(f32))
        normed_ref[chunk(number)] = (norm * row(GAIN1) + row(SHIFT1)).astype(bf16)


def forward_kernel(
    tokens_ref,
    segment_ref,
    params_ref,
    w_qkv_ref,
    projected_ref,
    attended_t_ref,
    lse_ref,
    mask_ref,
    normed_ref,
    values_t_ref,
):
    length, width = tokens_ref.shape
    pairs = width // (2 * HEAD)
    row = lambda at: params_ref[at : at + 1, 0:width]
    first_norm(tokens_ref, params_ref, normed_ref)
    for part, bias in enumerate((row(BIAS_Q), 0.0, row(BIAS_V))):
        columns = slice(part * width, (part + 1) * width)
        projected_ref[:, columns] = (
            matmul(normed_ref[...], w_qkv_ref[:, columns], NN) + bias
        ).astype(bf16)
    values_t_ref[...] = jnp.transpose(projected_ref[:, 2 * width :])
    build_mask(segment_ref, mask_ref)

    @pl.loop(0, pairs)
    def _(pair):
        attend_forward(
            pair,
            projected_ref[:, block(pair, 2 * HEAD)],
            projected_ref[:, block(pairs + pair, 2 * HEAD)],
            values_t_ref,
            mask_ref,
            attended_t_ref,
            lse_ref,
        )


GROUP = 4 * HEAD
GATHERED_EARLY = 1
SUMMED_EARLY = 1


(
    OWN,
    FIRST,
    LINE,
    SIDE,
    FAR,
    LAST,
    BEGIN_SUM,
    CORE_SUM,
    ME0_SUM,
    SEND_SUM,
    FAR_SUM,
    SIDE_SUM,
    ME_SUM,
    LINES_SUM,
    BACK_SUM,
    FINISH_SUM,
) = range(16)
P0, P1, P2, H0, H1, H2, H3, E0, E1, E2, E3, B0, B1, B2, B3, NEED, END = range(100, 117)

FORWARD_PLAN = {P0: [(OWN, 0), (FIRST, 0, 1)],
 P1: [(FIRST, 0, 3), (OWN, 1)],
 P2: [(FIRST, 0, 2), (LINE, 0, 1), (SIDE, 0, 0)],
 END: [(LAST, 5)],
 NEED: {0: [(FIRST, 1, 1), (SIDE, 1, 0), (OWN, 2), (OWN, 3), (FIRST, 1, 3), (LINE, 0, 3), (FIRST, 1, 2),
            (FAR, 0, 1, 0), (FAR, 0, 0, 1), (FAR, 1, 0, 1), (OWN, 4), (SIDE, 0, 1), (FAR, 0, 3, 0),
            (FIRST, 2, 1), (LINE, 1, 1), (SIDE, 2, 0), (SIDE, 3, 0), (LINE, 0, 2), (FAR, 0, 1, 1),
            (FIRST, 2, 3), (SIDE, 0, 3), (FIRST, 2, 2), (OWN, 5), (FAR, 1, 1, 0), (FAR, 2, 0, 1),
            (LINE, 1, 3), (SIDE, 4, 0), (FIRST, 3, 1), (FAR, 3, 0, 1), (FAR, 0, 2, 0), (SIDE, 1, 1),
            (FAR, 0, 3, 1), (LINE, 1, 2), (FIRST, 3, 3), (SIDE, 0, 2), (LINE, 2, 1), (FIRST, 3, 2),
            (FAR, 1, 3, 0), (FAR, 4, 0, 1), (SIDE, 5, 0), (FAR, 1, 1, 1), (SIDE, 1, 3), (LINE, 2, 3),
            (FAR, 1, 2, 0), (FIRST, 4, 1), (LINE, 2, 2), (FAR, 0, 2, 1), (FAR, 2, 1, 0), (SIDE, 1, 2),
            (LINE, 3, 1), (SIDE, 2, 1), (FIRST, 4, 3), (FAR, 5, 0, 1), (LAST, 0)]},
 0: {0: [(FIRST, 4, 2)],
     1: [(LAST, 1), (LINE, 4, 1), (FIRST, 5, 3)],
     2: [(FAR, 2, 2, 1), (FAR, 2, 3, 1), (SIDE, 3, 2), (SIDE, 3, 3), (FAR, 3, 2, 0), (FAR, 3, 3, 0),
         (FAR, 3, 1, 1), (LINE, 4, 2), (SIDE, 4, 1), (FAR, 4, 1, 0), (FAR, 4, 3, 0)],
     3: [(SIDE, 4, 2), (LINE, 5, 2), (FAR, 3, 2, 1)],
     4: [(LAST, 3), (FAR, 4, 2, 1), (SIDE, 5, 2), (FAR, 5, 2, 0), (FAR, 5, 3, 0), (FAR, 5, 1, 1)],
     5: [(LAST, 4), (FAR, 5, 2, 1)]},
 1: {0: [(FAR, 1, 2, 1), (FAR, 1, 3, 1), (SIDE, 2, 2), (SIDE, 2, 3), (FAR, 2, 2, 0), (FAR, 2, 3, 0),
         (FAR, 2, 1, 1), (LINE, 3, 2), (SIDE, 3, 1), (FAR, 3, 1, 0), (LINE, 3, 3), (FIRST, 5, 1)],
     1: [(LINE, 4, 3), (FIRST, 5, 2)],
     2: [(SIDE, 4, 3), (LAST, 2), (LINE, 5, 1)],
     3: [(FAR, 3, 3, 1), (FAR, 4, 2, 0), (FAR, 4, 1, 1), (FAR, 4, 3, 1), (LINE, 5, 3), (FAR, 5, 1, 0),
         (SIDE, 5, 1)],
     4: [(SIDE, 5, 3)],
     5: [(FAR, 5, 3, 1)]}}

HIDDEN_PLAN = {H0: [(OWN, 0), (FIRST, 0, 1), (FIRST, 0, 3)],
 H1: [(FIRST, 0, 2), (OWN, 1)],
 H2: [(LINE, 0, 1), (SIDE, 0, 0), (FIRST, 1, 1)],
 H3: [(FIRST, 1, 3), (OWN, 2)],
 E0: [(FINISH_SUM, 0)],
 E3: [(BACK_SUM, 1)],
 END: [(FINISH_SUM, 1)],
 1: {0: [(LINE, 0, 3), (FAR, 0, 1, 0), (FIRST, 1, 2), (SIDE, 1, 0)],
     1: [(SIDE, 2, 2), (FAR, 2, 2, 0), (LINE, 3, 3), (SEND_SUM, 1, 3)]},
 2: {0: [(LINE, 0, 2), (SIDE, 0, 1), (FAR, 0, 0, 1)],
     1: [(LINE, 3, 2), (SIDE, 3, 1)],
     2: [(LINES_SUM, 0), (SIDE_SUM, 1, 2), (SIDE_SUM, 1, 1)]},
 3: {0: [(FAR, 0, 3, 0), (LINE, 1, 1), (FIRST, 2, 1), (SIDE, 2, 0)],
     1: [(FAR, 2, 2, 1), (FAR, 2, 3, 1), (FAR, 3, 1, 0), (FAR_SUM, 0, 2), (SIDE_SUM, 0, 3),
         (SEND_SUM, 1, 2)]},
 4: {0: [(SIDE, 0, 3), (FAR, 0, 2, 0), (FAR, 1, 0, 1), (FIRST, 2, 3), (OWN, 3)],
     1: [(SIDE, 3, 3), (FAR, 3, 3, 0), (FAR_SUM, 0, 1), (SEND_SUM, 1, 1)]},
 5: {0: [(SIDE, 0, 2), (FAR, 0, 1, 1), (FAR, 1, 1, 0), (FIRST, 2, 2), (BEGIN_SUM, 0)],
     1: [(LAST, 2), (SIDE, 3, 2), (FAR, 3, 2, 0), (FAR, 3, 1, 1), (ME0_SUM, 1)]},
 6: {0: [(LINE, 1, 3), (SIDE, 1, 1), (FAR, 2, 0, 1), (FIRST, 3, 1), (BEGIN_SUM, 1)],
     1: [(SIDE_SUM, 0, 2), (FAR_SUM, 1, 3)],
     2: [(BACK_SUM, 0)]},
 7: {0: [(FAR, 0, 3, 1), (LINE, 1, 2), (SIDE, 3, 0)],
     1: [(FAR, 3, 3, 1), (SIDE_SUM, 0, 1), (FAR_SUM, 1, 2)],
     2: [(LINES_SUM, 1)]},
 NEED: {1: [(FAR, 0, 2, 1), (FAR, 1, 3, 0), (FAR, 1, 1, 1), (LINE, 2, 1), (FIRST, 3, 3), (CORE_SUM, 0),
            (SEND_SUM, 0, 3), (CORE_SUM, 1), (SIDE, 1, 3), (FAR, 1, 2, 0), (ME0_SUM, 0), (LAST, 0),
            (FAR, 3, 0, 1), (SEND_SUM, 0, 2), (SIDE, 1, 2), (FAR, 2, 1, 0), (FIRST, 3, 2), (LINE, 2, 3),
            (SIDE, 2, 1), (FAR, 1, 3, 1), (LINE, 2, 2), (SEND_SUM, 0, 1), (ME_SUM, 0), (LINE, 3, 1),
            (FAR, 1, 2, 1), (SIDE, 2, 3), (FAR, 2, 3, 0), (FAR_SUM, 0, 3), (LAST, 1), (FAR, 2, 1, 1)],
        2: [(FAR, 3, 2, 1), (FAR_SUM, 1, 1), (ME_SUM, 1), (SIDE_SUM, 1, 3), (LAST, 3)]}}

BACKWARD_PLAN = {B0: [(BEGIN_SUM, 0), (BEGIN_SUM, 1), (BEGIN_SUM, 2), (BEGIN_SUM, 3), (BEGIN_SUM, 4)],
 B2: [(CORE_SUM, 0), (ME0_SUM, 0), (SEND_SUM, 0, 3), (SEND_SUM, 0, 2)],
 B3: [(SEND_SUM, 0, 1), (CORE_SUM, 1), (ME0_SUM, 1)],
 E0: [(SIDE_SUM, 4, 1), (FAR_SUM, 6, 3), (FAR_SUM, 6, 2), (BEGIN_SUM, 7)],
 E1: [(BACK_SUM, 2), (SIDE_SUM, 5, 3), (FAR_SUM, 6, 1)],
 E2: [(FINISH_SUM, 2), (LINES_SUM, 3), (SIDE_SUM, 5, 2), (ME_SUM, 6), (CORE_SUM, 7), (ME0_SUM, 7),
      (SEND_SUM, 7, 3)],
 E3: [(SIDE_SUM, 5, 1), (SEND_SUM, 7, 2)],
 END: [(SIDE_SUM, 6, 3), (SEND_SUM, 7, 1), (BACK_SUM, 3), (ME_SUM, 7), (LINES_SUM, 4), (SIDE_SUM, 6, 2),
       (FAR_SUM, 7, 3), (FINISH_SUM, 3), (FAR_SUM, 7, 2), (SIDE_SUM, 6, 1), (FAR_SUM, 7, 1), (SIDE_SUM, 7, 3),
       (BACK_SUM, 4), (SIDE_SUM, 7, 2), (LINES_SUM, 5), (FINISH_SUM, 4), (SIDE_SUM, 7, 1), (BACK_SUM, 5),
       (FINISH_SUM, 5), (LINES_SUM, 6), (LINES_SUM, 7), (BACK_SUM, 6), (FINISH_SUM, 6), (BACK_SUM, 7),
       (FINISH_SUM, 7)],
 1: {0: [(FAR_SUM, 0, 3), (SEND_SUM, 1, 3), (CORE_SUM, 2), (ME_SUM, 0), (SEND_SUM, 1, 2), (ME0_SUM, 2),
         (CORE_SUM, 3)],
     1: [(FAR_SUM, 0, 1), (FAR_SUM, 1, 3), (SEND_SUM, 2, 2)],
     2: [(SIDE_SUM, 1, 3), (SIDE_SUM, 1, 2), (FAR_SUM, 2, 2), (SEND_SUM, 3, 1), (SEND_SUM, 4, 3)],
     3: [(SIDE_SUM, 2, 3), (FAR_SUM, 3, 3), (SEND_SUM, 4, 1)],
     4: [(FINISH_SUM, 0), (LINES_SUM, 1), (SIDE_SUM, 3, 3), (FAR_SUM, 4, 3), (FAR_SUM, 4, 2)],
     5: [(BACK_SUM, 1), (SIDE_SUM, 3, 1), (FAR_SUM, 5, 3), (FAR_SUM, 5, 2)]},
 2: {0: [(SEND_SUM, 1, 1), (CORE_SUM, 4), (ME_SUM, 1), (FAR_SUM, 0, 2)],
     1: [(FAR_SUM, 1, 2), (SEND_SUM, 2, 1), (ME_SUM, 2)],
     2: [(FAR_SUM, 2, 1), (SEND_SUM, 4, 2), (CORE_SUM, 5), (SIDE_SUM, 1, 1)],
     3: [(FAR_SUM, 3, 2), (SEND_SUM, 5, 3)],
     4: [(FAR_SUM, 4, 1), (CORE_SUM, 6), (SEND_SUM, 6, 3), (SEND_SUM, 6, 2), (SIDE_SUM, 3, 2)],
     5: [(FINISH_SUM, 1), (LINES_SUM, 2), (SIDE_SUM, 4, 3), (FAR_SUM, 5, 1)]},
 3: {0: [(SEND_SUM, 2, 3)],
     1: [(SIDE_SUM, 0, 2), (SEND_SUM, 3, 3)],
     2: [(LINES_SUM, 0), (ME0_SUM, 3)],
     3: [(SIDE_SUM, 2, 2), (FAR_SUM, 3, 1), (SEND_SUM, 5, 2)],
     4: [(ME_SUM, 4), (ME0_SUM, 5), (SEND_SUM, 6, 1)],
     5: [(ME_SUM, 5), (SIDE_SUM, 4, 2), (ME0_SUM, 6)]},
 0: {1: [(SIDE_SUM, 0, 3)],
     2: [(SIDE_SUM, 0, 1), (FAR_SUM, 1, 1), (FAR_SUM, 2, 3), (SEND_SUM, 3, 2), (BEGIN_SUM, 5)],
     4: [(BACK_SUM, 0), (SIDE_SUM, 2, 1), (ME_SUM, 3), (ME0_SUM, 4), (SEND_SUM, 5, 1), (BEGIN_SUM, 6)]}}


class Runner:
    def __init__(self, plan, gather, sums):
        self.plan, self.gather, self.sums = plan, gather, sums

    def act(self, events):
        gather = self.gather
        for what, item, *where in events:
            if what >= BEGIN_SUM:
                one = self.sums[item]
                acts = (
                    one.begin,
                    one.core,
                    one.me0,
                    one.send,
                    one.far,
                    one.side,
                    one.me,
                    one.lines,
                    one.back,
                    one.finish,
                )
                acts[what - BEGIN_SUM](*where)
            else:
                acts = (
                    gather.own_side,
                    gather.first,
                    gather.line,
                    gather.side,
                    gather.far,
                    gather.last,
                )
                acts[what](item, *where)

    def do(self, key):
        self.act(self.plan.get(key, ()))

    def at_step(self, step, key):
        self.on(step, self.plan.get(key, {}))

    def on(self, step, table):
        for number, events in table.items():

            @pl.when(step == number)
            def _(events=events):
                self.act(events)


def gather_forward_kernel(
    shards,
    tokens_ref,
    segment_ref,
    own_params_ref,
    own_qkv_ref,
    own_out_ref,
    own_fc_ref,
    own_proj_ref,
    projected_ref,
    attended_t_ref,
    lse_ref,
    params_ref,
    full_qkv_ref,
    full_out_ref,
    full_fc_ref,
    full_proj_ref,
    mask_ref,
    normed_ref,
    values_t_ref,
    held_ref,
    weights_ref,
    tables_ref,
    group_ref,
    own_block_ref,
    own_rows_ref,
    own_units_ref,
    send_sem,
    recv_sem,
    local_sem,
    params_send_sem,
    params_recv_sem,
    load_sem,
    out_sem,
):
    length, width = tokens_ref.shape
    groups = width // GROUP
    blocks = full_fc_ref.shape[0]
    place = Place(shards)
    others = place.others()
    own = [group_ref.at[g] for g in range(groups)] + [own_rows_ref]
    full = [weights_ref.at[g] for g in range(groups)] + [full_out_ref]
    for number in range(blocks):
        own += [own_block_ref.at[number], own_units_ref.at[number * 128 : number * 128 + 128]]
        full += [full_fc_ref.at[number], full_proj_ref.at[number]]
    gather = Gather(place, own, full, send_sem, recv_sem, local_sem)

    def move(source, target, number):
        pltpu.make_async_copy(source, target, load_sem.at[number]).start()

    def moved(whole, number):
        pltpu.make_async_copy(whole, whole, load_sem.at[number]).wait()

    for g in range(groups):
        for part in range(3):
            start = part * width + g * GROUP
            move(
                own_qkv_ref.at[:, start : start + GROUP],
                group_ref.at[g, :, part * GROUP : (part + 1) * GROUP],
                g,
            )
    for number in range(blocks):
        take_block(
            move, own_fc_ref, number, shards, own_block_ref.at[number], groups + number
        )
    move(own_out_ref, own_rows_ref, groups + blocks)
    move(own_proj_ref.at[0 : blocks * 128], own_units_ref, groups + blocks + 1)
    place.meet([place.peer(*other) for other in others] + [place.across(), place.sibling()])

    def table(number, other, arriving):
        target = tables_ref.at[place.shard(*other) if arriving else place.me]
        return remote(
            target if arriving else own_params_ref,
            target,
            params_send_sem.at[number],
            params_recv_sem.at[number],
            place.peer(*other),
        )

    for number, other in enumerate(others):
        table(number, other, False).start()
    runner = Runner(FORWARD_PLAN, gather, ())

    def outward(g):
        return (
            pltpu.make_async_copy(held_ref.at[g], projected_ref.at[g], out_sem.at[g, 0]),
            pltpu.make_async_copy(weights_ref.at[g], full_qkv_ref.at[g], out_sem.at[g, 1]),
        )

    for g in range(groups):
        moved(group_ref.at[g], g)
        runner.act([event for event in FORWARD_PLAN[P0] if event[1] == g])
    moved(own_rows_ref, groups + blocks)
    moved(own_units_ref, groups + blocks + 1)
    runner.act([event for event in FORWARD_PLAN[P0] if event[1] >= groups])
    for g in range(groups):
        gather.keep(g).start()
    for number in range(blocks):
        moved(own_block_ref.at[number], groups + number)
    for at in range(groups, groups + 1 + 2 * blocks):
        gather.keep(at).start()
    tables_ref[place.me] = own_params_ref[...]
    build_mask(segment_ref, mask_ref)
    runner.do(P1)
    for number, other in enumerate(others):
        table(number, other, True).wait_recv()
    spread_params(shards, width // shards, tables_ref, params_ref)
    first_norm(tokens_ref, params_ref, normed_ref)
    runner.do(P2)

    @pl.loop(0, 2 * groups)
    def _(pair):
        g, odd = pair // 2, pair % 2
        runner.at_step(pair, NEED)

        @pl.when(odd == 0)
        def _():
            part = block(g, GROUP)
            weights = weights_ref[g].reshape(width, 3 * GROUP)
            values = matmul(normed_ref[...], weights, NN)
            bias = jnp.concatenate(
                [
                    params_ref[BIAS_Q : BIAS_Q + 1, part],
                    jnp.zeros((1, GROUP), f32),
                    params_ref[BIAS_V : BIAS_V + 1, part],
                ],
                axis=1,
            )
            held_ref[g] = (values + bias).astype(bf16)
            values_t_ref[part, :] = jnp.transpose(held_ref[g, :, 2 * GROUP :])
            for copy in outward(g):
                copy.start()

        attend_forward(
            pair,
            held_ref[g, :, block(odd, 2 * HEAD)],
            held_ref[g, :, block(2 + odd, 2 * HEAD)],
            values_t_ref,
            mask_ref,
            attended_t_ref,
            lse_ref,
            lambda which: runner.at_step(pair, which),
        )

    runner.do(END)
    for g in range(groups):
        for copy in outward(g):
            copy.wait()
    for at in range(groups + 1 + 2 * blocks):
        gather.drain(at)
    for number, other in enumerate(others):
        table(number, other, False).wait_send()


def spread_params(shards, own, tables_ref, params_ref):
    span = params_ref.shape[1]
    lane = lax.broadcasted_iota(jnp.int32, (128, span), 0)
    column = lax.broadcasted_iota(jnp.int32, (128, span), 1)
    narrow = wide = 0.0
    for shard in range(shards):
        values = tables_ref[shard]
        place = (column == lane + shard * own) & (lane < own)
        narrow = narrow + matmul(values, place.astype(f32).astype(bf16), NN)
        place = column == lane + shard * 128
        wide = wide + matmul(values, place.astype(f32).astype(bf16), NN)
    params_ref[0:8] = narrow[0:8]
    params_ref[8:16] = wide[8:16]


def take_block(move, own_fc_ref, number, shards, target_ref, sem):
    own = own_fc_ref.shape[1] // shards
    for shard in range(shards):
        start = shard * own + number * 128
        move(
            own_fc_ref.at[:, start : start + 128],
            target_ref.at[:, shard * 128 : (shard + 1) * 128],
            sem,
        )


def hidden_kernel(
    attended_t_ref,
    tokens_ref,
    cotangent_ref,
    params_ref,
    w_out_ref,
    w_fc_ref,
    w_proj_ref,
    layer_out_ref,
    grad_middle_ref,
    grad_attended_ref,
    grad_w_out_ref,
    grad_w_fc_ref,
    grad_w_proj_t_ref,
    small_ref,
    middle_ref,
    normed_ref,
    normed_t_ref,
    cotangent_t_ref,
    mixed_ref,
    grad_normed_ref,
    activated_ref,
    grad_preact_ref,
):
    step, steps = pl.program_id(0), pl.num_programs(0)
    length, width = tokens_ref.shape
    row = lambda at: params_ref[at : at + 1, :]
    chunks = [slice(at, at + ROW_CHUNK) for at in range(0, length, ROW_CHUNK)]

    @pl.when(step == 0)
    def _():
        attended = jnp.transpose(attended_t_ref[...])
        middle_ref[...] = (
            tokens_ref[...].astype(f32) + matmul(attended, w_out_ref[...], NN) + row(BIAS_OUT)
        )
        for rows in chunks:
            norm, _ = normalized(middle_ref[rows])
            normed_ref[rows] = (norm * row(GAIN2) + row(SHIFT2)).astype(bf16)
        normed_t_ref[...] = jnp.transpose(normed_ref[...])
        cotangent_t_ref[...] = jnp.transpose(cotangent_ref[...])
        mixed_ref[...] = jnp.zeros_like(mixed_ref)
        grad_normed_ref[...] = jnp.zeros_like(grad_normed_ref)
        small_ref[...] = jnp.zeros_like(small_ref)

    bias_sum = 0.0
    bias_row = params_ref[pl.ds(BIAS_FC + step, 1), :]
    for rows in chunks:
        preact = matmul(normed_ref[rows], w_fc_ref[...], NN) + bias_row
        grad_act = matmul(cotangent_ref[rows], w_proj_ref[...], NT)
        square = preact * preact
        bend = jnp.tanh(GELU_SCALE * preact * (1.0 + GELU_CUBE * square))
        gate = 0.5 + 0.5 * bend
        activated_ref[rows] = (preact * gate).astype(bf16)
        slope = gate + (0.5 * GELU_SCALE) * preact * (1.0 - bend * bend) * (
            1.0 + (3 * GELU_CUBE) * square
        )
        grad_preact = (slope * grad_act).astype(bf16)
        grad_preact_ref[rows] = grad_preact
        bias_sum = bias_sum + total(grad_preact.astype(f32))
    small_ref[pl.ds(BIAS_FC + step, 1), :] = bias_sum
    mixed_ref[...] += matmul(activated_ref[...], w_proj_ref[...], NN)
    grad_w_proj_t = matmul(cotangent_t_ref[...], activated_ref[...], NN).astype(bf16)
    pieces, _, piece = grad_w_proj_t_ref.shape
    for at in range(pieces):
        grad_w_proj_t_ref[at] = grad_w_proj_t[:, at * piece : (at + 1) * piece]
    grad_w_fc_ref[...] = matmul(normed_t_ref[...], grad_preact_ref[...], NN).astype(bf16)
    grad_normed_ref[...] += matmul(grad_preact_ref[...], w_fc_ref[...], NT)

    @pl.when(step == steps - 1)
    def _():
        sums = [0.0] * 4
        for rows in chunks:
            middle = middle_ref[rows]
            layer_out_ref[rows] = (middle + mixed_ref[rows] + row(BIAS_PROJ)).astype(bf16)
            norm, inverse = normalized(middle)
            grad_normed = grad_normed_ref[rows]
            cotangent = cotangent_ref[rows].astype(f32)
            grad_middle = cotangent + norm_pull(grad_normed, row(GAIN2), norm, inverse)
            grad_middle_ref[rows] = grad_middle
            normed_ref[rows] = grad_middle.astype(bf16)
            terms = (grad_middle, grad_normed * norm, grad_normed, cotangent)
            sums = [a + total(b) for a, b in zip(sums, terms)]
        for at, value in zip((BIAS_OUT, GAIN2, SHIFT2, BIAS_PROJ), sums):
            small_ref[at : at + 1, :] = value
        grad_branch = normed_ref[...]
        grad_w_out_ref[...] = matmul(attended_t_ref[...], grad_branch, NN).astype(bf16)
        grad_attended_ref[...] = matmul(grad_branch, w_out_ref[...], NT).astype(bf16)


def sum_hidden_kernel(
    shards,
    attended_t_in_ref,
    tokens_in_ref,
    cotangent_in_ref,
    params_ref,
    w_out_in_ref,
    fc_in_ref,
    proj_in_ref,
    own_fc_ref,
    own_proj_ref,
    layer_out_ref,
    grad_middle_ref,
    grad_attended_out_ref,
    grad_out_out_ref,
    last_fc_ref,
    last_proj_ref,
    done_fc_ref,
    done_proj_ref,
    small_ref,
    middle_ref,
    normed_ref,
    normed_t_ref,
    cotangent_t_ref,
    mixed_ref,
    grad_normed_ref,
    activated_ref,
    grad_preact_ref,
    fc_ref,
    proj_ref,
    grad_fc_ref,
    grad_proj_ref,
    own_block_ref,
    attended_t_ref,
    tokens_ref,
    cotangent_ref,
    w_out_ref,
    layer_ref,
    grad_attended_ref,
    grad_out_ref,
    *rest,
):
    length, width = tokens_ref.shape
    blocks = fc_ref.shape[0]
    units = fc_ref.shape[3]
    early = fc_in_ref.shape[0]
    summed = done_fc_ref.shape[0]
    buffers, rest = [rest[SUM_BUFFERS * k :][:SUM_BUFFERS] for k in range(2 * summed)], rest[
        SUM_BUFFERS * 2 * summed :
    ]
    send_sem, recv_sem, local_sem, load_sem, sum_send_sem, sum_recv_sem = rest
    row = lambda at: params_ref[at : at + 1, 0:width]
    chunks = [slice(at, at + ROW_CHUNK) for at in range(0, length, ROW_CHUNK)]
    place = Place(shards)

    def move(source, target, number):
        pltpu.make_async_copy(source, target, load_sem.at[number]).start()

    def moved(whole, number):
        pltpu.make_async_copy(whole, whole, load_sem.at[number]).wait()

    own, full = [], []
    for number in range(early, blocks):
        own_block = own_block_ref.at[number - early]
        take_block(move, own_fc_ref, number, shards, own_block, number)
        own += [own_block, own_proj_ref.at[number * 128 : number * 128 + 128]]
        full += [fc_ref.at[number], proj_ref.at[number]]
    inputs = (
        (attended_t_in_ref, attended_t_ref),
        (w_out_in_ref, w_out_ref),
        (tokens_in_ref, tokens_ref),
        (cotangent_in_ref, cotangent_ref),
    )
    for number, pair in enumerate(inputs):
        move(*pair, 2 * blocks + number)
    for number in range(early):
        move(fc_in_ref.at[number], fc_ref.at[number], number)
        move(proj_in_ref.at[number], proj_ref.at[number], blocks + number)
    gather = Gather(place, own, full, send_sem, recv_sem, local_sem)
    sums = []
    for number in range(summed):
        for grad, done in ((grad_proj_ref, done_proj_ref), (grad_fc_ref, done_fc_ref)):
            k = len(sums)
            sums.append(
                Summed(
                    place,
                    grad.at[number],
                    done.at[number],
                    buffers[k],
                    sum_send_sem.at[k],
                    sum_recv_sem.at[k],
                )
            )
    runner = Runner(HIDDEN_PLAN, gather, sums)
    place.meet(
        [place.peer(hop, 0) for hop in range(1, place.lines)]
        + [place.peer(0, 1), place.across(), place.sibling()]
    )
    for number in range(early, blocks):
        moved(own_block_ref.at[number - early], number)
    runner.do(H0)
    for at in range(len(own)):
        gather.keep(at).start()

    for number, pair in enumerate(inputs):
        moved(pair[1], 2 * blocks + number)
    attended = jnp.transpose(attended_t_ref[...])
    w_out = w_out_ref[...].reshape(width, width)
    middle_ref[...] = tokens_ref[...].astype(f32) + matmul(attended, w_out, NN) + row(BIAS_OUT)
    runner.do(H1)

    @pl.loop(0, len(chunks))
    def _(number):
        norm, _ = normalized(middle_ref[chunk(number)])
        normed_ref[chunk(number)] = (norm * row(GAIN2) + row(SHIFT2)).astype(bf16)

    runner.do(H2)
    normed_t_ref[...] = jnp.transpose(normed_ref[...])
    cotangent_t_ref[...] = jnp.transpose(cotangent_ref[...])
    mixed_ref[...] = jnp.zeros_like(mixed_ref)
    grad_normed_ref[...] = jnp.zeros_like(grad_normed_ref)
    small_ref[...] = jnp.zeros_like(small_ref)
    for number in range(early):
        moved(fc_ref.at[number], number)
        moved(proj_ref.at[number], blocks + number)
    runner.do(H3)

    table = {
        step * len(chunks) + tick: events
        for tick in range(len(chunks))
        for step, events in HIDDEN_PLAN.get(tick, {}).items()
    }

    @pl.loop(0, blocks)
    def _(step):
        runner.at_step(step, NEED)
        w_fc = fc_ref.at[step]
        w_proj = proj_ref.at[step]
        bias_row = params_ref[pl.ds(BIAS_FC + step, 1), 0:units]

        @pl.loop(0, len(chunks))
        def _(number):
            runner.on(step * len(chunks) + number, table)
            rows = chunk(number)
            preact = matmul(normed_ref[rows], w_fc[...].reshape(width, units), NN) + bias_row
            grad_act = matmul(cotangent_ref[rows], w_proj[...].reshape(units, width), NT)
            square = preact * preact
            bend = jnp.tanh(GELU_SCALE * preact * (1.0 + GELU_CUBE * square))
            gate = 0.5 + 0.5 * bend
            activated_ref[rows] = (preact * gate).astype(bf16)
            slope = gate + (0.5 * GELU_SCALE) * preact * (1.0 - bend * bend) * (
                1.0 + (3 * GELU_CUBE) * square
            )
            grad_preact = (slope * grad_act).astype(bf16)
            grad_preact_ref[rows] = grad_preact
            small_ref[pl.ds(BIAS_FC + step, 1), 0:units] += total(grad_preact.astype(f32))

        runner.at_step(step, len(chunks))
        grad_proj = matmul(cotangent_t_ref[...], activated_ref[...], NN).astype(bf16)
        for shard in range(shards):
            grad_proj_ref[step, shard] = grad_proj[:, shard * 128 : (shard + 1) * 128]
        runner.at_step(step, len(chunks) + 1)
        grad_fc = matmul(normed_t_ref[...], grad_preact_ref[...], NN).astype(bf16)
        grad_fc_ref[step] = grad_fc.reshape(grad_fc_ref.shape[1:])
        runner.at_step(step, len(chunks) + 2)
        mixed_ref[...] += matmul(activated_ref[...], w_proj[...].reshape(units, width), NN)
        runner.at_step(step, len(chunks) + 3)
        grad_normed_ref[...] += matmul(
            grad_preact_ref[...], w_fc[...].reshape(width, units), NT
        )

    hand_over = []

    def hand(source, target):
        copy = pltpu.make_async_copy(source, target, load_sem.at[len(hand_over)])
        copy.start()
        hand_over.append(copy)

    hand(grad_fc_ref.at[summed:blocks], last_fc_ref)
    hand(grad_proj_ref.at[summed:blocks], last_proj_ref)
    runner.do(E0)

    @pl.loop(0, len(chunks))
    def _(number):
        rows = chunk(number)
        middle = middle_ref[rows]
        layer_ref[rows] = (middle + mixed_ref[rows] + row(BIAS_PROJ)).astype(bf16)
        norm, inverse = normalized(middle)
        grad_normed = grad_normed_ref[rows]
        cotangent = cotangent_ref[rows].astype(f32)
        grad_middle = cotangent + norm_pull(grad_normed, row(GAIN2), norm, inverse)
        middle_ref[rows] = grad_middle
        normed_ref[rows] = grad_middle.astype(bf16)
        terms = (grad_middle, grad_normed * norm, grad_normed, cotangent)
        for at, term in zip((BIAS_OUT, GAIN2, SHIFT2, BIAS_PROJ), terms):
            small_ref[at : at + 1, 0:width] += total(term)

    runner.do(E1)
    hand(middle_ref, grad_middle_ref)
    hand(layer_ref, layer_out_ref)
    runner.do(E2)
    grad_branch = normed_ref[...]
    grad_out = matmul(attended_t_ref[...], grad_branch, NN).astype(bf16)
    grad_out_ref[...] = grad_out.reshape(grad_out_ref.shape)
    hand(grad_out_ref, grad_out_out_ref)
    runner.do(E3)
    grad_attended_ref[...] = matmul(grad_branch, w_out, NT).astype(bf16)
    hand(grad_attended_ref, grad_attended_out_ref)
    runner.do(END)
    for copy in hand_over:
        copy.wait()
    for item in sums:
        item.drain()
    for at in range(len(own)):
        gather.drain(at)


def backward_kernel(
    tokens_ref,
    segment_ref,
    params_ref,
    w_qkv_ref,
    projected_ref,
    attended_t_ref,
    lse_ref,
    grad_attended_ref,
    grad_middle_ref,
    small_in_ref,
    grad_tokens_ref,
    grad_w_qkv_ref,
    small_ref,
    mask_ref,
    wide_t_ref,
    grad_queries_t_ref,
    dots_ref,
    grad_projected_ref,
    grad_keys_ref,
    grad_values_ref,
):
    length, width = tokens_ref.shape
    build_mask(segment_ref, mask_ref)
    dot_rows(attended_t_ref, grad_attended_ref, wide_t_ref, dots_ref)
    wide_t_ref[...] = jnp.transpose(projected_ref[:, width : 2 * width])

    pairs = width // (2 * HEAD)

    @pl.loop(0, pairs)
    def _(pair):
        parts = [projected_ref[:, block(k * pairs + pair, 2 * HEAD)] for k in range(3)]
        attend_backward(
            pair,
            parts + [grad_attended_ref[:, block(pair, 2 * HEAD)]],
            wide_t_ref,
            mask_ref,
            lse_ref,
            dots_ref,
            grad_queries_t_ref,
            grad_keys_ref,
            grad_values_ref,
        )
        for k, ref in ((1, grad_keys_ref), (2, grad_values_ref)):
            grad_projected_ref[:, block(k * pairs + pair, 2 * HEAD)] = ref[...].astype(bf16)

    grad_projected_ref[:, 0:width] = jnp.transpose(grad_queries_t_ref[...])
    normed_transposed(tokens_ref, params_ref, wide_t_ref)
    small_ref[...] = small_in_ref[...]
    bias_sums(grad_projected_ref, small_ref)
    grad_w_qkv_ref[...] = matmul(wide_t_ref[...], grad_projected_ref[...], NN).astype(bf16)
    gain_sum = shift_sum = 0.0
    for at in range(0, length, ROW_CHUNK):
        gain_part, shift_part = token_rows(
            slice(at, at + ROW_CHUNK),
            tokens_ref,
            params_ref,
            matmul(grad_projected_ref[at : at + ROW_CHUNK], w_qkv_ref[...], NT),
            grad_middle_ref[at : at + ROW_CHUNK],
            grad_tokens_ref,
        )
        gain_sum, shift_sum = gain_sum + gain_part, shift_sum + shift_part
    small_ref[GAIN1 : GAIN1 + 1, :] = gain_sum
    small_ref[SHIFT1 : SHIFT1 + 1, :] = shift_sum


def dot_rows(attended_t_ref, grad_attended_ref, wide_t_ref, dots_ref):
    wide_t_ref[...] = jnp.transpose(grad_attended_ref[...])
    for head in range(wide_t_ref.shape[0] // HEAD):
        rows = slice(head * HEAD, (head + 1) * HEAD)
        dots_ref[head : head + 1, :] = total(
            wide_t_ref[rows].astype(f32) * attended_t_ref[rows].astype(f32)
        )


def normed_transposed(tokens_ref, params_ref, wide_t_ref):
    width = tokens_ref.shape[1]
    row = lambda at: params_ref[at : at + 1, 0:width]

    @pl.loop(0, tokens_ref.shape[0] // ROW_CHUNK)
    def _(number):
        norm, _ = normalized(tokens_ref[chunk(number)].astype(f32))
        normed = (norm * row(GAIN1) + row(SHIFT1)).astype(bf16)
        wide_t_ref[:, chunk(number)] = jnp.transpose(normed)


def bias_sums(grad_projected_ref, small_ref):
    width = small_ref.shape[1]
    for at, part in ((BIAS_Q, 0), (BIAS_V, 2)):
        values = grad_projected_ref[:, part * width : (part + 1) * width]
        small_ref[at : at + 1, :] = total(values.astype(f32))


def token_rows(rows, tokens_ref, params_ref, grad_normed, middle, grad_tokens_ref):
    gain = params_ref[GAIN1 : GAIN1 + 1, 0 : tokens_ref.shape[1]]
    norm, inverse = normalized(tokens_ref[rows].astype(f32))
    grad_rows = norm_pull(grad_normed, gain, norm, inverse)
    grad_tokens_ref[rows] = (middle + grad_rows).astype(bf16)
    return total(grad_normed * norm), total(grad_normed)


def sum_backward_kernel(
    shards,
    tokens_in_ref,
    segment_ref,
    params_ref,
    attended_t_in_ref,
    lse_ref,
    grad_attended_in_ref,
    small_in_ref,
    projected_in_ref,
    w_qkv_in_ref,
    grad_middle_in_ref,
    grad_out_in_ref,
    grad_fc_in_ref,
    grad_proj_in_ref,
    grad_tokens_out_ref,
    done_qkv_ref,
    done_out_ref,
    done_fc_ref,
    done_proj_ref,
    own_small_ref,
    mask_ref,
    wide_t_ref,
    normed_t_ref,
    grad_queries_t_ref,
    dots_ref,
    projected_ref,
    grad_projected_ref,
    grad_keys_ref,
    grad_values_ref,
    grad_qkv_ref,
    grad_out_ref,
    grad_fc_ref,
    grad_proj_ref,
    weights_ref,
    tokens_ref,
    attended_t_ref,
    grad_attended_ref,
    grad_tokens_ref,
    *rest,
):
    length, width = tokens_ref.shape
    groups = width // GROUP
    late_blocks = grad_fc_ref.shape[0]
    items = 2 * late_blocks + 1 + groups
    buffers, rest = [rest[SUM_BUFFERS * k :][:SUM_BUFFERS] for k in range(items)], rest[
        SUM_BUFFERS * items :
    ]
    small_ref, parts_ref, core_parts_ref, far_parts_ref, side_parts_ref, line_parts_ref, *rest = rest
    send_sem, recv_sem, load_sem, small_send_sem, small_recv_sem = rest
    place = Place(shards)
    lines = place.lines
    arrays = []
    for number in range(late_blocks):
        arrays += [
            (grad_proj_ref.at[number], done_proj_ref.at[number], grad_proj_in_ref.at[number]),
            (grad_fc_ref.at[number], done_fc_ref.at[number], grad_fc_in_ref.at[number]),
        ]
    arrays.append((grad_out_ref, done_out_ref, grad_out_in_ref))
    arrays += [(grad_qkv_ref.at[g], done_qkv_ref.at[g], None) for g in range(groups)]
    sums = [
        Summed(
            place,
            grad,
            done,
            buffers[k],
            send_sem.at[k],
            recv_sem.at[k],
            source,
            None if source is None else load_sem.at[k],
        )
        for k, (grad, done, source) in enumerate(arrays)
    ]
    runner = Runner(BACKWARD_PLAN, None, sums)
    load_projected = pltpu.make_async_copy(projected_in_ref, projected_ref, load_sem.at[items])
    load_projected.start()
    inputs = [
        pltpu.make_async_copy(source, target, load_sem.at[items + 2 + number])
        for number, (source, target) in enumerate(
            (
                (attended_t_in_ref, attended_t_ref),
                (grad_attended_in_ref, grad_attended_ref),
                (tokens_in_ref, tokens_ref),
            )
        )
    ]
    for copy in inputs:
        copy.start()
    load_weights = pltpu.make_async_copy(w_qkv_in_ref, weights_ref, load_sem.at[items + 1])
    load_weights.start()
    place.meet(
        [place.peer(hop, 0) for hop in range(1, lines)]
        + [place.peer(0, 1), place.across(), place.sibling()]
    )
    runner.do(B0)
    build_mask(segment_ref, mask_ref)
    runner.do(B1)
    for copy in inputs:
        copy.wait()
    dot_rows(attended_t_ref, grad_attended_ref, wide_t_ref, dots_ref)
    runner.do(B2)
    normed_transposed(tokens_ref, params_ref, normed_t_ref)
    small_ref[...] = small_in_ref[...]
    parts_ref[...] = jnp.zeros_like(parts_ref)
    load_projected.wait()
    for g in range(groups):
        wide_t_ref[g * GROUP : (g + 1) * GROUP] = jnp.transpose(
            projected_ref[g, :, GROUP : 2 * GROUP]
        )
    runner.do(B3)

    @pl.loop(0, 2 * groups)
    def _(pair):
        g, odd = pair // 2, pair % 2
        parts = [projected_ref[g, :, block(2 * k + odd, 2 * HEAD)] for k in range(3)]
        attend_backward(
            pair,
            parts + [grad_attended_ref[:, block(pair, 2 * HEAD)]],
            wide_t_ref,
            mask_ref,
            lse_ref,
            dots_ref,
            grad_queries_t_ref,
            grad_keys_ref,
            grad_values_ref,
            lambda number: runner.at_step(pair, number),
        )
        grad_queries = jnp.transpose(grad_queries_t_ref[block(pair, 2 * HEAD), :])
        grad_projected_ref[g, :, block(odd, 2 * HEAD)] = grad_queries
        for k, ref in ((1, grad_keys_ref), (2, grad_values_ref)):
            grad_projected_ref[g, :, block(2 * k + odd, 2 * HEAD)] = ref[...].astype(bf16)

        @pl.when(odd == 1)
        def _():
            grad_group = matmul(normed_t_ref[...], grad_projected_ref[g], NN).astype(bf16)
            grad_qkv_ref[g] = grad_group.reshape(grad_qkv_ref.shape[1:])

    middle_ref = mask_ref.at[:, 0:width]
    load_middle = pltpu.make_async_copy(grad_middle_in_ref, middle_ref, load_sem.at[items])
    load_middle.start()
    for g in range(groups):
        part = slice(g * GROUP, (g + 1) * GROUP)
        for at, k in ((BIAS_Q, 0), (BIAS_V, 2)):
            values = grad_projected_ref[g, :, k * GROUP : (k + 1) * GROUP]
            small_ref[at : at + 1, part] = total(values.astype(f32))
    load_weights.wait()
    load_middle.wait()
    table = {k: BACKWARD_PLAN.get(E0 + k, ()) for k in range(length // ROW_CHUNK)}

    @pl.loop(0, length // ROW_CHUNK)
    def _(number):
        runner.on(number, table)
        rows = chunk(number)
        grad_normed = 0.0
        for g in range(groups):
            weights = weights_ref[g].reshape(width, 3 * GROUP)
            grad_normed = grad_normed + matmul(grad_projected_ref[g, rows], weights, NT)
        gain_part, shift_part = token_rows(
            rows, tokens_ref, params_ref, grad_normed, mask_ref[rows, 0:width], grad_tokens_ref
        )
        small_ref[GAIN1 : GAIN1 + 1, 0:width] += gain_part
        small_ref[SHIFT1 : SHIFT1 + 1, 0:width] += shift_part

    leave = pltpu.make_async_copy(grad_tokens_ref, grad_tokens_out_ref, load_sem.at[items])
    leave.start()
    own = width // shards
    for shard in range(shards):
        into = parts_ref.at[shard // 2, shard % 2]
        into[0:8, 0:own] = small_ref[0:8, shard * own : (shard + 1) * own]
        into[8:16, :] = small_ref[8:16, shard * 128 : (shard + 1) * 128]

    def exchange(slot, source, into, peer):
        copy = remote(source, into, small_send_sem.at[slot], small_recv_sem.at[slot], peer)
        copy.start()
        return copy

    line, side = place.line, place.side
    todo = BACKWARD_PLAN.get(END, ())
    portions = [todo[len(todo) * k // 5 : len(todo) * (k + 1) // 5] for k in range(5)]
    copy = exchange(0, parts_ref, core_parts_ref, place.sibling())
    runner.act(portions[0])
    copy.wait()
    parts_ref[...] += core_parts_ref[...]
    copy = exchange(1, parts_ref, far_parts_ref, place.across())
    runner.act(portions[1])
    copy.wait()
    parts_ref[...] += far_parts_ref[...]
    copy = exchange(2, parts_ref.at[:, 1 - side], side_parts_ref, place.peer(0, 1))
    runner.act(portions[2])
    copy.wait()
    parts_ref[:, side] += side_parts_ref[...]
    copies = [
        exchange(
            2 + hop,
            parts_ref.at[flip(line, hop), side],
            line_parts_ref.at[hop - 1],
            place.peer(hop, 0),
        )
        for hop in range(1, lines)
    ]
    runner.act(portions[3] + portions[4])
    for copy in copies:
        copy.wait()
    small = parts_ref[line, side]
    for hop in range(1, lines):
        small = small + line_parts_ref[hop - 1]
    own_small_ref[...] = small
    leave.wait()
    for item in sums:
        item.drain()


def finish_kernel(
    shards,
    qkv_ref,
    out_ref,
    fc_early_ref,
    fc_last_ref,
    proj_early_ref,
    proj_last_ref,
    small_ref,
    layer_in_ref,
    tokens_in_ref,
    sum_qkv_ref,
    sum_out_ref,
    sum_fc_ref,
    sum_proj_ref,
    layer_out_ref,
    grad_tokens_ref,
    *rest,
):
    *vector_refs, fc_bias_ref, copy_sem = rest
    copies = [
        pltpu.make_async_copy(source, target, copy_sem.at[k])
        for k, (source, target) in enumerate(
            ((layer_in_ref, layer_out_ref), (tokens_in_ref, grad_tokens_ref))
        )
    ]
    for copy in copies:
        copy.start()
    groups, own, _ = qkv_ref.shape
    width = groups * GROUP
    for g in range(groups):
        for part in range(3):
            start = part * width + g * GROUP
            sum_qkv_ref[:, start : start + GROUP] = qkv_ref[
                g, :, part * GROUP : (part + 1) * GROUP
            ].astype(f32)
    sum_out_ref[...] = out_ref[...].astype(f32)
    early = fc_early_ref.shape[0]
    blocks = early + fc_last_ref.shape[0]
    for number in range(blocks):
        fc = fc_early_ref.at[number] if number < early else fc_last_ref.at[number - early]
        proj = proj_early_ref.at[number] if number < early else proj_last_ref.at[number - early]
        for shard in range(shards):
            start = (shard * blocks + number) * 128
            sum_fc_ref[:, start : start + 128] = fc[:, shard * 128 : (shard + 1) * 128].astype(f32)
        sum_proj_ref[number * 128 : (number + 1) * 128] = jnp.transpose(proj[...].astype(f32))
    for at, vector_ref in enumerate(vector_refs):
        vector_ref[...] = small_ref[at, 0:own]
    for number in range(blocks):
        fc_bias_ref[number * 128 : (number + 1) * 128] = small_ref[BIAS_FC + number, :]
    for copy in copies:
        copy.wait()


def kernel_params():
    return pltpu.CompilerParams(vmem_limit_bytes=VMEM_LIMIT)


def run_forward(tokens, segment, params, w_qkv):
    length, width = tokens.shape
    return pl.pallas_call(
        forward_kernel,
        in_specs=[WHOLE] * 4,
        out_specs=(WHOLE,) * 3,
        out_shape=(
            jax.ShapeDtypeStruct((length, 3 * width), bf16),
            jax.ShapeDtypeStruct((width, length), bf16),
            jax.ShapeDtypeStruct((16, length), f32),
        ),
        scratch_shapes=[
            pltpu.VMEM((length, length), f32),
            pltpu.VMEM((length, width), bf16),
            pltpu.VMEM((width, length), bf16),
        ],
        compiler_params=kernel_params(),
        name="forward",
    )(tokens, segment, params, w_qkv)


def run_hidden(attended_t, tokens, cotangent, params, w_out, w_fc, w_proj, piece):
    length, width = tokens.shape
    hidden = w_fc.shape[1]
    shape = jax.ShapeDtypeStruct
    columns = pl.BlockSpec((width, width), lambda step: (0, step))
    return pl.pallas_call(
        hidden_kernel,
        grid=(hidden // width,),
        in_specs=[WHOLE] * 5 + [columns, pl.BlockSpec((width, width), lambda step: (step, 0))],
        out_specs=(
            WHOLE,
            WHOLE,
            WHOLE,
            WHOLE,
            columns,
            pl.BlockSpec((width // piece, width, piece), lambda step: (step, 0, 0)),
            WHOLE,
        ),
        out_shape=(
            shape((length, width), bf16),
            shape((length, width), f32),
            shape((length, width), bf16),
            shape((width, width), bf16),
            shape((width, hidden), bf16),
            shape((hidden // piece, width, piece), bf16),
            shape((16, width), f32),
        ),
        scratch_shapes=[
            pltpu.VMEM((length, width), f32),
            pltpu.VMEM((length, width), bf16),
            pltpu.VMEM((width, length), bf16),
            pltpu.VMEM((width, length), bf16),
            pltpu.VMEM((length, width), f32),
            pltpu.VMEM((length, width), f32),
            pltpu.VMEM((length, width), bf16),
            pltpu.VMEM((length, width), bf16),
        ],
        compiler_params=kernel_params(),
        name="hidden",
    )(attended_t, tokens, cotangent, params, w_out, w_fc, w_proj)


def run_backward(
    tokens, segment, params, w_qkv, projected, attended_t, lse, grad_attended, grad_middle, small
):
    length, width = tokens.shape
    shape = jax.ShapeDtypeStruct
    return pl.pallas_call(
        backward_kernel,
        in_specs=[WHOLE] * 10,
        out_specs=(WHOLE,) * 3,
        out_shape=(
            shape((length, width), bf16),
            shape((width, 3 * width), bf16),
            shape((16, width), f32),
        ),
        scratch_shapes=[
            pltpu.VMEM((length, length), f32),
            pltpu.VMEM((width, length), bf16),
            pltpu.VMEM((width, length), bf16),
            pltpu.VMEM((16, length), f32),
            pltpu.VMEM((length, 3 * width), bf16),
            pltpu.VMEM((length, 2 * HEAD), f32),
            pltpu.VMEM((length, 2 * HEAD), f32),
        ],
        compiler_params=kernel_params(),
        name="backward",
    )(
        tokens,
        segment,
        params,
        w_qkv,
        projected,
        attended_t,
        lse,
        grad_attended,
        grad_middle,
        small,
    )


def link_params(number):
    return pltpu.CompilerParams(
        vmem_limit_bytes=VMEM_LIMIT, collective_id=number, has_side_effects=True
    )


def run_gather_forward(
    shards, span, tokens, segment, own_params, w_qkv, w_out, w_fc, w_proj
):
    length, width = tokens.shape
    own = w_qkv.shape[0]
    groups = width // GROUP
    blocks = GATHERED_EARLY
    items = groups + 1 + 2 * blocks
    shape = jax.ShapeDtypeStruct
    copies = 3 * shards - 3
    dma = pltpu.SemaphoreType.DMA
    return pl.pallas_call(
        partial(gather_forward_kernel, shards),
        in_specs=[WHOLE] * 3 + [HBM] * 4,
        out_specs=(HBM,) + (WHOLE,) * 3 + (HBM,) * 4,
        out_shape=(
            shape((groups, length, 3 * GROUP), bf16),
            shape((width, length), bf16),
            shape((16, length), f32),
            shape((own_params.shape[0], span), f32),
            shape((groups, shards, own, 3 * GROUP), bf16),
            shape((shards, own, width), bf16),
            shape((blocks, shards, own, shards * 128), bf16),
            shape((blocks, shards, 128, width), bf16),
        ),
        scratch_shapes=[
            pltpu.VMEM((length, length), f32),
            pltpu.VMEM((length, width), bf16),
            pltpu.VMEM((width, length), bf16),
            pltpu.VMEM((groups, length, 3 * GROUP), bf16),
            pltpu.VMEM((groups, shards, own, 3 * GROUP), bf16),
            pltpu.VMEM((shards,) + own_params.shape, bf16),
            pltpu.VMEM((groups, own, 3 * GROUP), bf16),
            pltpu.VMEM((blocks, own, shards * 128), bf16),
            pltpu.VMEM((own, width), bf16),
            pltpu.VMEM((blocks * 128, width), bf16),
            dma((items, copies)),
            dma((items, copies)),
            dma((items,)),
            dma((shards - 1,)),
            dma((shards - 1,)),
            dma((groups + blocks + 2,)),
            dma((groups, 2)),
        ],
        compiler_params=link_params(0),
        name="gather_forward",
    )(tokens, segment, own_params, w_qkv, w_out, w_fc, w_proj)


def run_sum_hidden(
    shards, attended_t, tokens, cotangent, params, full_out, full_fc, full_proj, w_fc, w_proj
):
    length, width = tokens.shape
    own, units = w_fc.shape[0], shards * 128
    blocks = w_proj.shape[0] // 128
    lines = shards // 2
    shape = jax.ShapeDtypeStruct
    dma = pltpu.SemaphoreType.DMA
    grads = ((shards, own, units), (shards, width, 128))
    late, early = blocks - full_fc.shape[0], SUMMED_EARLY
    buffers = [
        ref
        for _ in range(early)
        for grad in reversed(grads)
        for ref in sum_buffers(lines, *grad)
    ]
    return pl.pallas_call(
        partial(sum_hidden_kernel, shards),
        in_specs=[HBM] * 3 + [WHOLE] + [HBM] * 5,
        out_specs=(HBM,) * 6 + (WHOLE,) * 3,
        out_shape=(
            shape((length, width), bf16),
            shape((length, width), f32),
            shape((length, width), bf16),
            shape((shards, own, width), bf16),
            shape((blocks - early,) + grads[0], bf16),
            shape((blocks - early,) + grads[1], bf16),
            shape((early, own, units), bf16),
            shape((early, width, 128), bf16),
            shape(params.shape, f32),
        ),
        scratch_shapes=[
            pltpu.VMEM((length, width), f32),
            pltpu.VMEM((length, width), bf16),
            pltpu.VMEM((width, length), bf16),
            pltpu.VMEM((width, length), bf16),
            pltpu.VMEM((length, width), f32),
            pltpu.VMEM((length, width), f32),
            pltpu.VMEM((length, units), bf16),
            pltpu.VMEM((length, units), bf16),
            pltpu.VMEM((blocks, shards, own, units), bf16),
            pltpu.VMEM((blocks, shards, 128, width), bf16),
            pltpu.VMEM((blocks,) + grads[0], bf16),
            pltpu.VMEM((blocks,) + grads[1], bf16),
            pltpu.VMEM((late, own, units), bf16),
            pltpu.VMEM((width, length), bf16),
            pltpu.VMEM((length, width), bf16),
            pltpu.VMEM((length, width), bf16),
            pltpu.VMEM((shards, own, width), bf16),
            pltpu.VMEM((length, width), bf16),
            pltpu.VMEM((length, width), bf16),
            pltpu.VMEM((shards, own, width), bf16),
        ]
        + buffers
        + [
            dma((2 * late, 3 * shards - 3)),
            dma((2 * late, 3 * shards - 3)),
            dma((2 * late,)),
            dma((2 * blocks + 4,)),
        ]
        + sum_sems(lines, 2 * early),
        compiler_params=link_params(1),
        name="sum_hidden",
    )(attended_t, tokens, cotangent, params, full_out, full_fc, full_proj, w_fc, w_proj)


def run_sum_backward(
    shards,
    tokens,
    segment,
    params,
    attended_t,
    lse,
    grad_attended,
    small,
    projected,
    w_qkv,
    grad_middle,
    grad_out,
    grad_fc,
    grad_proj,
):
    length, width = tokens.shape
    shape = jax.ShapeDtypeStruct
    lines, groups = shards // 2, width // GROUP
    own = width // shards
    qkv = (shards, own, 3 * GROUP)
    late_blocks = grad_fc.shape[0]
    grads = [grad_proj.shape[1:], grad_fc.shape[1:]] * late_blocks
    grads += [grad_out.shape] + [qkv] * groups
    buffers = [ref for grad in grads for ref in sum_buffers(lines, *grad)]
    parts = pltpu.VMEM((lines, 2, 16, 128), f32)
    dma = pltpu.SemaphoreType.DMA
    items = len(grads)
    return pl.pallas_call(
        partial(sum_backward_kernel, shards),
        in_specs=[HBM, WHOLE, WHOLE, HBM, WHOLE, HBM, WHOLE] + [HBM] * 6,
        out_specs=(HBM,) + (WHOLE,) * 5,
        out_shape=(
            shape((length, width), bf16),
            shape((groups,) + qkv[1:], bf16),
            shape(grad_out.shape[1:], bf16),
            shape((late_blocks,) + grad_fc.shape[2:], bf16),
            shape((late_blocks,) + grad_proj.shape[2:], bf16),
            shape((16, 128), f32),
        ),
        scratch_shapes=[
            pltpu.VMEM((length, length), f32),
            pltpu.VMEM((width, length), bf16),
            pltpu.VMEM((width, length), bf16),
            pltpu.VMEM((width, length), bf16),
            pltpu.VMEM((16, length), f32),
            pltpu.VMEM(projected.shape, bf16),
            pltpu.VMEM(projected.shape, bf16),
            pltpu.VMEM((length, 2 * HEAD), f32),
            pltpu.VMEM((length, 2 * HEAD), f32),
            pltpu.VMEM((groups,) + qkv, bf16),
            pltpu.VMEM(grad_out.shape, bf16),
            pltpu.VMEM(grad_fc.shape, bf16),
            pltpu.VMEM(grad_proj.shape, bf16),
            pltpu.VMEM(w_qkv.shape, bf16),
            pltpu.VMEM((length, width), bf16),
            pltpu.VMEM((width, length), bf16),
            pltpu.VMEM((length, width), bf16),
            pltpu.VMEM((length, width), bf16),
        ]
        + buffers
        + [pltpu.VMEM(params.shape, f32), parts, parts, parts]
        + [pltpu.VMEM((lines, 16, 128), f32), pltpu.VMEM((lines - 1, 16, 128), f32)]
        + sum_sems(lines, items)
        + [dma((items + 5,)), dma((lines + 2,)), dma((lines + 2,))],
        compiler_params=link_params(2),
        name="sum_backward",
    )(
        tokens,
        segment,
        params,
        attended_t,
        lse,
        grad_attended,
        small,
        projected,
        w_qkv,
        grad_middle,
        grad_out,
        grad_fc,
        grad_proj,
    )


def run_finish(
    shards, qkv, out, fc_early, fc_last, proj_early, proj_last, small, layer_out, grad_tokens
):
    groups, own, _ = qkv.shape
    width = out.shape[1]
    blocks = fc_early.shape[0] + fc_last.shape[0]
    shape = jax.ShapeDtypeStruct
    return pl.pallas_call(
        partial(finish_kernel, shards),
        in_specs=[WHOLE] * 9,
        out_specs=(WHOLE,) * 4 + (HBM,) * 2 + (WHOLE,) * 9,
        out_shape=(
            shape((own, 3 * width), f32),
            shape((own, width), f32),
            shape((own, blocks * shards * 128), f32),
            shape((blocks * 128, width), f32),
            shape(layer_out.shape, bf16),
            shape(grad_tokens.shape, bf16),
        )
        + (shape((own,), f32),) * 8
        + (shape((blocks * 128,), f32),),
        scratch_shapes=[pltpu.SemaphoreType.DMA((2,))],
        compiler_params=kernel_params(),
        name="finish",
    )(qkv, out, fc_early, fc_last, proj_early, proj_last, small, layer_out, grad_tokens)


def by_kernels(
    shards, tokens, segment_ids, vectors, fc_bias, w_qkv, w_out, w_fc, w_proj, cotangent
):
    width, hidden = tokens.shape[1], w_fc.shape[1]
    blocks, units = w_proj.shape[0] // 128, shards * 128
    span = max(width, units)
    rows = jnp.pad(jnp.stack(vectors), ((0, 0), (0, 128 - vectors[0].shape[0])))
    table = jnp.concatenate(
        [rows, jnp.pad(fc_bias.reshape(blocks, 128), ((0, 8 - blocks), (0, 0)))]
    )
    projected, attended_t, lse, params, full_qkv, full_out, full_fc, full_proj = (
        run_gather_forward(shards, span, tokens, segment_ids, table, w_qkv, w_out, w_fc, w_proj)
    )
    (
        layer_out,
        grad_middle,
        grad_attended,
        grad_out,
        grad_fc,
        grad_proj,
        fc_early,
        proj_early,
        small,
    ) = run_sum_hidden(
        shards, attended_t, tokens, cotangent, params, full_out, full_fc, full_proj, w_fc, w_proj
    )
    grad_tokens, done_qkv, done_out, fc_last, proj_last, small = run_sum_backward(
        shards,
        tokens,
        segment_ids,
        params,
        attended_t,
        lse,
        grad_attended,
        small,
        projected,
        full_qkv,
        grad_middle,
        grad_out,
        grad_fc,
        grad_proj,
    )
    sum_qkv, sum_out, sum_fc, sum_proj, layer_out, grad_tokens, *own_vectors = run_finish(
        shards,
        done_qkv,
        done_out,
        fc_early,
        fc_last,
        proj_early,
        proj_last,
        small,
        layer_out,
        grad_tokens,
    )
    pick = lambda at: own_vectors[at]
    return (
        layer_out,
        grad_tokens,
        pick(GAIN1),
        pick(SHIFT1),
        sum_qkv,
        pick(BIAS_Q),
        pick(BIAS_V),
        sum_out,
        pick(BIAS_OUT),
        pick(GAIN2),
        pick(SHIFT2),
        sum_fc,
        pick(BIAS_FC),
        sum_proj,
        pick(BIAS_PROJ),
    )


def on_device(
    replicas,
    shards,
    tokens,
    segment_ids,
    norm1_gain,
    norm1_shift,
    w_qkv,
    q_bias,
    v_bias,
    w_out,
    out_bias,
    norm2_gain,
    norm2_shift,
    w_fc,
    fc_bias,
    w_proj,
    proj_bias,
    cotangent,
):
    width, hidden = tokens.shape[1], w_fc.shape[1]
    vectors = (
        norm1_gain,
        norm1_shift,
        q_bias,
        v_bias,
        out_bias,
        norm2_gain,
        norm2_shift,
        proj_bias,
    )
    own, own_hidden = norm1_gain.shape[0], fc_bias.shape[0]
    if (
        replicas == 4
        and shards & (shards - 1) == 0
        and own % 96 == 0
        and own_hidden == 3 * 128
        and width == 3 * GROUP
    ):
        return by_kernels(
            shards, tokens, segment_ids, vectors, fc_bias, w_qkv, w_out, w_fc, w_proj, cotangent
        )
    me = lax.axis_index("shard")
    mine = (lax.broadcasted_iota(jnp.int32, (1, shards, 1), 1) == me).astype(bf16)
    table = jnp.concatenate(
        [
            (jnp.stack(vectors)[:, None, :] * mine).reshape(8, width),
            (fc_bias[None, None, :] * mine).reshape(hidden // width, width),
        ]
    )
    table = jnp.pad(table, ((0, 16 - table.shape[0]), (0, 0)))
    gather = partial(lax.all_gather, axis_name="shard", axis=0, tiled=True)
    params = lax.psum(table.astype(f32), "shard")
    full_qkv, full_out, full_fc, full_proj = (gather(w) for w in (w_qkv, w_out, w_fc, w_proj))
    projected, attended_t, lse = run_forward(tokens, segment_ids, params, full_qkv)
    (
        layer_out,
        grad_middle,
        grad_attended,
        grad_w_out,
        grad_w_fc,
        grad_w_proj_t,
        small,
    ) = run_hidden(attended_t, tokens, cotangent, params, full_out, full_fc, full_proj, width)
    grad_tokens, grad_w_qkv, small = run_backward(
        tokens,
        segment_ids,
        params,
        full_qkv,
        projected,
        attended_t,
        lse,
        grad_attended,
        grad_middle,
        small,
    )

    def reduced(grad):
        own_sum = lax.psum_scatter(grad.astype(f32), "shard", scatter_dimension=0, tiled=True)
        return lax.psum(own_sum.astype(bf16), "rep").astype(f32)

    sum_proj = reduced(grad_w_proj_t.transpose(0, 2, 1).reshape(hidden, width))
    sum_fc, sum_out, sum_qkv = reduced(grad_w_fc), reduced(grad_w_out), reduced(grad_w_qkv)
    small = lax.psum(small, ("rep", "shard"))
    mine = lax.dynamic_slice_in_dim(small[:8], me * own, own, 1)
    hidden_rows = small[BIAS_FC : BIAS_FC + hidden // width].reshape(-1)
    mine_fc = lax.dynamic_slice_in_dim(hidden_rows, me * own_hidden, own_hidden, 0)
    return (
        layer_out,
        grad_tokens,
        mine[GAIN1],
        mine[SHIFT1],
        sum_qkv,
        mine[BIAS_Q],
        mine[BIAS_V],
        sum_out,
        mine[BIAS_OUT],
        mine[GAIN2],
        mine[SHIFT2],
        sum_fc,
        mine_fc,
        sum_proj,
        mine[BIAS_PROJ],
    )


def solution(mesh):
    rows, own, own_rows = P(("rep", "shard"), None), P("shard"), P("shard", None)
    in_specs = (
        rows,
        rows,
        own,
        own,
        own_rows,
        own,
        own,
        own_rows,
        own,
        own,
        own,
        own_rows,
        own,
        own_rows,
        own,
        rows,
    )
    out_specs = (
        rows,
        rows,
        own,
        own,
        own_rows,
        own,
        own,
        own_rows,
        own,
        own,
        own,
        own_rows,
        own,
        own_rows,
        own,
    )
    sizes = mesh.shape["rep"], mesh.shape["shard"]
    return jax.shard_map(
        partial(on_device, *sizes), mesh=mesh, in_specs=in_specs, out_specs=out_specs, check_vma=False
    )
```
